256 devices in a mesh: seq: 32 (over z_lo, x, core), tp: 8 (over y, z_hi).
Axes of the slice: x: 4, y: 4, z: 8 (z_hi: 2, z_lo: 4; z = z_hi * 4 + z_lo), core: 2. Of those that a mesh axis runs over, the one named last changes fastest.
Arguments:
- hidden: bfloat16 [8192, 7168], P('seq', 'tp'), may hold values from -6 to 6
- norm_gain: bfloat16 [7168], replicated, may hold values from 0.5 to 1.5
- w_query: bfloat16 [7168, 4096], P(None, 'tp'), may hold values from -0.0625 to 0.0625
- w_key: bfloat16 [7168, 1024], P(None, 'tp'), may hold values from -0.0625 to 0.0625
- w_value: bfloat16 [7168, 1024], P(None, 'tp'), may hold values from -0.0625 to 0.0625
- prefix_keys: bfloat16 [8192, 1024], P('seq', 'tp'), may hold values from -64 to 64
- prefix_values: bfloat16 [8192, 1024], P('seq', 'tp'), may hold values from -6 to 6
- page_prefix: int32 [64], replicated, may hold values from 0 to 3, as said below
- request_prefix: int32 [32], replicated, may hold values from 0 to 3
- suffix_lengths: int32 [32], replicated, may hold values from 1 to 1024, 8192 in all
- row_order: int32 [8192], replicated, may hold values from 0 to 8191, as said below
Outputs:
- attended: bfloat16 [8192, 4096], P('seq', 'tp')
- suffix_keys: bfloat16 [8192, 1024], P('seq', 'tp')
- suffix_values: bfloat16 [8192, 1024], P('seq', 'tp')
The draws below stay inside these ranges and needn't reach their ends.
Inputs may be any that keep to these rules, and one draw needn't show every extreme that they name: `page_prefix`: each of the 4 prefixes owns exactly 16 pages. `suffix_lengths`: the lengths sum to 8192; the longest is exactly 1024. `row_order`: a permutation of 0 to 8191 made of aligned runs of 128 consecutive values.
All inputs are finite; a program needn't handle non-finite values.
Results may differ from the reference program's by a relative error of at most 0.0075.
The reference program's roundings to bfloat16 on the way (of `normed`, `queries` and `rounded`) count: a program that leaves them out, or rounds other values in their place, can miss the bound.
Values may be sent and summed in bfloat16 or wider, within the bound.
A program may use at most 128 MiB of HBM per device.

```python
import math
import jax
import jax.numpy as jnp
import numpy as np
from jax import lax

D = 7168
QH = 32
KVH = 8
HEAD = 128
PAGE = 128
PREFIXES = 4
REQUESTS = 32
BLOCK = 128
GROUP = 4
SUF_TOTAL = 8192
PAGES = 64
PREF_TOK = 2048
LONGEST = 1024


def draw_row_order(key, part):
    runs = jax.random.permutation(key, SUF_TOTAL // BLOCK)
    spread = runs[:, None] * BLOCK + jnp.arange(BLOCK)[None, :]
    return spread.reshape(-1).astype(jnp.int32)


def draw_page_prefix(key, part):
    shuffled = jax.random.permutation(key, PAGES)
    return (shuffled // (PAGES // PREFIXES)).astype(jnp.int32)


def draw_prefix_keys(key, part):
    row_count = PAGES * PAGE
    col_count = KVH * HEAD
    key_base = jax.random.fold_in(key, 11)
    base = jnp.clip(jax.random.normal(key_base, (row_count, col_count), jnp.float32), -4.0, 4.0)
    return base.astype(jnp.bfloat16)


def with_ends(drawn, rng, low, high):
    extent = drawn.shape
    place = [jax.random.randint(jax.random.fold_in(rng, axis), (), 0, extent[axis]) for axis in range(len(extent))]
    drawn = drawn.at[tuple(place)].set(low)
    longest = extent.index(max(extent))
    place[longest] = (place[longest] + 1) % extent[longest]
    return drawn.at[tuple(place)].set(high)


def level_of(key, dims, split, least, top_value):
    level, own = 1.0, jax.random.fold_in(key, 6)
    for dim, blocks in split:
        heights = jnp.exp(jax.random.uniform(jax.random.fold_in(own, dim), (blocks,), jnp.float32, least / len(split), top_value / len(split)))
        level = level * jnp.repeat(heights, dims[dim] // blocks).reshape([-1 if axis == dim else 1 for axis in range(len(dims))])
    return level


def profile(amount, total, most, skew):
    loads = [(1 << 20) // math.isqrt(rank ** skew) + 1 for rank in range(2, amount + 1)]
    surplus, given = total - most - (amount - 1), [1] * (amount - 1)
    while surplus > 0:
        movable = [i for i in range(amount - 1) if given[i] < most]
        mass, budget = sum([loads[i] for i in movable]), surplus
        for i in movable:
            addition = min(most - given[i], max(1, budget * loads[i] // mass), surplus)
            given[i] = given[i] + addition
            surplus = surplus - addition
    return np.array([most] + given)


def ragged(own_key, count, total, reach, slope):
    if count == 2:
        one = jax.random.randint(own_key, (), max(1, total - reach), min(reach, total - 1) + 1)
        return jnp.stack([one, total - one])
    tallies = jnp.asarray(profile(count, total, reach, slope), jnp.int32)
    twos = (count - 1) // 2
    giver, receiver = tallies[1:1 + 2 * twos:2], tallies[2:2 + 2 * twos:2]
    room = jnp.minimum(giver - 1, reach - receiver)
    shifted = jax.random.randint(jax.random.fold_in(own_key, 1), (twos,), 0, 1 << 20) % (room + 1)
    tallies = tallies.at[1:1 + 2 * twos:2].set(giver - shifted).at[2:2 + 2 * twos:2].set(receiver + shifted)
    return tallies[jax.random.permutation(jax.random.fold_in(own_key, 2), count)]


def centred(own_key, shape, scale, bound, cuts=(), kind=jnp.bfloat16):
    result = jax.random.normal(own_key, shape, jnp.float32) * scale
    if len(cuts) > 0:
        result = level_of(own_key, shape, cuts, -0.22, 0.18) * result
    return jnp.clip(result, min=-bound, max=bound).astype(kind)


def setup_inputs(seed: int = 0) -> dict:
    key_of = jax.random.split(jax.random.key(seed), 12)
    return {
        "hidden": centred(key_of[0], (SUF_TOTAL, D), 1.0, 6.0, ((0, 32), (1, 8))),
        "norm_gain": jnp.clip(1.0 + 0.1 * jax.random.normal(key_of[1], (D,), jnp.float32), 0.5, 1.5).astype(jnp.bfloat16),
        "w_query": centred(key_of[2], (D, QH * HEAD), D ** -0.5, 0.0625, ((1, 8),)),
        "w_key": centred(key_of[3], (D, KVH * HEAD), D ** -0.5, 0.0625, ((1, 8),)),
        "w_value": centred(key_of[4], (D, KVH * HEAD), D ** -0.5, 0.0625, ((1, 8),)),
        "prefix_keys": draw_prefix_keys(jax.random.fold_in(key_of[11], 71), 0),
        "prefix_values": centred(key_of[6], (PAGES * PAGE, KVH * HEAD), 1.0, 6.0, ((0, 32), (1, 8))),
        "page_prefix": draw_page_prefix(jax.random.fold_in(key_of[11], 71), 0),
        "request_prefix": with_ends(jax.random.randint(key_of[8], (REQUESTS,), 0, PREFIXES), jax.random.fold_in(key_of[8], 1), 0, PREFIXES - 1).astype(jnp.int32),
        "suffix_lengths": ragged(key_of[9], REQUESTS, SUF_TOTAL, LONGEST, 2).astype(jnp.int32),
        "row_order": draw_row_order(jax.random.fold_in(key_of[11], 71), 0),
    }


ROPE_BASE = 5000000.0

def rotate(tensor_in, positions):
    head_dim = tensor_in.shape[-1]
    half_dim = head_dim // 2
    frequency = ROPE_BASE ** (-(jnp.arange(half_dim, dtype=jnp.float32) * 2.0 / head_dim))
    angles = positions.astype(jnp.float32)[:, None] * frequency[None, :]
    cosine = jnp.cos(angles)[:, None, :]
    sine_part = jnp.sin(angles)[:, None, :]
    first_half = tensor_in[..., :half_dim]
    second_half = tensor_in[..., half_dim:]
    return jnp.concatenate([first_half * cosine - second_half * sine_part, second_half * cosine + first_half * sine_part], axis=-1)

def locate(row_order, suffix_lengths, request_prefix):
    end_rows = jnp.cumsum(suffix_lengths).astype(jnp.int32)
    starts = (end_rows - suffix_lengths).astype(jnp.int32)
    numbers = jnp.arange(suffix_lengths.shape[0], dtype=jnp.int32)
    request = lax.optimization_barrier(jnp.sum((row_order[:, None] >= end_rows[None, :]).astype(jnp.int32), axis=1)).astype(jnp.int32)
    chosen = request[:, None] == numbers[None, :]
    position = (row_order - lax.optimization_barrier(jnp.sum(jnp.where(chosen, starts[None, :], 0), axis=1))).astype(jnp.int32)
    wanted = lax.optimization_barrier(jnp.sum(jnp.where(chosen, request_prefix[None, :], 0), axis=1)).astype(jnp.int32)
    return (request, position, wanted)

def normalize(hidden, norm_gain):
    hidden_f = hidden.astype(jnp.float32)
    mean_sq = lax.optimization_barrier(jnp.mean(hidden_f * hidden_f, axis=1, keepdims=True))
    return (hidden_f * lax.rsqrt(mean_sq + 1e-05) * norm_gain.astype(jnp.float32)[None, :]).astype(jnp.bfloat16)

def reference(hidden, norm_gain, w_query, w_key, w_value, prefix_keys, prefix_values, page_prefix, request_prefix, suffix_lengths, row_order):
    total_rows = hidden.shape[0]
    normed = normalize(hidden, norm_gain)
    request, position, wanted = locate(row_order, suffix_lengths, request_prefix)
    rope_at = PREF_TOK + position
    queries = rotate(jnp.dot(normed, w_query, preferred_element_type=jnp.float32).reshape(total_rows, QH, HEAD), rope_at).astype(jnp.bfloat16)
    new_keys = rotate(jnp.dot(normed, w_key, preferred_element_type=jnp.float32).reshape(total_rows, KVH, HEAD), rope_at).astype(jnp.bfloat16)
    new_values = jnp.dot(normed, w_value, preferred_element_type=jnp.float32).astype(jnp.bfloat16)
    row_pages = jnp.repeat(page_prefix, PAGE).astype(jnp.int32)
    key_all = jnp.concatenate([prefix_keys.reshape(-1, KVH, HEAD), new_keys], axis=0).transpose(1, 0, 2)
    value_all = jnp.concatenate([prefix_values.reshape(-1, KVH, HEAD), new_values.reshape(total_rows, KVH, HEAD)], axis=0).transpose(1, 0, 2)
    block_rows = math.gcd(total_rows, 512)
    block_count = total_rows // block_rows
    query_heads = queries.reshape(total_rows, KVH, GROUP, HEAD).transpose(1, 0, 2, 3).reshape(KVH, block_count, block_rows, GROUP, HEAD)
    score_scale = 1.0 / math.sqrt(HEAD)

    def one_head(inputs):
        key_head, value_head, query_head = inputs
        key_f = key_head.astype(jnp.float32)
        value_f = value_head.astype(jnp.float32)

        def one_block(block_in):
            query_block, req_block, pos_block, want_block = block_in
            scores = jnp.einsum('tgd,kd->tgk', query_block.astype(jnp.float32), key_f) * score_scale
            see_pref = want_block[:, None] == row_pages[None, :]
            see_suf = (req_block[:, None] == request[None, :]) & (position[None, :] <= pos_block[:, None])
            visible = jnp.concatenate([see_pref, see_suf], axis=1)[:, None, :]
            row_max = lax.optimization_barrier(jnp.max(jnp.where(visible, scores, -1e+30), axis=-1))
            weights = jnp.where(visible, jnp.exp(scores - row_max[..., None]), 0.0)
            totals = lax.optimization_barrier(jnp.sum(weights, axis=-1))
            rounded = lax.optimization_barrier(weights.astype(jnp.bfloat16))
            summed = jnp.einsum('tgk,kd->tgd', rounded.astype(jnp.float32), value_f)
            return (summed / totals[..., None]).astype(jnp.bfloat16)
        return lax.map(one_block, (query_head, request.reshape(block_count, block_rows), position.reshape(block_count, block_rows), wanted.reshape(block_count, block_rows)))
    outputs = lax.map(one_head, (key_all, value_all, query_heads))
    attended = outputs.reshape(KVH, total_rows, GROUP, HEAD).transpose(1, 0, 2, 3).reshape(total_rows, QH * HEAD)
    return (attended, new_keys.reshape(total_rows, KVH * HEAD), new_values)
```

```python
import functools
import math

import jax
import jax.numpy as jnp
from jax import lax
from jax.sharding import PartitionSpec as P
from jax.experimental import pallas as pl
from jax.experimental.pallas import tpu as pltpu

HEAD = 128
PAGE = 128
PREFIXES = 4


ROPE_BASE = 5000000.0


def rotate(tensor_in, positions):
    head_dim = tensor_in.shape[-1]
    half_dim = head_dim // 2
    frequency = ROPE_BASE ** (-(jnp.arange(half_dim, dtype=jnp.float32) * 2.0 / head_dim))
    angles = positions.astype(jnp.float32)[:, None] * frequency[None, :]
    cosine = jnp.cos(angles)[:, None, :]
    sine_part = jnp.sin(angles)[:, None, :]
    first_half = tensor_in[..., :half_dim]
    second_half = tensor_in[..., half_dim:]
    return jnp.concatenate(
        [
            first_half * cosine - second_half * sine_part,
            second_half * cosine + first_half * sine_part,
        ],
        axis=-1,
    )


def locate(row_order, suffix_lengths, request_prefix):
    end_rows = jnp.cumsum(suffix_lengths)
    starts = end_rows - suffix_lengths
    numbers = jnp.arange(suffix_lengths.shape[0], dtype=jnp.int32)
    request = jnp.sum((row_order[:, None] >= end_rows[None, :]).astype(jnp.int32), axis=1)
    chosen = request[:, None] == numbers[None, :]
    position = row_order - jnp.sum(jnp.where(chosen, starts[None, :], 0), axis=1)
    wanted = jnp.sum(jnp.where(chosen, request_prefix[None, :], 0), axis=1)
    return (request, position, wanted)


def seq_gather_kernel(n, x_ref, o_ref, send_sem, recv_sem, local_sem):
    me = lax.axis_index("seq")
    parts = x_ref.shape[0]
    mesh_id = pl.DeviceIdType.MESH
    barrier = pltpu.get_barrier_semaphore()

    def greet(k, carry):
        peer = lax.rem(me + k, n)
        pl.semaphore_signal(barrier, inc=1, device_id={"seq": peer}, device_id_type=mesh_id)
        return carry

    lax.fori_loop(1, n, greet, 0)
    pl.semaphore_wait(barrier, n - 1)
    local = pltpu.make_async_copy(x_ref, o_ref.at[:, me], local_sem)
    local.start()

    def push(peer, sender, receiver):
        return [
            pltpu.make_async_remote_copy(
                src_ref=x_ref.at[a],
                dst_ref=o_ref.at[a, receiver],
                send_sem=send_sem.at[a, sender],
                recv_sem=recv_sem.at[a, receiver],
                device_id={"seq": peer},
                device_id_type=mesh_id,
            )
            for a in range(parts)
        ]

    def send(k, carry):
        peer = lax.rem(me + k, n)
        for copy in push(peer, peer, me):
            copy.start()
        return carry

    lax.fori_loop(1, n, send, 0)

    def finish(k, carry):
        peer = lax.rem(me + k, n)
        for copy in push(peer, peer, peer):
            copy.wait_send()
            copy.wait_recv()
        return carry

    lax.fori_loop(1, n, finish, 0)
    local.wait()


def seq_gather(stacked, n, cid):
    parts, rows, cols = stacked.shape
    return pl.pallas_call(
        functools.partial(seq_gather_kernel, n),
        out_shape=jax.ShapeDtypeStruct((parts, n, rows, cols), stacked.dtype),
        in_specs=[pl.BlockSpec(memory_space=pl.ANY)],
        out_specs=pl.BlockSpec(memory_space=pl.ANY),
        scratch_shapes=[
            pltpu.SemaphoreType.DMA((parts, n)),
            pltpu.SemaphoreType.DMA((parts, n)),
            pltpu.SemaphoreType.DMA,
        ],
        compiler_params=pltpu.CompilerParams(collective_id=cid, has_side_effects=True),
    )(stacked)


def body(
    seq_n,
    hidden,
    norm_gain,
    w_query,
    w_key,
    w_value,
    prefix_keys,
    prefix_values,
    page_prefix,
    request_prefix,
    suffix_lengths,
    row_order,
):
    gathered = lax.all_gather(hidden, "tp", axis=1, tiled=True)
    local_rows = gathered.shape[0]
    hidden_f = gathered.astype(jnp.float32)
    mean_sq = jnp.mean(hidden_f * hidden_f, axis=1, keepdims=True)
    normed = (
        hidden_f * lax.rsqrt(mean_sq + 1e-05) * norm_gain.astype(jnp.float32)[None, :]
    ).astype(jnp.bfloat16)
    request_all, position_all, wanted_all = locate(row_order, suffix_lengths, request_prefix)
    offset = lax.axis_index("seq") * local_rows
    request = lax.dynamic_slice_in_dim(request_all, offset, local_rows)
    position = lax.dynamic_slice_in_dim(position_all, offset, local_rows)
    wanted = lax.dynamic_slice_in_dim(wanted_all, offset, local_rows)
    prefix_len = page_prefix.shape[0] * PAGE // PREFIXES
    rope_at = prefix_len + position
    q_heads = w_query.shape[1] // HEAD
    kv_heads = w_key.shape[1] // HEAD
    group_size = q_heads // kv_heads
    queries = rotate(
        jnp.dot(normed, w_query, preferred_element_type=jnp.float32).reshape(
            local_rows, q_heads, HEAD
        ),
        rope_at,
    ).astype(jnp.bfloat16)
    queries = queries.reshape(local_rows, kv_heads, group_size, HEAD)
    new_keys = rotate(
        jnp.dot(normed, w_key, preferred_element_type=jnp.float32).reshape(
            local_rows, kv_heads, HEAD
        ),
        rope_at,
    ).astype(jnp.bfloat16)
    new_keys = new_keys.reshape(local_rows, kv_heads * HEAD)
    new_values = jnp.dot(normed, w_value, preferred_element_type=jnp.float32).astype(jnp.bfloat16)
    row_pages = jnp.repeat(page_prefix, PAGE)
    score_scale = 1.0 / math.sqrt(HEAD)
    initial = (
        jnp.full((kv_heads, local_rows, group_size), -1e30, jnp.float32),
        jnp.zeros((kv_heads, local_rows, group_size), jnp.float32),
        jnp.zeros((kv_heads, local_rows, group_size, HEAD), jnp.float32),
    )

    def attend(state, key_rows, value_rows, visible):
        row_count = key_rows.shape[0]
        block_width = math.gcd(row_count, 512)
        block_count = row_count // block_width
        key_blocks = key_rows.reshape(block_count, block_width, kv_heads, HEAD)
        value_blocks = value_rows.reshape(block_count, block_width, kv_heads, HEAD)
        mask_blocks = visible.reshape(local_rows, block_count, block_width).transpose(1, 0, 2)

        def step(carry_in, inputs):
            run_max, run_sum, run_acc = carry_in
            key_block, value_block, mask_block = inputs
            scores = (
                jnp.einsum("tngd,knd->ntgk", queries, key_block, preferred_element_type=jnp.float32)
                * score_scale
            )
            seen = mask_block[None, :, None, :]
            new_max = jnp.maximum(run_max, jnp.max(jnp.where(seen, scores, -1e30), axis=-1))
            weights = jnp.where(seen, jnp.exp(scores - new_max[..., None]), 0.0)
            fade = jnp.exp(run_max - new_max)
            run_sum = run_sum * fade + jnp.sum(weights, axis=-1)
            run_acc = run_acc * fade[..., None] + jnp.einsum(
                "ntgk,knd->ntgd",
                weights.astype(jnp.bfloat16),
                value_block,
                preferred_element_type=jnp.float32,
            )
            return ((new_max, run_sum, run_acc), None)

        result, unused = lax.scan(step, state, (key_blocks, value_blocks, mask_blocks))
        return result

    gathered_prefix = seq_gather(jnp.stack([prefix_keys, prefix_values]), seq_n, 0)
    key_rows = gathered_prefix[0].reshape(-1, kv_heads * HEAD)
    value_rows = gathered_prefix[1].reshape(-1, kv_heads * HEAD)
    visible = wanted[:, None] == row_pages[None, :]
    state = attend(initial, key_rows, value_rows, visible)
    gathered_suffix = seq_gather(jnp.stack([new_keys, new_values]), seq_n, 1)
    key_rows = gathered_suffix[0].reshape(-1, kv_heads * HEAD)
    value_rows = gathered_suffix[1].reshape(-1, kv_heads * HEAD)
    visible = (request[:, None] == request_all[None, :]) & (
        position_all[None, :] <= position[:, None]
    )
    state = attend(state, key_rows, value_rows, visible)
    run_max, run_sum, run_acc = state
    attended = (
        (run_acc / run_sum[..., None])
        .transpose(1, 0, 2, 3)
        .reshape(local_rows, q_heads * HEAD)
        .astype(jnp.bfloat16)
    )
    return (attended, new_keys, new_values)


def solution(mesh):
    return jax.shard_map(
        functools.partial(body, mesh.shape["seq"]),
        mesh=mesh,
        in_specs=(
            P("seq", "tp"),
            P(),
            P(None, "tp"),
            P(None, "tp"),
            P(None, "tp"),
            P("seq", "tp"),
            P("seq", "tp"),
            P(),
            P(),
            P(),
            P(),
        ),
        out_specs=(P("seq", "tp"), P("seq", "tp"), P("seq", "tp")),
        check_vma=False,
    )
```

```python
import functools
import math

import jax
import jax.numpy as jnp
from jax import lax
from jax.sharding import PartitionSpec as P
from jax.experimental import pallas as pl
from jax.experimental.pallas import tpu as pltpu

HEAD = 128
PAGE = 128
PREFIXES = 4


ROPE_BASE = 5000000.0


def rotate(tensor_in, positions):
    head_dim = tensor_in.shape[-1]
    half_dim = head_dim // 2
    frequency = ROPE_BASE ** (-(jnp.arange(half_dim, dtype=jnp.float32) * 2.0 / head_dim))
    angles = positions.astype(jnp.float32)[:, None] * frequency[None, :]
    cosine = jnp.cos(angles)[:, None, :]
    sine_part = jnp.sin(angles)[:, None, :]
    first_half = tensor_in[..., :half_dim]
    second_half = tensor_in[..., half_dim:]
    return jnp.concatenate(
        [
            first_half * cosine - second_half * sine_part,
            second_half * cosine + first_half * sine_part,
        ],
        axis=-1,
    )


def locate(row_order, suffix_lengths, request_prefix):
    end_rows = jnp.cumsum(suffix_lengths)
    starts = end_rows - suffix_lengths
    numbers = jnp.arange(suffix_lengths.shape[0], dtype=jnp.int32)
    request = jnp.sum((row_order[:, None] >= end_rows[None, :]).astype(jnp.int32), axis=1)
    chosen = request[:, None] == numbers[None, :]
    position = row_order - jnp.sum(jnp.where(chosen, starts[None, :], 0), axis=1)
    wanted = jnp.sum(jnp.where(chosen, request_prefix[None, :], 0), axis=1)
    return (request, position, wanted)


def seq_gather_kernel(chips, x_ref, o_ref, send_sem, recv_sem, fwd_send, fwd_recv, local_sem):
    me = lax.axis_index("seq")
    chip = me // 2
    core = me % 2
    partner = chip * 2 + (1 - core)
    parts = x_ref.shape[0]
    mesh_id = pl.DeviceIdType.MESH
    barrier = pltpu.get_barrier_semaphore()

    def greet(k, carry):
        peer = lax.rem(chip + k, chips) * 2 + core
        pl.semaphore_signal(barrier, inc=1, device_id={"seq": peer}, device_id_type=mesh_id)
        return carry

    lax.fori_loop(1, chips, greet, 0)
    pl.semaphore_signal(barrier, inc=1, device_id={"seq": partner}, device_id_type=mesh_id)
    pl.semaphore_wait(barrier, chips)
    local = pltpu.make_async_copy(x_ref, o_ref.at[:, chip, core], local_sem)
    local.start()

    def push(peer_chip, sender, receiver):
        return [
            pltpu.make_async_remote_copy(
                src_ref=x_ref.at[a],
                dst_ref=o_ref.at[a, receiver, core],
                send_sem=send_sem.at[a, sender],
                recv_sem=recv_sem.at[a, receiver],
                device_id={"seq": peer_chip * 2 + core},
                device_id_type=mesh_id,
            )
            for a in range(parts)
        ]

    def send(k, carry):
        peer_chip = lax.rem(chip + k, chips)
        for copy in push(peer_chip, peer_chip, chip):
            copy.start()
        return carry

    lax.fori_loop(1, chips, send, 0)

    def finish(k, carry):
        peer_chip = lax.rem(chip + k, chips)
        for copy in push(peer_chip, peer_chip, peer_chip):
            copy.wait_send()
            copy.wait_recv()
        return carry

    lax.fori_loop(1, chips, finish, 0)
    local.wait()
    forward = [
        pltpu.make_async_remote_copy(
            src_ref=o_ref.at[a, :, core],
            dst_ref=o_ref.at[a, :, core],
            send_sem=fwd_send.at[a],
            recv_sem=fwd_recv.at[a],
            device_id={"seq": partner},
            device_id_type=mesh_id,
        )
        for a in range(parts)
    ]
    for copy in forward:
        copy.start()
    for copy in forward:
        copy.wait_send()
        copy.wait_recv()


def seq_gather(stacked, n, cid):
    parts, rows, cols = stacked.shape
    chips = n // 2
    return pl.pallas_call(
        functools.partial(seq_gather_kernel, chips),
        out_shape=jax.ShapeDtypeStruct((parts, chips, 2, rows, cols), stacked.dtype),
        in_specs=[pl.BlockSpec(memory_space=pl.ANY)],
        out_specs=pl.BlockSpec(memory_space=pl.ANY),
        scratch_shapes=[
            pltpu.SemaphoreType.DMA((parts, chips)),
            pltpu.SemaphoreType.DMA((parts, chips)),
            pltpu.SemaphoreType.DMA((parts,)),
            pltpu.SemaphoreType.DMA((parts,)),
            pltpu.SemaphoreType.DMA,
        ],
        compiler_params=pltpu.CompilerParams(collective_id=cid, has_side_effects=True),
    )(stacked)


def body(
    seq_n,
    hidden,
    norm_gain,
    w_query,
    w_key,
    w_value,
    prefix_keys,
    prefix_values,
    page_prefix,
    request_prefix,
    suffix_lengths,
    row_order,
):
    gathered = lax.all_gather(hidden, "tp", axis=1, tiled=True)
    local_rows = gathered.shape[0]
    hidden_f = gathered.astype(jnp.float32)
    mean_sq = jnp.mean(hidden_f * hidden_f, axis=1, keepdims=True)
    normed = (
        hidden_f * lax.rsqrt(mean_sq + 1e-05) * norm_gain.astype(jnp.float32)[None, :]
    ).astype(jnp.bfloat16)
    request_all, position_all, wanted_all = locate(row_order, suffix_lengths, request_prefix)
    offset = lax.axis_index("seq") * local_rows
    request = lax.dynamic_slice_in_dim(request_all, offset, local_rows)
    position = lax.dynamic_slice_in_dim(position_all, offset, local_rows)
    wanted = lax.dynamic_slice_in_dim(wanted_all, offset, local_rows)
    prefix_len = page_prefix.shape[0] * PAGE // PREFIXES
    rope_at = prefix_len + position
    q_heads = w_query.shape[1] // HEAD
    kv_heads = w_key.shape[1] // HEAD
    group_size = q_heads // kv_heads
    queries = rotate(
        jnp.dot(normed, w_query, preferred_element_type=jnp.float32).reshape(
            local_rows, q_heads, HEAD
        ),
        rope_at,
    ).astype(jnp.bfloat16)
    queries = queries.reshape(local_rows, kv_heads, group_size, HEAD)
    new_keys = rotate(
        jnp.dot(normed, w_key, preferred_element_type=jnp.float32).reshape(
            local_rows, kv_heads, HEAD
        ),
        rope_at,
    ).astype(jnp.bfloat16)
    new_keys = new_keys.reshape(local_rows, kv_heads * HEAD)
    new_values = jnp.dot(normed, w_value, preferred_element_type=jnp.float32).astype(jnp.bfloat16)
    row_pages = jnp.repeat(page_prefix, PAGE)
    score_scale = 1.0 / math.sqrt(HEAD)
    initial = (
        jnp.full((kv_heads, local_rows, group_size), -1e30, jnp.float32),
        jnp.zeros((kv_heads, local_rows, group_size), jnp.float32),
        jnp.zeros((kv_heads, local_rows, group_size, HEAD), jnp.float32),
    )

    def attend(state, key_rows, value_rows, visible):
        row_count = key_rows.shape[0]
        block_width = math.gcd(row_count, 512)
        block_count = row_count // block_width
        key_blocks = key_rows.reshape(block_count, block_width, kv_heads, HEAD)
        value_blocks = value_rows.reshape(block_count, block_width, kv_heads, HEAD)
        mask_blocks = visible.reshape(local_rows, block_count, block_width).transpose(1, 0, 2)

        def step(carry_in, inputs):
            run_max, run_sum, run_acc = carry_in
            key_block, value_block, mask_block = inputs
            scores = (
                jnp.einsum("tngd,knd->ntgk", queries, key_block, preferred_element_type=jnp.float32)
                * score_scale
            )
            seen = mask_block[None, :, None, :]
            new_max = jnp.maximum(run_max, jnp.max(jnp.where(seen, scores, -1e30), axis=-1))
            weights = jnp.where(seen, jnp.exp(scores - new_max[..., None]), 0.0)
            fade = jnp.exp(run_max - new_max)
            run_sum = run_sum * fade + jnp.sum(weights, axis=-1)
            run_acc = run_acc * fade[..., None] + jnp.einsum(
                "ntgk,knd->ntgd",
                weights.astype(jnp.bfloat16),
                value_block,
                preferred_element_type=jnp.float32,
            )
            return ((new_max, run_sum, run_acc), None)

        result, unused = lax.scan(step, state, (key_blocks, value_blocks, mask_blocks))
        return result

    gathered_prefix = seq_gather(jnp.stack([prefix_keys, prefix_values]), seq_n, 0)
    key_rows = gathered_prefix[0].reshape(-1, kv_heads * HEAD)
    value_rows = gathered_prefix[1].reshape(-1, kv_heads * HEAD)
    visible = wanted[:, None] == row_pages[None, :]
    state = attend(initial, key_rows, value_rows, visible)
    gathered_suffix = seq_gather(jnp.stack([new_keys, new_values]), seq_n, 1)
    key_rows = gathered_suffix[0].reshape(-1, kv_heads * HEAD)
    value_rows = gathered_suffix[1].reshape(-1, kv_heads * HEAD)
    visible = (request[:, None] == request_all[None, :]) & (
        position_all[None, :] <= position[:, None]
    )
    state = attend(state, key_rows, value_rows, visible)
    run_max, run_sum, run_acc = state
    attended = (
        (run_acc / run_sum[..., None])
        .transpose(1, 0, 2, 3)
        .reshape(local_rows, q_heads * HEAD)
        .astype(jnp.bfloat16)
    )
    return (attended, new_keys, new_values)


def solution(mesh):
    return jax.shard_map(
        functools.partial(body, mesh.shape["seq"]),
        mesh=mesh,
        in_specs=(
            P("seq", "tp"),
            P(),
            P(None, "tp"),
            P(None, "tp"),
            P(None, "tp"),
            P("seq", "tp"),
            P("seq", "tp"),
            P(),
            P(),
            P(),
            P(),
        ),
        out_specs=(P("seq", "tp"), P("seq", "tp"), P("seq", "tp")),
        check_vma=False,
    )
```

```python
import functools
import math

import jax
import jax.numpy as jnp
from jax import lax
from jax.sharding import PartitionSpec as P
from jax.experimental import pallas as pl
from jax.experimental.pallas import tpu as pltpu

HEAD = 128
PAGE = 128
PREFIXES = 4


ROPE_BASE = 5000000.0


def rotate(tensor_in, positions):
    head_dim = tensor_in.shape[-1]
    half_dim = head_dim // 2
    frequency = ROPE_BASE ** (-(jnp.arange(half_dim, dtype=jnp.float32) * 2.0 / head_dim))
    angles = positions.astype(jnp.float32)[:, None] * frequency[None, :]
    cosine = jnp.cos(angles)[:, None, :]
    sine_part = jnp.sin(angles)[:, None, :]
    first_half = tensor_in[..., :half_dim]
    second_half = tensor_in[..., half_dim:]
    return jnp.concatenate(
        [
            first_half * cosine - second_half * sine_part,
            second_half * cosine + first_half * sine_part,
        ],
        axis=-1,
    )


def locate(row_order, suffix_lengths, request_prefix):
    end_rows = jnp.cumsum(suffix_lengths)
    starts = end_rows - suffix_lengths
    numbers = jnp.arange(suffix_lengths.shape[0], dtype=jnp.int32)
    request = jnp.sum((row_order[:, None] >= end_rows[None, :]).astype(jnp.int32), axis=1)
    chosen = request[:, None] == numbers[None, :]
    position = row_order - jnp.sum(jnp.where(chosen, starts[None, :], 0), axis=1)
    wanted = jnp.sum(jnp.where(chosen, request_prefix[None, :], 0), axis=1)
    return (request, position, wanted)


def seq_gather_kernel(chips, x_ref, o_ref, send_sem, recv_sem, fwd_send, fwd_recv, local_sem):
    me = lax.axis_index("seq")
    chip = me // 2
    core = me % 2
    partner = chip * 2 + (1 - core)
    parts = x_ref.shape[0]
    mesh_id = pl.DeviceIdType.MESH
    barrier = pltpu.get_barrier_semaphore()

    def greet(k, carry):
        peer = lax.rem(chip + k, chips) * 2 + core
        pl.semaphore_signal(barrier, inc=1, device_id={"seq": peer}, device_id_type=mesh_id)
        return carry

    lax.fori_loop(1, chips, greet, 0)
    pl.semaphore_signal(barrier, inc=1, device_id={"seq": partner}, device_id_type=mesh_id)
    pl.semaphore_wait(barrier, chips)
    local = pltpu.make_async_copy(x_ref, o_ref.at[:, chip, core], local_sem)
    local.start()

    def push(peer_chip, sender, receiver):
        return [
            pltpu.make_async_remote_copy(
                src_ref=x_ref.at[a],
                dst_ref=o_ref.at[a, receiver, core],
                send_sem=send_sem.at[a, sender],
                recv_sem=recv_sem.at[a, receiver],
                device_id={"seq": peer_chip * 2 + core},
                device_id_type=mesh_id,
            )
            for a in range(parts)
        ]

    def send(k, carry):
        peer_chip = lax.rem(chip + k, chips)
        for copy in push(peer_chip, peer_chip, chip):
            copy.start()
        return carry

    lax.fori_loop(1, chips, send, 0)

    def finish(k, carry):
        peer_chip = lax.rem(chip + k, chips)
        for copy in push(peer_chip, peer_chip, peer_chip):
            copy.wait_send()
            copy.wait_recv()
        return carry

    lax.fori_loop(1, chips, finish, 0)
    local.wait()
    forward = [
        pltpu.make_async_remote_copy(
            src_ref=o_ref.at[a, :, core],
            dst_ref=o_ref.at[a, :, core],
            send_sem=fwd_send.at[a],
            recv_sem=fwd_recv.at[a],
            device_id={"seq": partner},
            device_id_type=mesh_id,
        )
        for a in range(parts)
    ]
    for copy in forward:
        copy.start()
    for copy in forward:
        copy.wait_send()
        copy.wait_recv()


def seq_gather(stacked, n, cid):
    parts, rows, cols = stacked.shape
    chips = n // 2
    return pl.pallas_call(
        functools.partial(seq_gather_kernel, chips),
        out_shape=jax.ShapeDtypeStruct((parts, chips, 2, rows, cols), stacked.dtype),
        in_specs=[pl.BlockSpec(memory_space=pl.ANY)],
        out_specs=pl.BlockSpec(memory_space=pl.ANY),
        scratch_shapes=[
            pltpu.SemaphoreType.DMA((parts, chips)),
            pltpu.SemaphoreType.DMA((parts, chips)),
            pltpu.SemaphoreType.DMA((parts,)),
            pltpu.SemaphoreType.DMA((parts,)),
            pltpu.SemaphoreType.DMA,
        ],
        compiler_params=pltpu.CompilerParams(collective_id=cid, has_side_effects=True),
    )(stacked)


def attention_kernel(
    scale,
    p_idx, p_cnt, s_idx, s_cnt,
    q_ref, q_want, q_req, q_pos,
    pk_ref, pv_ref, p_tag, p_bound,
    sk_ref, sv_ref, s_tag, s_bound,
    o_ref, m_sc, l_sc, acc_sc,
):
    for i in range(q_ref.shape[0]):
        m_sc[...] = jnp.full(m_sc.shape, -1e30, jnp.float32)
        l_sc[...] = jnp.zeros(l_sc.shape, jnp.float32)
        acc_sc[...] = jnp.zeros(acc_sc.shape, jnp.float32)
        query = q_ref[i]
        want = q_want[i]
        req = q_req[i]
        pos = q_pos[i]

        def sweep(idx, cnt, k_ref, v_ref, tag_ref, bound_ref):
            def step(n, carry):
                b = idx[i, n]
                scores = lax.dot_general(
                    query, k_ref[b], (((1,), (1,)), ((), ())),
                    preferred_element_type=jnp.float32,
                ) * scale
                tag = tag_ref[b]
                seen = ((tag == want) | (tag == req)) & (bound_ref[b] <= pos)
                run_max = m_sc[...]
                new_max = jnp.maximum(
                    run_max, jnp.max(jnp.where(seen, scores, -1e30), axis=1, keepdims=True)
                )
                weights = jnp.where(seen, jnp.exp(scores - new_max), 0.0)
                fade = jnp.exp(run_max - new_max)
                l_sc[...] = l_sc[...] * fade + jnp.sum(weights, axis=1, keepdims=True)
                acc_sc[...] = acc_sc[...] * fade + jnp.dot(
                    weights.astype(jnp.bfloat16), v_ref[b],
                    preferred_element_type=jnp.float32,
                )
                m_sc[...] = new_max
                return carry

            lax.fori_loop(0, cnt[i], step, 0)

        sweep(p_idx, p_cnt, pk_ref, pv_ref, p_tag, p_bound)
        sweep(s_idx, s_cnt, sk_ref, sv_ref, s_tag, s_bound)
        o_ref[i] = (acc_sc[...] / l_sc[...]).astype(o_ref.dtype)


def block_attention(scale, lists, queries, query_meta, prefix_parts, suffix_parts):
    q_blocks, q_rows, width = queries.shape
    smem = pl.BlockSpec(memory_space=pltpu.SMEM)
    vmem = pl.BlockSpec(memory_space=pltpu.VMEM)
    return pl.pallas_call(
        functools.partial(attention_kernel, scale),
        out_shape=jax.ShapeDtypeStruct((q_blocks, q_rows, width), jnp.bfloat16),
        in_specs=[smem] * 4 + [vmem] * 12,
        out_specs=vmem,
        scratch_shapes=[
            pltpu.VMEM((q_rows, 1), jnp.float32),
            pltpu.VMEM((q_rows, 1), jnp.float32),
            pltpu.VMEM((q_rows, width), jnp.float32),
        ],
        compiler_params=pltpu.CompilerParams(vmem_limit_bytes=48 * 1024 * 1024),
    )(*lists, queries, *query_meta, *prefix_parts, *suffix_parts)


def visible_list(visible):
    order = jnp.argsort(jnp.logical_not(visible), axis=1, stable=True).astype(jnp.int32)
    return order, jnp.sum(visible.astype(jnp.int32), axis=1)


def body(
    seq_n,
    hidden,
    norm_gain,
    w_query,
    w_key,
    w_value,
    prefix_keys,
    prefix_values,
    page_prefix,
    request_prefix,
    suffix_lengths,
    row_order,
):
    gathered = lax.all_gather(hidden, "tp", axis=1, tiled=True)
    local_rows = gathered.shape[0]
    hidden_f = gathered.astype(jnp.float32)
    mean_sq = jnp.mean(hidden_f * hidden_f, axis=1, keepdims=True)
    normed = (
        hidden_f * lax.rsqrt(mean_sq + 1e-05) * norm_gain.astype(jnp.float32)[None, :]
    ).astype(jnp.bfloat16)
    request_all, position_all, wanted_all = locate(row_order, suffix_lengths, request_prefix)
    offset = lax.axis_index("seq") * local_rows
    request = lax.dynamic_slice_in_dim(request_all, offset, local_rows)
    position = lax.dynamic_slice_in_dim(position_all, offset, local_rows)
    wanted = lax.dynamic_slice_in_dim(wanted_all, offset, local_rows)
    prefix_len = page_prefix.shape[0] * PAGE // PREFIXES
    rope_at = prefix_len + position
    q_heads = w_query.shape[1] // HEAD
    kv_heads = w_key.shape[1] // HEAD
    group_size = q_heads // kv_heads
    queries = rotate(
        jnp.dot(normed, w_query, preferred_element_type=jnp.float32).reshape(
            local_rows, q_heads, HEAD
        ),
        rope_at,
    ).astype(jnp.bfloat16)
    queries = queries.reshape(local_rows, kv_heads, group_size, HEAD)
    new_keys = rotate(
        jnp.dot(normed, w_key, preferred_element_type=jnp.float32).reshape(
            local_rows, kv_heads, HEAD
        ),
        rope_at,
    ).astype(jnp.bfloat16)
    new_keys = new_keys.reshape(local_rows, kv_heads * HEAD)
    new_values = jnp.dot(normed, w_value, preferred_element_type=jnp.float32).astype(jnp.bfloat16)
    score_scale = 1.0 / math.sqrt(HEAD)
    block = PAGE
    q_blocks = local_rows // block
    pages = page_prefix.shape[0]
    runs = row_order.shape[0] // block
    stacked_q = (
        queries.reshape(q_blocks, block, group_size, HEAD)
        .transpose(0, 2, 1, 3)
        .reshape(q_blocks, group_size * block, HEAD)
    )

    def per_query(values):
        spread = jnp.broadcast_to(values.reshape(q_blocks, 1, block), (q_blocks, group_size, block))
        return spread.reshape(q_blocks, group_size * block, 1).astype(jnp.int32)

    query_meta = (per_query(wanted), per_query(request + PREFIXES), per_query(position))
    want_blocks = wanted.reshape(q_blocks, block)
    block_wants = jnp.any(
        want_blocks[:, :, None] == jnp.arange(PREFIXES, dtype=jnp.int32)[None, None, :], axis=1
    )
    page_visible = jnp.take(block_wants, page_prefix, axis=1)
    local_place = lax.dynamic_slice_in_dim(row_order, offset, local_rows).reshape(q_blocks, block)
    first_seen = jnp.min(local_place - position.reshape(q_blocks, block), axis=1)
    last_seen = jnp.max(local_place, axis=1)
    run_place = row_order.reshape(runs, block)
    run_low = jnp.min(run_place, axis=1)
    run_high = jnp.max(run_place, axis=1)
    run_visible = (run_low[None, :] <= last_seen[:, None]) & (run_high[None, :] >= first_seen[:, None])
    p_idx, p_cnt = visible_list(page_visible)
    s_idx, s_cnt = visible_list(run_visible)

    seq_n_blocks = seq_n
    gathered_prefix = seq_gather(jnp.stack([prefix_keys, prefix_values]), seq_n_blocks, 0)
    prefix_parts = (
        gathered_prefix[0].reshape(pages, block, HEAD),
        gathered_prefix[1].reshape(pages, block, HEAD),
        jnp.broadcast_to(page_prefix.reshape(pages, 1, 1), (pages, 1, block)).astype(jnp.int32),
        jnp.full((pages, 1, block), -1, jnp.int32),
    )
    gathered_suffix = seq_gather(jnp.stack([new_keys, new_values]), seq_n_blocks, 1)
    suffix_parts = (
        gathered_suffix[0].reshape(runs, block, HEAD),
        gathered_suffix[1].reshape(runs, block, HEAD),
        (request_all + PREFIXES).reshape(runs, 1, block).astype(jnp.int32),
        position_all.reshape(runs, 1, block).astype(jnp.int32),
    )
    out = block_attention(
        score_scale, (p_idx, p_cnt, s_idx, s_cnt), stacked_q, query_meta, prefix_parts, suffix_parts
    )
    attended = (
        out.reshape(q_blocks, group_size, block, HEAD)
        .transpose(0, 2, 1, 3)
        .reshape(local_rows, group_size * HEAD)
    )
    return (attended, new_keys, new_values)


def solution(mesh):
    return jax.shard_map(
        functools.partial(body, mesh.shape["seq"]),
        mesh=mesh,
        in_specs=(
            P("seq", "tp"),
            P(),
            P(None, "tp"),
            P(None, "tp"),
            P(None, "tp"),
            P("seq", "tp"),
            P("seq", "tp"),
            P(),
            P(),
            P(),
            P(),
        ),
        out_specs=(P("seq", "tp"), P("seq", "tp"), P("seq", "tp")),
        check_vma=False,
    )
```

```python
import functools
import math

import jax
import jax.numpy as jnp
from jax import lax
from jax.sharding import PartitionSpec as P
from jax.experimental import pallas as pl
from jax.experimental.pallas import tpu as pltpu

HEAD = 128
PAGE = 128
PREFIXES = 4


ROPE_BASE = 5000000.0


def rotate(tensor_in, positions):
    head_dim = tensor_in.shape[-1]
    half_dim = head_dim // 2
    frequency = ROPE_BASE ** (-(jnp.arange(half_dim, dtype=jnp.float32) * 2.0 / head_dim))
    angles = positions.astype(jnp.float32)[:, None] * frequency[None, :]
    cosine = jnp.cos(angles)[:, None, :]
    sine_part = jnp.sin(angles)[:, None, :]
    first_half = tensor_in[..., :half_dim]
    second_half = tensor_in[..., half_dim:]
    return jnp.concatenate(
        [
            first_half * cosine - second_half * sine_part,
            second_half * cosine + first_half * sine_part,
        ],
        axis=-1,
    )


def locate(row_order, suffix_lengths, request_prefix):
    end_rows = jnp.cumsum(suffix_lengths)
    starts = end_rows - suffix_lengths
    numbers = jnp.arange(suffix_lengths.shape[0], dtype=jnp.int32)
    request = jnp.sum((row_order[:, None] >= end_rows[None, :]).astype(jnp.int32), axis=1)
    chosen = request[:, None] == numbers[None, :]
    position = row_order - jnp.sum(jnp.where(chosen, starts[None, :], 0), axis=1)
    wanted = jnp.sum(jnp.where(chosen, request_prefix[None, :], 0), axis=1)
    return (request, position, wanted)


def seq_gather_kernel(chips, x_ref, o_ref, send_sem, recv_sem, fwd_send, fwd_recv, local_sem):
    me = lax.axis_index("seq")
    chip = me // 2
    core = me % 2
    partner = chip * 2 + (1 - core)
    parts = x_ref.shape[0]
    mesh_id = pl.DeviceIdType.MESH
    barrier = pltpu.get_barrier_semaphore()

    def greet(k, carry):
        peer = lax.rem(chip + k, chips) * 2 + core
        pl.semaphore_signal(barrier, inc=1, device_id={"seq": peer}, device_id_type=mesh_id)
        return carry

    lax.fori_loop(1, chips, greet, 0)
    pl.semaphore_signal(barrier, inc=1, device_id={"seq": partner}, device_id_type=mesh_id)
    pl.semaphore_wait(barrier, chips)
    local = pltpu.make_async_copy(x_ref, o_ref.at[:, chip, core], local_sem)
    local.start()

    def push(peer_chip, sender, receiver):
        return [
            pltpu.make_async_remote_copy(
                src_ref=x_ref.at[a],
                dst_ref=o_ref.at[a, receiver, core],
                send_sem=send_sem.at[a, sender],
                recv_sem=recv_sem.at[a, receiver],
                device_id={"seq": peer_chip * 2 + core},
                device_id_type=mesh_id,
            )
            for a in range(parts)
        ]

    def send(k, carry):
        peer_chip = lax.rem(chip + k, chips)
        for copy in push(peer_chip, peer_chip, chip):
            copy.start()
        return carry

    lax.fori_loop(1, chips, send, 0)

    def finish(k, carry):
        peer_chip = lax.rem(chip + k, chips)
        for copy in push(peer_chip, peer_chip, peer_chip):
            copy.wait_send()
            copy.wait_recv()
        return carry

    lax.fori_loop(1, chips, finish, 0)
    local.wait()
    forward = [
        pltpu.make_async_remote_copy(
            src_ref=o_ref.at[a, :, core],
            dst_ref=o_ref.at[a, :, core],
            send_sem=fwd_send.at[a],
            recv_sem=fwd_recv.at[a],
            device_id={"seq": partner},
            device_id_type=mesh_id,
        )
        for a in range(parts)
    ]
    for copy in forward:
        copy.start()
    for copy in forward:
        copy.wait_send()
        copy.wait_recv()


def seq_gather(stacked, n, cid):
    parts, rows, cols = stacked.shape
    chips = n // 2
    return pl.pallas_call(
        functools.partial(seq_gather_kernel, chips),
        out_shape=jax.ShapeDtypeStruct((parts, chips, 2, rows, cols), stacked.dtype),
        in_specs=[pl.BlockSpec(memory_space=pl.ANY)],
        out_specs=pl.BlockSpec(memory_space=pl.ANY),
        scratch_shapes=[
            pltpu.SemaphoreType.DMA((parts, chips)),
            pltpu.SemaphoreType.DMA((parts, chips)),
            pltpu.SemaphoreType.DMA((parts,)),
            pltpu.SemaphoreType.DMA((parts,)),
            pltpu.SemaphoreType.DMA,
        ],
        compiler_params=pltpu.CompilerParams(collective_id=cid, has_side_effects=True),
    )(stacked)


def attention_kernel(
    scale, group_pages,
    wants, page_order, s_idx, s_cnt,
    q_ref, q_want, q_req, q_pos,
    pk_ref, pv_ref,
    sk_ref, sv_ref, s_tag, s_bound,
    o_ref, m_sc, l_sc, acc_sc, pm_sc, pl_sc, pacc_sc,
):
    prefixes, per_prefix = page_order.shape

    def update(m_ref, l_ref, acc_ref, score_list, value_list):
        run_max = m_ref[...]
        new_max = run_max
        for scores in score_list:
            new_max = jnp.maximum(new_max, jnp.max(scores, axis=1, keepdims=True))
        fade = jnp.exp(run_max - new_max)
        total = l_ref[...] * fade
        acc = acc_ref[...] * fade
        for scores, values in zip(score_list, value_list):
            weights = jnp.exp(scores - new_max)
            total = total + jnp.sum(weights, axis=1, keepdims=True)
            acc = acc + jnp.dot(weights.astype(jnp.bfloat16), values, preferred_element_type=jnp.float32)
        l_ref[...] = total
        acc_ref[...] = acc
        m_ref[...] = new_max

    for i in range(q_ref.shape[0]):
        m_sc[...] = jnp.full(m_sc.shape, -1e30, jnp.float32)
        l_sc[...] = jnp.zeros(l_sc.shape, jnp.float32)
        acc_sc[...] = jnp.zeros(acc_sc.shape, jnp.float32)
        query = q_ref[i]
        want = q_want[i]
        req = q_req[i]
        pos = q_pos[i]

        def score(keys):
            return lax.dot_general(
                query, keys, (((1,), (1,)), ((), ())), preferred_element_type=jnp.float32
            ) * scale

        for p in range(prefixes):
            @pl.when(wants[i, p] > 0)
            def _():
                pm_sc[...] = jnp.full(pm_sc.shape, -1e30, jnp.float32)
                pl_sc[...] = jnp.zeros(pl_sc.shape, jnp.float32)
                pacc_sc[...] = jnp.zeros(pacc_sc.shape, jnp.float32)

                def page_step(g, carry):
                    pages = [page_order[p, g * group_pages + j] for j in range(group_pages)]
                    update(pm_sc, pl_sc, pacc_sc, [score(pk_ref[b]) for b in pages], [pv_ref[b] for b in pages])
                    return carry

                lax.fori_loop(0, per_prefix // group_pages, page_step, 0)
                mine = want == p
                m_sc[...] = jnp.where(mine, pm_sc[...], m_sc[...])
                l_sc[...] = jnp.where(mine, pl_sc[...], l_sc[...])
                acc_sc[...] = jnp.where(mine, pacc_sc[...], acc_sc[...])

        def step(n, carry):
            b = s_idx[i, n]
            scores = score(sk_ref[b])
            seen = (s_tag[b] == req) & (s_bound[b] <= pos)
            run_max = m_sc[...]
            new_max = jnp.maximum(
                run_max, jnp.max(jnp.where(seen, scores, -1e30), axis=1, keepdims=True)
            )
            weights = jnp.where(seen, jnp.exp(scores - new_max), 0.0)
            fade = jnp.exp(run_max - new_max)
            l_sc[...] = l_sc[...] * fade + jnp.sum(weights, axis=1, keepdims=True)
            acc_sc[...] = acc_sc[...] * fade + jnp.dot(
                weights.astype(jnp.bfloat16), sv_ref[b], preferred_element_type=jnp.float32
            )
            m_sc[...] = new_max
            return carry

        lax.fori_loop(0, s_cnt[i], step, 0)
        o_ref[i] = (acc_sc[...] / l_sc[...]).astype(o_ref.dtype)


def block_attention(scale, lists, queries, query_meta, prefix_parts, suffix_parts):
    q_blocks, q_rows, width = queries.shape
    smem = pl.BlockSpec(memory_space=pltpu.SMEM)
    vmem = pl.BlockSpec(memory_space=pltpu.VMEM)
    state = [
        pltpu.VMEM((q_rows, 1), jnp.float32),
        pltpu.VMEM((q_rows, 1), jnp.float32),
        pltpu.VMEM((q_rows, width), jnp.float32),
    ]
    return pl.pallas_call(
        functools.partial(attention_kernel, scale, 4),
        out_shape=jax.ShapeDtypeStruct((q_blocks, q_rows, width), jnp.bfloat16),
        in_specs=[smem] * 4 + [vmem] * 10,
        out_specs=vmem,
        scratch_shapes=state + state,
        compiler_params=pltpu.CompilerParams(vmem_limit_bytes=48 * 1024 * 1024),
    )(*lists, queries, *query_meta, *prefix_parts, *suffix_parts)


def visible_list(visible):
    order = jnp.argsort(jnp.logical_not(visible), axis=1, stable=True).astype(jnp.int32)
    return order, jnp.sum(visible.astype(jnp.int32), axis=1)


def body(
    seq_n,
    hidden,
    norm_gain,
    w_query,
    w_key,
    w_value,
    prefix_keys,
    prefix_values,
    page_prefix,
    request_prefix,
    suffix_lengths,
    row_order,
):
    gathered = lax.all_gather(hidden, "tp", axis=1, tiled=True)
    local_rows = gathered.shape[0]
    hidden_f = gathered.astype(jnp.float32)
    mean_sq = jnp.mean(hidden_f * hidden_f, axis=1, keepdims=True)
    normed = (
        hidden_f * lax.rsqrt(mean_sq + 1e-05) * norm_gain.astype(jnp.float32)[None, :]
    ).astype(jnp.bfloat16)
    request_all, position_all, wanted_all = locate(row_order, suffix_lengths, request_prefix)
    offset = lax.axis_index("seq") * local_rows
    request = lax.dynamic_slice_in_dim(request_all, offset, local_rows)
    position = lax.dynamic_slice_in_dim(position_all, offset, local_rows)
    wanted = lax.dynamic_slice_in_dim(wanted_all, offset, local_rows)
    prefix_len = page_prefix.shape[0] * PAGE // PREFIXES
    rope_at = prefix_len + position
    q_heads = w_query.shape[1] // HEAD
    kv_heads = w_key.shape[1] // HEAD
    group_size = q_heads // kv_heads
    queries = rotate(
        jnp.dot(normed, w_query, preferred_element_type=jnp.float32).reshape(
            local_rows, q_heads, HEAD
        ),
        rope_at,
    ).astype(jnp.bfloat16)
    queries = queries.reshape(local_rows, kv_heads, group_size, HEAD)
    new_keys = rotate(
        jnp.dot(normed, w_key, preferred_element_type=jnp.float32).reshape(
            local_rows, kv_heads, HEAD
        ),
        rope_at,
    ).astype(jnp.bfloat16)
    new_keys = new_keys.reshape(local_rows, kv_heads * HEAD)
    new_values = jnp.dot(normed, w_value, preferred_element_type=jnp.float32).astype(jnp.bfloat16)
    score_scale = 1.0 / math.sqrt(HEAD)
    block = PAGE
    q_blocks = local_rows // block
    pages = page_prefix.shape[0]
    runs = row_order.shape[0] // block
    stacked_q = (
        queries.reshape(q_blocks, block, group_size, HEAD)
        .transpose(0, 2, 1, 3)
        .reshape(q_blocks, group_size * block, HEAD)
    )

    def per_query(values):
        spread = jnp.broadcast_to(values.reshape(q_blocks, 1, block), (q_blocks, group_size, block))
        return spread.reshape(q_blocks, group_size * block, 1).astype(jnp.int32)

    query_meta = (per_query(wanted), per_query(request + PREFIXES), per_query(position))
    want_blocks = wanted.reshape(q_blocks, block)
    block_wants = jnp.any(
        want_blocks[:, :, None] == jnp.arange(PREFIXES, dtype=jnp.int32)[None, None, :], axis=1
    )
    page_order = jnp.argsort(page_prefix, stable=True).astype(jnp.int32).reshape(PREFIXES, -1)
    local_place = lax.dynamic_slice_in_dim(row_order, offset, local_rows).reshape(q_blocks, block)
    first_seen = jnp.min(local_place - position.reshape(q_blocks, block), axis=1)
    last_seen = jnp.max(local_place, axis=1)
    run_place = row_order.reshape(runs, block)
    run_low = jnp.min(run_place, axis=1)
    run_high = jnp.max(run_place, axis=1)
    run_visible = (run_low[None, :] <= last_seen[:, None]) & (run_high[None, :] >= first_seen[:, None])
    s_idx, s_cnt = visible_list(run_visible)

    seq_n_blocks = seq_n
    gathered_prefix = seq_gather(jnp.stack([prefix_keys, prefix_values]), seq_n_blocks, 0)
    prefix_parts = (
        gathered_prefix[0].reshape(pages, block, HEAD),
        gathered_prefix[1].reshape(pages, block, HEAD),
    )
    gathered_suffix = seq_gather(jnp.stack([new_keys, new_values]), seq_n_blocks, 1)
    suffix_parts = (
        gathered_suffix[0].reshape(runs, block, HEAD),
        gathered_suffix[1].reshape(runs, block, HEAD),
        (request_all + PREFIXES).reshape(runs, 1, block).astype(jnp.int32),
        position_all.reshape(runs, 1, block).astype(jnp.int32),
    )
    out = block_attention(
        score_scale, (block_wants.astype(jnp.int32), page_order, s_idx, s_cnt), stacked_q, query_meta, prefix_parts, suffix_parts
    )
    attended = (
        out.reshape(q_blocks, group_size, block, HEAD)
        .transpose(0, 2, 1, 3)
        .reshape(local_rows, group_size * HEAD)
    )
    return (attended, new_keys, new_values)


def solution(mesh):
    return jax.shard_map(
        functools.partial(body, mesh.shape["seq"]),
        mesh=mesh,
        in_specs=(
            P("seq", "tp"),
            P(),
            P(None, "tp"),
            P(None, "tp"),
            P(None, "tp"),
            P("seq", "tp"),
            P("seq", "tp"),
            P(),
            P(),
            P(),
            P(),
        ),
        out_specs=(P("seq", "tp"), P("seq", "tp"), P("seq", "tp")),
        check_vma=False,
    )
```

```python
import functools
import math

import jax
import jax.numpy as jnp
from jax import lax
from jax.sharding import PartitionSpec as P
from jax.experimental import pallas as pl
from jax.experimental.pallas import tpu as pltpu

HEAD = 128
PAGE = 128
PREFIXES = 4


ROPE_BASE = 5000000.0


def rotate(tensor_in, positions):
    head_dim = tensor_in.shape[-1]
    half_dim = head_dim // 2
    frequency = ROPE_BASE ** (-(jnp.arange(half_dim, dtype=jnp.float32) * 2.0 / head_dim))
    angles = positions.astype(jnp.float32)[:, None] * frequency[None, :]
    cosine = jnp.cos(angles)[:, None, :]
    sine_part = jnp.sin(angles)[:, None, :]
    first_half = tensor_in[..., :half_dim]
    second_half = tensor_in[..., half_dim:]
    return jnp.concatenate(
        [
            first_half * cosine - second_half * sine_part,
            second_half * cosine + first_half * sine_part,
        ],
        axis=-1,
    )


def locate(row_order, suffix_lengths, request_prefix):
    end_rows = jnp.cumsum(suffix_lengths)
    starts = end_rows - suffix_lengths
    numbers = jnp.arange(suffix_lengths.shape[0], dtype=jnp.int32)
    request = jnp.sum((row_order[:, None] >= end_rows[None, :]).astype(jnp.int32), axis=1)
    chosen = request[:, None] == numbers[None, :]
    position = row_order - jnp.sum(jnp.where(chosen, starts[None, :], 0), axis=1)
    wanted = jnp.sum(jnp.where(chosen, request_prefix[None, :], 0), axis=1)
    return (request, position, wanted)


def seq_gather_kernel(
    zs, xs, x_ref, o_ref, z_send, z_recv, r_send, r_recv, f_send, f_recv, c_send, c_recv, local_sem
):
    me = lax.axis_index("seq")
    core = me % 2
    chip = me // 2
    za = chip // xs
    xb = chip % xs
    right = lax.rem(xb + 1, xs)
    left = lax.rem(xb + xs - 1, xs)
    parts = x_ref.shape[0]
    mesh_id = pl.DeviceIdType.MESH

    def seq_of(z, x, c):
        return (z * xs + x) * 2 + c

    def signal(sem, target):
        pl.semaphore_signal(sem, inc=1, device_id={"seq": target}, device_id_type=mesh_id)

    barrier = pltpu.get_barrier_semaphore()

    def greet(k, carry):
        signal(barrier, seq_of(lax.rem(za + k, zs), xb, core))
        return carry

    lax.fori_loop(1, zs, greet, 0)
    signal(barrier, seq_of(za, right, core))
    signal(barrier, seq_of(za, left, core))
    signal(barrier, seq_of(za, xb, 1 - core))
    pl.semaphore_wait(barrier, zs + 2)

    local = pltpu.make_async_copy(x_ref, o_ref.at[:, za, xb, core], local_sem)
    local.start()

    def z_copy(a, peer_z, slot_z):
        return pltpu.make_async_remote_copy(
            src_ref=x_ref.at[a],
            dst_ref=o_ref.at[a, slot_z, xb, core],
            send_sem=z_send.at[a, peer_z],
            recv_sem=z_recv.at[a, slot_z],
            device_id={"seq": seq_of(peer_z, xb, core)},
            device_id_type=mesh_id,
        )

    def z_start(k, carry):
        peer_z = lax.rem(za + k, zs)
        for a in range(parts):
            z_copy(a, peer_z, za).start()
        return carry

    lax.fori_loop(1, zs, z_start, 0)

    def z_finish(k, carry):
        peer_z = lax.rem(za + k, zs)
        for a in range(parts):
            copy = z_copy(a, peer_z, peer_z)
            copy.wait_send()
            copy.wait_recv()
        return carry

    lax.fori_loop(1, zs, z_finish, 0)
    local.wait()

    def ring_copy(a, side, group, target_x, sem_side):
        return pltpu.make_async_remote_copy(
            src_ref=o_ref.at[a, :, group, core],
            dst_ref=o_ref.at[a, :, group, core],
            send_sem=r_send.at[a, side],
            recv_sem=r_recv.at[a, sem_side],
            device_id={"seq": seq_of(za, target_x, core)},
            device_id_type=mesh_id,
        )

    outgoing = []
    for a in range(parts):
        outgoing.append(ring_copy(a, 0, xb, right, 0))
        outgoing.append(ring_copy(a, 1, xb, left, 1))
    for copy in outgoing:
        copy.start()
    for a in range(parts):
        ring_copy(a, 0, left, right, 0).wait_recv()
        ring_copy(a, 1, right, left, 1).wait_recv()
    for copy in outgoing:
        copy.wait_send()

    far = lax.rem(xb + 2, xs)
    relay_k = pltpu.make_async_remote_copy(
        src_ref=o_ref.at[0, :, left, core],
        dst_ref=o_ref.at[0, :, left, core],
        send_sem=f_send.at[0],
        recv_sem=f_recv.at[0],
        device_id={"seq": seq_of(za, right, core)},
        device_id_type=mesh_id,
    )
    relay_v = pltpu.make_async_remote_copy(
        src_ref=o_ref.at[1, :, right, core],
        dst_ref=o_ref.at[1, :, right, core],
        send_sem=f_send.at[1],
        recv_sem=f_recv.at[1],
        device_id={"seq": seq_of(za, left, core)},
        device_id_type=mesh_id,
    )
    relay_k.start()
    relay_v.start()
    pltpu.make_async_remote_copy(
        src_ref=o_ref.at[0, :, far, core],
        dst_ref=o_ref.at[0, :, far, core],
        send_sem=f_send.at[0],
        recv_sem=f_recv.at[0],
        device_id={"seq": seq_of(za, right, core)},
        device_id_type=mesh_id,
    ).wait_recv()
    pltpu.make_async_remote_copy(
        src_ref=o_ref.at[1, :, far, core],
        dst_ref=o_ref.at[1, :, far, core],
        send_sem=f_send.at[1],
        recv_sem=f_recv.at[1],
        device_id={"seq": seq_of(za, left, core)},
        device_id_type=mesh_id,
    ).wait_recv()
    relay_k.wait_send()
    relay_v.wait_send()

    across = [
        pltpu.make_async_remote_copy(
            src_ref=o_ref.at[a, :, :, core],
            dst_ref=o_ref.at[a, :, :, core],
            send_sem=c_send.at[a],
            recv_sem=c_recv.at[a],
            device_id={"seq": seq_of(za, xb, 1 - core)},
            device_id_type=mesh_id,
        )
        for a in range(parts)
    ]
    for copy in across:
        copy.start()
    for copy in across:
        copy.wait_send()
        copy.wait_recv()


def seq_gather(stacked, n, cid):
    parts, rows, cols = stacked.shape
    chips = n // 2
    xs = 4
    zs = chips // xs
    return pl.pallas_call(
        functools.partial(seq_gather_kernel, zs, xs),
        out_shape=jax.ShapeDtypeStruct((parts, zs, xs, 2, rows, cols), stacked.dtype),
        in_specs=[pl.BlockSpec(memory_space=pl.ANY)],
        out_specs=pl.BlockSpec(memory_space=pl.ANY),
        scratch_shapes=[
            pltpu.SemaphoreType.DMA((parts, zs)),
            pltpu.SemaphoreType.DMA((parts, zs)),
            pltpu.SemaphoreType.DMA((parts, 2)),
            pltpu.SemaphoreType.DMA((parts, 2)),
            pltpu.SemaphoreType.DMA((parts,)),
            pltpu.SemaphoreType.DMA((parts,)),
            pltpu.SemaphoreType.DMA((parts,)),
            pltpu.SemaphoreType.DMA((parts,)),
            pltpu.SemaphoreType.DMA,
        ],
        compiler_params=pltpu.CompilerParams(collective_id=cid, has_side_effects=True),
    )(stacked)


def attention_kernel(
    scale, group_pages,
    wants, page_order, s_idx, s_cnt,
    q_ref, q_want, q_req, q_pos,
    pk_ref, pv_ref,
    sk_ref, sv_ref, s_tag, s_bound,
    o_ref, m_sc, l_sc, acc_sc, pm_sc, pl_sc, pacc_sc,
):
    prefixes, per_prefix = page_order.shape

    def update(m_ref, l_ref, acc_ref, score_list, value_list):
        run_max = m_ref[...]
        new_max = run_max
        for scores in score_list:
            new_max = jnp.maximum(new_max, jnp.max(scores, axis=1, keepdims=True))
        fade = jnp.exp(run_max - new_max)
        total = l_ref[...] * fade
        acc = acc_ref[...] * fade
        for scores, values in zip(score_list, value_list):
            weights = jnp.exp(scores - new_max)
            total = total + jnp.sum(weights, axis=1, keepdims=True)
            acc = acc + jnp.dot(weights.astype(jnp.bfloat16), values, preferred_element_type=jnp.float32)
        l_ref[...] = total
        acc_ref[...] = acc
        m_ref[...] = new_max

    for i in range(q_ref.shape[0]):
        m_sc[...] = jnp.full(m_sc.shape, -1e30, jnp.float32)
        l_sc[...] = jnp.zeros(l_sc.shape, jnp.float32)
        acc_sc[...] = jnp.zeros(acc_sc.shape, jnp.float32)
        query = q_ref[i]
        want = q_want[i]
        req = q_req[i]
        pos = q_pos[i]

        def score(keys):
            return lax.dot_general(
                query, keys, (((1,), (1,)), ((), ())), preferred_element_type=jnp.float32
            ) * scale

        for p in range(prefixes):
            @pl.when(wants[i, p] > 0)
            def _():
                pm_sc[...] = jnp.full(pm_sc.shape, -1e30, jnp.float32)
                pl_sc[...] = jnp.zeros(pl_sc.shape, jnp.float32)
                pacc_sc[...] = jnp.zeros(pacc_sc.shape, jnp.float32)

                def page_step(g, carry):
                    pages = [page_order[p, g * group_pages + j] for j in range(group_pages)]
                    update(pm_sc, pl_sc, pacc_sc, [score(pk_ref[b]) for b in pages], [pv_ref[b] for b in pages])
                    return carry

                lax.fori_loop(0, per_prefix // group_pages, page_step, 0)
                mine = want == p
                m_sc[...] = jnp.where(mine, pm_sc[...], m_sc[...])
                l_sc[...] = jnp.where(mine, pl_sc[...], l_sc[...])
                acc_sc[...] = jnp.where(mine, pacc_sc[...], acc_sc[...])

        def step(n, carry):
            b = s_idx[i, n]
            scores = score(sk_ref[b])
            seen = (s_tag[b] == req) & (s_bound[b] <= pos)
            run_max = m_sc[...]
            new_max = jnp.maximum(
                run_max, jnp.max(jnp.where(seen, scores, -1e30), axis=1, keepdims=True)
            )
            weights = jnp.where(seen, jnp.exp(scores - new_max), 0.0)
            fade = jnp.exp(run_max - new_max)
            l_sc[...] = l_sc[...] * fade + jnp.sum(weights, axis=1, keepdims=True)
            acc_sc[...] = acc_sc[...] * fade + jnp.dot(
                weights.astype(jnp.bfloat16), sv_ref[b], preferred_element_type=jnp.float32
            )
            m_sc[...] = new_max
            return carry

        lax.fori_loop(0, s_cnt[i], step, 0)
        o_ref[i] = (acc_sc[...] / l_sc[...]).astype(o_ref.dtype)


def block_attention(scale, lists, queries, query_meta, prefix_parts, suffix_parts):
    q_blocks, q_rows, width = queries.shape
    smem = pl.BlockSpec(memory_space=pltpu.SMEM)
    vmem = pl.BlockSpec(memory_space=pltpu.VMEM)
    state = [
        pltpu.VMEM((q_rows, 1), jnp.float32),
        pltpu.VMEM((q_rows, 1), jnp.float32),
        pltpu.VMEM((q_rows, width), jnp.float32),
    ]
    return pl.pallas_call(
        functools.partial(attention_kernel, scale, 4),
        out_shape=jax.ShapeDtypeStruct((q_blocks, q_rows, width), jnp.bfloat16),
        in_specs=[smem] * 4 + [vmem] * 10,
        out_specs=vmem,
        scratch_shapes=state + state,
        compiler_params=pltpu.CompilerParams(vmem_limit_bytes=48 * 1024 * 1024),
    )(*lists, queries, *query_meta, *prefix_parts, *suffix_parts)


def visible_list(visible):
    order = jnp.argsort(jnp.logical_not(visible), axis=1, stable=True).astype(jnp.int32)
    return order, jnp.sum(visible.astype(jnp.int32), axis=1)


def body(
    seq_n,
    hidden,
    norm_gain,
    w_query,
    w_key,
    w_value,
    prefix_keys,
    prefix_values,
    page_prefix,
    request_prefix,
    suffix_lengths,
    row_order,
):
    gathered = lax.all_gather(hidden, "tp", axis=1, tiled=True)
    local_rows = gathered.shape[0]
    hidden_f = gathered.astype(jnp.float32)
    mean_sq = jnp.mean(hidden_f * hidden_f, axis=1, keepdims=True)
    normed = (
        hidden_f * lax.rsqrt(mean_sq + 1e-05) * norm_gain.astype(jnp.float32)[None, :]
    ).astype(jnp.bfloat16)
    request_all, position_all, wanted_all = locate(row_order, suffix_lengths, request_prefix)
    offset = lax.axis_index("seq") * local_rows
    request = lax.dynamic_slice_in_dim(request_all, offset, local_rows)
    position = lax.dynamic_slice_in_dim(position_all, offset, local_rows)
    wanted = lax.dynamic_slice_in_dim(wanted_all, offset, local_rows)
    prefix_len = page_prefix.shape[0] * PAGE // PREFIXES
    rope_at = prefix_len + position
    q_heads = w_query.shape[1] // HEAD
    kv_heads = w_key.shape[1] // HEAD
    group_size = q_heads // kv_heads
    queries = rotate(
        jnp.dot(normed, w_query, preferred_element_type=jnp.float32).reshape(
            local_rows, q_heads, HEAD
        ),
        rope_at,
    ).astype(jnp.bfloat16)
    queries = queries.reshape(local_rows, kv_heads, group_size, HEAD)
    new_keys = rotate(
        jnp.dot(normed, w_key, preferred_element_type=jnp.float32).reshape(
            local_rows, kv_heads, HEAD
        ),
        rope_at,
    ).astype(jnp.bfloat16)
    new_keys = new_keys.reshape(local_rows, kv_heads * HEAD)
    new_values = jnp.dot(normed, w_value, preferred_element_type=jnp.float32).astype(jnp.bfloat16)
    score_scale = 1.0 / math.sqrt(HEAD)
    block = PAGE
    q_blocks = local_rows // block
    pages = page_prefix.shape[0]
    runs = row_order.shape[0] // block
    stacked_q = (
        queries.reshape(q_blocks, block, group_size, HEAD)
        .transpose(0, 2, 1, 3)
        .reshape(q_blocks, group_size * block, HEAD)
    )

    def per_query(values):
        spread = jnp.broadcast_to(values.reshape(q_blocks, 1, block), (q_blocks, group_size, block))
        return spread.reshape(q_blocks, group_size * block, 1).astype(jnp.int32)

    query_meta = (per_query(wanted), per_query(request + PREFIXES), per_query(position))
    want_blocks = wanted.reshape(q_blocks, block)
    block_wants = jnp.any(
        want_blocks[:, :, None] == jnp.arange(PREFIXES, dtype=jnp.int32)[None, None, :], axis=1
    )
    page_order = jnp.argsort(page_prefix, stable=True).astype(jnp.int32).reshape(PREFIXES, -1)
    local_place = lax.dynamic_slice_in_dim(row_order, offset, local_rows).reshape(q_blocks, block)
    first_seen = jnp.min(local_place - position.reshape(q_blocks, block), axis=1)
    last_seen = jnp.max(local_place, axis=1)
    run_place = row_order.reshape(runs, block)
    run_low = jnp.min(run_place, axis=1)
    run_high = jnp.max(run_place, axis=1)
    run_visible = (run_low[None, :] <= last_seen[:, None]) & (run_high[None, :] >= first_seen[:, None])
    s_idx, s_cnt = visible_list(run_visible)

    seq_n_blocks = seq_n
    gathered_prefix = seq_gather(jnp.stack([prefix_keys, prefix_values]), seq_n_blocks, 0)
    prefix_parts = (
        gathered_prefix[0].reshape(pages, block, HEAD),
        gathered_prefix[1].reshape(pages, block, HEAD),
    )
    gathered_suffix = seq_gather(jnp.stack([new_keys, new_values]), seq_n_blocks, 1)
    suffix_parts = (
        gathered_suffix[0].reshape(runs, block, HEAD),
        gathered_suffix[1].reshape(runs, block, HEAD),
        (request_all + PREFIXES).reshape(runs, 1, block).astype(jnp.int32),
        position_all.reshape(runs, 1, block).astype(jnp.int32),
    )
    out = block_attention(
        score_scale, (block_wants.astype(jnp.int32), page_order, s_idx, s_cnt), stacked_q, query_meta, prefix_parts, suffix_parts
    )
    attended = (
        out.reshape(q_blocks, group_size, block, HEAD)
        .transpose(0, 2, 1, 3)
        .reshape(local_rows, group_size * HEAD)
    )
    return (attended, new_keys, new_values)


def solution(mesh):
    return jax.shard_map(
        functools.partial(body, mesh.shape["seq"]),
        mesh=mesh,
        in_specs=(
            P("seq", "tp"),
            P(),
            P(None, "tp"),
            P(None, "tp"),
            P(None, "tp"),
            P("seq", "tp"),
            P("seq", "tp"),
            P(),
            P(),
            P(),
            P(),
        ),
        out_specs=(P("seq", "tp"), P("seq", "tp"), P("seq", "tp")),
        check_vma=False,
    )
```

```python
import functools
import math

import jax
import jax.numpy as jnp
from jax import lax
from jax.sharding import PartitionSpec as P
from jax.experimental import pallas as pl
from jax.experimental.pallas import tpu as pltpu

HEAD = 128
PAGE = 128
PREFIXES = 4


ROPE_BASE = 5000000.0


def rotate(tensor_in, positions):
    head_dim = tensor_in.shape[-1]
    half_dim = head_dim // 2
    frequency = ROPE_BASE ** (-(jnp.arange(half_dim, dtype=jnp.float32) * 2.0 / head_dim))
    angles = positions.astype(jnp.float32)[:, None] * frequency[None, :]
    cosine = jnp.cos(angles)[:, None, :]
    sine_part = jnp.sin(angles)[:, None, :]
    first_half = tensor_in[..., :half_dim]
    second_half = tensor_in[..., half_dim:]
    return jnp.concatenate(
        [
            first_half * cosine - second_half * sine_part,
            second_half * cosine + first_half * sine_part,
        ],
        axis=-1,
    )


def locate(row_order, suffix_lengths, request_prefix):
    end_rows = jnp.cumsum(suffix_lengths)
    starts = end_rows - suffix_lengths
    numbers = jnp.arange(suffix_lengths.shape[0], dtype=jnp.int32)
    request = jnp.sum((row_order[:, None] >= end_rows[None, :]).astype(jnp.int32), axis=1)
    chosen = request[:, None] == numbers[None, :]
    position = row_order - jnp.sum(jnp.where(chosen, starts[None, :], 0), axis=1)
    wanted = jnp.sum(jnp.where(chosen, request_prefix[None, :], 0), axis=1)
    return (request, position, wanted)


def seq_gather_kernel(
    zs, xs, x_ref, o_ref, z_send, z_recv, r_send, r_recv, f_send, f_recv, c_send, c_recv, local_sem
):
    me = lax.axis_index("seq")
    core = me % 2
    chip = me // 2
    za = chip // xs
    xb = chip % xs
    right = lax.rem(xb + 1, xs)
    left = lax.rem(xb + xs - 1, xs)
    parts = x_ref.shape[0]
    mesh_id = pl.DeviceIdType.MESH

    def seq_of(z, x, c):
        return (z * xs + x) * 2 + c

    def signal(sem, target):
        pl.semaphore_signal(sem, inc=1, device_id={"seq": target}, device_id_type=mesh_id)

    barrier = pltpu.get_barrier_semaphore()

    def greet(k, carry):
        signal(barrier, seq_of(lax.rem(za + k, zs), xb, core))
        return carry

    lax.fori_loop(1, zs, greet, 0)
    signal(barrier, seq_of(za, right, core))
    signal(barrier, seq_of(za, left, core))
    signal(barrier, seq_of(za, xb, 1 - core))
    pl.semaphore_wait(barrier, zs + 2)

    local = pltpu.make_async_copy(x_ref, o_ref.at[:, za, xb, core], local_sem)
    local.start()

    def z_copy(a, peer_z, slot_z):
        return pltpu.make_async_remote_copy(
            src_ref=x_ref.at[a],
            dst_ref=o_ref.at[a, slot_z, xb, core],
            send_sem=z_send.at[a, peer_z],
            recv_sem=z_recv.at[a, slot_z],
            device_id={"seq": seq_of(peer_z, xb, core)},
            device_id_type=mesh_id,
        )

    def z_start(k, carry):
        peer_z = lax.rem(za + k, zs)
        for a in range(parts):
            z_copy(a, peer_z, za).start()
        return carry

    lax.fori_loop(1, zs, z_start, 0)

    def z_finish(k, carry):
        peer_z = lax.rem(za + k, zs)
        for a in range(parts):
            copy = z_copy(a, peer_z, peer_z)
            copy.wait_send()
            copy.wait_recv()
        return carry

    lax.fori_loop(1, zs, z_finish, 0)
    local.wait()

    def ring_copy(a, side, group, target_x, sem_side):
        return pltpu.make_async_remote_copy(
            src_ref=o_ref.at[a, :, group, core],
            dst_ref=o_ref.at[a, :, group, core],
            send_sem=r_send.at[a, side],
            recv_sem=r_recv.at[a, sem_side],
            device_id={"seq": seq_of(za, target_x, core)},
            device_id_type=mesh_id,
        )

    outgoing = []
    for a in range(parts):
        outgoing.append(ring_copy(a, 0, xb, right, 0))
        outgoing.append(ring_copy(a, 1, xb, left, 1))
    for copy in outgoing:
        copy.start()
    for a in range(parts):
        ring_copy(a, 0, left, right, 0).wait_recv()
        ring_copy(a, 1, right, left, 1).wait_recv()
    for copy in outgoing:
        copy.wait_send()

    far = lax.rem(xb + 2, xs)
    relay_k = pltpu.make_async_remote_copy(
        src_ref=o_ref.at[0, :, left, core],
        dst_ref=o_ref.at[0, :, left, core],
        send_sem=f_send.at[0],
        recv_sem=f_recv.at[0],
        device_id={"seq": seq_of(za, right, core)},
        device_id_type=mesh_id,
    )
    relay_v = pltpu.make_async_remote_copy(
        src_ref=o_ref.at[1, :, right, core],
        dst_ref=o_ref.at[1, :, right, core],
        send_sem=f_send.at[1],
        recv_sem=f_recv.at[1],
        device_id={"seq": seq_of(za, left, core)},
        device_id_type=mesh_id,
    )
    relay_k.start()
    relay_v.start()
    pltpu.make_async_remote_copy(
        src_ref=o_ref.at[0, :, far, core],
        dst_ref=o_ref.at[0, :, far, core],
        send_sem=f_send.at[0],
        recv_sem=f_recv.at[0],
        device_id={"seq": seq_of(za, right, core)},
        device_id_type=mesh_id,
    ).wait_recv()
    pltpu.make_async_remote_copy(
        src_ref=o_ref.at[1, :, far, core],
        dst_ref=o_ref.at[1, :, far, core],
        send_sem=f_send.at[1],
        recv_sem=f_recv.at[1],
        device_id={"seq": seq_of(za, left, core)},
        device_id_type=mesh_id,
    ).wait_recv()
    relay_k.wait_send()
    relay_v.wait_send()

    across = [
        pltpu.make_async_remote_copy(
            src_ref=o_ref.at[a, :, :, core],
            dst_ref=o_ref.at[a, :, :, core],
            send_sem=c_send.at[a],
            recv_sem=c_recv.at[a],
            device_id={"seq": seq_of(za, xb, 1 - core)},
            device_id_type=mesh_id,
        )
        for a in range(parts)
    ]
    for copy in across:
        copy.start()
    for copy in across:
        copy.wait_send()
        copy.wait_recv()


def seq_gather(stacked, n, cid):
    parts, rows, cols = stacked.shape
    chips = n // 2
    xs = 4
    zs = chips // xs
    return pl.pallas_call(
        functools.partial(seq_gather_kernel, zs, xs),
        out_shape=jax.ShapeDtypeStruct((parts, zs, xs, 2, rows, cols), stacked.dtype),
        in_specs=[pl.BlockSpec(memory_space=pl.ANY)],
        out_specs=pl.BlockSpec(memory_space=pl.ANY),
        scratch_shapes=[
            pltpu.SemaphoreType.DMA((parts, zs)),
            pltpu.SemaphoreType.DMA((parts, zs)),
            pltpu.SemaphoreType.DMA((parts, 2)),
            pltpu.SemaphoreType.DMA((parts, 2)),
            pltpu.SemaphoreType.DMA((parts,)),
            pltpu.SemaphoreType.DMA((parts,)),
            pltpu.SemaphoreType.DMA((parts,)),
            pltpu.SemaphoreType.DMA((parts,)),
            pltpu.SemaphoreType.DMA,
        ],
        compiler_params=pltpu.CompilerParams(collective_id=cid, has_side_effects=True),
    )(stacked)


def tp_gather_kernel(ys, x_ref, o_ref, p_send, p_recv, r_send, r_recv, f_send, f_recv, local_sem):
    me = lax.axis_index("tp")
    yy = me // 2
    zh = me % 2
    right = lax.rem(yy + 1, ys)
    left = lax.rem(yy + ys - 1, ys)
    far = lax.rem(yy + 2, ys)
    width = x_ref.shape[1]
    mesh_id = pl.DeviceIdType.MESH

    def cols(y, h):
        return pl.ds(pl.multiple_of((y * 2 + h) * width, 128), width)

    def pair(y):
        return pl.ds(pl.multiple_of(y * 2 * width, 128), 2 * width)

    def signal(target):
        pl.semaphore_signal(barrier, inc=1, device_id={"tp": target}, device_id_type=mesh_id)

    barrier = pltpu.get_barrier_semaphore()
    signal(yy * 2 + 1 - zh)
    signal(right * 2 + zh)
    signal(left * 2 + zh)
    pl.semaphore_wait(barrier, 3)

    local = pltpu.make_async_copy(x_ref, o_ref.at[:, cols(yy, zh)], local_sem)
    local.start()
    to_partner = pltpu.make_async_remote_copy(
        src_ref=x_ref,
        dst_ref=o_ref.at[:, cols(yy, zh)],
        send_sem=p_send,
        recv_sem=p_recv,
        device_id={"tp": yy * 2 + 1 - zh},
        device_id_type=mesh_id,
    )
    to_partner.start()
    pltpu.make_async_remote_copy(
        src_ref=x_ref,
        dst_ref=o_ref.at[:, cols(yy, 1 - zh)],
        send_sem=p_send,
        recv_sem=p_recv,
        device_id={"tp": yy * 2 + 1 - zh},
        device_id_type=mesh_id,
    ).wait_recv()
    local.wait()
    to_partner.wait_send()

    def ring(group, target, side):
        return pltpu.make_async_remote_copy(
            src_ref=o_ref.at[:, pair(group)],
            dst_ref=o_ref.at[:, pair(group)],
            send_sem=r_send.at[side],
            recv_sem=r_recv.at[side],
            device_id={"tp": target * 2 + zh},
            device_id_type=mesh_id,
        )

    outgoing = [ring(yy, right, 0), ring(yy, left, 1)]
    for copy in outgoing:
        copy.start()
    ring(left, right, 0).wait_recv()
    ring(right, left, 1).wait_recv()
    for copy in outgoing:
        copy.wait_send()

    def relay(group, h, target, side):
        return pltpu.make_async_remote_copy(
            src_ref=o_ref.at[:, cols(group, h)],
            dst_ref=o_ref.at[:, cols(group, h)],
            send_sem=f_send.at[side],
            recv_sem=f_recv.at[side],
            device_id={"tp": target * 2 + zh},
            device_id_type=mesh_id,
        )

    relays = [relay(left, 0, right, 0), relay(right, 1, left, 1)]
    for copy in relays:
        copy.start()
    relay(far, 0, right, 0).wait_recv()
    relay(far, 1, left, 1).wait_recv()
    for copy in relays:
        copy.wait_send()


def tp_gather(block, n, cid):
    rows, width = block.shape
    return pl.pallas_call(
        functools.partial(tp_gather_kernel, n // 2),
        out_shape=jax.ShapeDtypeStruct((rows, width * n), block.dtype),
        in_specs=[pl.BlockSpec(memory_space=pl.ANY)],
        out_specs=pl.BlockSpec(memory_space=pl.ANY),
        scratch_shapes=[
            pltpu.SemaphoreType.DMA,
            pltpu.SemaphoreType.DMA,
            pltpu.SemaphoreType.DMA((2,)),
            pltpu.SemaphoreType.DMA((2,)),
            pltpu.SemaphoreType.DMA((2,)),
            pltpu.SemaphoreType.DMA((2,)),
            pltpu.SemaphoreType.DMA,
        ],
        compiler_params=pltpu.CompilerParams(collective_id=cid, has_side_effects=True),
    )(block)


def attention_kernel(
    scale, group_pages,
    wants, page_order, s_idx, s_cnt,
    q_ref, q_want, q_req, q_pos,
    pk_ref, pv_ref,
    sk_ref, sv_ref, s_tag, s_bound,
    o_ref, m_sc, l_sc, acc_sc, pm_sc, pl_sc, pacc_sc,
):
    prefixes, per_prefix = page_order.shape

    def update(m_ref, l_ref, acc_ref, score_list, value_list):
        run_max = m_ref[...]
        new_max = run_max
        for scores in score_list:
            new_max = jnp.maximum(new_max, jnp.max(scores, axis=1, keepdims=True))
        fade = jnp.exp(run_max - new_max)
        total = l_ref[...] * fade
        acc = acc_ref[...] * fade
        for scores, values in zip(score_list, value_list):
            weights = jnp.exp(scores - new_max)
            total = total + jnp.sum(weights, axis=1, keepdims=True)
            acc = acc + jnp.dot(weights.astype(jnp.bfloat16), values, preferred_element_type=jnp.float32)
        l_ref[...] = total
        acc_ref[...] = acc
        m_ref[...] = new_max

    for i in range(q_ref.shape[0]):
        m_sc[...] = jnp.full(m_sc.shape, -1e30, jnp.float32)
        l_sc[...] = jnp.zeros(l_sc.shape, jnp.float32)
        acc_sc[...] = jnp.zeros(acc_sc.shape, jnp.float32)
        query = q_ref[i]
        want = q_want[i]
        req = q_req[i]
        pos = q_pos[i]

        def score(keys):
            return lax.dot_general(
                query, keys, (((1,), (1,)), ((), ())), preferred_element_type=jnp.float32
            ) * scale

        for p in range(prefixes):
            @pl.when(wants[i, p] > 0)
            def _():
                pm_sc[...] = jnp.full(pm_sc.shape, -1e30, jnp.float32)
                pl_sc[...] = jnp.zeros(pl_sc.shape, jnp.float32)
                pacc_sc[...] = jnp.zeros(pacc_sc.shape, jnp.float32)

                def page_step(g, carry):
                    pages = [page_order[p, g * group_pages + j] for j in range(group_pages)]
                    update(pm_sc, pl_sc, pacc_sc, [score(pk_ref[b]) for b in pages], [pv_ref[b] for b in pages])
                    return carry

                lax.fori_loop(0, per_prefix // group_pages, page_step, 0)
                mine = want == p
                m_sc[...] = jnp.where(mine, pm_sc[...], m_sc[...])
                l_sc[...] = jnp.where(mine, pl_sc[...], l_sc[...])
                acc_sc[...] = jnp.where(mine, pacc_sc[...], acc_sc[...])

        def step(n, carry):
            b = s_idx[i, n]
            scores = score(sk_ref[b])
            seen = (s_tag[b] == req) & (s_bound[b] <= pos)
            run_max = m_sc[...]
            new_max = jnp.maximum(
                run_max, jnp.max(jnp.where(seen, scores, -1e30), axis=1, keepdims=True)
            )
            weights = jnp.where(seen, jnp.exp(scores - new_max), 0.0)
            fade = jnp.exp(run_max - new_max)
            l_sc[...] = l_sc[...] * fade + jnp.sum(weights, axis=1, keepdims=True)
            acc_sc[...] = acc_sc[...] * fade + jnp.dot(
                weights.astype(jnp.bfloat16), sv_ref[b], preferred_element_type=jnp.float32
            )
            m_sc[...] = new_max
            return carry

        lax.fori_loop(0, s_cnt[i], step, 0)
        o_ref[i] = (acc_sc[...] / l_sc[...]).astype(o_ref.dtype)


def block_attention(scale, lists, queries, query_meta, prefix_parts, suffix_parts):
    q_blocks, q_rows, width = queries.shape
    smem = pl.BlockSpec(memory_space=pltpu.SMEM)
    vmem = pl.BlockSpec(memory_space=pltpu.VMEM)
    state = [
        pltpu.VMEM((q_rows, 1), jnp.float32),
        pltpu.VMEM((q_rows, 1), jnp.float32),
        pltpu.VMEM((q_rows, width), jnp.float32),
    ]
    return pl.pallas_call(
        functools.partial(attention_kernel, scale, 4),
        out_shape=jax.ShapeDtypeStruct((q_blocks, q_rows, width), jnp.bfloat16),
        in_specs=[smem] * 4 + [vmem] * 10,
        out_specs=vmem,
        scratch_shapes=state + state,
        compiler_params=pltpu.CompilerParams(vmem_limit_bytes=48 * 1024 * 1024),
    )(*lists, queries, *query_meta, *prefix_parts, *suffix_parts)


def visible_list(visible):
    order = jnp.argsort(jnp.logical_not(visible), axis=1, stable=True).astype(jnp.int32)
    return order, jnp.sum(visible.astype(jnp.int32), axis=1)


def body(
    seq_n,
    tp_n,
    hidden,
    norm_gain,
    w_query,
    w_key,
    w_value,
    prefix_keys,
    prefix_values,
    page_prefix,
    request_prefix,
    suffix_lengths,
    row_order,
):
    gathered_prefix = lax.all_gather(
        jnp.concatenate([prefix_keys, prefix_values], axis=1), "seq", axis=0, tiled=True
    )
    gathered = tp_gather(hidden, tp_n, 2)
    local_rows = gathered.shape[0]
    hidden_f = gathered.astype(jnp.float32)
    mean_sq = jnp.mean(hidden_f * hidden_f, axis=1, keepdims=True)
    normed = (
        hidden_f * lax.rsqrt(mean_sq + 1e-05) * norm_gain.astype(jnp.float32)[None, :]
    ).astype(jnp.bfloat16)
    request_all, position_all, wanted_all = locate(row_order, suffix_lengths, request_prefix)
    offset = lax.axis_index("seq") * local_rows
    request = lax.dynamic_slice_in_dim(request_all, offset, local_rows)
    position = lax.dynamic_slice_in_dim(position_all, offset, local_rows)
    wanted = lax.dynamic_slice_in_dim(wanted_all, offset, local_rows)
    prefix_len = page_prefix.shape[0] * PAGE // PREFIXES
    rope_at = prefix_len + position
    q_heads = w_query.shape[1] // HEAD
    kv_heads = w_key.shape[1] // HEAD
    group_size = q_heads // kv_heads
    queries = rotate(
        jnp.dot(normed, w_query, preferred_element_type=jnp.float32).reshape(
            local_rows, q_heads, HEAD
        ),
        rope_at,
    ).astype(jnp.bfloat16)
    queries = queries.reshape(local_rows, kv_heads, group_size, HEAD)
    new_keys = rotate(
        jnp.dot(normed, w_key, preferred_element_type=jnp.float32).reshape(
            local_rows, kv_heads, HEAD
        ),
        rope_at,
    ).astype(jnp.bfloat16)
    new_keys = new_keys.reshape(local_rows, kv_heads * HEAD)
    new_values = jnp.dot(normed, w_value, preferred_element_type=jnp.float32).astype(jnp.bfloat16)
    score_scale = 1.0 / math.sqrt(HEAD)
    block = PAGE
    q_blocks = local_rows // block
    pages = page_prefix.shape[0]
    runs = row_order.shape[0] // block
    stacked_q = (
        queries.reshape(q_blocks, block, group_size, HEAD)
        .transpose(0, 2, 1, 3)
        .reshape(q_blocks, group_size * block, HEAD)
    )

    def per_query(values):
        spread = jnp.broadcast_to(values.reshape(q_blocks, 1, block), (q_blocks, group_size, block))
        return spread.reshape(q_blocks, group_size * block, 1).astype(jnp.int32)

    query_meta = (per_query(wanted), per_query(request + PREFIXES), per_query(position))
    want_blocks = wanted.reshape(q_blocks, block)
    block_wants = jnp.any(
        want_blocks[:, :, None] == jnp.arange(PREFIXES, dtype=jnp.int32)[None, None, :], axis=1
    )
    page_order = jnp.argsort(page_prefix, stable=True).astype(jnp.int32).reshape(PREFIXES, -1)
    local_place = lax.dynamic_slice_in_dim(row_order, offset, local_rows).reshape(q_blocks, block)
    first_seen = jnp.min(local_place - position.reshape(q_blocks, block), axis=1)
    last_seen = jnp.max(local_place, axis=1)
    run_place = row_order.reshape(runs, block)
    run_low = jnp.min(run_place, axis=1)
    run_high = jnp.max(run_place, axis=1)
    run_visible = (run_low[None, :] <= last_seen[:, None]) & (run_high[None, :] >= first_seen[:, None])
    s_idx, s_cnt = visible_list(run_visible)

    seq_n_blocks = seq_n
    prefix_parts = (
        gathered_prefix[:, :HEAD].reshape(pages, block, HEAD),
        gathered_prefix[:, HEAD:].reshape(pages, block, HEAD),
    )
    gathered_suffix = seq_gather(jnp.stack([new_keys, new_values]), seq_n_blocks, 1)
    suffix_parts = (
        gathered_suffix[0].reshape(runs, block, HEAD),
        gathered_suffix[1].reshape(runs, block, HEAD),
        (request_all + PREFIXES).reshape(runs, 1, block).astype(jnp.int32),
        position_all.reshape(runs, 1, block).astype(jnp.int32),
    )
    out = block_attention(
        score_scale, (block_wants.astype(jnp.int32), page_order, s_idx, s_cnt), stacked_q, query_meta, prefix_parts, suffix_parts
    )
    attended = (
        out.reshape(q_blocks, group_size, block, HEAD)
        .transpose(0, 2, 1, 3)
        .reshape(local_rows, group_size * HEAD)
    )
    return (attended, new_keys, new_values)


def solution(mesh):
    return jax.shard_map(
        functools.partial(body, mesh.shape["seq"], mesh.shape["tp"]),
        mesh=mesh,
        in_specs=(
            P("seq", "tp"),
            P(),
            P(None, "tp"),
            P(None, "tp"),
            P(None, "tp"),
            P("seq", "tp"),
            P("seq", "tp"),
            P(),
            P(),
            P(),
            P(),
        ),
        out_specs=(P("seq", "tp"), P("seq", "tp"), P("seq", "tp")),
        check_vma=False,
    )
```

```python
import functools
import math

import jax
import jax.numpy as jnp
from jax import lax
from jax.sharding import PartitionSpec as P
from jax.experimental import pallas as pl
from jax.experimental.pallas import tpu as pltpu

HEAD = 128
PAGE = 128
PREFIXES = 4


ROPE_BASE = 5000000.0


def rotate(tensor_in, positions):
    head_dim = tensor_in.shape[-1]
    half_dim = head_dim // 2
    frequency = ROPE_BASE ** (-(jnp.arange(half_dim, dtype=jnp.float32) * 2.0 / head_dim))
    angles = positions.astype(jnp.float32)[:, None] * frequency[None, :]
    cosine = jnp.cos(angles)[:, None, :]
    sine_part = jnp.sin(angles)[:, None, :]
    first_half = tensor_in[..., :half_dim]
    second_half = tensor_in[..., half_dim:]
    return jnp.concatenate(
        [
            first_half * cosine - second_half * sine_part,
            second_half * cosine + first_half * sine_part,
        ],
        axis=-1,
    )


def locate(row_order, suffix_lengths, request_prefix):
    end_rows = jnp.cumsum(suffix_lengths)
    starts = end_rows - suffix_lengths
    numbers = jnp.arange(suffix_lengths.shape[0], dtype=jnp.int32)
    request = jnp.sum((row_order[:, None] >= end_rows[None, :]).astype(jnp.int32), axis=1)
    chosen = request[:, None] == numbers[None, :]
    position = row_order - jnp.sum(jnp.where(chosen, starts[None, :], 0), axis=1)
    wanted = jnp.sum(jnp.where(chosen, request_prefix[None, :], 0), axis=1)
    return (request, position, wanted)


def seq_gather_kernel(
    zs, xs, x_ref, o_ref, z_send, z_recv, r_send, r_recv, f_send, f_recv, c_send, c_recv, local_sem
):
    me = lax.axis_index("seq")
    core = me % 2
    chip = me // 2
    za = chip // xs
    xb = chip % xs
    right = lax.rem(xb + 1, xs)
    left = lax.rem(xb + xs - 1, xs)
    parts = x_ref.shape[0]
    mesh_id = pl.DeviceIdType.MESH

    def seq_of(z, x, c):
        return (z * xs + x) * 2 + c

    def signal(sem, target):
        pl.semaphore_signal(sem, inc=1, device_id={"seq": target}, device_id_type=mesh_id)

    barrier = pltpu.get_barrier_semaphore()

    def greet(k, carry):
        signal(barrier, seq_of(lax.rem(za + k, zs), xb, core))
        return carry

    lax.fori_loop(1, zs, greet, 0)
    signal(barrier, seq_of(za, right, core))
    signal(barrier, seq_of(za, left, core))
    signal(barrier, seq_of(za, xb, 1 - core))
    pl.semaphore_wait(barrier, zs + 2)

    local = pltpu.make_async_copy(x_ref, o_ref.at[:, za, xb, core], local_sem)
    local.start()

    def z_copy(a, peer_z, slot_z):
        return pltpu.make_async_remote_copy(
            src_ref=x_ref.at[a],
            dst_ref=o_ref.at[a, slot_z, xb, core],
            send_sem=z_send.at[a, peer_z],
            recv_sem=z_recv.at[a, slot_z],
            device_id={"seq": seq_of(peer_z, xb, core)},
            device_id_type=mesh_id,
        )

    def z_start(k, carry):
        peer_z = lax.rem(za + k, zs)
        for a in range(parts):
            z_copy(a, peer_z, za).start()
        return carry

    lax.fori_loop(1, zs, z_start, 0)

    def z_finish(k, carry):
        peer_z = lax.rem(za + k, zs)
        for a in range(parts):
            copy = z_copy(a, peer_z, peer_z)
            copy.wait_send()
            copy.wait_recv()
        return carry

    lax.fori_loop(1, zs, z_finish, 0)
    local.wait()

    def ring_copy(a, side, group, target_x, sem_side):
        return pltpu.make_async_remote_copy(
            src_ref=o_ref.at[a, :, group, core],
            dst_ref=o_ref.at[a, :, group, core],
            send_sem=r_send.at[a, side],
            recv_sem=r_recv.at[a, sem_side],
            device_id={"seq": seq_of(za, target_x, core)},
            device_id_type=mesh_id,
        )

    outgoing = []
    for a in range(parts):
        outgoing.append(ring_copy(a, 0, xb, right, 0))
        outgoing.append(ring_copy(a, 1, xb, left, 1))
    for copy in outgoing:
        copy.start()
    for a in range(parts):
        ring_copy(a, 0, left, right, 0).wait_recv()
        ring_copy(a, 1, right, left, 1).wait_recv()
    for copy in outgoing:
        copy.wait_send()

    far = lax.rem(xb + 2, xs)
    relay_k = pltpu.make_async_remote_copy(
        src_ref=o_ref.at[0, :, left, core],
        dst_ref=o_ref.at[0, :, left, core],
        send_sem=f_send.at[0],
        recv_sem=f_recv.at[0],
        device_id={"seq": seq_of(za, right, core)},
        device_id_type=mesh_id,
    )
    relay_v = pltpu.make_async_remote_copy(
        src_ref=o_ref.at[1, :, right, core],
        dst_ref=o_ref.at[1, :, right, core],
        send_sem=f_send.at[1],
        recv_sem=f_recv.at[1],
        device_id={"seq": seq_of(za, left, core)},
        device_id_type=mesh_id,
    )
    relay_k.start()
    relay_v.start()
    pltpu.make_async_remote_copy(
        src_ref=o_ref.at[0, :, far, core],
        dst_ref=o_ref.at[0, :, far, core],
        send_sem=f_send.at[0],
        recv_sem=f_recv.at[0],
        device_id={"seq": seq_of(za, right, core)},
        device_id_type=mesh_id,
    ).wait_recv()
    pltpu.make_async_remote_copy(
        src_ref=o_ref.at[1, :, far, core],
        dst_ref=o_ref.at[1, :, far, core],
        send_sem=f_send.at[1],
        recv_sem=f_recv.at[1],
        device_id={"seq": seq_of(za, left, core)},
        device_id_type=mesh_id,
    ).wait_recv()
    relay_k.wait_send()
    relay_v.wait_send()

    across = [
        pltpu.make_async_remote_copy(
            src_ref=o_ref.at[a, :, :, core],
            dst_ref=o_ref.at[a, :, :, core],
            send_sem=c_send.at[a],
            recv_sem=c_recv.at[a],
            device_id={"seq": seq_of(za, xb, 1 - core)},
            device_id_type=mesh_id,
        )
        for a in range(parts)
    ]
    for copy in across:
        copy.start()
    for copy in across:
        copy.wait_send()
        copy.wait_recv()


def seq_gather(stacked, n, cid):
    parts, rows, cols = stacked.shape
    chips = n // 2
    xs = 4
    zs = chips // xs
    return pl.pallas_call(
        functools.partial(seq_gather_kernel, zs, xs),
        out_shape=jax.ShapeDtypeStruct((parts, zs, xs, 2, rows, cols), stacked.dtype),
        in_specs=[pl.BlockSpec(memory_space=pl.ANY)],
        out_specs=pl.BlockSpec(memory_space=pl.ANY),
        scratch_shapes=[
            pltpu.SemaphoreType.DMA((parts, zs)),
            pltpu.SemaphoreType.DMA((parts, zs)),
            pltpu.SemaphoreType.DMA((parts, 2)),
            pltpu.SemaphoreType.DMA((parts, 2)),
            pltpu.SemaphoreType.DMA((parts,)),
            pltpu.SemaphoreType.DMA((parts,)),
            pltpu.SemaphoreType.DMA((parts,)),
            pltpu.SemaphoreType.DMA((parts,)),
            pltpu.SemaphoreType.DMA,
        ],
        compiler_params=pltpu.CompilerParams(collective_id=cid, has_side_effects=True),
    )(stacked)


def tp_gather_kernel(ys, x_ref, o_ref, p_send, p_recv, r_send, r_recv, f_send, f_recv, local_sem):
    me = lax.axis_index("tp")
    yy = me // 2
    zh = me % 2
    right = lax.rem(yy + 1, ys)
    left = lax.rem(yy + ys - 1, ys)
    far = lax.rem(yy + 2, ys)
    width = x_ref.shape[1]
    mesh_id = pl.DeviceIdType.MESH

    def cols(y, h):
        return pl.ds(pl.multiple_of((y * 2 + h) * width, 128), width)

    def pair(y):
        return pl.ds(pl.multiple_of(y * 2 * width, 128), 2 * width)

    def signal(target):
        pl.semaphore_signal(barrier, inc=1, device_id={"tp": target}, device_id_type=mesh_id)

    barrier = pltpu.get_barrier_semaphore()
    signal(yy * 2 + 1 - zh)
    signal(right * 2 + zh)
    signal(left * 2 + zh)
    pl.semaphore_wait(barrier, 3)

    local = pltpu.make_async_copy(x_ref, o_ref.at[:, cols(yy, zh)], local_sem)
    local.start()
    to_partner = pltpu.make_async_remote_copy(
        src_ref=x_ref,
        dst_ref=o_ref.at[:, cols(yy, zh)],
        send_sem=p_send,
        recv_sem=p_recv,
        device_id={"tp": yy * 2 + 1 - zh},
        device_id_type=mesh_id,
    )
    to_partner.start()
    pltpu.make_async_remote_copy(
        src_ref=x_ref,
        dst_ref=o_ref.at[:, cols(yy, 1 - zh)],
        send_sem=p_send,
        recv_sem=p_recv,
        device_id={"tp": yy * 2 + 1 - zh},
        device_id_type=mesh_id,
    ).wait_recv()
    local.wait()
    to_partner.wait_send()

    def ring(group, target, side):
        return pltpu.make_async_remote_copy(
            src_ref=o_ref.at[:, pair(group)],
            dst_ref=o_ref.at[:, pair(group)],
            send_sem=r_send.at[side],
            recv_sem=r_recv.at[side],
            device_id={"tp": target * 2 + zh},
            device_id_type=mesh_id,
        )

    outgoing = [ring(yy, right, 0), ring(yy, left, 1)]
    for copy in outgoing:
        copy.start()
    ring(left, right, 0).wait_recv()
    ring(right, left, 1).wait_recv()
    for copy in outgoing:
        copy.wait_send()

    def relay(group, h, target, side):
        return pltpu.make_async_remote_copy(
            src_ref=o_ref.at[:, cols(group, h)],
            dst_ref=o_ref.at[:, cols(group, h)],
            send_sem=f_send.at[side],
            recv_sem=f_recv.at[side],
            device_id={"tp": target * 2 + zh},
            device_id_type=mesh_id,
        )

    relays = [relay(left, 0, right, 0), relay(right, 1, left, 1)]
    for copy in relays:
        copy.start()
    relay(far, 0, right, 0).wait_recv()
    relay(far, 1, left, 1).wait_recv()
    for copy in relays:
        copy.wait_send()


def tp_gather(block, n, cid):
    rows, width = block.shape
    return pl.pallas_call(
        functools.partial(tp_gather_kernel, n // 2),
        out_shape=jax.ShapeDtypeStruct((rows, width * n), block.dtype),
        in_specs=[pl.BlockSpec(memory_space=pl.ANY)],
        out_specs=pl.BlockSpec(memory_space=pl.ANY),
        scratch_shapes=[
            pltpu.SemaphoreType.DMA,
            pltpu.SemaphoreType.DMA,
            pltpu.SemaphoreType.DMA((2,)),
            pltpu.SemaphoreType.DMA((2,)),
            pltpu.SemaphoreType.DMA((2,)),
            pltpu.SemaphoreType.DMA((2,)),
            pltpu.SemaphoreType.DMA,
        ],
        compiler_params=pltpu.CompilerParams(collective_id=cid, has_side_effects=True),
    )(block)


def attention_kernel(
    scale, group_pages,
    wants, page_order, s_idx, s_cnt,
    q_ref, q_want, q_req, q_pos,
    p_ref,
    s_ref, s_tag, s_bound,
    o_ref, m_sc, l_sc, acc_sc, pm_sc, pl_sc, pacc_sc,
):
    prefixes, per_prefix = page_order.shape

    def update(m_ref, l_ref, acc_ref, score_list, value_list):
        run_max = m_ref[...]
        new_max = run_max
        for scores in score_list:
            new_max = jnp.maximum(new_max, jnp.max(scores, axis=1, keepdims=True))
        fade = jnp.exp(run_max - new_max)
        total = l_ref[...] * fade
        acc = acc_ref[...] * fade
        for scores, values in zip(score_list, value_list):
            weights = jnp.exp(scores - new_max)
            total = total + jnp.sum(weights, axis=1, keepdims=True)
            acc = acc + jnp.dot(weights.astype(jnp.bfloat16), values, preferred_element_type=jnp.float32)
        l_ref[...] = total
        acc_ref[...] = acc
        m_ref[...] = new_max

    for i in range(q_ref.shape[0]):
        m_sc[...] = jnp.full(m_sc.shape, -1e30, jnp.float32)
        l_sc[...] = jnp.zeros(l_sc.shape, jnp.float32)
        acc_sc[...] = jnp.zeros(acc_sc.shape, jnp.float32)
        heads = q_ref.shape[2] // q_ref.shape[1]
        size = q_ref.shape[1]
        query = jnp.concatenate([q_ref[i, :, h * size:(h + 1) * size] for h in range(heads)], axis=0)
        want = q_want[i]
        req = q_req[i]
        pos = q_pos[i]

        def score(keys):
            return lax.dot_general(
                query, keys, (((1,), (1,)), ((), ())), preferred_element_type=jnp.float32
            ) * scale

        for p in range(prefixes):
            @pl.when(wants[i, p] > 0)
            def _():
                pm_sc[...] = jnp.full(pm_sc.shape, -1e30, jnp.float32)
                pl_sc[...] = jnp.zeros(pl_sc.shape, jnp.float32)
                pacc_sc[...] = jnp.zeros(pacc_sc.shape, jnp.float32)

                def page_step(g, carry):
                    pages = [page_order[p, g * group_pages + j] for j in range(group_pages)]
                    blocks = [p_ref[b] for b in pages]
                    update(
                        pm_sc, pl_sc, pacc_sc,
                        [score(blk[:, :size]) for blk in blocks],
                        [blk[:, size:] for blk in blocks],
                    )
                    return carry

                lax.fori_loop(0, per_prefix // group_pages, page_step, 0)
                mine = want == p
                m_sc[...] = jnp.where(mine, pm_sc[...], m_sc[...])
                l_sc[...] = jnp.where(mine, pl_sc[...], l_sc[...])
                acc_sc[...] = jnp.where(mine, pacc_sc[...], acc_sc[...])

        def step(n, carry):
            b = s_idx[i, n]
            scores = score(s_ref[0, b])
            seen = (s_tag[b] == req) & (s_bound[b] <= pos)
            run_max = m_sc[...]
            new_max = jnp.maximum(
                run_max, jnp.max(jnp.where(seen, scores, -1e30), axis=1, keepdims=True)
            )
            weights = jnp.where(seen, jnp.exp(scores - new_max), 0.0)
            fade = jnp.exp(run_max - new_max)
            l_sc[...] = l_sc[...] * fade + jnp.sum(weights, axis=1, keepdims=True)
            acc_sc[...] = acc_sc[...] * fade + jnp.dot(
                weights.astype(jnp.bfloat16), s_ref[1, b], preferred_element_type=jnp.float32
            )
            m_sc[...] = new_max
            return carry

        lax.fori_loop(0, s_cnt[i], step, 0)
        result = (acc_sc[...] / l_sc[...]).astype(o_ref.dtype)
        for h in range(heads):
            o_ref[i, :, h * size:(h + 1) * size] = result[h * size:(h + 1) * size]


def block_attention(scale, lists, queries, query_meta, prefix_parts, suffix_parts):
    q_blocks, block_rows, q_width = queries.shape
    width = queries.shape[1]
    q_rows = q_width // width * block_rows
    smem = pl.BlockSpec(memory_space=pltpu.SMEM)
    vmem = pl.BlockSpec(memory_space=pltpu.VMEM)
    state = [
        pltpu.VMEM((q_rows, 1), jnp.float32),
        pltpu.VMEM((q_rows, 1), jnp.float32),
        pltpu.VMEM((q_rows, width), jnp.float32),
    ]
    return pl.pallas_call(
        functools.partial(attention_kernel, scale, 4),
        out_shape=jax.ShapeDtypeStruct((q_blocks, block_rows, q_width), jnp.bfloat16),
        in_specs=[smem] * 4 + [vmem] * 8,
        out_specs=vmem,
        scratch_shapes=state + state,
        compiler_params=pltpu.CompilerParams(vmem_limit_bytes=48 * 1024 * 1024),
    )(*lists, queries, *query_meta, *prefix_parts, *suffix_parts)


def visible_list(visible):
    count = visible.shape[1]
    ids = jnp.arange(count, dtype=jnp.int32)
    rank = jnp.sum((visible[:, :, None] & (ids[:, None] < ids[None, :])[None]).astype(jnp.int32), axis=1)
    pick = visible[:, None, :] & (rank[:, None, :] == ids[None, :, None])
    order = jnp.sum(jnp.where(pick, ids[None, None, :], 0), axis=2).astype(jnp.int32)
    return order, jnp.sum(visible.astype(jnp.int32), axis=1)


def body(
    seq_n,
    tp_n,
    hidden,
    norm_gain,
    w_query,
    w_key,
    w_value,
    prefix_keys,
    prefix_values,
    page_prefix,
    request_prefix,
    suffix_lengths,
    row_order,
):
    gathered_prefix = lax.all_gather(
        jnp.concatenate([prefix_keys, prefix_values], axis=1), "seq", axis=0, tiled=True
    )
    gathered = tp_gather(hidden, tp_n, 2)
    local_rows = gathered.shape[0]
    hidden_f = gathered.astype(jnp.float32)
    mean_sq = jnp.mean(hidden_f * hidden_f, axis=1, keepdims=True)
    normed = (
        hidden_f * lax.rsqrt(mean_sq + 1e-05) * norm_gain.astype(jnp.float32)[None, :]
    ).astype(jnp.bfloat16)
    request_all, position_all, wanted_all = locate(row_order, suffix_lengths, request_prefix)
    offset = lax.axis_index("seq") * local_rows
    request = lax.dynamic_slice_in_dim(request_all, offset, local_rows)
    position = lax.dynamic_slice_in_dim(position_all, offset, local_rows)
    wanted = lax.dynamic_slice_in_dim(wanted_all, offset, local_rows)
    prefix_len = page_prefix.shape[0] * PAGE // PREFIXES
    rope_at = prefix_len + position
    q_heads = w_query.shape[1] // HEAD
    kv_heads = w_key.shape[1] // HEAD
    group_size = q_heads // kv_heads
    queries = rotate(
        jnp.dot(normed, w_query, preferred_element_type=jnp.float32).reshape(
            local_rows, q_heads, HEAD
        ),
        rope_at,
    ).astype(jnp.bfloat16)
    queries = queries.reshape(local_rows, kv_heads, group_size, HEAD)
    new_keys = rotate(
        jnp.dot(normed, w_key, preferred_element_type=jnp.float32).reshape(
            local_rows, kv_heads, HEAD
        ),
        rope_at,
    ).astype(jnp.bfloat16)
    new_keys = new_keys.reshape(local_rows, kv_heads * HEAD)
    new_values = jnp.dot(normed, w_value, preferred_element_type=jnp.float32).astype(jnp.bfloat16)
    score_scale = 1.0 / math.sqrt(HEAD)
    block = PAGE
    q_blocks = local_rows // block
    pages = page_prefix.shape[0]
    runs = row_order.shape[0] // block
    stacked_q = queries.reshape(q_blocks, block, group_size * HEAD)

    def per_query(values):
        spread = jnp.broadcast_to(values.reshape(q_blocks, 1, block), (q_blocks, group_size, block))
        return spread.reshape(q_blocks, group_size * block, 1).astype(jnp.int32)

    query_meta = (per_query(wanted), per_query(request + PREFIXES), per_query(position))
    want_blocks = wanted.reshape(q_blocks, block)
    block_wants = jnp.any(
        want_blocks[:, :, None] == jnp.arange(PREFIXES, dtype=jnp.int32)[None, None, :], axis=1
    )
    page_ids = jnp.arange(pages, dtype=jnp.int32)
    same = (page_prefix[:, None] == page_prefix[None, :]) & (page_ids[:, None] < page_ids[None, :])
    page_rank = jnp.sum(same.astype(jnp.int32), axis=0)
    per_prefix = pages // PREFIXES
    pick = (page_prefix[None, None, :] == jnp.arange(PREFIXES, dtype=jnp.int32)[:, None, None]) & (
        page_rank[None, None, :] == jnp.arange(per_prefix, dtype=jnp.int32)[None, :, None]
    )
    page_order = jnp.sum(jnp.where(pick, page_ids[None, None, :], 0), axis=2).astype(jnp.int32)
    local_place = lax.dynamic_slice_in_dim(row_order, offset, local_rows).reshape(q_blocks, block)
    first_seen = jnp.min(local_place - position.reshape(q_blocks, block), axis=1)
    last_seen = jnp.max(local_place, axis=1)
    run_place = row_order.reshape(runs, block)
    run_low = jnp.min(run_place, axis=1)
    run_high = jnp.max(run_place, axis=1)
    run_visible = (run_low[None, :] <= last_seen[:, None]) & (run_high[None, :] >= first_seen[:, None])
    s_idx, s_cnt = visible_list(run_visible)

    seq_n_blocks = seq_n
    prefix_parts = (gathered_prefix.reshape(pages, block, 2 * HEAD),)
    gathered_suffix = seq_gather(jnp.stack([new_keys, new_values]), seq_n_blocks, 1)
    suffix_parts = (
        gathered_suffix.reshape(2, runs, block, HEAD),
        (request_all + PREFIXES).reshape(runs, 1, block).astype(jnp.int32),
        position_all.reshape(runs, 1, block).astype(jnp.int32),
    )
    out = block_attention(
        score_scale, (block_wants.astype(jnp.int32), page_order, s_idx, s_cnt), stacked_q, query_meta, prefix_parts, suffix_parts
    )
    attended = out.reshape(local_rows, group_size * HEAD)
    return (attended, new_keys, new_values)


def solution(mesh):
    return jax.shard_map(
        functools.partial(body, mesh.shape["seq"], mesh.shape["tp"]),
        mesh=mesh,
        in_specs=(
            P("seq", "tp"),
            P(),
            P(None, "tp"),
            P(None, "tp"),
            P(None, "tp"),
            P("seq", "tp"),
            P("seq", "tp"),
            P(),
            P(),
            P(),
            P(),
        ),
        out_specs=(P("seq", "tp"), P("seq", "tp"), P("seq", "tp")),
        check_vma=False,
    )
```

```python
import functools
import math

import jax
import jax.numpy as jnp
from jax import lax
from jax.sharding import PartitionSpec as P
from jax.experimental import pallas as pl
from jax.experimental.pallas import tpu as pltpu

HEAD = 128
PAGE = 128
PREFIXES = 4


ROPE_BASE = 5000000.0


def rotate(tensor_in, positions):
    head_dim = tensor_in.shape[-1]
    half_dim = head_dim // 2
    frequency = ROPE_BASE ** (-(jnp.arange(half_dim, dtype=jnp.float32) * 2.0 / head_dim))
    angles = positions.astype(jnp.float32)[:, None] * frequency[None, :]
    cosine = jnp.cos(angles)[:, None, :]
    sine_part = jnp.sin(angles)[:, None, :]
    first_half = tensor_in[..., :half_dim]
    second_half = tensor_in[..., half_dim:]
    return jnp.concatenate(
        [
            first_half * cosine - second_half * sine_part,
            second_half * cosine + first_half * sine_part,
        ],
        axis=-1,
    )


def locate(row_order, suffix_lengths, request_prefix):
    end_rows = jnp.cumsum(suffix_lengths)
    starts = end_rows - suffix_lengths
    numbers = jnp.arange(suffix_lengths.shape[0], dtype=jnp.int32)
    request = jnp.sum((row_order[:, None] >= end_rows[None, :]).astype(jnp.int32), axis=1)
    chosen = request[:, None] == numbers[None, :]
    position = row_order - jnp.sum(jnp.where(chosen, starts[None, :], 0), axis=1)
    wanted = jnp.sum(jnp.where(chosen, request_prefix[None, :], 0), axis=1)
    return (request, position, wanted)


def seq_gather_kernel(
    zs, xs, x_ref, o_ref, z_send, z_recv, r_send, r_recv, f_send, f_recv, c_send, c_recv, local_sem
):
    me = lax.axis_index("seq")
    core = me % 2
    chip = me // 2
    za = chip // xs
    xb = chip % xs
    right = lax.rem(xb + 1, xs)
    left = lax.rem(xb + xs - 1, xs)
    parts = x_ref.shape[0]
    mesh_id = pl.DeviceIdType.MESH

    def seq_of(z, x, c):
        return (z * xs + x) * 2 + c

    def signal(sem, target):
        pl.semaphore_signal(sem, inc=1, device_id={"seq": target}, device_id_type=mesh_id)

    barrier = pltpu.get_barrier_semaphore()

    def greet(k, carry):
        signal(barrier, seq_of(lax.rem(za + k, zs), xb, core))
        return carry

    lax.fori_loop(1, zs, greet, 0)
    signal(barrier, seq_of(za, right, core))
    signal(barrier, seq_of(za, left, core))
    signal(barrier, seq_of(za, xb, 1 - core))
    pl.semaphore_wait(barrier, zs + 2)

    local = pltpu.make_async_copy(x_ref, o_ref.at[:, za, xb, core], local_sem)
    local.start()

    def z_copy(a, peer_z, slot_z):
        return pltpu.make_async_remote_copy(
            src_ref=x_ref.at[a],
            dst_ref=o_ref.at[a, slot_z, xb, core],
            send_sem=z_send.at[a, peer_z],
            recv_sem=z_recv.at[a, slot_z],
            device_id={"seq": seq_of(peer_z, xb, core)},
            device_id_type=mesh_id,
        )

    def z_start(k, carry):
        peer_z = lax.rem(za + k, zs)
        for a in range(parts):
            z_copy(a, peer_z, za).start()
        return carry

    lax.fori_loop(1, zs, z_start, 0)

    def z_finish(k, carry):
        peer_z = lax.rem(za + k, zs)
        for a in range(parts):
            copy = z_copy(a, peer_z, peer_z)
            copy.wait_send()
            copy.wait_recv()
        return carry

    lax.fori_loop(1, zs, z_finish, 0)
    local.wait()

    def ring_copy(a, side, group, target_x, sem_side):
        return pltpu.make_async_remote_copy(
            src_ref=o_ref.at[a, :, group, core],
            dst_ref=o_ref.at[a, :, group, core],
            send_sem=r_send.at[a, side],
            recv_sem=r_recv.at[a, sem_side],
            device_id={"seq": seq_of(za, target_x, core)},
            device_id_type=mesh_id,
        )

    outgoing = []
    for a in range(parts):
        outgoing.append(ring_copy(a, 0, xb, right, 0))
        outgoing.append(ring_copy(a, 1, xb, left, 1))
    for copy in outgoing:
        copy.start()
    for a in range(parts):
        ring_copy(a, 0, left, right, 0).wait_recv()
        ring_copy(a, 1, right, left, 1).wait_recv()
    for copy in outgoing:
        copy.wait_send()

    far = lax.rem(xb + 2, xs)
    relay_k = pltpu.make_async_remote_copy(
        src_ref=o_ref.at[0, :, left, core],
        dst_ref=o_ref.at[0, :, left, core],
        send_sem=f_send.at[0],
        recv_sem=f_recv.at[0],
        device_id={"seq": seq_of(za, right, core)},
        device_id_type=mesh_id,
    )
    relay_v = pltpu.make_async_remote_copy(
        src_ref=o_ref.at[1, :, right, core],
        dst_ref=o_ref.at[1, :, right, core],
        send_sem=f_send.at[1],
        recv_sem=f_recv.at[1],
        device_id={"seq": seq_of(za, left, core)},
        device_id_type=mesh_id,
    )
    relay_k.start()
    relay_v.start()
    pltpu.make_async_remote_copy(
        src_ref=o_ref.at[0, :, far, core],
        dst_ref=o_ref.at[0, :, far, core],
        send_sem=f_send.at[0],
        recv_sem=f_recv.at[0],
        device_id={"seq": seq_of(za, right, core)},
        device_id_type=mesh_id,
    ).wait_recv()
    pltpu.make_async_remote_copy(
        src_ref=o_ref.at[1, :, far, core],
        dst_ref=o_ref.at[1, :, far, core],
        send_sem=f_send.at[1],
        recv_sem=f_recv.at[1],
        device_id={"seq": seq_of(za, left, core)},
        device_id_type=mesh_id,
    ).wait_recv()
    relay_k.wait_send()
    relay_v.wait_send()

    across = [
        pltpu.make_async_remote_copy(
            src_ref=o_ref.at[a, :, :, core],
            dst_ref=o_ref.at[a, :, :, core],
            send_sem=c_send.at[a],
            recv_sem=c_recv.at[a],
            device_id={"seq": seq_of(za, xb, 1 - core)},
            device_id_type=mesh_id,
        )
        for a in range(parts)
    ]
    for copy in across:
        copy.start()
    for copy in across:
        copy.wait_send()
        copy.wait_recv()


def seq_gather(stacked, n, cid):
    parts, rows, cols = stacked.shape
    chips = n // 2
    xs = 4
    zs = chips // xs
    return pl.pallas_call(
        functools.partial(seq_gather_kernel, zs, xs),
        out_shape=jax.ShapeDtypeStruct((parts, zs, xs, 2, rows, cols), stacked.dtype),
        in_specs=[pl.BlockSpec(memory_space=pl.ANY)],
        out_specs=pl.BlockSpec(memory_space=pl.ANY),
        scratch_shapes=[
            pltpu.SemaphoreType.DMA((parts, zs)),
            pltpu.SemaphoreType.DMA((parts, zs)),
            pltpu.SemaphoreType.DMA((parts, 2)),
            pltpu.SemaphoreType.DMA((parts, 2)),
            pltpu.SemaphoreType.DMA((parts,)),
            pltpu.SemaphoreType.DMA((parts,)),
            pltpu.SemaphoreType.DMA((parts,)),
            pltpu.SemaphoreType.DMA((parts,)),
            pltpu.SemaphoreType.DMA,
        ],
        compiler_params=pltpu.CompilerParams(collective_id=cid, has_side_effects=True),
    )(stacked)


def tp_gather_kernel(ys, x_ref, o_ref, p_send, p_recv, r_send, r_recv, f_send, f_recv, local_sem):
    me = lax.axis_index("tp")
    yy = me // 2
    zh = me % 2
    right = lax.rem(yy + 1, ys)
    left = lax.rem(yy + ys - 1, ys)
    far = lax.rem(yy + 2, ys)
    width = x_ref.shape[1]
    mesh_id = pl.DeviceIdType.MESH

    def cols(y, h):
        return pl.ds(pl.multiple_of((y * 2 + h) * width, 128), width)

    def pair(y):
        return pl.ds(pl.multiple_of(y * 2 * width, 128), 2 * width)

    def signal(target):
        pl.semaphore_signal(barrier, inc=1, device_id={"tp": target}, device_id_type=mesh_id)

    barrier = pltpu.get_barrier_semaphore()
    signal(yy * 2 + 1 - zh)
    signal(right * 2 + zh)
    signal(left * 2 + zh)
    pl.semaphore_wait(barrier, 3)

    local = pltpu.make_async_copy(x_ref, o_ref.at[:, cols(yy, zh)], local_sem)
    local.start()
    to_partner = pltpu.make_async_remote_copy(
        src_ref=x_ref,
        dst_ref=o_ref.at[:, cols(yy, zh)],
        send_sem=p_send,
        recv_sem=p_recv,
        device_id={"tp": yy * 2 + 1 - zh},
        device_id_type=mesh_id,
    )
    to_partner.start()
    pltpu.make_async_remote_copy(
        src_ref=x_ref,
        dst_ref=o_ref.at[:, cols(yy, 1 - zh)],
        send_sem=p_send,
        recv_sem=p_recv,
        device_id={"tp": yy * 2 + 1 - zh},
        device_id_type=mesh_id,
    ).wait_recv()
    local.wait()
    to_partner.wait_send()

    def ring(group, target, side):
        return pltpu.make_async_remote_copy(
            src_ref=o_ref.at[:, pair(group)],
            dst_ref=o_ref.at[:, pair(group)],
            send_sem=r_send.at[side],
            recv_sem=r_recv.at[side],
            device_id={"tp": target * 2 + zh},
            device_id_type=mesh_id,
        )

    outgoing = [ring(yy, right, 0), ring(yy, left, 1)]
    for copy in outgoing:
        copy.start()
    ring(left, right, 0).wait_recv()
    ring(right, left, 1).wait_recv()
    for copy in outgoing:
        copy.wait_send()

    def relay(group, h, target, side):
        return pltpu.make_async_remote_copy(
            src_ref=o_ref.at[:, cols(group, h)],
            dst_ref=o_ref.at[:, cols(group, h)],
            send_sem=f_send.at[side],
            recv_sem=f_recv.at[side],
            device_id={"tp": target * 2 + zh},
            device_id_type=mesh_id,
        )

    relays = [relay(left, 0, right, 0), relay(right, 1, left, 1)]
    for copy in relays:
        copy.start()
    relay(far, 0, right, 0).wait_recv()
    relay(far, 1, left, 1).wait_recv()
    for copy in relays:
        copy.wait_send()


def tp_gather(block, n, cid):
    rows, width = block.shape
    return pl.pallas_call(
        functools.partial(tp_gather_kernel, n // 2),
        out_shape=jax.ShapeDtypeStruct((rows, width * n), block.dtype),
        in_specs=[pl.BlockSpec(memory_space=pl.ANY)],
        out_specs=pl.BlockSpec(memory_space=pl.ANY),
        scratch_shapes=[
            pltpu.SemaphoreType.DMA,
            pltpu.SemaphoreType.DMA,
            pltpu.SemaphoreType.DMA((2,)),
            pltpu.SemaphoreType.DMA((2,)),
            pltpu.SemaphoreType.DMA((2,)),
            pltpu.SemaphoreType.DMA((2,)),
            pltpu.SemaphoreType.DMA,
        ],
        compiler_params=pltpu.CompilerParams(collective_id=cid, has_side_effects=True),
    )(block)


def project_kernel(x_ref, g_ref, wq_ref, wk_ref, wv_ref, cos_ref, sin_ref, q_ref, k_ref, v_ref):
    x = x_ref[...].astype(jnp.float32)
    mean_sq = jnp.mean(x * x, axis=1, keepdims=True)
    normed = (x * lax.rsqrt(mean_sq + 1e-05) * g_ref[...].astype(jnp.float32)).astype(jnp.bfloat16)
    cosine = cos_ref[...]
    sine = sin_ref[...]

    def rotated(values):
        half = values.shape[1] // 2
        return values * cosine + pltpu.roll(values, half, 1) * sine

    queries = jnp.dot(normed, wq_ref[...], preferred_element_type=jnp.float32)
    for h in range(queries.shape[1] // HEAD):
        q_ref[0, :, h * HEAD:(h + 1) * HEAD] = rotated(queries[:, h * HEAD:(h + 1) * HEAD]).astype(q_ref.dtype)
    keys = jnp.dot(normed, wk_ref[...], preferred_element_type=jnp.float32)
    for h in range(keys.shape[1] // HEAD):
        k_ref[:, h * HEAD:(h + 1) * HEAD] = rotated(keys[:, h * HEAD:(h + 1) * HEAD]).astype(k_ref.dtype)
    v_ref[...] = jnp.dot(normed, wv_ref[...], preferred_element_type=jnp.float32).astype(v_ref.dtype)


def project(gathered, norm_gain, w_query, w_key, w_value, cosine, sine, block):
    rows, width = gathered.shape
    steps = rows // block
    q_width = w_query.shape[1]
    kv_width = w_key.shape[1]
    whole = lambda i: (0, 0)
    return pl.pallas_call(
        project_kernel,
        grid=(steps,),
        out_shape=(
            jax.ShapeDtypeStruct((steps, block, q_width), jnp.bfloat16),
            jax.ShapeDtypeStruct((rows, kv_width), jnp.bfloat16),
            jax.ShapeDtypeStruct((rows, kv_width), jnp.bfloat16),
        ),
        in_specs=[
            pl.BlockSpec((block, width), lambda i: (i, 0)),
            pl.BlockSpec((1, width), whole),
            pl.BlockSpec((width, q_width), whole),
            pl.BlockSpec((width, kv_width), whole),
            pl.BlockSpec((width, kv_width), whole),
            pl.BlockSpec((block, HEAD), lambda i: (i, 0)),
            pl.BlockSpec((block, HEAD), lambda i: (i, 0)),
        ],
        out_specs=(
            pl.BlockSpec((1, block, q_width), lambda i: (i, 0, 0)),
            pl.BlockSpec((block, kv_width), lambda i: (i, 0)),
            pl.BlockSpec((block, kv_width), lambda i: (i, 0)),
        ),
        compiler_params=pltpu.CompilerParams(vmem_limit_bytes=60 * 1024 * 1024),
    )(gathered, norm_gain.reshape(1, width), w_query, w_key, w_value, cosine, sine)


def attention_kernel(
    scale, group_pages,
    wants, page_order, s_idx, s_cnt,
    q_ref, q_want, q_req, q_pos,
    p_ref,
    s_ref, s_tag, s_bound,
    o_ref, m_sc, l_sc, acc_sc, pm_sc, pl_sc, pacc_sc,
):
    prefixes, per_prefix = page_order.shape

    def update(m_ref, l_ref, acc_ref, score_list, value_list):
        run_max = m_ref[...]
        new_max = run_max
        for scores in score_list:
            new_max = jnp.maximum(new_max, jnp.max(scores, axis=1, keepdims=True))
        fade = jnp.exp(run_max - new_max)
        total = l_ref[...] * fade
        acc = acc_ref[...] * fade
        for scores, values in zip(score_list, value_list):
            weights = jnp.exp(scores - new_max)
            total = total + jnp.sum(weights, axis=1, keepdims=True)
            acc = acc + jnp.dot(weights.astype(jnp.bfloat16), values, preferred_element_type=jnp.float32)
        l_ref[...] = total
        acc_ref[...] = acc
        m_ref[...] = new_max

    for i in range(q_ref.shape[0]):
        m_sc[...] = jnp.full(m_sc.shape, -1e30, jnp.float32)
        l_sc[...] = jnp.zeros(l_sc.shape, jnp.float32)
        acc_sc[...] = jnp.zeros(acc_sc.shape, jnp.float32)
        heads = q_ref.shape[2] // q_ref.shape[1]
        size = q_ref.shape[1]
        query = jnp.concatenate([q_ref[i, :, h * size:(h + 1) * size] for h in range(heads)], axis=0)
        want = q_want[i]
        req = q_req[i]
        pos = q_pos[i]

        def score(keys):
            return lax.dot_general(
                query, keys, (((1,), (1,)), ((), ())), preferred_element_type=jnp.float32
            ) * scale

        for p in range(prefixes):
            @pl.when(wants[i, p] > 0)
            def _():
                pm_sc[...] = jnp.full(pm_sc.shape, -1e30, jnp.float32)
                pl_sc[...] = jnp.zeros(pl_sc.shape, jnp.float32)
                pacc_sc[...] = jnp.zeros(pacc_sc.shape, jnp.float32)

                def page_step(g, carry):
                    pages = [page_order[p, g * group_pages + j] for j in range(group_pages)]
                    blocks = [p_ref[b] for b in pages]
                    update(
                        pm_sc, pl_sc, pacc_sc,
                        [score(blk[:, :size]) for blk in blocks],
                        [blk[:, size:] for blk in blocks],
                    )
                    return carry

                lax.fori_loop(0, per_prefix // group_pages, page_step, 0)
                mine = want == p
                m_sc[...] = jnp.where(mine, pm_sc[...], m_sc[...])
                l_sc[...] = jnp.where(mine, pl_sc[...], l_sc[...])
                acc_sc[...] = jnp.where(mine, pacc_sc[...], acc_sc[...])

        def step(n, carry):
            b = s_idx[i, n]
            scores = score(s_ref[0, b])
            seen = (s_tag[b] == req) & (s_bound[b] <= pos)
            run_max = m_sc[...]
            new_max = jnp.maximum(
                run_max, jnp.max(jnp.where(seen, scores, -1e30), axis=1, keepdims=True)
            )
            weights = jnp.where(seen, jnp.exp(scores - new_max), 0.0)
            fade = jnp.exp(run_max - new_max)
            l_sc[...] = l_sc[...] * fade + jnp.sum(weights, axis=1, keepdims=True)
            acc_sc[...] = acc_sc[...] * fade + jnp.dot(
                weights.astype(jnp.bfloat16), s_ref[1, b], preferred_element_type=jnp.float32
            )
            m_sc[...] = new_max
            return carry

        lax.fori_loop(0, s_cnt[i], step, 0)
        result = (acc_sc[...] / l_sc[...]).astype(o_ref.dtype)
        for h in range(heads):
            o_ref[i, :, h * size:(h + 1) * size] = result[h * size:(h + 1) * size]


def block_attention(scale, lists, queries, query_meta, prefix_parts, suffix_parts):
    q_blocks, block_rows, q_width = queries.shape
    width = queries.shape[1]
    q_rows = q_width // width * block_rows
    smem = pl.BlockSpec(memory_space=pltpu.SMEM)
    vmem = pl.BlockSpec(memory_space=pltpu.VMEM)
    state = [
        pltpu.VMEM((q_rows, 1), jnp.float32),
        pltpu.VMEM((q_rows, 1), jnp.float32),
        pltpu.VMEM((q_rows, width), jnp.float32),
    ]
    return pl.pallas_call(
        functools.partial(attention_kernel, scale, 4),
        out_shape=jax.ShapeDtypeStruct((q_blocks, block_rows, q_width), jnp.bfloat16),
        in_specs=[smem] * 4 + [vmem] * 8,
        out_specs=vmem,
        scratch_shapes=state + state,
        compiler_params=pltpu.CompilerParams(vmem_limit_bytes=48 * 1024 * 1024),
    )(*lists, queries, *query_meta, *prefix_parts, *suffix_parts)


def visible_list(visible):
    count = visible.shape[1]
    ids = jnp.arange(count, dtype=jnp.int32)
    rank = jnp.sum((visible[:, :, None] & (ids[:, None] < ids[None, :])[None]).astype(jnp.int32), axis=1)
    pick = visible[:, None, :] & (rank[:, None, :] == ids[None, :, None])
    order = jnp.sum(jnp.where(pick, ids[None, None, :], 0), axis=2).astype(jnp.int32)
    return order, jnp.sum(visible.astype(jnp.int32), axis=1)


def body(
    seq_n,
    tp_n,
    hidden,
    norm_gain,
    w_query,
    w_key,
    w_value,
    prefix_keys,
    prefix_values,
    page_prefix,
    request_prefix,
    suffix_lengths,
    row_order,
):
    gathered_prefix = lax.all_gather(
        jnp.concatenate([prefix_keys, prefix_values], axis=1), "seq", axis=0, tiled=True
    )
    gathered = tp_gather(hidden, tp_n, 2)
    local_rows = gathered.shape[0]
    request_all, position_all, wanted_all = locate(row_order, suffix_lengths, request_prefix)
    offset = lax.axis_index("seq") * local_rows
    request = lax.dynamic_slice_in_dim(request_all, offset, local_rows)
    position = lax.dynamic_slice_in_dim(position_all, offset, local_rows)
    wanted = lax.dynamic_slice_in_dim(wanted_all, offset, local_rows)
    prefix_len = page_prefix.shape[0] * PAGE // PREFIXES
    rope_at = prefix_len + position
    q_heads = w_query.shape[1] // HEAD
    kv_heads = w_key.shape[1] // HEAD
    group_size = q_heads // kv_heads
    half_dim = HEAD // 2
    frequency = ROPE_BASE ** (-(jnp.arange(half_dim, dtype=jnp.float32) * 2.0 / HEAD))
    angles = rope_at.astype(jnp.float32)[:, None] * frequency[None, :]
    cosine = jnp.cos(angles)
    sine_part = jnp.sin(angles)
    cos_full = jnp.concatenate([cosine, cosine], axis=1)
    sin_signed = jnp.concatenate([-sine_part, sine_part], axis=1)
    stacked_q, new_keys, new_values = project(
        gathered, norm_gain, w_query, w_key, w_value, cos_full, sin_signed, PAGE
    )
    score_scale = 1.0 / math.sqrt(HEAD)
    block = PAGE
    q_blocks = local_rows // block
    pages = page_prefix.shape[0]
    runs = row_order.shape[0] // block

    def per_query(values):
        spread = jnp.broadcast_to(values.reshape(q_blocks, 1, block), (q_blocks, group_size, block))
        return spread.reshape(q_blocks, group_size * block, 1).astype(jnp.int32)

    query_meta = (per_query(wanted), per_query(request + PREFIXES), per_query(position))
    want_blocks = wanted.reshape(q_blocks, block)
    block_wants = jnp.any(
        want_blocks[:, :, None] == jnp.arange(PREFIXES, dtype=jnp.int32)[None, None, :], axis=1
    )
    page_ids = jnp.arange(pages, dtype=jnp.int32)
    same = (page_prefix[:, None] == page_prefix[None, :]) & (page_ids[:, None] < page_ids[None, :])
    page_rank = jnp.sum(same.astype(jnp.int32), axis=0)
    per_prefix = pages // PREFIXES
    pick = (page_prefix[None, None, :] == jnp.arange(PREFIXES, dtype=jnp.int32)[:, None, None]) & (
        page_rank[None, None, :] == jnp.arange(per_prefix, dtype=jnp.int32)[None, :, None]
    )
    page_order = jnp.sum(jnp.where(pick, page_ids[None, None, :], 0), axis=2).astype(jnp.int32)
    local_place = lax.dynamic_slice_in_dim(row_order, offset, local_rows).reshape(q_blocks, block)
    first_seen = jnp.min(local_place - position.reshape(q_blocks, block), axis=1)
    last_seen = jnp.max(local_place, axis=1)
    run_place = row_order.reshape(runs, block)
    run_low = jnp.min(run_place, axis=1)
    run_high = jnp.max(run_place, axis=1)
    run_visible = (run_low[None, :] <= last_seen[:, None]) & (run_high[None, :] >= first_seen[:, None])
    s_idx, s_cnt = visible_list(run_visible)

    seq_n_blocks = seq_n
    prefix_parts = (gathered_prefix.reshape(pages, block, 2 * HEAD),)
    gathered_suffix = seq_gather(jnp.stack([new_keys, new_values]), seq_n_blocks, 1)
    suffix_parts = (
        gathered_suffix.reshape(2, runs, block, HEAD),
        (request_all + PREFIXES).reshape(runs, 1, block).astype(jnp.int32),
        position_all.reshape(runs, 1, block).astype(jnp.int32),
    )
    out = block_attention(
        score_scale, (block_wants.astype(jnp.int32), page_order, s_idx, s_cnt), stacked_q, query_meta, prefix_parts, suffix_parts
    )
    attended = out.reshape(local_rows, group_size * HEAD)
    return (attended, new_keys, new_values)


def solution(mesh):
    return jax.shard_map(
        functools.partial(body, mesh.shape["seq"], mesh.shape["tp"]),
        mesh=mesh,
        in_specs=(
            P("seq", "tp"),
            P(),
            P(None, "tp"),
            P(None, "tp"),
            P(None, "tp"),
            P("seq", "tp"),
            P("seq", "tp"),
            P(),
            P(),
            P(),
            P(),
        ),
        out_specs=(P("seq", "tp"), P("seq", "tp"), P("seq", "tp")),
        check_vma=False,
    )
```

```python
import functools
import math

import jax
import jax.numpy as jnp
from jax import lax
from jax.sharding import PartitionSpec as P
from jax.experimental import pallas as pl
from jax.experimental.pallas import tpu as pltpu

HEAD = 128
PAGE = 128
PREFIXES = 4


ROPE_BASE = 5000000.0


def rotate(tensor_in, positions):
    head_dim = tensor_in.shape[-1]
    half_dim = head_dim // 2
    frequency = ROPE_BASE ** (-(jnp.arange(half_dim, dtype=jnp.float32) * 2.0 / head_dim))
    angles = positions.astype(jnp.float32)[:, None] * frequency[None, :]
    cosine = jnp.cos(angles)[:, None, :]
    sine_part = jnp.sin(angles)[:, None, :]
    first_half = tensor_in[..., :half_dim]
    second_half = tensor_in[..., half_dim:]
    return jnp.concatenate(
        [
            first_half * cosine - second_half * sine_part,
            second_half * cosine + first_half * sine_part,
        ],
        axis=-1,
    )


def locate(row_order, suffix_lengths, request_prefix):
    end_rows = jnp.cumsum(suffix_lengths)
    starts = end_rows - suffix_lengths
    numbers = jnp.arange(suffix_lengths.shape[0], dtype=jnp.int32)
    request = jnp.sum((row_order[:, None] >= end_rows[None, :]).astype(jnp.int32), axis=1)
    chosen = request[:, None] == numbers[None, :]
    position = row_order - jnp.sum(jnp.where(chosen, starts[None, :], 0), axis=1)
    wanted = jnp.sum(jnp.where(chosen, request_prefix[None, :], 0), axis=1)
    return (request, position, wanted)


def seq_gather_kernel(
    zs, xs, x_ref, o_ref, z_send, z_recv, r_send, r_recv, f_send, f_recv, c_send, c_recv, local_sem
):
    me = lax.axis_index("seq")
    core = me % 2
    chip = me // 2
    za = chip // xs
    xb = chip % xs
    right = lax.rem(xb + 1, xs)
    left = lax.rem(xb + xs - 1, xs)
    parts = x_ref.shape[0]
    mesh_id = pl.DeviceIdType.MESH

    def seq_of(z, x, c):
        return (z * xs + x) * 2 + c

    def signal(sem, target):
        pl.semaphore_signal(sem, inc=1, device_id={"seq": target}, device_id_type=mesh_id)

    barrier = pltpu.get_barrier_semaphore()

    def greet(k, carry):
        signal(barrier, seq_of(lax.rem(za + k, zs), xb, core))
        return carry

    lax.fori_loop(1, zs, greet, 0)
    signal(barrier, seq_of(za, right, core))
    signal(barrier, seq_of(za, left, core))
    signal(barrier, seq_of(za, xb, 1 - core))
    pl.semaphore_wait(barrier, zs + 2)

    local = pltpu.make_async_copy(x_ref, o_ref.at[:, za, xb, core], local_sem)
    local.start()

    def z_copy(a, peer_z, slot_z):
        return pltpu.make_async_remote_copy(
            src_ref=x_ref.at[a],
            dst_ref=o_ref.at[a, slot_z, xb, core],
            send_sem=z_send.at[a, peer_z],
            recv_sem=z_recv.at[a, slot_z],
            device_id={"seq": seq_of(peer_z, xb, core)},
            device_id_type=mesh_id,
        )

    def z_start(k, carry):
        peer_z = lax.rem(za + k, zs)
        for a in range(parts):
            z_copy(a, peer_z, za).start()
        return carry

    lax.fori_loop(1, zs, z_start, 0)

    def z_finish(k, carry):
        peer_z = lax.rem(za + k, zs)
        for a in range(parts):
            copy = z_copy(a, peer_z, peer_z)
            copy.wait_send()
            copy.wait_recv()
        return carry

    lax.fori_loop(1, zs, z_finish, 0)
    local.wait()

    def ring_copy(a, side, group, target_x, sem_side):
        return pltpu.make_async_remote_copy(
            src_ref=o_ref.at[a, :, group, core],
            dst_ref=o_ref.at[a, :, group, core],
            send_sem=r_send.at[a, side],
            recv_sem=r_recv.at[a, sem_side],
            device_id={"seq": seq_of(za, target_x, core)},
            device_id_type=mesh_id,
        )

    outgoing = []
    for a in range(parts):
        outgoing.append(ring_copy(a, 0, xb, right, 0))
        outgoing.append(ring_copy(a, 1, xb, left, 1))
    for copy in outgoing:
        copy.start()
    for a in range(parts):
        ring_copy(a, 0, left, right, 0).wait_recv()
        ring_copy(a, 1, right, left, 1).wait_recv()
    for copy in outgoing:
        copy.wait_send()

    far = lax.rem(xb + 2, xs)
    relay_k = pltpu.make_async_remote_copy(
        src_ref=o_ref.at[0, :, left, core],
        dst_ref=o_ref.at[0, :, left, core],
        send_sem=f_send.at[0],
        recv_sem=f_recv.at[0],
        device_id={"seq": seq_of(za, right, core)},
        device_id_type=mesh_id,
    )
    relay_v = pltpu.make_async_remote_copy(
        src_ref=o_ref.at[1, :, right, core],
        dst_ref=o_ref.at[1, :, right, core],
        send_sem=f_send.at[1],
        recv_sem=f_recv.at[1],
        device_id={"seq": seq_of(za, left, core)},
        device_id_type=mesh_id,
    )
    relay_k.start()
    relay_v.start()
    pltpu.make_async_remote_copy(
        src_ref=o_ref.at[0, :, far, core],
        dst_ref=o_ref.at[0, :, far, core],
        send_sem=f_send.at[0],
        recv_sem=f_recv.at[0],
        device_id={"seq": seq_of(za, right, core)},
        device_id_type=mesh_id,
    ).wait_recv()
    pltpu.make_async_remote_copy(
        src_ref=o_ref.at[1, :, far, core],
        dst_ref=o_ref.at[1, :, far, core],
        send_sem=f_send.at[1],
        recv_sem=f_recv.at[1],
        device_id={"seq": seq_of(za, left, core)},
        device_id_type=mesh_id,
    ).wait_recv()
    relay_k.wait_send()
    relay_v.wait_send()

    across = [
        pltpu.make_async_remote_copy(
            src_ref=o_ref.at[a, :, :, core],
            dst_ref=o_ref.at[a, :, :, core],
            send_sem=c_send.at[a],
            recv_sem=c_recv.at[a],
            device_id={"seq": seq_of(za, xb, 1 - core)},
            device_id_type=mesh_id,
        )
        for a in range(parts)
    ]
    for copy in across:
        copy.start()
    for copy in across:
        copy.wait_send()
        copy.wait_recv()


def seq_gather(stacked, n, cid):
    parts, rows, cols = stacked.shape
    chips = n // 2
    xs = 4
    zs = chips // xs
    return pl.pallas_call(
        functools.partial(seq_gather_kernel, zs, xs),
        out_shape=jax.ShapeDtypeStruct((parts, zs, xs, 2, rows, cols), stacked.dtype),
        in_specs=[pl.BlockSpec(memory_space=pl.ANY)],
        out_specs=pl.BlockSpec(memory_space=pl.ANY),
        scratch_shapes=[
            pltpu.SemaphoreType.DMA((parts, zs)),
            pltpu.SemaphoreType.DMA((parts, zs)),
            pltpu.SemaphoreType.DMA((parts, 2)),
            pltpu.SemaphoreType.DMA((parts, 2)),
            pltpu.SemaphoreType.DMA((parts,)),
            pltpu.SemaphoreType.DMA((parts,)),
            pltpu.SemaphoreType.DMA((parts,)),
            pltpu.SemaphoreType.DMA((parts,)),
            pltpu.SemaphoreType.DMA,
        ],
        compiler_params=pltpu.CompilerParams(collective_id=cid, has_side_effects=True),
    )(stacked)


def tp_gather_kernel(ys, x_ref, z_ref, o_ref, r_send, r_recv, f_send, f_recv, local_sem):
    me = lax.axis_index("tp")
    yy = me // 2
    zh = me % 2
    right = lax.rem(yy + 1, ys)
    left = lax.rem(yy + ys - 1, ys)
    far = lax.rem(yy + 2, ys)
    width = x_ref.shape[1]
    mesh_id = pl.DeviceIdType.MESH

    def cols(y, h):
        return pl.ds(pl.multiple_of((y * 2 + h) * width, 128), width)

    def pair(y):
        return pl.ds(pl.multiple_of(y * 2 * width, 128), 2 * width)

    def signal(target):
        pl.semaphore_signal(barrier, inc=1, device_id={"tp": target}, device_id_type=mesh_id)

    barrier = pltpu.get_barrier_semaphore()
    signal(right * 2 + zh)
    signal(left * 2 + zh)
    pl.semaphore_wait(barrier, 2)

    own = pltpu.make_async_copy(x_ref, o_ref.at[:, cols(yy, zh)], local_sem.at[0])
    other = pltpu.make_async_copy(z_ref, o_ref.at[:, cols(yy, 1 - zh)], local_sem.at[1])
    own.start()
    other.start()
    own.wait()
    other.wait()

    def ring(group, target, side):
        return pltpu.make_async_remote_copy(
            src_ref=o_ref.at[:, pair(group)],
            dst_ref=o_ref.at[:, pair(group)],
            send_sem=r_send.at[side],
            recv_sem=r_recv.at[side],
            device_id={"tp": target * 2 + zh},
            device_id_type=mesh_id,
        )

    outgoing = [ring(yy, right, 0), ring(yy, left, 1)]
    for copy in outgoing:
        copy.start()
    ring(left, right, 0).wait_recv()
    ring(right, left, 1).wait_recv()
    for copy in outgoing:
        copy.wait_send()

    def relay(group, h, target, side):
        return pltpu.make_async_remote_copy(
            src_ref=o_ref.at[:, cols(group, h)],
            dst_ref=o_ref.at[:, cols(group, h)],
            send_sem=f_send.at[side],
            recv_sem=f_recv.at[side],
            device_id={"tp": target * 2 + zh},
            device_id_type=mesh_id,
        )

    relays = [relay(left, 0, right, 0), relay(right, 1, left, 1)]
    for copy in relays:
        copy.start()
    relay(far, 0, right, 0).wait_recv()
    relay(far, 1, left, 1).wait_recv()
    for copy in relays:
        copy.wait_send()


def tp_gather(block, partner_block, n, cid):
    rows, width = block.shape
    return pl.pallas_call(
        functools.partial(tp_gather_kernel, n // 2),
        out_shape=jax.ShapeDtypeStruct((rows, width * n), block.dtype),
        in_specs=[pl.BlockSpec(memory_space=pl.ANY)] * 2,
        out_specs=pl.BlockSpec(memory_space=pl.ANY),
        scratch_shapes=[
            pltpu.SemaphoreType.DMA((2,)),
            pltpu.SemaphoreType.DMA((2,)),
            pltpu.SemaphoreType.DMA((2,)),
            pltpu.SemaphoreType.DMA((2,)),
            pltpu.SemaphoreType.DMA((2,)),
        ],
        compiler_params=pltpu.CompilerParams(collective_id=cid, has_side_effects=True),
    )(block, partner_block)


def project_kernel(x_ref, g_ref, wq_ref, wk_ref, wv_ref, cos_ref, sin_ref, q_ref, k_ref, v_ref, kv_ref):
    x = x_ref[...].astype(jnp.float32)
    mean_sq = jnp.mean(x * x, axis=1, keepdims=True)
    normed = (x * lax.rsqrt(mean_sq + 1e-05) * g_ref[...].astype(jnp.float32)).astype(jnp.bfloat16)
    cosine = cos_ref[...]
    sine = sin_ref[...]

    def rotated(values):
        half = values.shape[1] // 2
        return values * cosine + pltpu.roll(values, half, 1) * sine

    queries = jnp.dot(normed, wq_ref[...], preferred_element_type=jnp.float32)
    for h in range(queries.shape[1] // HEAD):
        q_ref[0, :, h * HEAD:(h + 1) * HEAD] = rotated(queries[:, h * HEAD:(h + 1) * HEAD]).astype(q_ref.dtype)
    keys = jnp.dot(normed, wk_ref[...], preferred_element_type=jnp.float32)
    for h in range(keys.shape[1] // HEAD):
        part = rotated(keys[:, h * HEAD:(h + 1) * HEAD]).astype(k_ref.dtype)
        k_ref[:, h * HEAD:(h + 1) * HEAD] = part
        kv_ref[0, :, h * HEAD:(h + 1) * HEAD] = part
    values = jnp.dot(normed, wv_ref[...], preferred_element_type=jnp.float32).astype(v_ref.dtype)
    v_ref[...] = values
    kv_ref[1] = values


def project(gathered, norm_gain, w_query, w_key, w_value, cosine, sine, block):
    rows, width = gathered.shape
    steps = rows // block
    q_width = w_query.shape[1]
    kv_width = w_key.shape[1]
    whole = lambda i: (0, 0)
    return pl.pallas_call(
        project_kernel,
        grid=(steps,),
        out_shape=(
            jax.ShapeDtypeStruct((steps, block, q_width), jnp.bfloat16),
            jax.ShapeDtypeStruct((rows, kv_width), jnp.bfloat16),
            jax.ShapeDtypeStruct((rows, kv_width), jnp.bfloat16),
            jax.ShapeDtypeStruct((2, rows, kv_width), jnp.bfloat16),
        ),
        in_specs=[
            pl.BlockSpec((block, width), lambda i: (i, 0)),
            pl.BlockSpec((1, width), whole),
            pl.BlockSpec((width, q_width), whole),
            pl.BlockSpec((width, kv_width), whole),
            pl.BlockSpec((width, kv_width), whole),
            pl.BlockSpec((block, HEAD), lambda i: (i, 0)),
            pl.BlockSpec((block, HEAD), lambda i: (i, 0)),
        ],
        out_specs=(
            pl.BlockSpec((1, block, q_width), lambda i: (i, 0, 0)),
            pl.BlockSpec((block, kv_width), lambda i: (i, 0)),
            pl.BlockSpec((block, kv_width), lambda i: (i, 0)),
            pl.BlockSpec((2, block, kv_width), lambda i: (0, i, 0)),
        ),
        compiler_params=pltpu.CompilerParams(vmem_limit_bytes=60 * 1024 * 1024),
    )(gathered, norm_gain.reshape(1, width), w_query, w_key, w_value, cosine, sine)


def attention_kernel(
    scale, group_pages,
    wants, page_order, s_idx, s_cnt,
    q_ref, q_want, q_req, q_pos,
    p_ref,
    s_ref, s_tag, s_bound,
    o_ref, m_sc, l_sc, acc_sc, pm_sc, pl_sc, pacc_sc,
):
    prefixes, per_prefix = page_order.shape

    def update(m_ref, l_ref, acc_ref, score_list, value_list):
        run_max = m_ref[...]
        new_max = run_max
        for scores in score_list:
            new_max = jnp.maximum(new_max, jnp.max(scores, axis=1, keepdims=True))
        fade = jnp.exp(run_max - new_max)
        total = l_ref[...] * fade
        acc = acc_ref[...] * fade
        for scores, values in zip(score_list, value_list):
            weights = jnp.exp(scores - new_max)
            total = total + jnp.sum(weights, axis=1, keepdims=True)
            acc = acc + jnp.dot(weights.astype(jnp.bfloat16), values, preferred_element_type=jnp.float32)
        l_ref[...] = total
        acc_ref[...] = acc
        m_ref[...] = new_max

    for i in range(q_ref.shape[0]):
        m_sc[...] = jnp.full(m_sc.shape, -1e30, jnp.float32)
        l_sc[...] = jnp.zeros(l_sc.shape, jnp.float32)
        acc_sc[...] = jnp.zeros(acc_sc.shape, jnp.float32)
        heads = q_ref.shape[2] // q_ref.shape[1]
        size = q_ref.shape[1]
        query = jnp.concatenate([q_ref[i, :, h * size:(h + 1) * size] for h in range(heads)], axis=0)
        want = q_want[i]
        req = q_req[i]
        pos = q_pos[i]

        def score(keys):
            return lax.dot_general(
                query, keys, (((1,), (1,)), ((), ())), preferred_element_type=jnp.float32
            ) * scale

        for p in range(prefixes):
            @pl.when(wants[i, p] > 0)
            def _():
                pm_sc[...] = jnp.full(pm_sc.shape, -1e30, jnp.float32)
                pl_sc[...] = jnp.zeros(pl_sc.shape, jnp.float32)
                pacc_sc[...] = jnp.zeros(pacc_sc.shape, jnp.float32)

                def page_step(g, carry):
                    pages = [page_order[p, g * group_pages + j] for j in range(group_pages)]
                    blocks = [p_ref[b] for b in pages]
                    update(
                        pm_sc, pl_sc, pacc_sc,
                        [score(blk[:, :size]) for blk in blocks],
                        [blk[:, size:] for blk in blocks],
                    )
                    return carry

                lax.fori_loop(0, per_prefix // group_pages, page_step, 0)
                mine = want == p
                m_sc[...] = jnp.where(mine, pm_sc[...], m_sc[...])
                l_sc[...] = jnp.where(mine, pl_sc[...], l_sc[...])
                acc_sc[...] = jnp.where(mine, pacc_sc[...], acc_sc[...])

        def step(n, carry):
            b = s_idx[i, n]
            scores = score(s_ref[0, b])
            seen = (s_tag[b] == req) & (s_bound[b] <= pos)
            run_max = m_sc[...]
            new_max = jnp.maximum(
                run_max, jnp.max(jnp.where(seen, scores, -1e30), axis=1, keepdims=True)
            )
            weights = jnp.where(seen, jnp.exp(scores - new_max), 0.0)
            fade = jnp.exp(run_max - new_max)
            l_sc[...] = l_sc[...] * fade + jnp.sum(weights, axis=1, keepdims=True)
            acc_sc[...] = acc_sc[...] * fade + jnp.dot(
                weights.astype(jnp.bfloat16), s_ref[1, b], preferred_element_type=jnp.float32
            )
            m_sc[...] = new_max
            return carry

        lax.fori_loop(0, s_cnt[i], step, 0)
        result = (acc_sc[...] / l_sc[...]).astype(o_ref.dtype)
        for h in range(heads):
            o_ref[i, :, h * size:(h + 1) * size] = result[h * size:(h + 1) * size]


def block_attention(scale, lists, queries, query_meta, prefix_parts, suffix_parts):
    q_blocks, block_rows, q_width = queries.shape
    width = queries.shape[1]
    q_rows = q_width // width * block_rows
    smem = pl.BlockSpec(memory_space=pltpu.SMEM)
    vmem = pl.BlockSpec(memory_space=pltpu.VMEM)
    state = [
        pltpu.VMEM((q_rows, 1), jnp.float32),
        pltpu.VMEM((q_rows, 1), jnp.float32),
        pltpu.VMEM((q_rows, width), jnp.float32),
    ]
    return pl.pallas_call(
        functools.partial(attention_kernel, scale, 4),
        out_shape=jax.ShapeDtypeStruct((q_blocks, block_rows, q_width), jnp.bfloat16),
        in_specs=[smem] * 4 + [vmem] * 8,
        out_specs=vmem,
        scratch_shapes=state + state,
        compiler_params=pltpu.CompilerParams(vmem_limit_bytes=48 * 1024 * 1024),
    )(*lists, queries, *query_meta, *prefix_parts, *suffix_parts)


def visible_list(visible):
    count = visible.shape[1]
    ids = jnp.arange(count, dtype=jnp.int32)
    rank = jnp.sum((visible[:, :, None] & (ids[:, None] < ids[None, :])[None]).astype(jnp.int32), axis=1)
    pick = visible[:, None, :] & (rank[:, None, :] == ids[None, :, None])
    order = jnp.sum(jnp.where(pick, ids[None, None, :], 0), axis=2).astype(jnp.int32)
    return order, jnp.sum(visible.astype(jnp.int32), axis=1)


def body(
    seq_n,
    tp_n,
    hidden,
    norm_gain,
    w_query,
    w_key,
    w_value,
    prefix_keys,
    prefix_values,
    page_prefix,
    request_prefix,
    suffix_lengths,
    row_order,
):
    gathered_prefix = lax.all_gather(
        jnp.concatenate([prefix_keys, prefix_values], axis=1), "seq", axis=0, tiled=True
    )
    partner_block = lax.ppermute(hidden, "tp", [(t, t ^ 1) for t in range(tp_n)])
    gathered = tp_gather(hidden, partner_block, tp_n, 2)
    local_rows = gathered.shape[0]
    request_all, position_all, wanted_all = locate(row_order, suffix_lengths, request_prefix)
    offset = lax.axis_index("seq") * local_rows
    request = lax.dynamic_slice_in_dim(request_all, offset, local_rows)
    position = lax.dynamic_slice_in_dim(position_all, offset, local_rows)
    wanted = lax.dynamic_slice_in_dim(wanted_all, offset, local_rows)
    prefix_len = page_prefix.shape[0] * PAGE // PREFIXES
    rope_at = prefix_len + position
    q_heads = w_query.shape[1] // HEAD
    kv_heads = w_key.shape[1] // HEAD
    group_size = q_heads // kv_heads
    half_dim = HEAD // 2
    frequency = ROPE_BASE ** (-(jnp.arange(half_dim, dtype=jnp.float32) * 2.0 / HEAD))
    angles = rope_at.astype(jnp.float32)[:, None] * frequency[None, :]
    cosine = jnp.cos(angles)
    sine_part = jnp.sin(angles)
    cos_full = jnp.concatenate([cosine, cosine], axis=1)
    sin_signed = jnp.concatenate([-sine_part, sine_part], axis=1)
    stacked_q, new_keys, new_values, stacked_kv = project(
        gathered, norm_gain, w_query, w_key, w_value, cos_full, sin_signed, PAGE
    )
    score_scale = 1.0 / math.sqrt(HEAD)
    block = PAGE
    q_blocks = local_rows // block
    pages = page_prefix.shape[0]
    runs = row_order.shape[0] // block

    def per_query(values):
        spread = jnp.broadcast_to(values.reshape(q_blocks, 1, block), (q_blocks, group_size, block))
        return spread.reshape(q_blocks, group_size * block, 1).astype(jnp.int32)

    query_meta = (per_query(wanted), per_query(request + PREFIXES), per_query(position))
    want_blocks = wanted.reshape(q_blocks, block)
    block_wants = jnp.any(
        want_blocks[:, :, None] == jnp.arange(PREFIXES, dtype=jnp.int32)[None, None, :], axis=1
    )
    page_ids = jnp.arange(pages, dtype=jnp.int32)
    same = (page_prefix[:, None] == page_prefix[None, :]) & (page_ids[:, None] < page_ids[None, :])
    page_rank = jnp.sum(same.astype(jnp.int32), axis=0)
    per_prefix = pages // PREFIXES
    pick = (page_prefix[None, None, :] == jnp.arange(PREFIXES, dtype=jnp.int32)[:, None, None]) & (
        page_rank[None, None, :] == jnp.arange(per_prefix, dtype=jnp.int32)[None, :, None]
    )
    page_order = jnp.sum(jnp.where(pick, page_ids[None, None, :], 0), axis=2).astype(jnp.int32)
    local_place = lax.dynamic_slice_in_dim(row_order, offset, local_rows).reshape(q_blocks, block)
    first_seen = jnp.min(local_place - position.reshape(q_blocks, block), axis=1)
    last_seen = jnp.max(local_place, axis=1)
    run_place = row_order.reshape(runs, block)
    run_low = jnp.min(run_place, axis=1)
    run_high = jnp.max(run_place, axis=1)
    run_visible = (run_low[None, :] <= last_seen[:, None]) & (run_high[None, :] >= first_seen[:, None])
    s_idx, s_cnt = visible_list(run_visible)

    seq_n_blocks = seq_n
    prefix_parts = (gathered_prefix.reshape(pages, block, 2 * HEAD),)
    gathered_suffix = seq_gather(stacked_kv, seq_n_blocks, 1)
    suffix_parts = (
        gathered_suffix.reshape(2, runs, block, HEAD),
        (request_all + PREFIXES).reshape(runs, 1, block).astype(jnp.int32),
        position_all.reshape(runs, 1, block).astype(jnp.int32),
    )
    out = block_attention(
        score_scale, (block_wants.astype(jnp.int32), page_order, s_idx, s_cnt), stacked_q, query_meta, prefix_parts, suffix_parts
    )
    attended = out.reshape(local_rows, group_size * HEAD)
    return (attended, new_keys, new_values)


def solution(mesh):
    return jax.shard_map(
        functools.partial(body, mesh.shape["seq"], mesh.shape["tp"]),
        mesh=mesh,
        in_specs=(
            P("seq", "tp"),
            P(),
            P(None, "tp"),
            P(None, "tp"),
            P(None, "tp"),
            P("seq", "tp"),
            P("seq", "tp"),
            P(),
            P(),
            P(),
            P(),
        ),
        out_specs=(P("seq", "tp"), P("seq", "tp"), P("seq", "tp")),
        check_vma=False,
    )
```

```python
import functools
import math

import jax
import jax.numpy as jnp
from jax import lax
from jax.sharding import PartitionSpec as P
from jax.experimental import pallas as pl
from jax.experimental.pallas import tpu as pltpu

HEAD = 128
PAGE = 128
PREFIXES = 4


ROPE_BASE = 5000000.0


def rotate(tensor_in, positions):
    head_dim = tensor_in.shape[-1]
    half_dim = head_dim // 2
    frequency = ROPE_BASE ** (-(jnp.arange(half_dim, dtype=jnp.float32) * 2.0 / head_dim))
    angles = positions.astype(jnp.float32)[:, None] * frequency[None, :]
    cosine = jnp.cos(angles)[:, None, :]
    sine_part = jnp.sin(angles)[:, None, :]
    first_half = tensor_in[..., :half_dim]
    second_half = tensor_in[..., half_dim:]
    return jnp.concatenate(
        [
            first_half * cosine - second_half * sine_part,
            second_half * cosine + first_half * sine_part,
        ],
        axis=-1,
    )


def locate(row_order, suffix_lengths, request_prefix):
    end_rows = jnp.cumsum(suffix_lengths)
    starts = end_rows - suffix_lengths
    numbers = jnp.arange(suffix_lengths.shape[0], dtype=jnp.int32)
    request = jnp.sum((row_order[:, None] >= end_rows[None, :]).astype(jnp.int32), axis=1)
    chosen = request[:, None] == numbers[None, :]
    position = row_order - jnp.sum(jnp.where(chosen, starts[None, :], 0), axis=1)
    wanted = jnp.sum(jnp.where(chosen, request_prefix[None, :], 0), axis=1)
    return (request, position, wanted)


def seq_gather_kernel(
    zs, xs, x_ref, o_ref, z_send, z_recv, r_send, r_recv, f_send, f_recv, c_send, c_recv, local_sem
):
    me = lax.axis_index("seq")
    core = me % 2
    chip = me // 2
    za = chip // xs
    xb = chip % xs
    right = lax.rem(xb + 1, xs)
    left = lax.rem(xb + xs - 1, xs)
    parts = x_ref.shape[0]
    mesh_id = pl.DeviceIdType.MESH

    def seq_of(z, x, c):
        return (z * xs + x) * 2 + c

    def signal(sem, target):
        pl.semaphore_signal(sem, inc=1, device_id={"seq": target}, device_id_type=mesh_id)

    barrier = pltpu.get_barrier_semaphore()

    def greet(k, carry):
        signal(barrier, seq_of(lax.rem(za + k, zs), xb, core))
        return carry

    lax.fori_loop(1, zs, greet, 0)
    signal(barrier, seq_of(za, right, core))
    signal(barrier, seq_of(za, left, core))
    signal(barrier, seq_of(za, xb, 1 - core))
    pl.semaphore_wait(barrier, zs + 2)

    local = pltpu.make_async_copy(x_ref, o_ref.at[:, za, xb, core], local_sem)
    local.start()

    def z_copy(a, peer_z, slot_z):
        return pltpu.make_async_remote_copy(
            src_ref=x_ref.at[a],
            dst_ref=o_ref.at[a, slot_z, xb, core],
            send_sem=z_send.at[a, peer_z],
            recv_sem=z_recv.at[a, slot_z],
            device_id={"seq": seq_of(peer_z, xb, core)},
            device_id_type=mesh_id,
        )

    def z_start(k, carry):
        peer_z = lax.rem(za + k, zs)
        for a in range(parts):
            z_copy(a, peer_z, za).start()
        return carry

    lax.fori_loop(1, zs, z_start, 0)

    def z_finish(k, carry):
        peer_z = lax.rem(za + k, zs)
        for a in range(parts):
            copy = z_copy(a, peer_z, peer_z)
            copy.wait_send()
            copy.wait_recv()
        return carry

    lax.fori_loop(1, zs, z_finish, 0)
    local.wait()

    def ring_copy(a, side, group, target_x, sem_side):
        return pltpu.make_async_remote_copy(
            src_ref=o_ref.at[a, :, group, core],
            dst_ref=o_ref.at[a, :, group, core],
            send_sem=r_send.at[a, side],
            recv_sem=r_recv.at[a, sem_side],
            device_id={"seq": seq_of(za, target_x, core)},
            device_id_type=mesh_id,
        )

    outgoing = []
    for a in range(parts):
        outgoing.append(ring_copy(a, 0, xb, right, 0))
        outgoing.append(ring_copy(a, 1, xb, left, 1))
    for copy in outgoing:
        copy.start()
    for a in range(parts):
        ring_copy(a, 0, left, right, 0).wait_recv()
        ring_copy(a, 1, right, left, 1).wait_recv()
    for copy in outgoing:
        copy.wait_send()

    far = lax.rem(xb + 2, xs)
    relay_k = pltpu.make_async_remote_copy(
        src_ref=o_ref.at[0, :, left, core],
        dst_ref=o_ref.at[0, :, left, core],
        send_sem=f_send.at[0],
        recv_sem=f_recv.at[0],
        device_id={"seq": seq_of(za, right, core)},
        device_id_type=mesh_id,
    )
    relay_v = pltpu.make_async_remote_copy(
        src_ref=o_ref.at[1, :, right, core],
        dst_ref=o_ref.at[1, :, right, core],
        send_sem=f_send.at[1],
        recv_sem=f_recv.at[1],
        device_id={"seq": seq_of(za, left, core)},
        device_id_type=mesh_id,
    )
    relay_k.start()
    relay_v.start()
    pltpu.make_async_remote_copy(
        src_ref=o_ref.at[0, :, far, core],
        dst_ref=o_ref.at[0, :, far, core],
        send_sem=f_send.at[0],
        recv_sem=f_recv.at[0],
        device_id={"seq": seq_of(za, right, core)},
        device_id_type=mesh_id,
    ).wait_recv()
    pltpu.make_async_remote_copy(
        src_ref=o_ref.at[1, :, far, core],
        dst_ref=o_ref.at[1, :, far, core],
        send_sem=f_send.at[1],
        recv_sem=f_recv.at[1],
        device_id={"seq": seq_of(za, left, core)},
        device_id_type=mesh_id,
    ).wait_recv()
    relay_k.wait_send()
    relay_v.wait_send()

    across = [
        pltpu.make_async_remote_copy(
            src_ref=o_ref.at[a, :, :, core],
            dst_ref=o_ref.at[a, :, :, core],
            send_sem=c_send.at[a],
            recv_sem=c_recv.at[a],
            device_id={"seq": seq_of(za, xb, 1 - core)},
            device_id_type=mesh_id,
        )
        for a in range(parts)
    ]
    for copy in across:
        copy.start()
    for copy in across:
        copy.wait_send()
        copy.wait_recv()


def seq_gather(stacked, n, cid):
    parts, rows, cols = stacked.shape
    chips = n // 2
    xs = 4
    zs = chips // xs
    return pl.pallas_call(
        functools.partial(seq_gather_kernel, zs, xs),
        out_shape=jax.ShapeDtypeStruct((parts, zs, xs, 2, rows, cols), stacked.dtype),
        in_specs=[pl.BlockSpec(memory_space=pl.ANY)],
        out_specs=pl.BlockSpec(memory_space=pl.ANY),
        scratch_shapes=[
            pltpu.SemaphoreType.DMA((parts, zs)),
            pltpu.SemaphoreType.DMA((parts, zs)),
            pltpu.SemaphoreType.DMA((parts, 2)),
            pltpu.SemaphoreType.DMA((parts, 2)),
            pltpu.SemaphoreType.DMA((parts,)),
            pltpu.SemaphoreType.DMA((parts,)),
            pltpu.SemaphoreType.DMA((parts,)),
            pltpu.SemaphoreType.DMA((parts,)),
            pltpu.SemaphoreType.DMA,
        ],
        compiler_params=pltpu.CompilerParams(collective_id=cid, has_side_effects=True),
    )(stacked)


def tp_gather_kernel(ys, x_ref, o_ref, p_send, p_recv, r_send, r_recv, f_send, f_recv, local_sem):
    me = lax.axis_index("tp")
    yy = me // 2
    zh = me % 2
    right = lax.rem(yy + 1, ys)
    left = lax.rem(yy + ys - 1, ys)
    far = lax.rem(yy + 2, ys)
    width = x_ref.shape[1]
    mesh_id = pl.DeviceIdType.MESH

    def cols(y, h):
        return pl.ds(pl.multiple_of((y * 2 + h) * width, 128), width)

    def pair(y):
        return pl.ds(pl.multiple_of(y * 2 * width, 128), 2 * width)

    def signal(target):
        pl.semaphore_signal(barrier, inc=1, device_id={"tp": target}, device_id_type=mesh_id)

    barrier = pltpu.get_barrier_semaphore()
    signal(yy * 2 + 1 - zh)
    signal(right * 2 + zh)
    signal(left * 2 + zh)
    pl.semaphore_wait(barrier, 3)

    local = pltpu.make_async_copy(x_ref, o_ref.at[:, cols(yy, zh)], local_sem)
    local.start()
    to_partner = pltpu.make_async_remote_copy(
        src_ref=x_ref,
        dst_ref=o_ref.at[:, cols(yy, zh)],
        send_sem=p_send,
        recv_sem=p_recv,
        device_id={"tp": yy * 2 + 1 - zh},
        device_id_type=mesh_id,
    )
    to_partner.start()
    pltpu.make_async_remote_copy(
        src_ref=x_ref,
        dst_ref=o_ref.at[:, cols(yy, 1 - zh)],
        send_sem=p_send,
        recv_sem=p_recv,
        device_id={"tp": yy * 2 + 1 - zh},
        device_id_type=mesh_id,
    ).wait_recv()
    local.wait()
    to_partner.wait_send()

    pieces = r_send.shape[1]
    span = x_ref.shape[0] // pieces

    def ring(group, target, side, c):
        rows = pl.ds(c * span, span)
        return pltpu.make_async_remote_copy(
            src_ref=o_ref.at[rows, pair(group)],
            dst_ref=o_ref.at[rows, pair(group)],
            send_sem=r_send.at[side, c],
            recv_sem=r_recv.at[side, c],
            device_id={"tp": target * 2 + zh},
            device_id_type=mesh_id,
        )

    outgoing = []
    for c in range(pieces):
        outgoing += [ring(yy, right, 0, c), ring(yy, left, 1, c)]
    for copy in outgoing:
        copy.start()
    for c in range(pieces):
        ring(left, right, 0, c).wait_recv()
        ring(right, left, 1, c).wait_recv()
    for copy in outgoing:
        copy.wait_send()

    def relay(group, h, target, side, c):
        rows = pl.ds(c * span, span)
        return pltpu.make_async_remote_copy(
            src_ref=o_ref.at[rows, cols(group, h)],
            dst_ref=o_ref.at[rows, cols(group, h)],
            send_sem=f_send.at[side, c],
            recv_sem=f_recv.at[side, c],
            device_id={"tp": target * 2 + zh},
            device_id_type=mesh_id,
        )

    relays = []
    for c in range(pieces):
        relays += [relay(left, 0, right, 0, c), relay(right, 1, left, 1, c)]
    for copy in relays:
        copy.start()
    for c in range(pieces):
        relay(far, 0, right, 0, c).wait_recv()
        relay(far, 1, left, 1, c).wait_recv()
    for copy in relays:
        copy.wait_send()


def tp_gather(block, n, cid):
    rows, width = block.shape
    return pl.pallas_call(
        functools.partial(tp_gather_kernel, n // 2),
        out_shape=jax.ShapeDtypeStruct((rows, width * n), block.dtype),
        in_specs=[pl.BlockSpec(memory_space=pl.ANY)],
        out_specs=pl.BlockSpec(memory_space=pl.ANY),
        scratch_shapes=[
            pltpu.SemaphoreType.DMA,
            pltpu.SemaphoreType.DMA,
            pltpu.SemaphoreType.DMA((2, 4)),
            pltpu.SemaphoreType.DMA((2, 4)),
            pltpu.SemaphoreType.DMA((2, 4)),
            pltpu.SemaphoreType.DMA((2, 4)),
            pltpu.SemaphoreType.DMA,
        ],
        compiler_params=pltpu.CompilerParams(collective_id=cid, has_side_effects=True),
    )(block)


def project_kernel(x_ref, g_ref, wq_ref, wk_ref, wv_ref, cos_ref, sin_ref, q_ref, k_ref, v_ref, kv_ref):
    x = x_ref[...].astype(jnp.float32)
    mean_sq = jnp.mean(x * x, axis=1, keepdims=True)
    normed = (x * lax.rsqrt(mean_sq + 1e-05) * g_ref[...].astype(jnp.float32)).astype(jnp.bfloat16)
    cosine = cos_ref[...]
    sine = sin_ref[...]

    def rotated(values):
        half = values.shape[1] // 2
        return values * cosine + pltpu.roll(values, half, 1) * sine

    queries = jnp.dot(normed, wq_ref[...], preferred_element_type=jnp.float32)
    for h in range(queries.shape[1] // HEAD):
        q_ref[0, :, h * HEAD:(h + 1) * HEAD] = rotated(queries[:, h * HEAD:(h + 1) * HEAD]).astype(q_ref.dtype)
    keys = jnp.dot(normed, wk_ref[...], preferred_element_type=jnp.float32)
    for h in range(keys.shape[1] // HEAD):
        part = rotated(keys[:, h * HEAD:(h + 1) * HEAD]).astype(k_ref.dtype)
        k_ref[:, h * HEAD:(h + 1) * HEAD] = part
        kv_ref[0, :, h * HEAD:(h + 1) * HEAD] = part
    values = jnp.dot(normed, wv_ref[...], preferred_element_type=jnp.float32).astype(v_ref.dtype)
    v_ref[...] = values
    kv_ref[1] = values


def project(gathered, norm_gain, w_query, w_key, w_value, cosine, sine, block):
    rows, width = gathered.shape
    steps = rows // block
    q_width = w_query.shape[1]
    kv_width = w_key.shape[1]
    whole = lambda i: (0, 0)
    return pl.pallas_call(
        project_kernel,
        grid=(steps,),
        out_shape=(
            jax.ShapeDtypeStruct((steps, block, q_width), jnp.bfloat16),
            jax.ShapeDtypeStruct((rows, kv_width), jnp.bfloat16),
            jax.ShapeDtypeStruct((rows, kv_width), jnp.bfloat16),
            jax.ShapeDtypeStruct((2, rows, kv_width), jnp.bfloat16),
        ),
        in_specs=[
            pl.BlockSpec((block, width), lambda i: (i, 0)),
            pl.BlockSpec((1, width), whole),
            pl.BlockSpec((width, q_width), whole),
            pl.BlockSpec((width, kv_width), whole),
            pl.BlockSpec((width, kv_width), whole),
            pl.BlockSpec((block, HEAD), lambda i: (i, 0)),
            pl.BlockSpec((block, HEAD), lambda i: (i, 0)),
        ],
        out_specs=(
            pl.BlockSpec((1, block, q_width), lambda i: (i, 0, 0)),
            pl.BlockSpec((block, kv_width), lambda i: (i, 0)),
            pl.BlockSpec((block, kv_width), lambda i: (i, 0)),
            pl.BlockSpec((2, block, kv_width), lambda i: (0, i, 0)),
        ),
        compiler_params=pltpu.CompilerParams(vmem_limit_bytes=60 * 1024 * 1024),
    )(gathered, norm_gain.reshape(1, width), w_query, w_key, w_value, cosine, sine)


def attention_kernel(
    scale, group_pages,
    wants, page_order, s_idx, s_cnt,
    q_ref, q_want, q_req, q_pos,
    p_ref,
    s_ref, s_tag, s_bound,
    o_ref, m_sc, l_sc, acc_sc, pm_sc, pl_sc, pacc_sc,
):
    prefixes, per_prefix = page_order.shape

    def update(m_ref, l_ref, acc_ref, score_list, value_list):
        run_max = m_ref[...]
        new_max = run_max
        for scores in score_list:
            new_max = jnp.maximum(new_max, jnp.max(scores, axis=1, keepdims=True))
        fade = jnp.exp(run_max - new_max)
        total = l_ref[...] * fade
        acc = acc_ref[...] * fade
        for scores, values in zip(score_list, value_list):
            weights = jnp.exp(scores - new_max)
            total = total + jnp.sum(weights, axis=1, keepdims=True)
            acc = acc + jnp.dot(weights.astype(jnp.bfloat16), values, preferred_element_type=jnp.float32)
        l_ref[...] = total
        acc_ref[...] = acc
        m_ref[...] = new_max

    for i in range(q_ref.shape[0]):
        m_sc[...] = jnp.full(m_sc.shape, -1e30, jnp.float32)
        l_sc[...] = jnp.zeros(l_sc.shape, jnp.float32)
        acc_sc[...] = jnp.zeros(acc_sc.shape, jnp.float32)
        heads = q_ref.shape[2] // q_ref.shape[1]
        size = q_ref.shape[1]
        query = jnp.concatenate([q_ref[i, :, h * size:(h + 1) * size] for h in range(heads)], axis=0)
        want = q_want[i]
        req = q_req[i]
        pos = q_pos[i]

        def score(keys):
            return lax.dot_general(
                query, keys, (((1,), (1,)), ((), ())), preferred_element_type=jnp.float32
            ) * scale

        for p in range(prefixes):
            @pl.when(wants[i, p] > 0)
            def _():
                pm_sc[...] = jnp.full(pm_sc.shape, -1e30, jnp.float32)
                pl_sc[...] = jnp.zeros(pl_sc.shape, jnp.float32)
                pacc_sc[...] = jnp.zeros(pacc_sc.shape, jnp.float32)

                def page_step(g, carry):
                    pages = [page_order[p, g * group_pages + j] for j in range(group_pages)]
                    blocks = [p_ref[b] for b in pages]
                    update(
                        pm_sc, pl_sc, pacc_sc,
                        [score(blk[:, :size]) for blk in blocks],
                        [blk[:, size:] for blk in blocks],
                    )
                    return carry

                lax.fori_loop(0, per_prefix // group_pages, page_step, 0)
                mine = want == p
                m_sc[...] = jnp.where(mine, pm_sc[...], m_sc[...])
                l_sc[...] = jnp.where(mine, pl_sc[...], l_sc[...])
                acc_sc[...] = jnp.where(mine, pacc_sc[...], acc_sc[...])

        def step(n, carry):
            b = s_idx[i, n]
            scores = score(s_ref[0, b])
            seen = (s_tag[b] == req) & (s_bound[b] <= pos)
            run_max = m_sc[...]
            new_max = jnp.maximum(
                run_max, jnp.max(jnp.where(seen, scores, -1e30), axis=1, keepdims=True)
            )
            weights = jnp.where(seen, jnp.exp(scores - new_max), 0.0)
            fade = jnp.exp(run_max - new_max)
            l_sc[...] = l_sc[...] * fade + jnp.sum(weights, axis=1, keepdims=True)
            acc_sc[...] = acc_sc[...] * fade + jnp.dot(
                weights.astype(jnp.bfloat16), s_ref[1, b], preferred_element_type=jnp.float32
            )
            m_sc[...] = new_max
            return carry

        lax.fori_loop(0, s_cnt[i], step, 0)
        result = (acc_sc[...] / l_sc[...]).astype(o_ref.dtype)
        for h in range(heads):
            o_ref[i, :, h * size:(h + 1) * size] = result[h * size:(h + 1) * size]


def block_attention(scale, lists, queries, query_meta, prefix_parts, suffix_parts):
    q_blocks, block_rows, q_width = queries.shape
    width = queries.shape[1]
    q_rows = q_width // width * block_rows
    smem = pl.BlockSpec(memory_space=pltpu.SMEM)
    vmem = pl.BlockSpec(memory_space=pltpu.VMEM)
    state = [
        pltpu.VMEM((q_rows, 1), jnp.float32),
        pltpu.VMEM((q_rows, 1), jnp.float32),
        pltpu.VMEM((q_rows, width), jnp.float32),
    ]
    return pl.pallas_call(
        functools.partial(attention_kernel, scale, 4),
        out_shape=jax.ShapeDtypeStruct((q_blocks, block_rows, q_width), jnp.bfloat16),
        in_specs=[smem] * 4 + [vmem] * 8,
        out_specs=vmem,
        scratch_shapes=state + state,
        compiler_params=pltpu.CompilerParams(vmem_limit_bytes=48 * 1024 * 1024),
    )(*lists, queries, *query_meta, *prefix_parts, *suffix_parts)


def visible_list(visible):
    count = visible.shape[1]
    ids = jnp.arange(count, dtype=jnp.int32)
    rank = jnp.sum((visible[:, :, None] & (ids[:, None] < ids[None, :])[None]).astype(jnp.int32), axis=1)
    pick = visible[:, None, :] & (rank[:, None, :] == ids[None, :, None])
    order = jnp.sum(jnp.where(pick, ids[None, None, :], 0), axis=2).astype(jnp.int32)
    return order, jnp.sum(visible.astype(jnp.int32), axis=1)


def body(
    seq_n,
    tp_n,
    hidden,
    norm_gain,
    w_query,
    w_key,
    w_value,
    prefix_keys,
    prefix_values,
    page_prefix,
    request_prefix,
    suffix_lengths,
    row_order,
):
    gathered_prefix = lax.all_gather(
        jnp.concatenate([prefix_keys, prefix_values], axis=1), "seq", axis=0, tiled=True
    )
    gathered = tp_gather(hidden, tp_n, 2)
    local_rows = gathered.shape[0]
    request_all, position_all, wanted_all = locate(row_order, suffix_lengths, request_prefix)
    offset = lax.axis_index("seq") * local_rows
    request = lax.dynamic_slice_in_dim(request_all, offset, local_rows)
    position = lax.dynamic_slice_in_dim(position_all, offset, local_rows)
    wanted = lax.dynamic_slice_in_dim(wanted_all, offset, local_rows)
    prefix_len = page_prefix.shape[0] * PAGE // PREFIXES
    rope_at = prefix_len + position
    q_heads = w_query.shape[1] // HEAD
    kv_heads = w_key.shape[1] // HEAD
    group_size = q_heads // kv_heads
    half_dim = HEAD // 2
    frequency = ROPE_BASE ** (-(jnp.arange(half_dim, dtype=jnp.float32) * 2.0 / HEAD))
    angles = rope_at.astype(jnp.float32)[:, None] * frequency[None, :]
    cosine = jnp.cos(angles)
    sine_part = jnp.sin(angles)
    cos_full = jnp.concatenate([cosine, cosine], axis=1)
    sin_signed = jnp.concatenate([-sine_part, sine_part], axis=1)
    stacked_q, new_keys, new_values, stacked_kv = project(
        gathered, norm_gain, w_query, w_key, w_value, cos_full, sin_signed, PAGE
    )
    score_scale = 1.0 / math.sqrt(HEAD)
    block = PAGE
    q_blocks = local_rows // block
    pages = page_prefix.shape[0]
    runs = row_order.shape[0] // block

    def per_query(values):
        spread = jnp.broadcast_to(values.reshape(q_blocks, 1, block), (q_blocks, group_size, block))
        return spread.reshape(q_blocks, group_size * block, 1).astype(jnp.int32)

    query_meta = (per_query(wanted), per_query(request + PREFIXES), per_query(position))
    want_blocks = wanted.reshape(q_blocks, block)
    block_wants = jnp.any(
        want_blocks[:, :, None] == jnp.arange(PREFIXES, dtype=jnp.int32)[None, None, :], axis=1
    )
    page_ids = jnp.arange(pages, dtype=jnp.int32)
    same = (page_prefix[:, None] == page_prefix[None, :]) & (page_ids[:, None] < page_ids[None, :])
    page_rank = jnp.sum(same.astype(jnp.int32), axis=0)
    per_prefix = pages // PREFIXES
    pick = (page_prefix[None, None, :] == jnp.arange(PREFIXES, dtype=jnp.int32)[:, None, None]) & (
        page_rank[None, None, :] == jnp.arange(per_prefix, dtype=jnp.int32)[None, :, None]
    )
    page_order = jnp.sum(jnp.where(pick, page_ids[None, None, :], 0), axis=2).astype(jnp.int32)
    local_place = lax.dynamic_slice_in_dim(row_order, offset, local_rows).reshape(q_blocks, block)
    first_seen = jnp.min(local_place - position.reshape(q_blocks, block), axis=1)
    last_seen = jnp.max(local_place, axis=1)
    run_place = row_order.reshape(runs, block)
    run_low = jnp.min(run_place, axis=1)
    run_high = jnp.max(run_place, axis=1)
    run_visible = (run_low[None, :] <= last_seen[:, None]) & (run_high[None, :] >= first_seen[:, None])
    s_idx, s_cnt = visible_list(run_visible)

    seq_n_blocks = seq_n
    prefix_parts = (gathered_prefix.reshape(pages, block, 2 * HEAD),)
    gathered_suffix = seq_gather(stacked_kv, seq_n_blocks, 1)
    suffix_parts = (
        gathered_suffix.reshape(2, runs, block, HEAD),
        (request_all + PREFIXES).reshape(runs, 1, block).astype(jnp.int32),
        position_all.reshape(runs, 1, block).astype(jnp.int32),
    )
    out = block_attention(
        score_scale, (block_wants.astype(jnp.int32), page_order, s_idx, s_cnt), stacked_q, query_meta, prefix_parts, suffix_parts
    )
    attended = out.reshape(local_rows, group_size * HEAD)
    return (attended, new_keys, new_values)


def solution(mesh):
    return jax.shard_map(
        functools.partial(body, mesh.shape["seq"], mesh.shape["tp"]),
        mesh=mesh,
        in_specs=(
            P("seq", "tp"),
            P(),
            P(None, "tp"),
            P(None, "tp"),
            P(None, "tp"),
            P("seq", "tp"),
            P("seq", "tp"),
            P(),
            P(),
            P(),
            P(),
        ),
        out_specs=(P("seq", "tp"), P("seq", "tp"), P("seq", "tp")),
        check_vma=False,
    )
```

```python
import functools
import math

import jax
import jax.numpy as jnp
from jax import lax
from jax.sharding import PartitionSpec as P
from jax.experimental import pallas as pl
from jax.experimental.pallas import tpu as pltpu

HEAD = 128
PAGE = 128
PREFIXES = 4


ROPE_BASE = 5000000.0


def rotate(tensor_in, positions):
    head_dim = tensor_in.shape[-1]
    half_dim = head_dim // 2
    frequency = ROPE_BASE ** (-(jnp.arange(half_dim, dtype=jnp.float32) * 2.0 / head_dim))
    angles = positions.astype(jnp.float32)[:, None] * frequency[None, :]
    cosine = jnp.cos(angles)[:, None, :]
    sine_part = jnp.sin(angles)[:, None, :]
    first_half = tensor_in[..., :half_dim]
    second_half = tensor_in[..., half_dim:]
    return jnp.concatenate(
        [
            first_half * cosine - second_half * sine_part,
            second_half * cosine + first_half * sine_part,
        ],
        axis=-1,
    )


def locate(row_order, suffix_lengths, request_prefix):
    end_rows = jnp.cumsum(suffix_lengths)
    starts = end_rows - suffix_lengths
    numbers = jnp.arange(suffix_lengths.shape[0], dtype=jnp.int32)
    request = jnp.sum((row_order[:, None] >= end_rows[None, :]).astype(jnp.int32), axis=1)
    chosen = request[:, None] == numbers[None, :]
    position = row_order - jnp.sum(jnp.where(chosen, starts[None, :], 0), axis=1)
    wanted = jnp.sum(jnp.where(chosen, request_prefix[None, :], 0), axis=1)
    return (request, position, wanted)


def seq_gather_kernel(
    zs, xs, x_ref, o_ref, z_send, z_recv, r_send, r_recv, f_send, f_recv, c_send, c_recv, local_sem
):
    me = lax.axis_index("seq")
    core = me % 2
    chip = me // 2
    za = chip // xs
    xb = chip % xs
    right = lax.rem(xb + 1, xs)
    left = lax.rem(xb + xs - 1, xs)
    parts = x_ref.shape[0]
    mesh_id = pl.DeviceIdType.MESH

    def seq_of(z, x, c):
        return (z * xs + x) * 2 + c

    def signal(sem, target):
        pl.semaphore_signal(sem, inc=1, device_id={"seq": target}, device_id_type=mesh_id)

    barrier = pltpu.get_barrier_semaphore()

    def greet(k, carry):
        signal(barrier, seq_of(lax.rem(za + k, zs), xb, core))
        return carry

    lax.fori_loop(1, zs, greet, 0)
    signal(barrier, seq_of(za, right, core))
    signal(barrier, seq_of(za, left, core))
    signal(barrier, seq_of(za, xb, 1 - core))
    pl.semaphore_wait(barrier, zs + 2)

    local = pltpu.make_async_copy(x_ref, o_ref.at[:, za, xb, core], local_sem)
    local.start()

    def z_copy(a, peer_z, slot_z):
        return pltpu.make_async_remote_copy(
            src_ref=x_ref.at[a],
            dst_ref=o_ref.at[a, slot_z, xb, core],
            send_sem=z_send.at[a, peer_z],
            recv_sem=z_recv.at[a, slot_z],
            device_id={"seq": seq_of(peer_z, xb, core)},
            device_id_type=mesh_id,
        )

    def z_start(k, carry):
        peer_z = lax.rem(za + k, zs)
        for a in range(parts):
            z_copy(a, peer_z, za).start()
        return carry

    lax.fori_loop(1, zs, z_start, 0)

    def z_finish(k, carry):
        peer_z = lax.rem(za + k, zs)
        for a in range(parts):
            copy = z_copy(a, peer_z, peer_z)
            copy.wait_send()
            copy.wait_recv()
        return carry

    lax.fori_loop(1, zs, z_finish, 0)
    local.wait()

    def hand(a, group, slot):
        return pltpu.make_async_remote_copy(
            src_ref=o_ref.at[a, :, group, slot],
            dst_ref=o_ref.at[a, :, group, slot],
            send_sem=c_send.at[a, group],
            recv_sem=c_recv.at[a, group],
            device_id={"seq": seq_of(za, xb, 1 - core)},
            device_id_type=mesh_id,
        )

    across = []
    for a in range(parts):
        across.append(hand(a, xb, core))
        across[-1].start()

    def ring_copy(a, side, group, target_x, sem_side):
        return pltpu.make_async_remote_copy(
            src_ref=o_ref.at[a, :, group, core],
            dst_ref=o_ref.at[a, :, group, core],
            send_sem=r_send.at[a, side],
            recv_sem=r_recv.at[a, sem_side],
            device_id={"seq": seq_of(za, target_x, core)},
            device_id_type=mesh_id,
        )

    outgoing = []
    for a in range(parts):
        outgoing.append(ring_copy(a, 0, xb, right, 0))
        outgoing.append(ring_copy(a, 1, xb, left, 1))
    for copy in outgoing:
        copy.start()
    for a in range(parts):
        ring_copy(a, 0, left, right, 0).wait_recv()
        ring_copy(a, 1, right, left, 1).wait_recv()
    for a in range(parts):
        for group in (left, right):
            across.append(hand(a, group, core))
            across[-1].start()
    for copy in outgoing:
        copy.wait_send()

    far = lax.rem(xb + 2, xs)
    relay_k = pltpu.make_async_remote_copy(
        src_ref=o_ref.at[0, :, left, core],
        dst_ref=o_ref.at[0, :, left, core],
        send_sem=f_send.at[0],
        recv_sem=f_recv.at[0],
        device_id={"seq": seq_of(za, right, core)},
        device_id_type=mesh_id,
    )
    relay_v = pltpu.make_async_remote_copy(
        src_ref=o_ref.at[1, :, right, core],
        dst_ref=o_ref.at[1, :, right, core],
        send_sem=f_send.at[1],
        recv_sem=f_recv.at[1],
        device_id={"seq": seq_of(za, left, core)},
        device_id_type=mesh_id,
    )
    relay_k.start()
    relay_v.start()
    pltpu.make_async_remote_copy(
        src_ref=o_ref.at[0, :, far, core],
        dst_ref=o_ref.at[0, :, far, core],
        send_sem=f_send.at[0],
        recv_sem=f_recv.at[0],
        device_id={"seq": seq_of(za, right, core)},
        device_id_type=mesh_id,
    ).wait_recv()
    pltpu.make_async_remote_copy(
        src_ref=o_ref.at[1, :, far, core],
        dst_ref=o_ref.at[1, :, far, core],
        send_sem=f_send.at[1],
        recv_sem=f_recv.at[1],
        device_id={"seq": seq_of(za, left, core)},
        device_id_type=mesh_id,
    ).wait_recv()
    relay_k.wait_send()
    relay_v.wait_send()
    for a in range(parts):
        across.append(hand(a, far, core))
        across[-1].start()

    for copy in across:
        copy.wait_send()
    for a in range(parts):
        for g in range(xs):
            hand(a, g, 1 - core).wait_recv()


def seq_gather(stacked, n, cid):
    parts, rows, cols = stacked.shape
    chips = n // 2
    xs = 4
    zs = chips // xs
    return pl.pallas_call(
        functools.partial(seq_gather_kernel, zs, xs),
        out_shape=jax.ShapeDtypeStruct((parts, zs, xs, 2, rows, cols), stacked.dtype),
        in_specs=[pl.BlockSpec(memory_space=pl.ANY)],
        out_specs=pl.BlockSpec(memory_space=pl.ANY),
        scratch_shapes=[
            pltpu.SemaphoreType.DMA((parts, zs)),
            pltpu.SemaphoreType.DMA((parts, zs)),
            pltpu.SemaphoreType.DMA((parts, 2)),
            pltpu.SemaphoreType.DMA((parts, 2)),
            pltpu.SemaphoreType.DMA((parts,)),
            pltpu.SemaphoreType.DMA((parts,)),
            pltpu.SemaphoreType.DMA((parts, xs)),
            pltpu.SemaphoreType.DMA((parts, xs)),
            pltpu.SemaphoreType.DMA,
        ],
        compiler_params=pltpu.CompilerParams(collective_id=cid, has_side_effects=True),
    )(stacked)


def tp_gather_kernel(ys, x_ref, o_ref, p_send, p_recv, r_send, r_recv, f_send, f_recv, local_sem):
    me = lax.axis_index("tp")
    yy = me // 2
    zh = me % 2
    right = lax.rem(yy + 1, ys)
    left = lax.rem(yy + ys - 1, ys)
    far = lax.rem(yy + 2, ys)
    width = x_ref.shape[1]
    mesh_id = pl.DeviceIdType.MESH

    def cols(y, h):
        return pl.ds(pl.multiple_of((y * 2 + h) * width, 128), width)

    def pair(y):
        return pl.ds(pl.multiple_of(y * 2 * width, 128), 2 * width)

    def signal(target):
        pl.semaphore_signal(barrier, inc=1, device_id={"tp": target}, device_id_type=mesh_id)

    barrier = pltpu.get_barrier_semaphore()
    signal(yy * 2 + 1 - zh)
    signal(right * 2 + zh)
    signal(left * 2 + zh)
    pl.semaphore_wait(barrier, 3)

    local = pltpu.make_async_copy(x_ref, o_ref.at[:, cols(yy, zh)], local_sem)
    local.start()
    to_partner = pltpu.make_async_remote_copy(
        src_ref=x_ref,
        dst_ref=o_ref.at[:, cols(yy, zh)],
        send_sem=p_send,
        recv_sem=p_recv,
        device_id={"tp": yy * 2 + 1 - zh},
        device_id_type=mesh_id,
    )
    to_partner.start()
    pltpu.make_async_remote_copy(
        src_ref=x_ref,
        dst_ref=o_ref.at[:, cols(yy, 1 - zh)],
        send_sem=p_send,
        recv_sem=p_recv,
        device_id={"tp": yy * 2 + 1 - zh},
        device_id_type=mesh_id,
    ).wait_recv()
    local.wait()
    to_partner.wait_send()

    pieces = r_send.shape[1]
    span = x_ref.shape[0] // pieces

    def ring(group, target, side, c):
        rows = pl.ds(c * span, span)
        return pltpu.make_async_remote_copy(
            src_ref=o_ref.at[rows, pair(group)],
            dst_ref=o_ref.at[rows, pair(group)],
            send_sem=r_send.at[side, c],
            recv_sem=r_recv.at[side, c],
            device_id={"tp": target * 2 + zh},
            device_id_type=mesh_id,
        )

    outgoing = []
    for c in range(pieces):
        outgoing += [ring(yy, right, 0, c), ring(yy, left, 1, c)]
    for copy in outgoing:
        copy.start()
    for c in range(pieces):
        ring(left, right, 0, c).wait_recv()
        ring(right, left, 1, c).wait_recv()
    for copy in outgoing:
        copy.wait_send()

    def relay(group, h, target, side, c):
        rows = pl.ds(c * span, span)
        return pltpu.make_async_remote_copy(
            src_ref=o_ref.at[rows, cols(group, h)],
            dst_ref=o_ref.at[rows, cols(group, h)],
            send_sem=f_send.at[side, c],
            recv_sem=f_recv.at[side, c],
            device_id={"tp": target * 2 + zh},
            device_id_type=mesh_id,
        )

    relays = []
    for c in range(pieces):
        relays += [relay(left, 0, right, 0, c), relay(right, 1, left, 1, c)]
    for copy in relays:
        copy.start()
    for c in range(pieces):
        relay(far, 0, right, 0, c).wait_recv()
        relay(far, 1, left, 1, c).wait_recv()
    for copy in relays:
        copy.wait_send()


def tp_gather(block, n, cid):
    rows, width = block.shape
    return pl.pallas_call(
        functools.partial(tp_gather_kernel, n // 2),
        out_shape=jax.ShapeDtypeStruct((rows, width * n), block.dtype),
        in_specs=[pl.BlockSpec(memory_space=pl.ANY)],
        out_specs=pl.BlockSpec(memory_space=pl.ANY),
        scratch_shapes=[
            pltpu.SemaphoreType.DMA,
            pltpu.SemaphoreType.DMA,
            pltpu.SemaphoreType.DMA((2, 4)),
            pltpu.SemaphoreType.DMA((2, 4)),
            pltpu.SemaphoreType.DMA((2, 4)),
            pltpu.SemaphoreType.DMA((2, 4)),
            pltpu.SemaphoreType.DMA,
        ],
        compiler_params=pltpu.CompilerParams(collective_id=cid, has_side_effects=True),
    )(block)


def project_kernel(x_ref, g_ref, wq_ref, wk_ref, wv_ref, cos_ref, sin_ref, q_ref, k_ref, v_ref, kv_ref):
    x = x_ref[...].astype(jnp.float32)
    mean_sq = jnp.mean(x * x, axis=1, keepdims=True)
    normed = (x * lax.rsqrt(mean_sq + 1e-05) * g_ref[...].astype(jnp.float32)).astype(jnp.bfloat16)
    cosine = cos_ref[...]
    sine = sin_ref[...]

    def rotated(values):
        half = values.shape[1] // 2
        return values * cosine + pltpu.roll(values, half, 1) * sine

    queries = jnp.dot(normed, wq_ref[...], preferred_element_type=jnp.float32)
    for h in range(queries.shape[1] // HEAD):
        q_ref[0, :, h * HEAD:(h + 1) * HEAD] = rotated(queries[:, h * HEAD:(h + 1) * HEAD]).astype(q_ref.dtype)
    keys = jnp.dot(normed, wk_ref[...], preferred_element_type=jnp.float32)
    for h in range(keys.shape[1] // HEAD):
        part = rotated(keys[:, h * HEAD:(h + 1) * HEAD]).astype(k_ref.dtype)
        k_ref[:, h * HEAD:(h + 1) * HEAD] = part
        kv_ref[0, :, h * HEAD:(h + 1) * HEAD] = part
    values = jnp.dot(normed, wv_ref[...], preferred_element_type=jnp.float32).astype(v_ref.dtype)
    v_ref[...] = values
    kv_ref[1] = values


def project(gathered, norm_gain, w_query, w_key, w_value, cosine, sine, block):
    rows, width = gathered.shape
    steps = rows // block
    q_width = w_query.shape[1]
    kv_width = w_key.shape[1]
    whole = lambda i: (0, 0)
    return pl.pallas_call(
        project_kernel,
        grid=(steps,),
        out_shape=(
            jax.ShapeDtypeStruct((steps, block, q_width), jnp.bfloat16),
            jax.ShapeDtypeStruct((rows, kv_width), jnp.bfloat16),
            jax.ShapeDtypeStruct((rows, kv_width), jnp.bfloat16),
            jax.ShapeDtypeStruct((2, rows, kv_width), jnp.bfloat16),
        ),
        in_specs=[
            pl.BlockSpec((block, width), lambda i: (i, 0)),
            pl.BlockSpec((1, width), whole),
            pl.BlockSpec((width, q_width), whole),
            pl.BlockSpec((width, kv_width), whole),
            pl.BlockSpec((width, kv_width), whole),
            pl.BlockSpec((block, HEAD), lambda i: (i, 0)),
            pl.BlockSpec((block, HEAD), lambda i: (i, 0)),
        ],
        out_specs=(
            pl.BlockSpec((1, block, q_width), lambda i: (i, 0, 0)),
            pl.BlockSpec((block, kv_width), lambda i: (i, 0)),
            pl.BlockSpec((block, kv_width), lambda i: (i, 0)),
            pl.BlockSpec((2, block, kv_width), lambda i: (0, i, 0)),
        ),
        compiler_params=pltpu.CompilerParams(vmem_limit_bytes=60 * 1024 * 1024),
    )(gathered, norm_gain.reshape(1, width), w_query, w_key, w_value, cosine, sine)


def attention_kernel(
    scale, group_pages,
    wants, page_order, s_idx, s_cnt,
    q_ref, q_want, q_req, q_pos,
    p_ref,
    s_ref, s_tag, s_bound,
    o_ref, m_sc, l_sc, acc_sc, pm_sc, pl_sc, pacc_sc,
):
    prefixes, per_prefix = page_order.shape

    def update(m_ref, l_ref, acc_ref, score_list, value_list):
        run_max = m_ref[...]
        new_max = run_max
        for scores in score_list:
            new_max = jnp.maximum(new_max, jnp.max(scores, axis=1, keepdims=True))
        fade = jnp.exp(run_max - new_max)
        total = l_ref[...] * fade
        acc = acc_ref[...] * fade
        for scores, values in zip(score_list, value_list):
            weights = jnp.exp(scores - new_max)
            total = total + jnp.sum(weights, axis=1, keepdims=True)
            acc = acc + jnp.dot(weights.astype(jnp.bfloat16), values, preferred_element_type=jnp.float32)
        l_ref[...] = total
        acc_ref[...] = acc
        m_ref[...] = new_max

    for i in range(q_ref.shape[0]):
        m_sc[...] = jnp.full(m_sc.shape, -1e30, jnp.float32)
        l_sc[...] = jnp.zeros(l_sc.shape, jnp.float32)
        acc_sc[...] = jnp.zeros(acc_sc.shape, jnp.float32)
        heads = q_ref.shape[2] // q_ref.shape[1]
        size = q_ref.shape[1]
        query = jnp.concatenate([q_ref[i, :, h * size:(h + 1) * size] for h in range(heads)], axis=0)
        want = q_want[i]
        req = q_req[i]
        pos = q_pos[i]

        def score(keys):
            return lax.dot_general(
                query, keys, (((1,), (1,)), ((), ())), preferred_element_type=jnp.float32
            ) * scale

        for p in range(prefixes):
            @pl.when(wants[i, p] > 0)
            def _():
                pm_sc[...] = jnp.full(pm_sc.shape, -1e30, jnp.float32)
                pl_sc[...] = jnp.zeros(pl_sc.shape, jnp.float32)
                pacc_sc[...] = jnp.zeros(pacc_sc.shape, jnp.float32)

                def page_step(g, carry):
                    pages = [page_order[p, g * group_pages + j] for j in range(group_pages)]
                    blocks = [p_ref[b] for b in pages]
                    update(
                        pm_sc, pl_sc, pacc_sc,
                        [score(blk[:, :size]) for blk in blocks],
                        [blk[:, size:] for blk in blocks],
                    )
                    return carry

                lax.fori_loop(0, per_prefix // group_pages, page_step, 0)
                mine = want == p
                m_sc[...] = jnp.where(mine, pm_sc[...], m_sc[...])
                l_sc[...] = jnp.where(mine, pl_sc[...], l_sc[...])
                acc_sc[...] = jnp.where(mine, pacc_sc[...], acc_sc[...])

        def step(n, carry):
            b = s_idx[i, n]
            scores = score(s_ref[0, b])
            seen = (s_tag[b] == req) & (s_bound[b] <= pos)
            run_max = m_sc[...]
            new_max = jnp.maximum(
                run_max, jnp.max(jnp.where(seen, scores, -1e30), axis=1, keepdims=True)
            )
            weights = jnp.where(seen, jnp.exp(scores - new_max), 0.0)
            fade = jnp.exp(run_max - new_max)
            l_sc[...] = l_sc[...] * fade + jnp.sum(weights, axis=1, keepdims=True)
            acc_sc[...] = acc_sc[...] * fade + jnp.dot(
                weights.astype(jnp.bfloat16), s_ref[1, b], preferred_element_type=jnp.float32
            )
            m_sc[...] = new_max
            return carry

        lax.fori_loop(0, s_cnt[i], step, 0)
        result = (acc_sc[...] / l_sc[...]).astype(o_ref.dtype)
        for h in range(heads):
            o_ref[i, :, h * size:(h + 1) * size] = result[h * size:(h + 1) * size]


def block_attention(scale, lists, queries, query_meta, prefix_parts, suffix_parts):
    q_blocks, block_rows, q_width = queries.shape
    width = queries.shape[1]
    q_rows = q_width // width * block_rows
    smem = pl.BlockSpec(memory_space=pltpu.SMEM)
    vmem = pl.BlockSpec(memory_space=pltpu.VMEM)
    state = [
        pltpu.VMEM((q_rows, 1), jnp.float32),
        pltpu.VMEM((q_rows, 1), jnp.float32),
        pltpu.VMEM((q_rows, width), jnp.float32),
    ]
    return pl.pallas_call(
        functools.partial(attention_kernel, scale, 4),
        out_shape=jax.ShapeDtypeStruct((q_blocks, block_rows, q_width), jnp.bfloat16),
        in_specs=[smem] * 4 + [vmem] * 8,
        out_specs=vmem,
        scratch_shapes=state + state,
        compiler_params=pltpu.CompilerParams(vmem_limit_bytes=48 * 1024 * 1024),
    )(*lists, queries, *query_meta, *prefix_parts, *suffix_parts)


def visible_list(visible):
    count = visible.shape[1]
    ids = jnp.arange(count, dtype=jnp.int32)
    rank = jnp.sum((visible[:, :, None] & (ids[:, None] < ids[None, :])[None]).astype(jnp.int32), axis=1)
    pick = visible[:, None, :] & (rank[:, None, :] == ids[None, :, None])
    order = jnp.sum(jnp.where(pick, ids[None, None, :], 0), axis=2).astype(jnp.int32)
    return order, jnp.sum(visible.astype(jnp.int32), axis=1)


def body(
    seq_n,
    tp_n,
    hidden,
    norm_gain,
    w_query,
    w_key,
    w_value,
    prefix_keys,
    prefix_values,
    page_prefix,
    request_prefix,
    suffix_lengths,
    row_order,
):
    gathered_prefix = lax.all_gather(
        jnp.concatenate([prefix_keys, prefix_values], axis=1), "seq", axis=0, tiled=True
    )
    gathered = tp_gather(hidden, tp_n, 2)
    local_rows = gathered.shape[0]
    request_all, position_all, wanted_all = locate(row_order, suffix_lengths, request_prefix)
    offset = lax.axis_index("seq") * local_rows
    request = lax.dynamic_slice_in_dim(request_all, offset, local_rows)
    position = lax.dynamic_slice_in_dim(position_all, offset, local_rows)
    wanted = lax.dynamic_slice_in_dim(wanted_all, offset, local_rows)
    prefix_len = page_prefix.shape[0] * PAGE // PREFIXES
    rope_at = prefix_len + position
    q_heads = w_query.shape[1] // HEAD
    kv_heads = w_key.shape[1] // HEAD
    group_size = q_heads // kv_heads
    half_dim = HEAD // 2
    frequency = ROPE_BASE ** (-(jnp.arange(half_dim, dtype=jnp.float32) * 2.0 / HEAD))
    angles = rope_at.astype(jnp.float32)[:, None] * frequency[None, :]
    cosine = jnp.cos(angles)
    sine_part = jnp.sin(angles)
    cos_full = jnp.concatenate([cosine, cosine], axis=1)
    sin_signed = jnp.concatenate([-sine_part, sine_part], axis=1)
    stacked_q, new_keys, new_values, stacked_kv = project(
        gathered, norm_gain, w_query, w_key, w_value, cos_full, sin_signed, PAGE
    )
    score_scale = 1.0 / math.sqrt(HEAD)
    block = PAGE
    q_blocks = local_rows // block
    pages = page_prefix.shape[0]
    runs = row_order.shape[0] // block

    def per_query(values):
        spread = jnp.broadcast_to(values.reshape(q_blocks, 1, block), (q_blocks, group_size, block))
        return spread.reshape(q_blocks, group_size * block, 1).astype(jnp.int32)

    query_meta = (per_query(wanted), per_query(request + PREFIXES), per_query(position))
    want_blocks = wanted.reshape(q_blocks, block)
    block_wants = jnp.any(
        want_blocks[:, :, None] == jnp.arange(PREFIXES, dtype=jnp.int32)[None, None, :], axis=1
    )
    page_ids = jnp.arange(pages, dtype=jnp.int32)
    same = (page_prefix[:, None] == page_prefix[None, :]) & (page_ids[:, None] < page_ids[None, :])
    page_rank = jnp.sum(same.astype(jnp.int32), axis=0)
    per_prefix = pages // PREFIXES
    pick = (page_prefix[None, None, :] == jnp.arange(PREFIXES, dtype=jnp.int32)[:, None, None]) & (
        page_rank[None, None, :] == jnp.arange(per_prefix, dtype=jnp.int32)[None, :, None]
    )
    page_order = jnp.sum(jnp.where(pick, page_ids[None, None, :], 0), axis=2).astype(jnp.int32)
    local_place = lax.dynamic_slice_in_dim(row_order, offset, local_rows).reshape(q_blocks, block)
    first_seen = jnp.min(local_place - position.reshape(q_blocks, block), axis=1)
    last_seen = jnp.max(local_place, axis=1)
    run_place = row_order.reshape(runs, block)
    run_low = jnp.min(run_place, axis=1)
    run_high = jnp.max(run_place, axis=1)
    run_visible = (run_low[None, :] <= last_seen[:, None]) & (run_high[None, :] >= first_seen[:, None])
    s_idx, s_cnt = visible_list(run_visible)

    seq_n_blocks = seq_n
    prefix_parts = (gathered_prefix.reshape(pages, block, 2 * HEAD),)
    gathered_suffix = seq_gather(stacked_kv, seq_n_blocks, 1)
    suffix_parts = (
        gathered_suffix.reshape(2, runs, block, HEAD),
        (request_all + PREFIXES).reshape(runs, 1, block).astype(jnp.int32),
        position_all.reshape(runs, 1, block).astype(jnp.int32),
    )
    out = block_attention(
        score_scale, (block_wants.astype(jnp.int32), page_order, s_idx, s_cnt), stacked_q, query_meta, prefix_parts, suffix_parts
    )
    attended = out.reshape(local_rows, group_size * HEAD)
    return (attended, new_keys, new_values)


def solution(mesh):
    return jax.shard_map(
        functools.partial(body, mesh.shape["seq"], mesh.shape["tp"]),
        mesh=mesh,
        in_specs=(
            P("seq", "tp"),
            P(),
            P(None, "tp"),
            P(None, "tp"),
            P(None, "tp"),
            P("seq", "tp"),
            P("seq", "tp"),
            P(),
            P(),
            P(),
            P(),
        ),
        out_specs=(P("seq", "tp"), P("seq", "tp"), P("seq", "tp")),
        check_vma=False,
    )
```

```python
import functools
import math

import jax
import jax.numpy as jnp
from jax import lax
from jax.sharding import PartitionSpec as P
from jax.experimental import pallas as pl
from jax.experimental.pallas import tpu as pltpu

HEAD = 128
PAGE = 128
PREFIXES = 4


ROPE_BASE = 5000000.0


def rotate(tensor_in, positions):
    head_dim = tensor_in.shape[-1]
    half_dim = head_dim // 2
    frequency = ROPE_BASE ** (-(jnp.arange(half_dim, dtype=jnp.float32) * 2.0 / head_dim))
    angles = positions.astype(jnp.float32)[:, None] * frequency[None, :]
    cosine = jnp.cos(angles)[:, None, :]
    sine_part = jnp.sin(angles)[:, None, :]
    first_half = tensor_in[..., :half_dim]
    second_half = tensor_in[..., half_dim:]
    return jnp.concatenate(
        [
            first_half * cosine - second_half * sine_part,
            second_half * cosine + first_half * sine_part,
        ],
        axis=-1,
    )


def locate(row_order, suffix_lengths, request_prefix):
    end_rows = jnp.cumsum(suffix_lengths)
    starts = end_rows - suffix_lengths
    numbers = jnp.arange(suffix_lengths.shape[0], dtype=jnp.int32)
    request = jnp.sum((row_order[:, None] >= end_rows[None, :]).astype(jnp.int32), axis=1)
    chosen = request[:, None] == numbers[None, :]
    position = row_order - jnp.sum(jnp.where(chosen, starts[None, :], 0), axis=1)
    wanted = jnp.sum(jnp.where(chosen, request_prefix[None, :], 0), axis=1)
    return (request, position, wanted)


def seq_gather_kernel(
    zs, xs, x_ref, o_ref, z_send, z_recv, r_send, r_recv, f_send, f_recv, c_send, c_recv, local_sem
):
    me = lax.axis_index("seq")
    core = me % 2
    chip = me // 2
    za = chip // xs
    xb = chip % xs
    right = lax.rem(xb + 1, xs)
    left = lax.rem(xb + xs - 1, xs)
    parts = x_ref.shape[0]
    mesh_id = pl.DeviceIdType.MESH

    def seq_of(z, x, c):
        return (z * xs + x) * 2 + c

    def signal(sem, target):
        pl.semaphore_signal(sem, inc=1, device_id={"seq": target}, device_id_type=mesh_id)

    barrier = pltpu.get_barrier_semaphore()

    def greet(k, carry):
        signal(barrier, seq_of(lax.rem(za + k, zs), xb, core))
        return carry

    lax.fori_loop(1, zs, greet, 0)
    signal(barrier, seq_of(za, right, core))
    signal(barrier, seq_of(za, left, core))
    signal(barrier, seq_of(za, xb, 1 - core))
    pl.semaphore_wait(barrier, zs + 2)

    local = pltpu.make_async_copy(x_ref, o_ref.at[:, za, xb, core], local_sem)
    local.start()

    def z_copy(a, peer_z, slot_z):
        return pltpu.make_async_remote_copy(
            src_ref=x_ref.at[a],
            dst_ref=o_ref.at[a, slot_z, xb, core],
            send_sem=z_send.at[a, peer_z],
            recv_sem=z_recv.at[a, slot_z],
            device_id={"seq": seq_of(peer_z, xb, core)},
            device_id_type=mesh_id,
        )

    def z_start(k, carry):
        peer_z = lax.rem(za + k, zs)
        for a in range(parts):
            z_copy(a, peer_z, za).start()
        return carry

    lax.fori_loop(1, zs, z_start, 0)

    def z_finish(k, carry):
        peer_z = lax.rem(za + k, zs)
        for a in range(parts):
            copy = z_copy(a, peer_z, peer_z)
            copy.wait_send()
            copy.wait_recv()
        return carry

    lax.fori_loop(1, zs, z_finish, 0)
    local.wait()

    def hand(a, group, slot):
        return pltpu.make_async_remote_copy(
            src_ref=o_ref.at[a, :, group, slot],
            dst_ref=o_ref.at[a, :, group, slot],
            send_sem=c_send.at[a, group],
            recv_sem=c_recv.at[a, group],
            device_id={"seq": seq_of(za, xb, 1 - core)},
            device_id_type=mesh_id,
        )

    across = []
    for a in range(parts):
        across.append(hand(a, xb, core))
        across[-1].start()

    def ring_copy(a, side, group, target_x, sem_side):
        return pltpu.make_async_remote_copy(
            src_ref=o_ref.at[a, :, group, core],
            dst_ref=o_ref.at[a, :, group, core],
            send_sem=r_send.at[a, side],
            recv_sem=r_recv.at[a, sem_side],
            device_id={"seq": seq_of(za, target_x, core)},
            device_id_type=mesh_id,
        )

    outgoing = []
    for a in range(parts):
        outgoing.append(ring_copy(a, 0, xb, right, 0))
        outgoing.append(ring_copy(a, 1, xb, left, 1))
    for copy in outgoing:
        copy.start()
    for a in range(parts):
        ring_copy(a, 0, left, right, 0).wait_recv()
        ring_copy(a, 1, right, left, 1).wait_recv()
    for a in range(parts):
        for group in (left, right):
            across.append(hand(a, group, core))
            across[-1].start()
    for copy in outgoing:
        copy.wait_send()

    far = lax.rem(xb + 2, xs)
    relay_k = pltpu.make_async_remote_copy(
        src_ref=o_ref.at[0, :, left, core],
        dst_ref=o_ref.at[0, :, left, core],
        send_sem=f_send.at[0],
        recv_sem=f_recv.at[0],
        device_id={"seq": seq_of(za, right, core)},
        device_id_type=mesh_id,
    )
    relay_v = pltpu.make_async_remote_copy(
        src_ref=o_ref.at[1, :, right, core],
        dst_ref=o_ref.at[1, :, right, core],
        send_sem=f_send.at[1],
        recv_sem=f_recv.at[1],
        device_id={"seq": seq_of(za, left, core)},
        device_id_type=mesh_id,
    )
    relay_k.start()
    relay_v.start()
    pltpu.make_async_remote_copy(
        src_ref=o_ref.at[0, :, far, core],
        dst_ref=o_ref.at[0, :, far, core],
        send_sem=f_send.at[0],
        recv_sem=f_recv.at[0],
        device_id={"seq": seq_of(za, right, core)},
        device_id_type=mesh_id,
    ).wait_recv()
    pltpu.make_async_remote_copy(
        src_ref=o_ref.at[1, :, far, core],
        dst_ref=o_ref.at[1, :, far, core],
        send_sem=f_send.at[1],
        recv_sem=f_recv.at[1],
        device_id={"seq": seq_of(za, left, core)},
        device_id_type=mesh_id,
    ).wait_recv()
    relay_k.wait_send()
    relay_v.wait_send()
    for a in range(parts):
        across.append(hand(a, far, core))
        across[-1].start()

    for copy in across:
        copy.wait_send()
    for a in range(parts):
        for g in range(xs):
            hand(a, g, 1 - core).wait_recv()


def seq_gather(stacked, n, cid):
    parts, rows, cols = stacked.shape
    chips = n // 2
    xs = 4
    zs = chips // xs
    return pl.pallas_call(
        functools.partial(seq_gather_kernel, zs, xs),
        out_shape=jax.ShapeDtypeStruct((parts, zs, xs, 2, rows, cols), stacked.dtype),
        in_specs=[pl.BlockSpec(memory_space=pl.ANY)],
        out_specs=pl.BlockSpec(memory_space=pl.ANY),
        scratch_shapes=[
            pltpu.SemaphoreType.DMA((parts, zs)),
            pltpu.SemaphoreType.DMA((parts, zs)),
            pltpu.SemaphoreType.DMA((parts, 2)),
            pltpu.SemaphoreType.DMA((parts, 2)),
            pltpu.SemaphoreType.DMA((parts,)),
            pltpu.SemaphoreType.DMA((parts,)),
            pltpu.SemaphoreType.DMA((parts, xs)),
            pltpu.SemaphoreType.DMA((parts, xs)),
            pltpu.SemaphoreType.DMA,
        ],
        compiler_params=pltpu.CompilerParams(collective_id=cid, has_side_effects=True),
    )(stacked)


def tp_gather_kernel(ys, x_ref, o_ref, p_send, p_recv, r_send, r_recv, f_send, f_recv, local_sem):
    me = lax.axis_index("tp")
    yy = me // 2
    zh = me % 2
    right = lax.rem(yy + 1, ys)
    left = lax.rem(yy + ys - 1, ys)
    far = lax.rem(yy + 2, ys)
    width = x_ref.shape[1]
    mesh_id = pl.DeviceIdType.MESH

    def cols(y, h):
        return pl.ds(pl.multiple_of((y * 2 + h) * width, 128), width)

    def pair(y):
        return pl.ds(pl.multiple_of(y * 2 * width, 128), 2 * width)

    def signal(target):
        pl.semaphore_signal(barrier, inc=1, device_id={"tp": target}, device_id_type=mesh_id)

    barrier = pltpu.get_barrier_semaphore()
    signal(yy * 2 + 1 - zh)
    signal(right * 2 + zh)
    signal(left * 2 + zh)
    pl.semaphore_wait(barrier, 3)

    local = pltpu.make_async_copy(x_ref, o_ref.at[:, cols(yy, zh)], local_sem)
    local.start()
    to_partner = pltpu.make_async_remote_copy(
        src_ref=x_ref,
        dst_ref=o_ref.at[:, cols(yy, zh)],
        send_sem=p_send,
        recv_sem=p_recv,
        device_id={"tp": yy * 2 + 1 - zh},
        device_id_type=mesh_id,
    )
    to_partner.start()

    def ring(src, h, group, target, side):
        return pltpu.make_async_remote_copy(
            src_ref=src,
            dst_ref=o_ref.at[:, cols(group, h)],
            send_sem=r_send.at[side, h],
            recv_sem=r_recv.at[side, h],
            device_id={"tp": target * 2 + zh},
            device_id_type=mesh_id,
        )

    outgoing = [ring(x_ref, zh, yy, right, 0), ring(x_ref, zh, yy, left, 1)]
    for copy in outgoing:
        copy.start()
    pltpu.make_async_remote_copy(
        src_ref=x_ref,
        dst_ref=o_ref.at[:, cols(yy, 1 - zh)],
        send_sem=p_send,
        recv_sem=p_recv,
        device_id={"tp": yy * 2 + 1 - zh},
        device_id_type=mesh_id,
    ).wait_recv()
    partner_src = o_ref.at[:, cols(yy, 1 - zh)]
    later = [ring(partner_src, 1 - zh, yy, right, 0), ring(partner_src, 1 - zh, yy, left, 1)]
    for copy in later:
        copy.start()
    local.wait()
    to_partner.wait_send()
    for h in range(2):
        ring(x_ref, h, left, right, 0).wait_recv()
        ring(x_ref, h, right, left, 1).wait_recv()
    for copy in outgoing + later:
        copy.wait_send()
    pieces = f_send.shape[1]
    span = x_ref.shape[0] // pieces

    def relay(group, h, target, side, c):
        rows = pl.ds(c * span, span)
        return pltpu.make_async_remote_copy(
            src_ref=o_ref.at[rows, cols(group, h)],
            dst_ref=o_ref.at[rows, cols(group, h)],
            send_sem=f_send.at[side, c],
            recv_sem=f_recv.at[side, c],
            device_id={"tp": target * 2 + zh},
            device_id_type=mesh_id,
        )

    relays = []
    for c in range(pieces):
        relays += [relay(left, 0, right, 0, c), relay(right, 1, left, 1, c)]
    for copy in relays:
        copy.start()
    for c in range(pieces):
        relay(far, 0, right, 0, c).wait_recv()
        relay(far, 1, left, 1, c).wait_recv()
    for copy in relays:
        copy.wait_send()


def tp_gather(block, n, cid):
    rows, width = block.shape
    return pl.pallas_call(
        functools.partial(tp_gather_kernel, n // 2),
        out_shape=jax.ShapeDtypeStruct((rows, width * n), block.dtype),
        in_specs=[pl.BlockSpec(memory_space=pl.ANY)],
        out_specs=pl.BlockSpec(memory_space=pl.ANY),
        scratch_shapes=[
            pltpu.SemaphoreType.DMA,
            pltpu.SemaphoreType.DMA,
            pltpu.SemaphoreType.DMA((2, 2)),
            pltpu.SemaphoreType.DMA((2, 2)),
            pltpu.SemaphoreType.DMA((2, 4)),
            pltpu.SemaphoreType.DMA((2, 4)),
            pltpu.SemaphoreType.DMA,
        ],
        compiler_params=pltpu.CompilerParams(collective_id=cid, has_side_effects=True),
    )(block)


def project_kernel(x_ref, g_ref, wq_ref, wk_ref, wv_ref, cos_ref, sin_ref, q_ref, k_ref, v_ref, kv_ref):
    x = x_ref[...].astype(jnp.float32)
    mean_sq = jnp.mean(x * x, axis=1, keepdims=True)
    normed = (x * lax.rsqrt(mean_sq + 1e-05) * g_ref[...].astype(jnp.float32)).astype(jnp.bfloat16)
    cosine = cos_ref[...]
    sine = sin_ref[...]

    def rotated(values):
        half = values.shape[1] // 2
        return values * cosine + pltpu.roll(values, half, 1) * sine

    queries = jnp.dot(normed, wq_ref[...], preferred_element_type=jnp.float32)
    for h in range(queries.shape[1] // HEAD):
        q_ref[0, :, h * HEAD:(h + 1) * HEAD] = rotated(queries[:, h * HEAD:(h + 1) * HEAD]).astype(q_ref.dtype)
    keys = jnp.dot(normed, wk_ref[...], preferred_element_type=jnp.float32)
    for h in range(keys.shape[1] // HEAD):
        part = rotated(keys[:, h * HEAD:(h + 1) * HEAD]).astype(k_ref.dtype)
        k_ref[:, h * HEAD:(h + 1) * HEAD] = part
        kv_ref[0, :, h * HEAD:(h + 1) * HEAD] = part
    values = jnp.dot(normed, wv_ref[...], preferred_element_type=jnp.float32).astype(v_ref.dtype)
    v_ref[...] = values
    kv_ref[1] = values


def project(gathered, norm_gain, w_query, w_key, w_value, cosine, sine, block):
    rows, width = gathered.shape
    steps = rows // block
    q_width = w_query.shape[1]
    kv_width = w_key.shape[1]
    whole = lambda i: (0, 0)
    return pl.pallas_call(
        project_kernel,
        grid=(steps,),
        out_shape=(
            jax.ShapeDtypeStruct((steps, block, q_width), jnp.bfloat16),
            jax.ShapeDtypeStruct((rows, kv_width), jnp.bfloat16),
            jax.ShapeDtypeStruct((rows, kv_width), jnp.bfloat16),
            jax.ShapeDtypeStruct((2, rows, kv_width), jnp.bfloat16),
        ),
        in_specs=[
            pl.BlockSpec((block, width), lambda i: (i, 0)),
            pl.BlockSpec((1, width), whole),
            pl.BlockSpec((width, q_width), whole),
            pl.BlockSpec((width, kv_width), whole),
            pl.BlockSpec((width, kv_width), whole),
            pl.BlockSpec((block, HEAD), lambda i: (i, 0)),
            pl.BlockSpec((block, HEAD), lambda i: (i, 0)),
        ],
        out_specs=(
            pl.BlockSpec((1, block, q_width), lambda i: (i, 0, 0)),
            pl.BlockSpec((block, kv_width), lambda i: (i, 0)),
            pl.BlockSpec((block, kv_width), lambda i: (i, 0)),
            pl.BlockSpec((2, block, kv_width), lambda i: (0, i, 0)),
        ),
        compiler_params=pltpu.CompilerParams(vmem_limit_bytes=60 * 1024 * 1024),
    )(gathered, norm_gain.reshape(1, width), w_query, w_key, w_value, cosine, sine)


def attention_kernel(
    scale, group_pages,
    wants, page_order, s_idx, s_cnt,
    q_ref, q_want, q_req, q_pos,
    p_ref,
    s_ref, s_tag, s_bound,
    o_ref, m_sc, l_sc, acc_sc, pm_sc, pl_sc, pacc_sc,
):
    prefixes, per_prefix = page_order.shape

    def update(m_ref, l_ref, acc_ref, score_list, value_list):
        run_max = m_ref[...]
        new_max = run_max
        for scores in score_list:
            new_max = jnp.maximum(new_max, jnp.max(scores, axis=1, keepdims=True))
        fade = jnp.exp(run_max - new_max)
        total = l_ref[...] * fade
        acc = acc_ref[...] * fade
        for scores, values in zip(score_list, value_list):
            weights = jnp.exp(scores - new_max)
            total = total + jnp.sum(weights, axis=1, keepdims=True)
            acc = acc + jnp.dot(weights.astype(jnp.bfloat16), values, preferred_element_type=jnp.float32)
        l_ref[...] = total
        acc_ref[...] = acc
        m_ref[...] = new_max

    for i in range(q_ref.shape[0]):
        m_sc[...] = jnp.full(m_sc.shape, -1e30, jnp.float32)
        l_sc[...] = jnp.zeros(l_sc.shape, jnp.float32)
        acc_sc[...] = jnp.zeros(acc_sc.shape, jnp.float32)
        heads = q_ref.shape[2] // q_ref.shape[1]
        size = q_ref.shape[1]
        query = jnp.concatenate([q_ref[i, :, h * size:(h + 1) * size] for h in range(heads)], axis=0)
        want = q_want[i]
        req = q_req[i]
        pos = q_pos[i]

        def score(keys):
            return lax.dot_general(
                query, keys, (((1,), (1,)), ((), ())), preferred_element_type=jnp.float32
            ) * scale

        for p in range(prefixes):
            @pl.when(wants[i, p] > 0)
            def _():
                pm_sc[...] = jnp.full(pm_sc.shape, -1e30, jnp.float32)
                pl_sc[...] = jnp.zeros(pl_sc.shape, jnp.float32)
                pacc_sc[...] = jnp.zeros(pacc_sc.shape, jnp.float32)

                def page_step(g, carry):
                    pages = [page_order[p, g * group_pages + j] for j in range(group_pages)]
                    blocks = [p_ref[b] for b in pages]
                    update(
                        pm_sc, pl_sc, pacc_sc,
                        [score(blk[:, :size]) for blk in blocks],
                        [blk[:, size:] for blk in blocks],
                    )
                    return carry

                lax.fori_loop(0, per_prefix // group_pages, page_step, 0)
                mine = want == p
                m_sc[...] = jnp.where(mine, pm_sc[...], m_sc[...])
                l_sc[...] = jnp.where(mine, pl_sc[...], l_sc[...])
                acc_sc[...] = jnp.where(mine, pacc_sc[...], acc_sc[...])

        def step(n, carry):
            b = s_idx[i, n]
            scores = score(s_ref[0, b])
            seen = (s_tag[b] == req) & (s_bound[b] <= pos)
            run_max = m_sc[...]
            new_max = jnp.maximum(
                run_max, jnp.max(jnp.where(seen, scores, -1e30), axis=1, keepdims=True)
            )
            weights = jnp.where(seen, jnp.exp(scores - new_max), 0.0)
            fade = jnp.exp(run_max - new_max)
            l_sc[...] = l_sc[...] * fade + jnp.sum(weights, axis=1, keepdims=True)
            acc_sc[...] = acc_sc[...] * fade + jnp.dot(
                weights.astype(jnp.bfloat16), s_ref[1, b], preferred_element_type=jnp.float32
            )
            m_sc[...] = new_max
            return carry

        lax.fori_loop(0, s_cnt[i], step, 0)
        result = (acc_sc[...] / l_sc[...]).astype(o_ref.dtype)
        for h in range(heads):
            o_ref[i, :, h * size:(h + 1) * size] = result[h * size:(h + 1) * size]


def block_attention(scale, lists, queries, query_meta, prefix_parts, suffix_parts):
    q_blocks, block_rows, q_width = queries.shape
    width = queries.shape[1]
    q_rows = q_width // width * block_rows
    smem = pl.BlockSpec(memory_space=pltpu.SMEM)
    vmem = pl.BlockSpec(memory_space=pltpu.VMEM)
    state = [
        pltpu.VMEM((q_rows, 1), jnp.float32),
        pltpu.VMEM((q_rows, 1), jnp.float32),
        pltpu.VMEM((q_rows, width), jnp.float32),
    ]
    return pl.pallas_call(
        functools.partial(attention_kernel, scale, 4),
        out_shape=jax.ShapeDtypeStruct((q_blocks, block_rows, q_width), jnp.bfloat16),
        in_specs=[smem] * 4 + [vmem] * 8,
        out_specs=vmem,
        scratch_shapes=state + state,
        compiler_params=pltpu.CompilerParams(vmem_limit_bytes=48 * 1024 * 1024),
    )(*lists, queries, *query_meta, *prefix_parts, *suffix_parts)


def visible_list(visible):
    count = visible.shape[1]
    ids = jnp.arange(count, dtype=jnp.int32)
    rank = jnp.sum((visible[:, :, None] & (ids[:, None] < ids[None, :])[None]).astype(jnp.int32), axis=1)
    pick = visible[:, None, :] & (rank[:, None, :] == ids[None, :, None])
    order = jnp.sum(jnp.where(pick, ids[None, None, :], 0), axis=2).astype(jnp.int32)
    return order, jnp.sum(visible.astype(jnp.int32), axis=1)


def body(
    seq_n,
    tp_n,
    hidden,
    norm_gain,
    w_query,
    w_key,
    w_value,
    prefix_keys,
    prefix_values,
    page_prefix,
    request_prefix,
    suffix_lengths,
    row_order,
):
    gathered_prefix = lax.all_gather(
        jnp.concatenate([prefix_keys, prefix_values], axis=1), "seq", axis=0, tiled=True
    )
    gathered = tp_gather(hidden, tp_n, 2)
    local_rows = gathered.shape[0]
    request_all, position_all, wanted_all = locate(row_order, suffix_lengths, request_prefix)
    offset = lax.axis_index("seq") * local_rows
    request = lax.dynamic_slice_in_dim(request_all, offset, local_rows)
    position = lax.dynamic_slice_in_dim(position_all, offset, local_rows)
    wanted = lax.dynamic_slice_in_dim(wanted_all, offset, local_rows)
    prefix_len = page_prefix.shape[0] * PAGE // PREFIXES
    rope_at = prefix_len + position
    q_heads = w_query.shape[1] // HEAD
    kv_heads = w_key.shape[1] // HEAD
    group_size = q_heads // kv_heads
    half_dim = HEAD // 2
    frequency = ROPE_BASE ** (-(jnp.arange(half_dim, dtype=jnp.float32) * 2.0 / HEAD))
    angles = rope_at.astype(jnp.float32)[:, None] * frequency[None, :]
    cosine = jnp.cos(angles)
    sine_part = jnp.sin(angles)
    cos_full = jnp.concatenate([cosine, cosine], axis=1)
    sin_signed = jnp.concatenate([-sine_part, sine_part], axis=1)
    stacked_q, new_keys, new_values, stacked_kv = project(
        gathered, norm_gain, w_query, w_key, w_value, cos_full, sin_signed, PAGE
    )
    score_scale = 1.0 / math.sqrt(HEAD)
    block = PAGE
    q_blocks = local_rows // block
    pages = page_prefix.shape[0]
    runs = row_order.shape[0] // block

    def per_query(values):
        spread = jnp.broadcast_to(values.reshape(q_blocks, 1, block), (q_blocks, group_size, block))
        return spread.reshape(q_blocks, group_size * block, 1).astype(jnp.int32)

    query_meta = (per_query(wanted), per_query(request + PREFIXES), per_query(position))
    want_blocks = wanted.reshape(q_blocks, block)
    block_wants = jnp.any(
        want_blocks[:, :, None] == jnp.arange(PREFIXES, dtype=jnp.int32)[None, None, :], axis=1
    )
    page_ids = jnp.arange(pages, dtype=jnp.int32)
    same = (page_prefix[:, None] == page_prefix[None, :]) & (page_ids[:, None] < page_ids[None, :])
    page_rank = jnp.sum(same.astype(jnp.int32), axis=0)
    per_prefix = pages // PREFIXES
    pick = (page_prefix[None, None, :] == jnp.arange(PREFIXES, dtype=jnp.int32)[:, None, None]) & (
        page_rank[None, None, :] == jnp.arange(per_prefix, dtype=jnp.int32)[None, :, None]
    )
    page_order = jnp.sum(jnp.where(pick, page_ids[None, None, :], 0), axis=2).astype(jnp.int32)
    local_place = lax.dynamic_slice_in_dim(row_order, offset, local_rows).reshape(q_blocks, block)
    first_seen = jnp.min(local_place - position.reshape(q_blocks, block), axis=1)
    last_seen = jnp.max(local_place, axis=1)
    run_place = row_order.reshape(runs, block)
    run_low = jnp.min(run_place, axis=1)
    run_high = jnp.max(run_place, axis=1)
    run_visible = (run_low[None, :] <= last_seen[:, None]) & (run_high[None, :] >= first_seen[:, None])
    s_idx, s_cnt = visible_list(run_visible)

    seq_n_blocks = seq_n
    prefix_parts = (gathered_prefix.reshape(pages, block, 2 * HEAD),)
    gathered_suffix = seq_gather(stacked_kv, seq_n_blocks, 1)
    suffix_parts = (
        gathered_suffix.reshape(2, runs, block, HEAD),
        (request_all + PREFIXES).reshape(runs, 1, block).astype(jnp.int32),
        position_all.reshape(runs, 1, block).astype(jnp.int32),
    )
    out = block_attention(
        score_scale, (block_wants.astype(jnp.int32), page_order, s_idx, s_cnt), stacked_q, query_meta, prefix_parts, suffix_parts
    )
    attended = out.reshape(local_rows, group_size * HEAD)
    return (attended, new_keys, new_values)


def solution(mesh):
    return jax.shard_map(
        functools.partial(body, mesh.shape["seq"], mesh.shape["tp"]),
        mesh=mesh,
        in_specs=(
            P("seq", "tp"),
            P(),
            P(None, "tp"),
            P(None, "tp"),
            P(None, "tp"),
            P("seq", "tp"),
            P("seq", "tp"),
            P(),
            P(),
            P(),
            P(),
        ),
        out_specs=(P("seq", "tp"), P("seq", "tp"), P("seq", "tp")),
        check_vma=False,
    )
```

```python
import functools
import math

import jax
import jax.numpy as jnp
from jax import lax
from jax.sharding import PartitionSpec as P
from jax.experimental import pallas as pl
from jax.experimental.pallas import tpu as pltpu

HEAD = 128
PAGE = 128
PREFIXES = 4


ROPE_BASE = 5000000.0


def rotate(tensor_in, positions):
    head_dim = tensor_in.shape[-1]
    half_dim = head_dim // 2
    frequency = ROPE_BASE ** (-(jnp.arange(half_dim, dtype=jnp.float32) * 2.0 / head_dim))
    angles = positions.astype(jnp.float32)[:, None] * frequency[None, :]
    cosine = jnp.cos(angles)[:, None, :]
    sine_part = jnp.sin(angles)[:, None, :]
    first_half = tensor_in[..., :half_dim]
    second_half = tensor_in[..., half_dim:]
    return jnp.concatenate(
        [
            first_half * cosine - second_half * sine_part,
            second_half * cosine + first_half * sine_part,
        ],
        axis=-1,
    )


def locate(row_order, suffix_lengths, request_prefix):
    end_rows = jnp.cumsum(suffix_lengths)
    starts = end_rows - suffix_lengths
    numbers = jnp.arange(suffix_lengths.shape[0], dtype=jnp.int32)
    request = jnp.sum((row_order[:, None] >= end_rows[None, :]).astype(jnp.int32), axis=1)
    chosen = request[:, None] == numbers[None, :]
    position = row_order - jnp.sum(jnp.where(chosen, starts[None, :], 0), axis=1)
    wanted = jnp.sum(jnp.where(chosen, request_prefix[None, :], 0), axis=1)
    return (request, position, wanted)


def seq_gather_kernel(
    zs, xs, x_ref, o_ref, z_send, z_recv, r_send, r_recv, f_send, f_recv, c_send, c_recv, local_sem
):
    me = lax.axis_index("seq")
    core = me % 2
    chip = me // 2
    za = chip // xs
    xb = chip % xs
    right = lax.rem(xb + 1, xs)
    left = lax.rem(xb + xs - 1, xs)
    parts = x_ref.shape[0]
    mesh_id = pl.DeviceIdType.MESH

    def seq_of(z, x, c):
        return (z * xs + x) * 2 + c

    def signal(sem, target):
        pl.semaphore_signal(sem, inc=1, device_id={"seq": target}, device_id_type=mesh_id)

    barrier = pltpu.get_barrier_semaphore()

    def greet(k, carry):
        signal(barrier, seq_of(lax.rem(za + k, zs), xb, core))
        return carry

    lax.fori_loop(1, zs, greet, 0)
    signal(barrier, seq_of(za, right, core))
    signal(barrier, seq_of(za, left, core))
    signal(barrier, seq_of(za, xb, 1 - core))
    pl.semaphore_wait(barrier, zs + 2)

    local = pltpu.make_async_copy(x_ref, o_ref.at[:, za, xb, core], local_sem)
    local.start()

    def z_copy(a, peer_z, slot_z):
        return pltpu.make_async_remote_copy(
            src_ref=x_ref.at[a],
            dst_ref=o_ref.at[a, slot_z, xb, core],
            send_sem=z_send.at[a, peer_z],
            recv_sem=z_recv.at[a, slot_z],
            device_id={"seq": seq_of(peer_z, xb, core)},
            device_id_type=mesh_id,
        )

    def ring_slot(a, slot, side, group, target_x, sem_side, src=None):
        return pltpu.make_async_remote_copy(
            src_ref=o_ref.at[a, slot, group, core] if src is None else src,
            dst_ref=o_ref.at[a, slot, group, core],
            send_sem=r_send.at[a, side, slot],
            recv_sem=r_recv.at[a, sem_side, slot],
            device_id={"seq": seq_of(za, target_x, core)},
            device_id_type=mesh_id,
        )

    def z_start(k, carry):
        peer_z = lax.rem(za + k, zs)
        for a in range(parts):
            z_copy(a, peer_z, za).start()
        return carry

    lax.fori_loop(1, zs, z_start, 0)
    for a in range(parts):
        ring_slot(a, za, 0, xb, right, 0, x_ref.at[a]).start()
        ring_slot(a, za, 1, xb, left, 1, x_ref.at[a]).start()

    def z_finish(k, carry):
        peer_z = lax.rem(za + k, zs)
        for a in range(parts):
            copy = z_copy(a, peer_z, peer_z)
            copy.wait_recv()
            ring_slot(a, peer_z, 0, xb, right, 0).start()
            ring_slot(a, peer_z, 1, xb, left, 1).start()
            copy.wait_send()
        return carry

    lax.fori_loop(1, zs, z_finish, 0)
    local.wait()

    def hand(a, group, slot):
        return pltpu.make_async_remote_copy(
            src_ref=o_ref.at[a, :, group, slot],
            dst_ref=o_ref.at[a, :, group, slot],
            send_sem=c_send.at[a, group],
            recv_sem=c_recv.at[a, group],
            device_id={"seq": seq_of(za, xb, 1 - core)},
            device_id_type=mesh_id,
        )

    across = []
    for a in range(parts):
        across.append(hand(a, xb, core))
        across[-1].start()

    for a in range(parts):
        for slot in range(zs):
            ring_slot(a, slot, 0, left, right, 0).wait_recv()
            ring_slot(a, slot, 1, right, left, 1).wait_recv()
    for a in range(parts):
        for group in (left, right):
            across.append(hand(a, group, core))
            across[-1].start()
    for a in range(parts):
        for slot in range(zs):
            ring_slot(a, slot, 0, xb, right, 0).wait_send()
            ring_slot(a, slot, 1, xb, left, 1).wait_send()

    far = lax.rem(xb + 2, xs)
    relay_k = pltpu.make_async_remote_copy(
        src_ref=o_ref.at[0, :, left, core],
        dst_ref=o_ref.at[0, :, left, core],
        send_sem=f_send.at[0],
        recv_sem=f_recv.at[0],
        device_id={"seq": seq_of(za, right, core)},
        device_id_type=mesh_id,
    )
    relay_v = pltpu.make_async_remote_copy(
        src_ref=o_ref.at[1, :, right, core],
        dst_ref=o_ref.at[1, :, right, core],
        send_sem=f_send.at[1],
        recv_sem=f_recv.at[1],
        device_id={"seq": seq_of(za, left, core)},
        device_id_type=mesh_id,
    )
    relay_k.start()
    relay_v.start()
    pltpu.make_async_remote_copy(
        src_ref=o_ref.at[0, :, far, core],
        dst_ref=o_ref.at[0, :, far, core],
        send_sem=f_send.at[0],
        recv_sem=f_recv.at[0],
        device_id={"seq": seq_of(za, right, core)},
        device_id_type=mesh_id,
    ).wait_recv()
    pltpu.make_async_remote_copy(
        src_ref=o_ref.at[1, :, far, core],
        dst_ref=o_ref.at[1, :, far, core],
        send_sem=f_send.at[1],
        recv_sem=f_recv.at[1],
        device_id={"seq": seq_of(za, left, core)},
        device_id_type=mesh_id,
    ).wait_recv()
    relay_k.wait_send()
    relay_v.wait_send()
    for a in range(parts):
        across.append(hand(a, far, core))
        across[-1].start()

    for copy in across:
        copy.wait_send()
    for a in range(parts):
        for g in range(xs):
            hand(a, g, 1 - core).wait_recv()


def seq_gather(stacked, n, cid):
    parts, rows, cols = stacked.shape
    chips = n // 2
    xs = 4
    zs = chips // xs
    return pl.pallas_call(
        functools.partial(seq_gather_kernel, zs, xs),
        out_shape=jax.ShapeDtypeStruct((parts, zs, xs, 2, rows, cols), stacked.dtype),
        in_specs=[pl.BlockSpec(memory_space=pl.ANY)],
        out_specs=pl.BlockSpec(memory_space=pl.ANY),
        scratch_shapes=[
            pltpu.SemaphoreType.DMA((parts, zs)),
            pltpu.SemaphoreType.DMA((parts, zs)),
            pltpu.SemaphoreType.DMA((parts, 2, zs)),
            pltpu.SemaphoreType.DMA((parts, 2, zs)),
            pltpu.SemaphoreType.DMA((parts,)),
            pltpu.SemaphoreType.DMA((parts,)),
            pltpu.SemaphoreType.DMA((parts, xs)),
            pltpu.SemaphoreType.DMA((parts, xs)),
            pltpu.SemaphoreType.DMA,
        ],
        compiler_params=pltpu.CompilerParams(collective_id=cid, has_side_effects=True),
    )(stacked)


def tp_gather_kernel(ys, x_ref, o_ref, p_send, p_recv, r_send, r_recv, f_send, f_recv, local_sem):
    me = lax.axis_index("tp")
    yy = me // 2
    zh = me % 2
    right = lax.rem(yy + 1, ys)
    left = lax.rem(yy + ys - 1, ys)
    far = lax.rem(yy + 2, ys)
    width = x_ref.shape[1]
    mesh_id = pl.DeviceIdType.MESH

    def cols(y, h):
        return pl.ds(pl.multiple_of((y * 2 + h) * width, 128), width)

    def pair(y):
        return pl.ds(pl.multiple_of(y * 2 * width, 128), 2 * width)

    def signal(target):
        pl.semaphore_signal(barrier, inc=1, device_id={"tp": target}, device_id_type=mesh_id)

    barrier = pltpu.get_barrier_semaphore()
    signal(yy * 2 + 1 - zh)
    signal(right * 2 + zh)
    signal(left * 2 + zh)
    pl.semaphore_wait(barrier, 3)

    local = pltpu.make_async_copy(x_ref, o_ref.at[:, cols(yy, zh)], local_sem)
    local.start()
    to_partner = pltpu.make_async_remote_copy(
        src_ref=x_ref,
        dst_ref=o_ref.at[:, cols(yy, zh)],
        send_sem=p_send,
        recv_sem=p_recv,
        device_id={"tp": yy * 2 + 1 - zh},
        device_id_type=mesh_id,
    )
    to_partner.start()

    def ring(src, h, group, target, side):
        return pltpu.make_async_remote_copy(
            src_ref=src,
            dst_ref=o_ref.at[:, cols(group, h)],
            send_sem=r_send.at[side, h],
            recv_sem=r_recv.at[side, h],
            device_id={"tp": target * 2 + zh},
            device_id_type=mesh_id,
        )

    outgoing = [ring(x_ref, zh, yy, right, 0), ring(x_ref, zh, yy, left, 1)]
    for copy in outgoing:
        copy.start()
    pltpu.make_async_remote_copy(
        src_ref=x_ref,
        dst_ref=o_ref.at[:, cols(yy, 1 - zh)],
        send_sem=p_send,
        recv_sem=p_recv,
        device_id={"tp": yy * 2 + 1 - zh},
        device_id_type=mesh_id,
    ).wait_recv()
    partner_src = o_ref.at[:, cols(yy, 1 - zh)]
    later = [ring(partner_src, 1 - zh, yy, right, 0), ring(partner_src, 1 - zh, yy, left, 1)]
    for copy in later:
        copy.start()
    local.wait()
    to_partner.wait_send()
    for h in range(2):
        ring(x_ref, h, left, right, 0).wait_recv()
        ring(x_ref, h, right, left, 1).wait_recv()
    for copy in outgoing + later:
        copy.wait_send()
    pieces = f_send.shape[1]
    span = x_ref.shape[0] // pieces

    def relay(group, h, target, side, c):
        rows = pl.ds(c * span, span)
        return pltpu.make_async_remote_copy(
            src_ref=o_ref.at[rows, cols(group, h)],
            dst_ref=o_ref.at[rows, cols(group, h)],
            send_sem=f_send.at[side, c],
            recv_sem=f_recv.at[side, c],
            device_id={"tp": target * 2 + zh},
            device_id_type=mesh_id,
        )

    relays = []
    for c in range(pieces):
        relays += [relay(left, 0, right, 0, c), relay(right, 1, left, 1, c)]
    for copy in relays:
        copy.start()
    for c in range(pieces):
        relay(far, 0, right, 0, c).wait_recv()
        relay(far, 1, left, 1, c).wait_recv()
    for copy in relays:
        copy.wait_send()


def tp_gather(block, n, cid):
    rows, width = block.shape
    return pl.pallas_call(
        functools.partial(tp_gather_kernel, n // 2),
        out_shape=jax.ShapeDtypeStruct((rows, width * n), block.dtype),
        in_specs=[pl.BlockSpec(memory_space=pl.ANY)],
        out_specs=pl.BlockSpec(memory_space=pl.ANY),
        scratch_shapes=[
            pltpu.SemaphoreType.DMA,
            pltpu.SemaphoreType.DMA,
            pltpu.SemaphoreType.DMA((2, 2)),
            pltpu.SemaphoreType.DMA((2, 2)),
            pltpu.SemaphoreType.DMA((2, 4)),
            pltpu.SemaphoreType.DMA((2, 4)),
            pltpu.SemaphoreType.DMA,
        ],
        compiler_params=pltpu.CompilerParams(collective_id=cid, has_side_effects=True),
    )(block)


def project_kernel(x_ref, g_ref, wq_ref, wk_ref, wv_ref, cos_ref, sin_ref, q_ref, k_ref, v_ref, kv_ref):
    x = x_ref[...].astype(jnp.float32)
    mean_sq = jnp.mean(x * x, axis=1, keepdims=True)
    normed = (x * lax.rsqrt(mean_sq + 1e-05) * g_ref[...].astype(jnp.float32)).astype(jnp.bfloat16)
    cosine = cos_ref[...]
    sine = sin_ref[...]

    def rotated(values):
        half = values.shape[1] // 2
        return values * cosine + pltpu.roll(values, half, 1) * sine

    queries = jnp.dot(normed, wq_ref[...], preferred_element_type=jnp.float32)
    for h in range(queries.shape[1] // HEAD):
        q_ref[0, :, h * HEAD:(h + 1) * HEAD] = rotated(queries[:, h * HEAD:(h + 1) * HEAD]).astype(q_ref.dtype)
    keys = jnp.dot(normed, wk_ref[...], preferred_element_type=jnp.float32)
    for h in range(keys.shape[1] // HEAD):
        part = rotated(keys[:, h * HEAD:(h + 1) * HEAD]).astype(k_ref.dtype)
        k_ref[:, h * HEAD:(h + 1) * HEAD] = part
        kv_ref[0, :, h * HEAD:(h + 1) * HEAD] = part
    values = jnp.dot(normed, wv_ref[...], preferred_element_type=jnp.float32).astype(v_ref.dtype)
    v_ref[...] = values
    kv_ref[1] = values


def project(gathered, norm_gain, w_query, w_key, w_value, cosine, sine, block):
    rows, width = gathered.shape
    steps = rows // block
    q_width = w_query.shape[1]
    kv_width = w_key.shape[1]
    whole = lambda i: (0, 0)
    return pl.pallas_call(
        project_kernel,
        grid=(steps,),
        out_shape=(
            jax.ShapeDtypeStruct((steps, block, q_width), jnp.bfloat16),
            jax.ShapeDtypeStruct((rows, kv_width), jnp.bfloat16),
            jax.ShapeDtypeStruct((rows, kv_width), jnp.bfloat16),
            jax.ShapeDtypeStruct((2, rows, kv_width), jnp.bfloat16),
        ),
        in_specs=[
            pl.BlockSpec((block, width), lambda i: (i, 0)),
            pl.BlockSpec((1, width), whole),
            pl.BlockSpec((width, q_width), whole),
            pl.BlockSpec((width, kv_width), whole),
            pl.BlockSpec((width, kv_width), whole),
            pl.BlockSpec((block, HEAD), lambda i: (i, 0)),
            pl.BlockSpec((block, HEAD), lambda i: (i, 0)),
        ],
        out_specs=(
            pl.BlockSpec((1, block, q_width), lambda i: (i, 0, 0)),
            pl.BlockSpec((block, kv_width), lambda i: (i, 0)),
            pl.BlockSpec((block, kv_width), lambda i: (i, 0)),
            pl.BlockSpec((2, block, kv_width), lambda i: (0, i, 0)),
        ),
        compiler_params=pltpu.CompilerParams(vmem_limit_bytes=60 * 1024 * 1024),
    )(gathered, norm_gain.reshape(1, width), w_query, w_key, w_value, cosine, sine)


def attention_kernel(
    scale, group_pages,
    wants, page_order, s_idx, s_cnt,
    q_ref, q_want, q_req, q_pos,
    p_ref,
    s_ref, s_tag, s_bound,
    o_ref, m_sc, l_sc, acc_sc, pm_sc, pl_sc, pacc_sc,
):
    prefixes, per_prefix = page_order.shape

    def update(m_ref, l_ref, acc_ref, score_list, value_list):
        run_max = m_ref[...]
        new_max = run_max
        for scores in score_list:
            new_max = jnp.maximum(new_max, jnp.max(scores, axis=1, keepdims=True))
        fade = jnp.exp(run_max - new_max)
        total = l_ref[...] * fade
        acc = acc_ref[...] * fade
        for scores, values in zip(score_list, value_list):
            weights = jnp.exp(scores - new_max)
            total = total + jnp.sum(weights, axis=1, keepdims=True)
            acc = acc + jnp.dot(weights.astype(jnp.bfloat16), values, preferred_element_type=jnp.float32)
        l_ref[...] = total
        acc_ref[...] = acc
        m_ref[...] = new_max

    for i in range(q_ref.shape[0]):
        m_sc[...] = jnp.full(m_sc.shape, -1e30, jnp.float32)
        l_sc[...] = jnp.zeros(l_sc.shape, jnp.float32)
        acc_sc[...] = jnp.zeros(acc_sc.shape, jnp.float32)
        heads = q_ref.shape[2] // q_ref.shape[1]
        size = q_ref.shape[1]
        query = jnp.concatenate([q_ref[i, :, h * size:(h + 1) * size] for h in range(heads)], axis=0)
        want = q_want[i]
        req = q_req[i]
        pos = q_pos[i]

        def score(keys):
            return lax.dot_general(
                query, keys, (((1,), (1,)), ((), ())), preferred_element_type=jnp.float32
            ) * scale

        for p in range(prefixes):
            @pl.when(wants[i, p] > 0)
            def _():
                pm_sc[...] = jnp.full(pm_sc.shape, -1e30, jnp.float32)
                pl_sc[...] = jnp.zeros(pl_sc.shape, jnp.float32)
                pacc_sc[...] = jnp.zeros(pacc_sc.shape, jnp.float32)

                def page_step(g, carry):
                    pages = [page_order[p, g * group_pages + j] for j in range(group_pages)]
                    blocks = [p_ref[b] for b in pages]
                    update(
                        pm_sc, pl_sc, pacc_sc,
                        [score(blk[:, :size]) for blk in blocks],
                        [blk[:, size:] for blk in blocks],
                    )
                    return carry

                lax.fori_loop(0, per_prefix // group_pages, page_step, 0)
                mine = want == p
                m_sc[...] = jnp.where(mine, pm_sc[...], m_sc[...])
                l_sc[...] = jnp.where(mine, pl_sc[...], l_sc[...])
                acc_sc[...] = jnp.where(mine, pacc_sc[...], acc_sc[...])

        def step(n, carry):
            b = s_idx[i, n]
            scores = score(s_ref[0, b])
            seen = (s_tag[b] == req) & (s_bound[b] <= pos)
            run_max = m_sc[...]
            new_max = jnp.maximum(
                run_max, jnp.max(jnp.where(seen, scores, -1e30), axis=1, keepdims=True)
            )
            weights = jnp.where(seen, jnp.exp(scores - new_max), 0.0)
            fade = jnp.exp(run_max - new_max)
            l_sc[...] = l_sc[...] * fade + jnp.sum(weights, axis=1, keepdims=True)
            acc_sc[...] = acc_sc[...] * fade + jnp.dot(
                weights.astype(jnp.bfloat16), s_ref[1, b], preferred_element_type=jnp.float32
            )
            m_sc[...] = new_max
            return carry

        lax.fori_loop(0, s_cnt[i], step, 0)
        result = (acc_sc[...] / l_sc[...]).astype(o_ref.dtype)
        for h in range(heads):
            o_ref[i, :, h * size:(h + 1) * size] = result[h * size:(h + 1) * size]


def block_attention(scale, lists, queries, query_meta, prefix_parts, suffix_parts):
    q_blocks, block_rows, q_width = queries.shape
    width = queries.shape[1]
    q_rows = q_width // width * block_rows
    smem = pl.BlockSpec(memory_space=pltpu.SMEM)
    vmem = pl.BlockSpec(memory_space=pltpu.VMEM)
    state = [
        pltpu.VMEM((q_rows, 1), jnp.float32),
        pltpu.VMEM((q_rows, 1), jnp.float32),
        pltpu.VMEM((q_rows, width), jnp.float32),
    ]
    return pl.pallas_call(
        functools.partial(attention_kernel, scale, 4),
        out_shape=jax.ShapeDtypeStruct((q_blocks, block_rows, q_width), jnp.bfloat16),
        in_specs=[smem] * 4 + [vmem] * 8,
        out_specs=vmem,
        scratch_shapes=state + state,
        compiler_params=pltpu.CompilerParams(vmem_limit_bytes=48 * 1024 * 1024),
    )(*lists, queries, *query_meta, *prefix_parts, *suffix_parts)


def visible_list(visible):
    count = visible.shape[1]
    ids = jnp.arange(count, dtype=jnp.int32)
    rank = jnp.sum((visible[:, :, None] & (ids[:, None] < ids[None, :])[None]).astype(jnp.int32), axis=1)
    pick = visible[:, None, :] & (rank[:, None, :] == ids[None, :, None])
    order = jnp.sum(jnp.where(pick, ids[None, None, :], 0), axis=2).astype(jnp.int32)
    return order, jnp.sum(visible.astype(jnp.int32), axis=1)


def body(
    seq_n,
    tp_n,
    hidden,
    norm_gain,
    w_query,
    w_key,
    w_value,
    prefix_keys,
    prefix_values,
    page_prefix,
    request_prefix,
    suffix_lengths,
    row_order,
):
    gathered_prefix = lax.all_gather(
        jnp.concatenate([prefix_keys, prefix_values], axis=1), "seq", axis=0, tiled=True
    )
    gathered = tp_gather(hidden, tp_n, 2)
    local_rows = gathered.shape[0]
    request_all, position_all, wanted_all = locate(row_order, suffix_lengths, request_prefix)
    offset = lax.axis_index("seq") * local_rows
    request = lax.dynamic_slice_in_dim(request_all, offset, local_rows)
    position = lax.dynamic_slice_in_dim(position_all, offset, local_rows)
    wanted = lax.dynamic_slice_in_dim(wanted_all, offset, local_rows)
    prefix_len = page_prefix.shape[0] * PAGE // PREFIXES
    rope_at = prefix_len + position
    q_heads = w_query.shape[1] // HEAD
    kv_heads = w_key.shape[1] // HEAD
    group_size = q_heads // kv_heads
    half_dim = HEAD // 2
    frequency = ROPE_BASE ** (-(jnp.arange(half_dim, dtype=jnp.float32) * 2.0 / HEAD))
    angles = rope_at.astype(jnp.float32)[:, None] * frequency[None, :]
    cosine = jnp.cos(angles)
    sine_part = jnp.sin(angles)
    cos_full = jnp.concatenate([cosine, cosine], axis=1)
    sin_signed = jnp.concatenate([-sine_part, sine_part], axis=1)
    stacked_q, new_keys, new_values, stacked_kv = project(
        gathered, norm_gain, w_query, w_key, w_value, cos_full, sin_signed, PAGE
    )
    score_scale = 1.0 / math.sqrt(HEAD)
    block = PAGE
    q_blocks = local_rows // block
    pages = page_prefix.shape[0]
    runs = row_order.shape[0] // block

    def per_query(values):
        spread = jnp.broadcast_to(values.reshape(q_blocks, 1, block), (q_blocks, group_size, block))
        return spread.reshape(q_blocks, group_size * block, 1).astype(jnp.int32)

    query_meta = (per_query(wanted), per_query(request + PREFIXES), per_query(position))
    want_blocks = wanted.reshape(q_blocks, block)
    block_wants = jnp.any(
        want_blocks[:, :, None] == jnp.arange(PREFIXES, dtype=jnp.int32)[None, None, :], axis=1
    )
    page_ids = jnp.arange(pages, dtype=jnp.int32)
    same = (page_prefix[:, None] == page_prefix[None, :]) & (page_ids[:, None] < page_ids[None, :])
    page_rank = jnp.sum(same.astype(jnp.int32), axis=0)
    per_prefix = pages // PREFIXES
    pick = (page_prefix[None, None, :] == jnp.arange(PREFIXES, dtype=jnp.int32)[:, None, None]) & (
        page_rank[None, None, :] == jnp.arange(per_prefix, dtype=jnp.int32)[None, :, None]
    )
    page_order = jnp.sum(jnp.where(pick, page_ids[None, None, :], 0), axis=2).astype(jnp.int32)
    local_place = lax.dynamic_slice_in_dim(row_order, offset, local_rows).reshape(q_blocks, block)
    first_seen = jnp.min(local_place - position.reshape(q_blocks, block), axis=1)
    last_seen = jnp.max(local_place, axis=1)
    run_place = row_order.reshape(runs, block)
    run_low = jnp.min(run_place, axis=1)
    run_high = jnp.max(run_place, axis=1)
    run_visible = (run_low[None, :] <= last_seen[:, None]) & (run_high[None, :] >= first_seen[:, None])
    s_idx, s_cnt = visible_list(run_visible)

    seq_n_blocks = seq_n
    prefix_parts = (gathered_prefix.reshape(pages, block, 2 * HEAD),)
    gathered_suffix = seq_gather(stacked_kv, seq_n_blocks, 1)
    suffix_parts = (
        gathered_suffix.reshape(2, runs, block, HEAD),
        (request_all + PREFIXES).reshape(runs, 1, block).astype(jnp.int32),
        position_all.reshape(runs, 1, block).astype(jnp.int32),
    )
    out = block_attention(
        score_scale, (block_wants.astype(jnp.int32), page_order, s_idx, s_cnt), stacked_q, query_meta, prefix_parts, suffix_parts
    )
    attended = out.reshape(local_rows, group_size * HEAD)
    return (attended, new_keys, new_values)


def solution(mesh):
    return jax.shard_map(
        functools.partial(body, mesh.shape["seq"], mesh.shape["tp"]),
        mesh=mesh,
        in_specs=(
            P("seq", "tp"),
            P(),
            P(None, "tp"),
            P(None, "tp"),
            P(None, "tp"),
            P("seq", "tp"),
            P("seq", "tp"),
            P(),
            P(),
            P(),
            P(),
        ),
        out_specs=(P("seq", "tp"), P("seq", "tp"), P("seq", "tp")),
        check_vma=False,
    )
```

```python
import functools
import math

import jax
import jax.numpy as jnp
from jax import lax
from jax.sharding import PartitionSpec as P
from jax.experimental import pallas as pl
from jax.experimental.pallas import tpu as pltpu

HEAD = 128
PAGE = 128
PREFIXES = 4


ROPE_BASE = 5000000.0


def rotate(tensor_in, positions):
    head_dim = tensor_in.shape[-1]
    half_dim = head_dim // 2
    frequency = ROPE_BASE ** (-(jnp.arange(half_dim, dtype=jnp.float32) * 2.0 / head_dim))
    angles = positions.astype(jnp.float32)[:, None] * frequency[None, :]
    cosine = jnp.cos(angles)[:, None, :]
    sine_part = jnp.sin(angles)[:, None, :]
    first_half = tensor_in[..., :half_dim]
    second_half = tensor_in[..., half_dim:]
    return jnp.concatenate(
        [
            first_half * cosine - second_half * sine_part,
            second_half * cosine + first_half * sine_part,
        ],
        axis=-1,
    )


def locate(row_order, suffix_lengths, request_prefix):
    end_rows = jnp.cumsum(suffix_lengths)
    starts = end_rows - suffix_lengths
    numbers = jnp.arange(suffix_lengths.shape[0], dtype=jnp.int32)
    request = jnp.sum((row_order[:, None] >= end_rows[None, :]).astype(jnp.int32), axis=1)
    chosen = request[:, None] == numbers[None, :]
    position = row_order - jnp.sum(jnp.where(chosen, starts[None, :], 0), axis=1)
    wanted = jnp.sum(jnp.where(chosen, request_prefix[None, :], 0), axis=1)
    return (request, position, wanted)


def seq_gather_kernel(
    zs, xs, x_ref, o_ref, z_send, z_recv, r_send, r_recv, f_send, f_recv, c_send, c_recv, local_sem
):
    me = lax.axis_index("seq")
    core = me % 2
    chip = me // 2
    za = chip // xs
    xb = chip % xs
    right = lax.rem(xb + 1, xs)
    left = lax.rem(xb + xs - 1, xs)
    parts = x_ref.shape[0]
    mesh_id = pl.DeviceIdType.MESH

    def seq_of(z, x, c):
        return (z * xs + x) * 2 + c

    def signal(sem, target):
        pl.semaphore_signal(sem, inc=1, device_id={"seq": target}, device_id_type=mesh_id)

    barrier = pltpu.get_barrier_semaphore()

    def greet(k, carry):
        signal(barrier, seq_of(lax.rem(za + k, zs), xb, core))
        return carry

    lax.fori_loop(1, zs, greet, 0)
    signal(barrier, seq_of(za, right, core))
    signal(barrier, seq_of(za, left, core))
    signal(barrier, seq_of(za, xb, 1 - core))
    pl.semaphore_wait(barrier, zs + 2)

    local = pltpu.make_async_copy(x_ref, o_ref.at[:, za, xb, core], local_sem)
    local.start()

    def z_copy(a, peer_z, slot_z):
        return pltpu.make_async_remote_copy(
            src_ref=x_ref.at[a],
            dst_ref=o_ref.at[a, slot_z, xb, core],
            send_sem=z_send.at[a, peer_z],
            recv_sem=z_recv.at[a, slot_z],
            device_id={"seq": seq_of(peer_z, xb, core)},
            device_id_type=mesh_id,
        )

    def ring_slot(a, slot, side, group, target_x, sem_side, src=None):
        return pltpu.make_async_remote_copy(
            src_ref=o_ref.at[a, slot, group, core] if src is None else src,
            dst_ref=o_ref.at[a, slot, group, core],
            send_sem=r_send.at[a, side, slot],
            recv_sem=r_recv.at[a, sem_side, slot],
            device_id={"seq": seq_of(za, target_x, core)},
            device_id_type=mesh_id,
        )

    def z_start(k, carry):
        peer_z = lax.rem(za + k, zs)
        for a in range(parts):
            z_copy(a, peer_z, za).start()
        return carry

    lax.fori_loop(1, zs, z_start, 0)
    for a in range(parts):
        ring_slot(a, za, 0, xb, right, 0, x_ref.at[a]).start()
        ring_slot(a, za, 1, xb, left, 1, x_ref.at[a]).start()

    def z_finish(k, carry):
        peer_z = lax.rem(za + k, zs)
        for a in range(parts):
            copy = z_copy(a, peer_z, peer_z)
            copy.wait_recv()
            ring_slot(a, peer_z, 0, xb, right, 0).start()
            ring_slot(a, peer_z, 1, xb, left, 1).start()
            copy.wait_send()
        return carry

    lax.fori_loop(1, zs, z_finish, 0)
    local.wait()

    def hand(a, group, slot):
        return pltpu.make_async_remote_copy(
            src_ref=o_ref.at[a, :, group, slot],
            dst_ref=o_ref.at[a, :, group, slot],
            send_sem=c_send.at[a, group],
            recv_sem=c_recv.at[a, group],
            device_id={"seq": seq_of(za, xb, 1 - core)},
            device_id_type=mesh_id,
        )

    across = []
    for a in range(parts):
        across.append(hand(a, xb, core))
        across[-1].start()

    far = lax.rem(xb + 2, xs)

    def relay(a, slot, group, target_x, src_group):
        return pltpu.make_async_remote_copy(
            src_ref=o_ref.at[a, slot, src_group, core],
            dst_ref=o_ref.at[a, slot, group, core],
            send_sem=f_send.at[a, slot],
            recv_sem=f_recv.at[a, slot],
            device_id={"seq": seq_of(za, target_x, core)},
            device_id_type=mesh_id,
        )

    for slot in range(zs):
        ring_slot(0, slot, 0, left, right, 0).wait_recv()
        relay(0, slot, left, right, left).start()
        ring_slot(1, slot, 1, right, left, 1).wait_recv()
        relay(1, slot, right, left, right).start()
    for slot in range(zs):
        ring_slot(1, slot, 0, left, right, 0).wait_recv()
        ring_slot(0, slot, 1, right, left, 1).wait_recv()
    for a in range(parts):
        for group in (left, right):
            across.append(hand(a, group, core))
            across[-1].start()
    for a in range(parts):
        for slot in range(zs):
            ring_slot(a, slot, 0, xb, right, 0).wait_send()
            ring_slot(a, slot, 1, xb, left, 1).wait_send()
    for slot in range(zs):
        relay(0, slot, far, right, left).wait_recv()
        relay(1, slot, far, left, right).wait_recv()
    for slot in range(zs):
        relay(0, slot, left, right, left).wait_send()
        relay(1, slot, right, left, right).wait_send()
    for a in range(parts):
        across.append(hand(a, far, core))
        across[-1].start()

    for copy in across:
        copy.wait_send()
    for a in range(parts):
        for g in range(xs):
            hand(a, g, 1 - core).wait_recv()


def seq_gather(stacked, n, cid):
    parts, rows, cols = stacked.shape
    chips = n // 2
    xs = 4
    zs = chips // xs
    return pl.pallas_call(
        functools.partial(seq_gather_kernel, zs, xs),
        out_shape=jax.ShapeDtypeStruct((parts, zs, xs, 2, rows, cols), stacked.dtype),
        in_specs=[pl.BlockSpec(memory_space=pl.ANY)],
        out_specs=pl.BlockSpec(memory_space=pl.ANY),
        scratch_shapes=[
            pltpu.SemaphoreType.DMA((parts, zs)),
            pltpu.SemaphoreType.DMA((parts, zs)),
            pltpu.SemaphoreType.DMA((parts, 2, zs)),
            pltpu.SemaphoreType.DMA((parts, 2, zs)),
            pltpu.SemaphoreType.DMA((parts, zs)),
            pltpu.SemaphoreType.DMA((parts, zs)),
            pltpu.SemaphoreType.DMA((parts, xs)),
            pltpu.SemaphoreType.DMA((parts, xs)),
            pltpu.SemaphoreType.DMA,
        ],
        compiler_params=pltpu.CompilerParams(collective_id=cid, has_side_effects=True),
    )(stacked)


def tp_gather_kernel(ys, x_ref, o_ref, p_send, p_recv, r_send, r_recv, f_send, f_recv, local_sem):
    me = lax.axis_index("tp")
    yy = me // 2
    zh = me % 2
    right = lax.rem(yy + 1, ys)
    left = lax.rem(yy + ys - 1, ys)
    far = lax.rem(yy + 2, ys)
    width = x_ref.shape[1]
    mesh_id = pl.DeviceIdType.MESH

    def cols(y, h):
        return pl.ds(pl.multiple_of((y * 2 + h) * width, 128), width)

    def pair(y):
        return pl.ds(pl.multiple_of(y * 2 * width, 128), 2 * width)

    def signal(target):
        pl.semaphore_signal(barrier, inc=1, device_id={"tp": target}, device_id_type=mesh_id)

    barrier = pltpu.get_barrier_semaphore()
    signal(yy * 2 + 1 - zh)
    signal(right * 2 + zh)
    signal(left * 2 + zh)
    pl.semaphore_wait(barrier, 3)

    local = pltpu.make_async_copy(x_ref, o_ref.at[:, cols(yy, zh)], local_sem)
    local.start()
    to_partner = pltpu.make_async_remote_copy(
        src_ref=x_ref,
        dst_ref=o_ref.at[:, cols(yy, zh)],
        send_sem=p_send,
        recv_sem=p_recv,
        device_id={"tp": yy * 2 + 1 - zh},
        device_id_type=mesh_id,
    )
    to_partner.start()

    def ring(src, h, group, target, side):
        return pltpu.make_async_remote_copy(
            src_ref=src,
            dst_ref=o_ref.at[:, cols(group, h)],
            send_sem=r_send.at[side, h],
            recv_sem=r_recv.at[side, h],
            device_id={"tp": target * 2 + zh},
            device_id_type=mesh_id,
        )

    outgoing = [ring(x_ref, zh, yy, right, 0), ring(x_ref, zh, yy, left, 1)]
    for copy in outgoing:
        copy.start()
    pltpu.make_async_remote_copy(
        src_ref=x_ref,
        dst_ref=o_ref.at[:, cols(yy, 1 - zh)],
        send_sem=p_send,
        recv_sem=p_recv,
        device_id={"tp": yy * 2 + 1 - zh},
        device_id_type=mesh_id,
    ).wait_recv()
    partner_src = o_ref.at[:, cols(yy, 1 - zh)]
    later = [ring(partner_src, 1 - zh, yy, right, 0), ring(partner_src, 1 - zh, yy, left, 1)]
    for copy in later:
        copy.start()
    local.wait()
    to_partner.wait_send()
    pieces = f_send.shape[1]
    span = x_ref.shape[0] // pieces

    def relay(group, h, target, side, c):
        rows = pl.ds(c * span, span)
        return pltpu.make_async_remote_copy(
            src_ref=o_ref.at[rows, cols(group, h)],
            dst_ref=o_ref.at[rows, cols(group, h)],
            send_sem=f_send.at[side, c],
            recv_sem=f_recv.at[side, c],
            device_id={"tp": target * 2 + zh},
            device_id_type=mesh_id,
        )

    relays = []
    ring(x_ref, 0, left, right, 0).wait_recv()
    for c in range(pieces):
        relays.append(relay(left, 0, right, 0, c))
        relays[-1].start()
    ring(x_ref, 1, right, left, 1).wait_recv()
    for c in range(pieces):
        relays.append(relay(right, 1, left, 1, c))
        relays[-1].start()
    ring(x_ref, 1, left, right, 0).wait_recv()
    ring(x_ref, 0, right, left, 1).wait_recv()
    for copy in outgoing + later:
        copy.wait_send()
    for c in range(pieces):
        relay(far, 0, right, 0, c).wait_recv()
        relay(far, 1, left, 1, c).wait_recv()
    for copy in relays:
        copy.wait_send()


def tp_gather(block, n, cid):
    rows, width = block.shape
    return pl.pallas_call(
        functools.partial(tp_gather_kernel, n // 2),
        out_shape=jax.ShapeDtypeStruct((rows, width * n), block.dtype),
        in_specs=[pl.BlockSpec(memory_space=pl.ANY)],
        out_specs=pl.BlockSpec(memory_space=pl.ANY),
        scratch_shapes=[
            pltpu.SemaphoreType.DMA,
            pltpu.SemaphoreType.DMA,
            pltpu.SemaphoreType.DMA((2, 2)),
            pltpu.SemaphoreType.DMA((2, 2)),
            pltpu.SemaphoreType.DMA((2, 4)),
            pltpu.SemaphoreType.DMA((2, 4)),
            pltpu.SemaphoreType.DMA,
        ],
        compiler_params=pltpu.CompilerParams(collective_id=cid, has_side_effects=True),
    )(block)


def project_kernel(x_ref, g_ref, wq_ref, wk_ref, wv_ref, cos_ref, sin_ref, q_ref, k_ref, v_ref, kv_ref):
    x = x_ref[...].astype(jnp.float32)
    mean_sq = jnp.mean(x * x, axis=1, keepdims=True)
    normed = (x * lax.rsqrt(mean_sq + 1e-05) * g_ref[...].astype(jnp.float32)).astype(jnp.bfloat16)
    cosine = cos_ref[...]
    sine = sin_ref[...]

    def rotated(values):
        half = values.shape[1] // 2
        return values * cosine + pltpu.roll(values, half, 1) * sine

    queries = jnp.dot(normed, wq_ref[...], preferred_element_type=jnp.float32)
    for h in range(queries.shape[1] // HEAD):
        q_ref[0, :, h * HEAD:(h + 1) * HEAD] = rotated(queries[:, h * HEAD:(h + 1) * HEAD]).astype(q_ref.dtype)
    keys = jnp.dot(normed, wk_ref[...], preferred_element_type=jnp.float32)
    for h in range(keys.shape[1] // HEAD):
        part = rotated(keys[:, h * HEAD:(h + 1) * HEAD]).astype(k_ref.dtype)
        k_ref[:, h * HEAD:(h + 1) * HEAD] = part
        kv_ref[0, :, h * HEAD:(h + 1) * HEAD] = part
    values = jnp.dot(normed, wv_ref[...], preferred_element_type=jnp.float32).astype(v_ref.dtype)
    v_ref[...] = values
    kv_ref[1] = values


def project(gathered, norm_gain, w_query, w_key, w_value, cosine, sine, block):
    rows, width = gathered.shape
    steps = rows // block
    q_width = w_query.shape[1]
    kv_width = w_key.shape[1]
    whole = lambda i: (0, 0)
    return pl.pallas_call(
        project_kernel,
        grid=(steps,),
        out_shape=(
            jax.ShapeDtypeStruct((steps, block, q_width), jnp.bfloat16),
            jax.ShapeDtypeStruct((rows, kv_width), jnp.bfloat16),
            jax.ShapeDtypeStruct((rows, kv_width), jnp.bfloat16),
            jax.ShapeDtypeStruct((2, rows, kv_width), jnp.bfloat16),
        ),
        in_specs=[
            pl.BlockSpec((block, width), lambda i: (i, 0)),
            pl.BlockSpec((1, width), whole),
            pl.BlockSpec((width, q_width), whole),
            pl.BlockSpec((width, kv_width), whole),
            pl.BlockSpec((width, kv_width), whole),
            pl.BlockSpec((block, HEAD), lambda i: (i, 0)),
            pl.BlockSpec((block, HEAD), lambda i: (i, 0)),
        ],
        out_specs=(
            pl.BlockSpec((1, block, q_width), lambda i: (i, 0, 0)),
            pl.BlockSpec((block, kv_width), lambda i: (i, 0)),
            pl.BlockSpec((block, kv_width), lambda i: (i, 0)),
            pl.BlockSpec((2, block, kv_width), lambda i: (0, i, 0)),
        ),
        compiler_params=pltpu.CompilerParams(vmem_limit_bytes=60 * 1024 * 1024),
    )(gathered, norm_gain.reshape(1, width), w_query, w_key, w_value, cosine, sine)


def attention_kernel(
    scale, group_pages,
    wants, page_order, s_idx, s_cnt,
    q_ref, q_want, q_req, q_pos,
    p_ref,
    s_ref, s_tag, s_bound,
    o_ref, m_sc, l_sc, acc_sc, pm_sc, pl_sc, pacc_sc,
):
    prefixes, per_prefix = page_order.shape

    def update(m_ref, l_ref, acc_ref, score_list, value_list):
        run_max = m_ref[...]
        new_max = run_max
        for scores in score_list:
            new_max = jnp.maximum(new_max, jnp.max(scores, axis=1, keepdims=True))
        fade = jnp.exp(run_max - new_max)
        total = l_ref[...] * fade
        acc = acc_ref[...] * fade
        for scores, values in zip(score_list, value_list):
            weights = jnp.exp(scores - new_max)
            total = total + jnp.sum(weights, axis=1, keepdims=True)
            acc = acc + jnp.dot(weights.astype(jnp.bfloat16), values, preferred_element_type=jnp.float32)
        l_ref[...] = total
        acc_ref[...] = acc
        m_ref[...] = new_max

    for i in range(q_ref.shape[0]):
        m_sc[...] = jnp.full(m_sc.shape, -1e30, jnp.float32)
        l_sc[...] = jnp.zeros(l_sc.shape, jnp.float32)
        acc_sc[...] = jnp.zeros(acc_sc.shape, jnp.float32)
        heads = q_ref.shape[2] // q_ref.shape[1]
        size = q_ref.shape[1]
        query = jnp.concatenate([q_ref[i, :, h * size:(h + 1) * size] for h in range(heads)], axis=0)
        want = q_want[i]
        req = q_req[i]
        pos = q_pos[i]

        def score(keys):
            return lax.dot_general(
                query, keys, (((1,), (1,)), ((), ())), preferred_element_type=jnp.float32
            ) * scale

        for p in range(prefixes):
            @pl.when(wants[i, p] > 0)
            def _():
                pm_sc[...] = jnp.full(pm_sc.shape, -1e30, jnp.float32)
                pl_sc[...] = jnp.zeros(pl_sc.shape, jnp.float32)
                pacc_sc[...] = jnp.zeros(pacc_sc.shape, jnp.float32)

                def page_step(g, carry):
                    pages = [page_order[p, g * group_pages + j] for j in range(group_pages)]
                    blocks = [p_ref[b] for b in pages]
                    update(
                        pm_sc, pl_sc, pacc_sc,
                        [score(blk[:, :size]) for blk in blocks],
                        [blk[:, size:] for blk in blocks],
                    )
                    return carry

                lax.fori_loop(0, per_prefix // group_pages, page_step, 0)
                mine = want == p
                m_sc[...] = jnp.where(mine, pm_sc[...], m_sc[...])
                l_sc[...] = jnp.where(mine, pl_sc[...], l_sc[...])
                acc_sc[...] = jnp.where(mine, pacc_sc[...], acc_sc[...])

        def step(n, carry):
            b = s_idx[i, n]
            scores = score(s_ref[0, b])
            seen = (s_tag[b] == req) & (s_bound[b] <= pos)
            run_max = m_sc[...]
            new_max = jnp.maximum(
                run_max, jnp.max(jnp.where(seen, scores, -1e30), axis=1, keepdims=True)
            )
            weights = jnp.where(seen, jnp.exp(scores - new_max), 0.0)
            fade = jnp.exp(run_max - new_max)
            l_sc[...] = l_sc[...] * fade + jnp.sum(weights, axis=1, keepdims=True)
            acc_sc[...] = acc_sc[...] * fade + jnp.dot(
                weights.astype(jnp.bfloat16), s_ref[1, b], preferred_element_type=jnp.float32
            )
            m_sc[...] = new_max
            return carry

        lax.fori_loop(0, s_cnt[i], step, 0)
        result = (acc_sc[...] / l_sc[...]).astype(o_ref.dtype)
        for h in range(heads):
            o_ref[i, :, h * size:(h + 1) * size] = result[h * size:(h + 1) * size]


def block_attention(scale, lists, queries, query_meta, prefix_parts, suffix_parts):
    q_blocks, block_rows, q_width = queries.shape
    width = queries.shape[1]
    q_rows = q_width // width * block_rows
    smem = pl.BlockSpec(memory_space=pltpu.SMEM)
    vmem = pl.BlockSpec(memory_space=pltpu.VMEM)
    state = [
        pltpu.VMEM((q_rows, 1), jnp.float32),
        pltpu.VMEM((q_rows, 1), jnp.float32),
        pltpu.VMEM((q_rows, width), jnp.float32),
    ]
    return pl.pallas_call(
        functools.partial(attention_kernel, scale, 4),
        out_shape=jax.ShapeDtypeStruct((q_blocks, block_rows, q_width), jnp.bfloat16),
        in_specs=[smem] * 4 + [vmem] * 8,
        out_specs=vmem,
        scratch_shapes=state + state,
        compiler_params=pltpu.CompilerParams(vmem_limit_bytes=48 * 1024 * 1024),
    )(*lists, queries, *query_meta, *prefix_parts, *suffix_parts)


def visible_list(visible):
    count = visible.shape[1]
    ids = jnp.arange(count, dtype=jnp.int32)
    rank = jnp.sum((visible[:, :, None] & (ids[:, None] < ids[None, :])[None]).astype(jnp.int32), axis=1)
    pick = visible[:, None, :] & (rank[:, None, :] == ids[None, :, None])
    order = jnp.sum(jnp.where(pick, ids[None, None, :], 0), axis=2).astype(jnp.int32)
    return order, jnp.sum(visible.astype(jnp.int32), axis=1)


def body(
    seq_n,
    tp_n,
    hidden,
    norm_gain,
    w_query,
    w_key,
    w_value,
    prefix_keys,
    prefix_values,
    page_prefix,
    request_prefix,
    suffix_lengths,
    row_order,
):
    gathered_prefix = lax.all_gather(
        jnp.concatenate([prefix_keys, prefix_values], axis=1), "seq", axis=0, tiled=True
    )
    gathered = tp_gather(hidden, tp_n, 2)
    local_rows = gathered.shape[0]
    request_all, position_all, wanted_all = locate(row_order, suffix_lengths, request_prefix)
    offset = lax.axis_index("seq") * local_rows
    request = lax.dynamic_slice_in_dim(request_all, offset, local_rows)
    position = lax.dynamic_slice_in_dim(position_all, offset, local_rows)
    wanted = lax.dynamic_slice_in_dim(wanted_all, offset, local_rows)
    prefix_len = page_prefix.shape[0] * PAGE // PREFIXES
    rope_at = prefix_len + position
    q_heads = w_query.shape[1] // HEAD
    kv_heads = w_key.shape[1] // HEAD
    group_size = q_heads // kv_heads
    half_dim = HEAD // 2
    frequency = ROPE_BASE ** (-(jnp.arange(half_dim, dtype=jnp.float32) * 2.0 / HEAD))
    angles = rope_at.astype(jnp.float32)[:, None] * frequency[None, :]
    cosine = jnp.cos(angles)
    sine_part = jnp.sin(angles)
    cos_full = jnp.concatenate([cosine, cosine], axis=1)
    sin_signed = jnp.concatenate([-sine_part, sine_part], axis=1)
    stacked_q, new_keys, new_values, stacked_kv = project(
        gathered, norm_gain, w_query, w_key, w_value, cos_full, sin_signed, PAGE
    )
    score_scale = 1.0 / math.sqrt(HEAD)
    block = PAGE
    q_blocks = local_rows // block
    pages = page_prefix.shape[0]
    runs = row_order.shape[0] // block

    def per_query(values):
        spread = jnp.broadcast_to(values.reshape(q_blocks, 1, block), (q_blocks, group_size, block))
        return spread.reshape(q_blocks, group_size * block, 1).astype(jnp.int32)

    query_meta = (per_query(wanted), per_query(request + PREFIXES), per_query(position))
    want_blocks = wanted.reshape(q_blocks, block)
    block_wants = jnp.any(
        want_blocks[:, :, None] == jnp.arange(PREFIXES, dtype=jnp.int32)[None, None, :], axis=1
    )
    page_ids = jnp.arange(pages, dtype=jnp.int32)
    same = (page_prefix[:, None] == page_prefix[None, :]) & (page_ids[:, None] < page_ids[None, :])
    page_rank = jnp.sum(same.astype(jnp.int32), axis=0)
    per_prefix = pages // PREFIXES
    pick = (page_prefix[None, None, :] == jnp.arange(PREFIXES, dtype=jnp.int32)[:, None, None]) & (
        page_rank[None, None, :] == jnp.arange(per_prefix, dtype=jnp.int32)[None, :, None]
    )
    page_order = jnp.sum(jnp.where(pick, page_ids[None, None, :], 0), axis=2).astype(jnp.int32)
    local_place = lax.dynamic_slice_in_dim(row_order, offset, local_rows).reshape(q_blocks, block)
    first_seen = jnp.min(local_place - position.reshape(q_blocks, block), axis=1)
    last_seen = jnp.max(local_place, axis=1)
    run_place = row_order.reshape(runs, block)
    run_low = jnp.min(run_place, axis=1)
    run_high = jnp.max(run_place, axis=1)
    run_visible = (run_low[None, :] <= last_seen[:, None]) & (run_high[None, :] >= first_seen[:, None])
    s_idx, s_cnt = visible_list(run_visible)

    seq_n_blocks = seq_n
    prefix_parts = (gathered_prefix.reshape(pages, block, 2 * HEAD),)
    gathered_suffix = seq_gather(stacked_kv, seq_n_blocks, 1)
    suffix_parts = (
        gathered_suffix.reshape(2, runs, block, HEAD),
        (request_all + PREFIXES).reshape(runs, 1, block).astype(jnp.int32),
        position_all.reshape(runs, 1, block).astype(jnp.int32),
    )
    out = block_attention(
        score_scale, (block_wants.astype(jnp.int32), page_order, s_idx, s_cnt), stacked_q, query_meta, prefix_parts, suffix_parts
    )
    attended = out.reshape(local_rows, group_size * HEAD)
    return (attended, new_keys, new_values)


def solution(mesh):
    return jax.shard_map(
        functools.partial(body, mesh.shape["seq"], mesh.shape["tp"]),
        mesh=mesh,
        in_specs=(
            P("seq", "tp"),
            P(),
            P(None, "tp"),
            P(None, "tp"),
            P(None, "tp"),
            P("seq", "tp"),
            P("seq", "tp"),
            P(),
            P(),
            P(),
            P(),
        ),
        out_specs=(P("seq", "tp"), P("seq", "tp"), P("seq", "tp")),
        check_vma=False,
    )
```

```python
import functools
import math

import jax
import jax.numpy as jnp
from jax import lax
from jax.sharding import PartitionSpec as P
from jax.experimental import pallas as pl
from jax.experimental.pallas import tpu as pltpu

HEAD = 128
PAGE = 128
PREFIXES = 4


ROPE_BASE = 5000000.0


def rotate(tensor_in, positions):
    head_dim = tensor_in.shape[-1]
    half_dim = head_dim // 2
    frequency = ROPE_BASE ** (-(jnp.arange(half_dim, dtype=jnp.float32) * 2.0 / head_dim))
    angles = positions.astype(jnp.float32)[:, None] * frequency[None, :]
    cosine = jnp.cos(angles)[:, None, :]
    sine_part = jnp.sin(angles)[:, None, :]
    first_half = tensor_in[..., :half_dim]
    second_half = tensor_in[..., half_dim:]
    return jnp.concatenate(
        [
            first_half * cosine - second_half * sine_part,
            second_half * cosine + first_half * sine_part,
        ],
        axis=-1,
    )


def locate(row_order, suffix_lengths, request_prefix):
    end_rows = jnp.cumsum(suffix_lengths)
    starts = end_rows - suffix_lengths
    numbers = jnp.arange(suffix_lengths.shape[0], dtype=jnp.int32)
    request = jnp.sum((row_order[:, None] >= end_rows[None, :]).astype(jnp.int32), axis=1)
    chosen = request[:, None] == numbers[None, :]
    position = row_order - jnp.sum(jnp.where(chosen, starts[None, :], 0), axis=1)
    wanted = jnp.sum(jnp.where(chosen, request_prefix[None, :], 0), axis=1)
    return (request, position, wanted)


def seq_gather_kernel(
    zs, xs, x_ref, o_ref, z_send, z_recv, r_send, r_recv, f_send, f_recv, c_send, c_recv, local_sem
):
    me = lax.axis_index("seq")
    core = me % 2
    chip = me // 2
    za = chip // xs
    xb = chip % xs
    right = lax.rem(xb + 1, xs)
    left = lax.rem(xb + xs - 1, xs)
    parts = x_ref.shape[0]
    mesh_id = pl.DeviceIdType.MESH

    def seq_of(z, x, c):
        return (z * xs + x) * 2 + c

    def signal(sem, target):
        pl.semaphore_signal(sem, inc=1, device_id={"seq": target}, device_id_type=mesh_id)

    barrier = pltpu.get_barrier_semaphore()

    def greet(k, carry):
        signal(barrier, seq_of(lax.rem(za + k, zs), xb, core))
        return carry

    lax.fori_loop(1, zs, greet, 0)
    signal(barrier, seq_of(za, right, core))
    signal(barrier, seq_of(za, left, core))
    signal(barrier, seq_of(za, xb, 1 - core))
    pl.semaphore_wait(barrier, zs + 2)

    local = pltpu.make_async_copy(x_ref, o_ref.at[:, za, xb, core], local_sem)
    local.start()

    def z_copy(a, peer_z, slot_z):
        return pltpu.make_async_remote_copy(
            src_ref=x_ref.at[a],
            dst_ref=o_ref.at[a, slot_z, xb, core],
            send_sem=z_send.at[a, peer_z],
            recv_sem=z_recv.at[a, slot_z],
            device_id={"seq": seq_of(peer_z, xb, core)},
            device_id_type=mesh_id,
        )

    def ring_slot(a, slot, side, group, target_x, sem_side, src=None):
        return pltpu.make_async_remote_copy(
            src_ref=o_ref.at[a, slot, group, core] if src is None else src,
            dst_ref=o_ref.at[a, slot, group, core],
            send_sem=r_send.at[a, side, slot],
            recv_sem=r_recv.at[a, sem_side, slot],
            device_id={"seq": seq_of(za, target_x, core)},
            device_id_type=mesh_id,
        )

    def z_start(k, carry):
        peer_z = lax.rem(za + k, zs)
        for a in range(parts):
            z_copy(a, peer_z, za).start()
        return carry

    lax.fori_loop(1, zs, z_start, 0)
    for a in range(parts):
        ring_slot(a, za, 0, xb, right, 0, x_ref.at[a]).start()
        ring_slot(a, za, 1, xb, left, 1, x_ref.at[a]).start()

    def z_finish(k, carry):
        peer_z = lax.rem(za + k, zs)
        for a in range(parts):
            copy = z_copy(a, peer_z, peer_z)
            copy.wait_recv()
            ring_slot(a, peer_z, 0, xb, right, 0).start()
            ring_slot(a, peer_z, 1, xb, left, 1).start()
            copy.wait_send()
        return carry

    lax.fori_loop(1, zs, z_finish, 0)
    local.wait()

    def hand(a, group, slot):
        return pltpu.make_async_remote_copy(
            src_ref=o_ref.at[a, :, group, slot],
            dst_ref=o_ref.at[a, :, group, slot],
            send_sem=c_send.at[a, group],
            recv_sem=c_recv.at[a, group],
            device_id={"seq": seq_of(za, xb, 1 - core)},
            device_id_type=mesh_id,
        )

    across = []
    for a in range(parts):
        across.append(hand(a, xb, core))
        across[-1].start()

    far = lax.rem(xb + 2, xs)

    def relay(a, slot, group, target_x, src_group):
        return pltpu.make_async_remote_copy(
            src_ref=o_ref.at[a, slot, src_group, core],
            dst_ref=o_ref.at[a, slot, group, core],
            send_sem=f_send.at[a, slot],
            recv_sem=f_recv.at[a, slot],
            device_id={"seq": seq_of(za, target_x, core)},
            device_id_type=mesh_id,
        )

    for slot in range(zs):
        ring_slot(0, slot, 0, left, right, 0).wait_recv()
        relay(0, slot, left, right, left).start()
        ring_slot(1, slot, 1, right, left, 1).wait_recv()
        relay(1, slot, right, left, right).start()
    for slot in range(zs):
        ring_slot(1, slot, 0, left, right, 0).wait_recv()
        ring_slot(0, slot, 1, right, left, 1).wait_recv()
    for a in range(parts):
        for group in (left, right):
            across.append(hand(a, group, core))
            across[-1].start()
    for a in range(parts):
        for slot in range(zs):
            ring_slot(a, slot, 0, xb, right, 0).wait_send()
            ring_slot(a, slot, 1, xb, left, 1).wait_send()
    for slot in range(zs):
        relay(0, slot, far, right, left).wait_recv()
        relay(1, slot, far, left, right).wait_recv()
    for slot in range(zs):
        relay(0, slot, left, right, left).wait_send()
        relay(1, slot, right, left, right).wait_send()
    for a in range(parts):
        across.append(hand(a, far, core))
        across[-1].start()

    for copy in across:
        copy.wait_send()
    for a in range(parts):
        for g in range(xs):
            hand(a, g, 1 - core).wait_recv()


def seq_gather(stacked, n, cid):
    parts, rows, cols = stacked.shape
    chips = n // 2
    xs = 4
    zs = chips // xs
    return pl.pallas_call(
        functools.partial(seq_gather_kernel, zs, xs),
        out_shape=jax.ShapeDtypeStruct((parts, zs, xs, 2, rows, cols), stacked.dtype),
        in_specs=[pl.BlockSpec(memory_space=pl.ANY)],
        out_specs=pl.BlockSpec(memory_space=pl.ANY),
        scratch_shapes=[
            pltpu.SemaphoreType.DMA((parts, zs)),
            pltpu.SemaphoreType.DMA((parts, zs)),
            pltpu.SemaphoreType.DMA((parts, 2, zs)),
            pltpu.SemaphoreType.DMA((parts, 2, zs)),
            pltpu.SemaphoreType.DMA((parts, zs)),
            pltpu.SemaphoreType.DMA((parts, zs)),
            pltpu.SemaphoreType.DMA((parts, xs)),
            pltpu.SemaphoreType.DMA((parts, xs)),
            pltpu.SemaphoreType.DMA,
        ],
        compiler_params=pltpu.CompilerParams(collective_id=cid, has_side_effects=True),
    )(stacked)


def tp_gather_kernel(ys, x_ref, o_ref, p_send, p_recv, r_send, r_recv, f_send, f_recv, local_sem):
    me = lax.axis_index("tp")
    yy = me // 2
    zh = me % 2
    right = lax.rem(yy + 1, ys)
    left = lax.rem(yy + ys - 1, ys)
    far = lax.rem(yy + 2, ys)
    width = x_ref.shape[1]
    mesh_id = pl.DeviceIdType.MESH

    def cols(y, h):
        return pl.ds(pl.multiple_of((y * 2 + h) * width, 128), width)

    def pair(y):
        return pl.ds(pl.multiple_of(y * 2 * width, 128), 2 * width)

    def signal(target):
        pl.semaphore_signal(barrier, inc=1, device_id={"tp": target}, device_id_type=mesh_id)

    barrier = pltpu.get_barrier_semaphore()
    signal(yy * 2 + 1 - zh)
    signal(right * 2 + zh)
    signal(left * 2 + zh)
    pl.semaphore_wait(barrier, 3)

    local = pltpu.make_async_copy(x_ref, o_ref.at[:, cols(yy, zh)], local_sem)
    local.start()
    to_partner = pltpu.make_async_remote_copy(
        src_ref=x_ref,
        dst_ref=o_ref.at[:, cols(yy, zh)],
        send_sem=p_send,
        recv_sem=p_recv,
        device_id={"tp": yy * 2 + 1 - zh},
        device_id_type=mesh_id,
    )
    to_partner.start()

    def ring(src, h, group, target, side):
        return pltpu.make_async_remote_copy(
            src_ref=src,
            dst_ref=o_ref.at[:, cols(group, h)],
            send_sem=r_send.at[side, h],
            recv_sem=r_recv.at[side, h],
            device_id={"tp": target * 2 + zh},
            device_id_type=mesh_id,
        )

    outgoing = [ring(x_ref, zh, yy, right, 0), ring(x_ref, zh, yy, left, 1)]
    for copy in outgoing:
        copy.start()
    pltpu.make_async_remote_copy(
        src_ref=x_ref,
        dst_ref=o_ref.at[:, cols(yy, 1 - zh)],
        send_sem=p_send,
        recv_sem=p_recv,
        device_id={"tp": yy * 2 + 1 - zh},
        device_id_type=mesh_id,
    ).wait_recv()
    partner_src = o_ref.at[:, cols(yy, 1 - zh)]
    later = [ring(partner_src, 1 - zh, yy, right, 0), ring(partner_src, 1 - zh, yy, left, 1)]
    for copy in later:
        copy.start()
    local.wait()
    to_partner.wait_send()
    pieces = f_send.shape[1]
    span = x_ref.shape[0] // pieces

    def relay(group, h, target, side, c):
        rows = pl.ds(c * span, span)
        return pltpu.make_async_remote_copy(
            src_ref=o_ref.at[rows, cols(group, h)],
            dst_ref=o_ref.at[rows, cols(group, h)],
            send_sem=f_send.at[side, c],
            recv_sem=f_recv.at[side, c],
            device_id={"tp": target * 2 + zh},
            device_id_type=mesh_id,
        )

    relays = []
    ring(x_ref, 0, left, right, 0).wait_recv()
    for c in range(pieces):
        relays.append(relay(left, 0, right, 0, c))
        relays[-1].start()
    ring(x_ref, 1, right, left, 1).wait_recv()
    for c in range(pieces):
        relays.append(relay(right, 1, left, 1, c))
        relays[-1].start()
    ring(x_ref, 1, left, right, 0).wait_recv()
    ring(x_ref, 0, right, left, 1).wait_recv()
    for copy in outgoing + later:
        copy.wait_send()
    for c in range(pieces):
        relay(far, 0, right, 0, c).wait_recv()
        relay(far, 1, left, 1, c).wait_recv()
    for copy in relays:
        copy.wait_send()


def tp_gather(block, n, cid):
    rows, width = block.shape
    return pl.pallas_call(
        functools.partial(tp_gather_kernel, n // 2),
        out_shape=jax.ShapeDtypeStruct((rows, width * n), block.dtype),
        in_specs=[pl.BlockSpec(memory_space=pl.ANY)],
        out_specs=pl.BlockSpec(memory_space=pl.ANY),
        scratch_shapes=[
            pltpu.SemaphoreType.DMA,
            pltpu.SemaphoreType.DMA,
            pltpu.SemaphoreType.DMA((2, 2)),
            pltpu.SemaphoreType.DMA((2, 2)),
            pltpu.SemaphoreType.DMA((2, 4)),
            pltpu.SemaphoreType.DMA((2, 4)),
            pltpu.SemaphoreType.DMA,
        ],
        compiler_params=pltpu.CompilerParams(collective_id=cid, has_side_effects=True),
    )(block)


def project_kernel(x_ref, g_ref, wq_ref, wk_ref, wv_ref, cos_ref, sin_ref, q_ref, k_ref, v_ref, kv_ref):
    x = x_ref[...].astype(jnp.float32)
    mean_sq = jnp.mean(x * x, axis=1, keepdims=True)
    normed = (x * lax.rsqrt(mean_sq + 1e-05) * g_ref[...].astype(jnp.float32)).astype(jnp.bfloat16)
    cosine = cos_ref[...]
    sine = sin_ref[...]

    def rotated(values):
        half = values.shape[1] // 2
        return values * cosine + pltpu.roll(values, half, 1) * sine

    queries = jnp.dot(normed, wq_ref[...], preferred_element_type=jnp.float32)
    for h in range(queries.shape[1] // HEAD):
        q_ref[0, :, h * HEAD:(h + 1) * HEAD] = rotated(queries[:, h * HEAD:(h + 1) * HEAD]).astype(q_ref.dtype)
    keys = jnp.dot(normed, wk_ref[...], preferred_element_type=jnp.float32)
    for h in range(keys.shape[1] // HEAD):
        part = rotated(keys[:, h * HEAD:(h + 1) * HEAD]).astype(k_ref.dtype)
        k_ref[:, h * HEAD:(h + 1) * HEAD] = part
        kv_ref[0, :, h * HEAD:(h + 1) * HEAD] = part
    values = jnp.dot(normed, wv_ref[...], preferred_element_type=jnp.float32).astype(v_ref.dtype)
    v_ref[...] = values
    kv_ref[1] = values


def project(gathered, norm_gain, w_query, w_key, w_value, cosine, sine, block):
    rows, width = gathered.shape
    steps = rows // block
    q_width = w_query.shape[1]
    kv_width = w_key.shape[1]
    whole = lambda i: (0, 0)
    return pl.pallas_call(
        project_kernel,
        grid=(steps,),
        out_shape=(
            jax.ShapeDtypeStruct((steps, block, q_width), jnp.bfloat16),
            jax.ShapeDtypeStruct((rows, kv_width), jnp.bfloat16),
            jax.ShapeDtypeStruct((rows, kv_width), jnp.bfloat16),
            jax.ShapeDtypeStruct((2, rows, kv_width), jnp.bfloat16),
        ),
        in_specs=[
            pl.BlockSpec((block, width), lambda i: (i, 0)),
            pl.BlockSpec((1, width), whole),
            pl.BlockSpec((width, q_width), whole),
            pl.BlockSpec((width, kv_width), whole),
            pl.BlockSpec((width, kv_width), whole),
            pl.BlockSpec((block, HEAD), lambda i: (i, 0)),
            pl.BlockSpec((block, HEAD), lambda i: (i, 0)),
        ],
        out_specs=(
            pl.BlockSpec((1, block, q_width), lambda i: (i, 0, 0)),
            pl.BlockSpec((block, kv_width), lambda i: (i, 0)),
            pl.BlockSpec((block, kv_width), lambda i: (i, 0)),
            pl.BlockSpec((2, block, kv_width), lambda i: (0, i, 0)),
        ),
        compiler_params=pltpu.CompilerParams(vmem_limit_bytes=60 * 1024 * 1024),
    )(gathered, norm_gain.reshape(1, width), w_query, w_key, w_value, cosine, sine)


def attention_kernel(
    scale, group_pages,
    wants, page_order, s_idx, s_cnt,
    q_ref, q_want, q_req, q_pos,
    p_ref,
    s_ref, s_tag, s_bound,
    o_ref, m_sc, l_sc, acc_sc, pm_sc, pl_sc, pacc_sc,
):
    prefixes, per_prefix = page_order.shape

    def update(m_ref, l_ref, acc_ref, score_list, value_list):
        run_max = m_ref[...]
        new_max = run_max
        for scores in score_list:
            new_max = jnp.maximum(new_max, jnp.max(scores, axis=1, keepdims=True))
        fade = jnp.exp(run_max - new_max)
        total = l_ref[...] * fade
        acc = acc_ref[...] * fade
        for scores, values in zip(score_list, value_list):
            weights = jnp.exp(scores - new_max)
            total = total + jnp.sum(weights, axis=1, keepdims=True)
            acc = acc + jnp.dot(weights.astype(jnp.bfloat16), values, preferred_element_type=jnp.float32)
        l_ref[...] = total
        acc_ref[...] = acc
        m_ref[...] = new_max

    for i in range(q_ref.shape[0]):
        m_sc[...] = jnp.full(m_sc.shape, -1e30, jnp.float32)
        l_sc[...] = jnp.zeros(l_sc.shape, jnp.float32)
        acc_sc[...] = jnp.zeros(acc_sc.shape, jnp.float32)
        heads = q_ref.shape[2] // q_ref.shape[1]
        size = q_ref.shape[1]
        query = jnp.concatenate([q_ref[i, :, h * size:(h + 1) * size] for h in range(heads)], axis=0)
        want = q_want[i]
        req = q_req[i]
        pos = q_pos[i]

        def score(keys):
            return lax.dot_general(
                query, keys, (((1,), (1,)), ((), ())), preferred_element_type=jnp.float32
            ) * scale

        for p in range(prefixes):
            @pl.when(wants[i, p] > 0)
            def _():
                pm_sc[...] = jnp.full(pm_sc.shape, -1e30, jnp.float32)
                pl_sc[...] = jnp.zeros(pl_sc.shape, jnp.float32)
                pacc_sc[...] = jnp.zeros(pacc_sc.shape, jnp.float32)

                def page_step(g, carry):
                    pages = [page_order[p, g * group_pages + j] for j in range(group_pages)]
                    blocks = [p_ref[b] for b in pages]
                    update(
                        pm_sc, pl_sc, pacc_sc,
                        [score(blk[:, :size]) for blk in blocks],
                        [blk[:, size:] for blk in blocks],
                    )
                    return carry

                lax.fori_loop(0, per_prefix // group_pages, page_step, 0)
                mine = want == p
                m_sc[...] = jnp.where(mine, pm_sc[...], m_sc[...])
                l_sc[...] = jnp.where(mine, pl_sc[...], l_sc[...])
                acc_sc[...] = jnp.where(mine, pacc_sc[...], acc_sc[...])

        def step(n, carry):
            b = s_idx[i, n]
            scores = score(s_ref[0, b])
            seen = (s_tag[b] == req) & (s_bound[b] <= pos)
            run_max = m_sc[...]
            new_max = jnp.maximum(
                run_max, jnp.max(jnp.where(seen, scores, -1e30), axis=1, keepdims=True)
            )
            weights = jnp.where(seen, jnp.exp(scores - new_max), 0.0)
            fade = jnp.exp(run_max - new_max)
            l_sc[...] = l_sc[...] * fade + jnp.sum(weights, axis=1, keepdims=True)
            acc_sc[...] = acc_sc[...] * fade + jnp.dot(
                weights.astype(jnp.bfloat16), s_ref[1, b], preferred_element_type=jnp.float32
            )
            m_sc[...] = new_max
            return carry

        lax.fori_loop(0, s_cnt[i], step, 0)
        result = (acc_sc[...] / l_sc[...]).astype(o_ref.dtype)
        for h in range(heads):
            o_ref[i, :, h * size:(h + 1) * size] = result[h * size:(h + 1) * size]


def block_attention(scale, lists, queries, query_meta, prefix_parts, suffix_parts):
    q_blocks, block_rows, q_width = queries.shape
    width = queries.shape[1]
    q_rows = q_width // width * block_rows
    smem = pl.BlockSpec(memory_space=pltpu.SMEM)
    vmem = pl.BlockSpec(memory_space=pltpu.VMEM)
    state = [
        pltpu.VMEM((q_rows, 1), jnp.float32),
        pltpu.VMEM((q_rows, 1), jnp.float32),
        pltpu.VMEM((q_rows, width), jnp.float32),
    ]
    return pl.pallas_call(
        functools.partial(attention_kernel, scale, 4),
        out_shape=jax.ShapeDtypeStruct((q_blocks, block_rows, q_width), jnp.bfloat16),
        in_specs=[smem] * 4 + [vmem] * 8,
        out_specs=vmem,
        scratch_shapes=state + state,
        compiler_params=pltpu.CompilerParams(vmem_limit_bytes=48 * 1024 * 1024),
    )(*lists, queries, *query_meta, *prefix_parts, *suffix_parts)


def visible_list(visible):
    count = visible.shape[1]
    ids = jnp.arange(count, dtype=jnp.int32)
    rank = jnp.sum((visible[:, :, None] & (ids[:, None] < ids[None, :])[None]).astype(jnp.int32), axis=1)
    pick = visible[:, None, :] & (rank[:, None, :] == ids[None, :, None])
    order = jnp.sum(jnp.where(pick, ids[None, None, :], 0), axis=2).astype(jnp.int32)
    return order, jnp.sum(visible.astype(jnp.int32), axis=1)


def body(
    seq_n,
    tp_n,
    hidden,
    norm_gain,
    w_query,
    w_key,
    w_value,
    prefix_keys,
    prefix_values,
    page_prefix,
    request_prefix,
    suffix_lengths,
    row_order,
):
    own_pages = jnp.concatenate([prefix_keys, prefix_values], axis=1)
    chips = seq_n // 2
    same_core = [own_pages] + [
        lax.ppermute(own_pages, "seq", [(i, (i + 2 * k) % seq_n) for i in range(seq_n)])
        for k in range(1, chips)
    ]
    mine = jnp.stack(same_core)
    theirs = lax.ppermute(mine, "seq", [(i, i ^ 1) for i in range(seq_n)])
    gathered_prefix = jnp.concatenate([mine, theirs], axis=0)
    gathered = tp_gather(hidden, tp_n, 2)
    local_rows = gathered.shape[0]
    request_all, position_all, wanted_all = locate(row_order, suffix_lengths, request_prefix)
    offset = lax.axis_index("seq") * local_rows
    request = lax.dynamic_slice_in_dim(request_all, offset, local_rows)
    position = lax.dynamic_slice_in_dim(position_all, offset, local_rows)
    wanted = lax.dynamic_slice_in_dim(wanted_all, offset, local_rows)
    prefix_len = page_prefix.shape[0] * PAGE // PREFIXES
    rope_at = prefix_len + position
    q_heads = w_query.shape[1] // HEAD
    kv_heads = w_key.shape[1] // HEAD
    group_size = q_heads // kv_heads
    half_dim = HEAD // 2
    frequency = ROPE_BASE ** (-(jnp.arange(half_dim, dtype=jnp.float32) * 2.0 / HEAD))
    angles = rope_at.astype(jnp.float32)[:, None] * frequency[None, :]
    cosine = jnp.cos(angles)
    sine_part = jnp.sin(angles)
    cos_full = jnp.concatenate([cosine, cosine], axis=1)
    sin_signed = jnp.concatenate([-sine_part, sine_part], axis=1)
    stacked_q, new_keys, new_values, stacked_kv = project(
        gathered, norm_gain, w_query, w_key, w_value, cos_full, sin_signed, PAGE
    )
    score_scale = 1.0 / math.sqrt(HEAD)
    block = PAGE
    q_blocks = local_rows // block
    pages = page_prefix.shape[0]
    runs = row_order.shape[0] // block

    def per_query(values):
        spread = jnp.broadcast_to(values.reshape(q_blocks, 1, block), (q_blocks, group_size, block))
        return spread.reshape(q_blocks, group_size * block, 1).astype(jnp.int32)

    query_meta = (per_query(wanted), per_query(request + PREFIXES), per_query(position))
    want_blocks = wanted.reshape(q_blocks, block)
    block_wants = jnp.any(
        want_blocks[:, :, None] == jnp.arange(PREFIXES, dtype=jnp.int32)[None, None, :], axis=1
    )
    page_ids = jnp.arange(pages, dtype=jnp.int32)
    same = (page_prefix[:, None] == page_prefix[None, :]) & (page_ids[:, None] < page_ids[None, :])
    page_rank = jnp.sum(same.astype(jnp.int32), axis=0)
    per_prefix = pages // PREFIXES
    pick = (page_prefix[None, None, :] == jnp.arange(PREFIXES, dtype=jnp.int32)[:, None, None]) & (
        page_rank[None, None, :] == jnp.arange(per_prefix, dtype=jnp.int32)[None, :, None]
    )
    page_order = jnp.sum(jnp.where(pick, page_ids[None, None, :], 0), axis=2).astype(jnp.int32)
    me_seq = lax.axis_index("seq")
    page_device = page_order // 2
    same = (page_device % 2) == (me_seq % 2)
    holder = jnp.where(same, me_seq, me_seq ^ 1)
    slot = jnp.where(same, 0, seq_n // 2) + ((holder - page_device) % seq_n) // 2
    page_order = (slot * 2 + page_order % 2).astype(jnp.int32)
    local_place = lax.dynamic_slice_in_dim(row_order, offset, local_rows).reshape(q_blocks, block)
    first_seen = jnp.min(local_place - position.reshape(q_blocks, block), axis=1)
    last_seen = jnp.max(local_place, axis=1)
    run_place = row_order.reshape(runs, block)
    run_low = jnp.min(run_place, axis=1)
    run_high = jnp.max(run_place, axis=1)
    run_visible = (run_low[None, :] <= last_seen[:, None]) & (run_high[None, :] >= first_seen[:, None])
    s_idx, s_cnt = visible_list(run_visible)

    seq_n_blocks = seq_n
    prefix_parts = (gathered_prefix.reshape(pages, block, 2 * HEAD),)
    gathered_suffix = seq_gather(stacked_kv, seq_n_blocks, 1)
    suffix_parts = (
        gathered_suffix.reshape(2, runs, block, HEAD),
        (request_all + PREFIXES).reshape(runs, 1, block).astype(jnp.int32),
        position_all.reshape(runs, 1, block).astype(jnp.int32),
    )
    out = block_attention(
        score_scale, (block_wants.astype(jnp.int32), page_order, s_idx, s_cnt), stacked_q, query_meta, prefix_parts, suffix_parts
    )
    attended = out.reshape(local_rows, group_size * HEAD)
    return (attended, new_keys, new_values)


def solution(mesh):
    return jax.shard_map(
        functools.partial(body, mesh.shape["seq"], mesh.shape["tp"]),
        mesh=mesh,
        in_specs=(
            P("seq", "tp"),
            P(),
            P(None, "tp"),
            P(None, "tp"),
            P(None, "tp"),
            P("seq", "tp"),
            P("seq", "tp"),
            P(),
            P(),
            P(),
            P(),
        ),
        out_specs=(P("seq", "tp"), P("seq", "tp"), P("seq", "tp")),
        check_vma=False,
    )
```

```python
import functools
import math

import jax
import jax.numpy as jnp
from jax import lax
from jax.sharding import PartitionSpec as P
from jax.experimental import pallas as pl
from jax.experimental.pallas import tpu as pltpu

HEAD = 128
PAGE = 128
PREFIXES = 4


ROPE_BASE = 5000000.0


def rotate(tensor_in, positions):
    head_dim = tensor_in.shape[-1]
    half_dim = head_dim // 2
    frequency = ROPE_BASE ** (-(jnp.arange(half_dim, dtype=jnp.float32) * 2.0 / head_dim))
    angles = positions.astype(jnp.float32)[:, None] * frequency[None, :]
    cosine = jnp.cos(angles)[:, None, :]
    sine_part = jnp.sin(angles)[:, None, :]
    first_half = tensor_in[..., :half_dim]
    second_half = tensor_in[..., half_dim:]
    return jnp.concatenate(
        [
            first_half * cosine - second_half * sine_part,
            second_half * cosine + first_half * sine_part,
        ],
        axis=-1,
    )


def locate(row_order, suffix_lengths, request_prefix):
    end_rows = jnp.cumsum(suffix_lengths)
    starts = end_rows - suffix_lengths
    numbers = jnp.arange(suffix_lengths.shape[0], dtype=jnp.int32)
    request = jnp.sum((row_order[:, None] >= end_rows[None, :]).astype(jnp.int32), axis=1)
    chosen = request[:, None] == numbers[None, :]
    position = row_order - jnp.sum(jnp.where(chosen, starts[None, :], 0), axis=1)
    wanted = jnp.sum(jnp.where(chosen, request_prefix[None, :], 0), axis=1)
    return (request, position, wanted)


def seq_gather_kernel(
    zs, xs, x_ref, o_ref, z_send, z_recv, r_send, r_recv, f_send, f_recv, c_send, c_recv, local_sem
):
    me = lax.axis_index("seq")
    core = me % 2
    chip = me // 2
    za = chip // xs
    xb = chip % xs
    right = lax.rem(xb + 1, xs)
    left = lax.rem(xb + xs - 1, xs)
    parts = x_ref.shape[0]
    mesh_id = pl.DeviceIdType.MESH

    def seq_of(z, x, c):
        return (z * xs + x) * 2 + c

    def signal(sem, target):
        pl.semaphore_signal(sem, inc=1, device_id={"seq": target}, device_id_type=mesh_id)

    barrier = pltpu.get_barrier_semaphore()

    def greet(k, carry):
        signal(barrier, seq_of(lax.rem(za + k, zs), xb, core))
        return carry

    lax.fori_loop(1, zs, greet, 0)
    signal(barrier, seq_of(za, right, core))
    signal(barrier, seq_of(za, left, core))
    signal(barrier, seq_of(za, xb, 1 - core))
    pl.semaphore_wait(barrier, zs + 2)

    local = pltpu.make_async_copy(x_ref, o_ref.at[:, za, xb, core], local_sem)
    local.start()

    def z_copy(a, peer_z, slot_z):
        return pltpu.make_async_remote_copy(
            src_ref=x_ref.at[a],
            dst_ref=o_ref.at[a, slot_z, xb, core],
            send_sem=z_send.at[a, peer_z],
            recv_sem=z_recv.at[a, slot_z],
            device_id={"seq": seq_of(peer_z, xb, core)},
            device_id_type=mesh_id,
        )

    def ring_slot(a, slot, side, group, target_x, sem_side, src=None):
        return pltpu.make_async_remote_copy(
            src_ref=o_ref.at[a, slot, group, core] if src is None else src,
            dst_ref=o_ref.at[a, slot, group, core],
            send_sem=r_send.at[a, side, slot],
            recv_sem=r_recv.at[a, sem_side, slot],
            device_id={"seq": seq_of(za, target_x, core)},
            device_id_type=mesh_id,
        )

    def z_start(k, carry):
        peer_z = lax.rem(za + k, zs)
        for a in range(parts):
            z_copy(a, peer_z, za).start()
        return carry

    lax.fori_loop(1, zs, z_start, 0)
    for a in range(parts):
        ring_slot(a, za, 0, xb, right, 0, x_ref.at[a]).start()
        ring_slot(a, za, 1, xb, left, 1, x_ref.at[a]).start()

    def z_finish(k, carry):
        peer_z = lax.rem(za + k, zs)
        for a in range(parts):
            copy = z_copy(a, peer_z, peer_z)
            copy.wait_recv()
            ring_slot(a, peer_z, 0, xb, right, 0).start()
            ring_slot(a, peer_z, 1, xb, left, 1).start()
            copy.wait_send()
        return carry

    lax.fori_loop(1, zs, z_finish, 0)
    local.wait()

    def hand(a, group, slot):
        return pltpu.make_async_remote_copy(
            src_ref=o_ref.at[a, :, group, slot],
            dst_ref=o_ref.at[a, :, group, slot],
            send_sem=c_send.at[a, group],
            recv_sem=c_recv.at[a, group],
            device_id={"seq": seq_of(za, xb, 1 - core)},
            device_id_type=mesh_id,
        )

    across = []
    for a in range(parts):
        across.append(hand(a, xb, core))
        across[-1].start()

    far = lax.rem(xb + 2, xs)

    def relay(a, slot, group, target_x, src_group):
        return pltpu.make_async_remote_copy(
            src_ref=o_ref.at[a, slot, src_group, core],
            dst_ref=o_ref.at[a, slot, group, core],
            send_sem=f_send.at[a, slot],
            recv_sem=f_recv.at[a, slot],
            device_id={"seq": seq_of(za, target_x, core)},
            device_id_type=mesh_id,
        )

    for slot in range(zs):
        ring_slot(0, slot, 0, left, right, 0).wait_recv()
        relay(0, slot, left, right, left).start()
        ring_slot(1, slot, 1, right, left, 1).wait_recv()
        relay(1, slot, right, left, right).start()
    for slot in range(zs):
        ring_slot(1, slot, 0, left, right, 0).wait_recv()
        ring_slot(0, slot, 1, right, left, 1).wait_recv()
    for a in range(parts):
        for group in (left, right):
            across.append(hand(a, group, core))
            across[-1].start()
    for a in range(parts):
        for slot in range(zs):
            ring_slot(a, slot, 0, xb, right, 0).wait_send()
            ring_slot(a, slot, 1, xb, left, 1).wait_send()
    for slot in range(zs):
        relay(0, slot, far, right, left).wait_recv()
        relay(1, slot, far, left, right).wait_recv()
    for slot in range(zs):
        relay(0, slot, left, right, left).wait_send()
        relay(1, slot, right, left, right).wait_send()
    for a in range(parts):
        across.append(hand(a, far, core))
        across[-1].start()

    for copy in across:
        copy.wait_send()
    for a in range(parts):
        for g in range(xs):
            hand(a, g, 1 - core).wait_recv()


def seq_gather(stacked, n, cid):
    parts, rows, cols = stacked.shape
    chips = n // 2
    xs = 4
    zs = chips // xs
    return pl.pallas_call(
        functools.partial(seq_gather_kernel, zs, xs),
        out_shape=jax.ShapeDtypeStruct((parts, zs, xs, 2, rows, cols), stacked.dtype),
        in_specs=[pl.BlockSpec(memory_space=pl.ANY)],
        out_specs=pl.BlockSpec(memory_space=pl.ANY),
        scratch_shapes=[
            pltpu.SemaphoreType.DMA((parts, zs)),
            pltpu.SemaphoreType.DMA((parts, zs)),
            pltpu.SemaphoreType.DMA((parts, 2, zs)),
            pltpu.SemaphoreType.DMA((parts, 2, zs)),
            pltpu.SemaphoreType.DMA((parts, zs)),
            pltpu.SemaphoreType.DMA((parts, zs)),
            pltpu.SemaphoreType.DMA((parts, xs)),
            pltpu.SemaphoreType.DMA((parts, xs)),
            pltpu.SemaphoreType.DMA,
        ],
        compiler_params=pltpu.CompilerParams(collective_id=cid, has_side_effects=True),
    )(stacked)


def tp_gather_kernel(ys, x_ref, o_ref, p_send, p_recv, r_send, r_recv, f_send, f_recv, local_sem):
    me = lax.axis_index("tp")
    yy = me // 2
    zh = me % 2
    right = lax.rem(yy + 1, ys)
    left = lax.rem(yy + ys - 1, ys)
    far = lax.rem(yy + 2, ys)
    width = x_ref.shape[1]
    mesh_id = pl.DeviceIdType.MESH

    def cols(y, h):
        return pl.ds(pl.multiple_of((y * 2 + h) * width, 128), width)

    def pair(y):
        return pl.ds(pl.multiple_of(y * 2 * width, 128), 2 * width)

    def signal(target):
        pl.semaphore_signal(barrier, inc=1, device_id={"tp": target}, device_id_type=mesh_id)

    barrier = pltpu.get_barrier_semaphore()
    signal(yy * 2 + 1 - zh)
    signal(right * 2 + zh)
    signal(left * 2 + zh)
    pl.semaphore_wait(barrier, 3)

    local = pltpu.make_async_copy(x_ref, o_ref.at[:, cols(yy, zh)], local_sem)
    local.start()
    to_partner = pltpu.make_async_remote_copy(
        src_ref=x_ref,
        dst_ref=o_ref.at[:, cols(yy, zh)],
        send_sem=p_send,
        recv_sem=p_recv,
        device_id={"tp": yy * 2 + 1 - zh},
        device_id_type=mesh_id,
    )
    to_partner.start()

    def ring(src, h, group, target, side):
        return pltpu.make_async_remote_copy(
            src_ref=src,
            dst_ref=o_ref.at[:, cols(group, h)],
            send_sem=r_send.at[side, h],
            recv_sem=r_recv.at[side, h],
            device_id={"tp": target * 2 + zh},
            device_id_type=mesh_id,
        )

    outgoing = [ring(x_ref, zh, yy, right, 0), ring(x_ref, zh, yy, left, 1)]
    for copy in outgoing:
        copy.start()
    pltpu.make_async_remote_copy(
        src_ref=x_ref,
        dst_ref=o_ref.at[:, cols(yy, 1 - zh)],
        send_sem=p_send,
        recv_sem=p_recv,
        device_id={"tp": yy * 2 + 1 - zh},
        device_id_type=mesh_id,
    ).wait_recv()
    partner_src = o_ref.at[:, cols(yy, 1 - zh)]
    later = [ring(partner_src, 1 - zh, yy, right, 0), ring(partner_src, 1 - zh, yy, left, 1)]
    for copy in later:
        copy.start()
    local.wait()
    to_partner.wait_send()
    pieces = f_send.shape[1]
    span = x_ref.shape[0] // pieces

    def relay(group, h, target, side, c):
        rows = pl.ds(c * span, span)
        return pltpu.make_async_remote_copy(
            src_ref=o_ref.at[rows, cols(group, h)],
            dst_ref=o_ref.at[rows, cols(group, h)],
            send_sem=f_send.at[side, c],
            recv_sem=f_recv.at[side, c],
            device_id={"tp": target * 2 + zh},
            device_id_type=mesh_id,
        )

    relays = []
    ring(x_ref, 0, left, right, 0).wait_recv()
    for c in range(pieces):
        relays.append(relay(left, 0, right, 0, c))
        relays[-1].start()
    ring(x_ref, 1, right, left, 1).wait_recv()
    for c in range(pieces):
        relays.append(relay(right, 1, left, 1, c))
        relays[-1].start()
    ring(x_ref, 1, left, right, 0).wait_recv()
    ring(x_ref, 0, right, left, 1).wait_recv()
    for copy in outgoing + later:
        copy.wait_send()
    for c in range(pieces):
        relay(far, 0, right, 0, c).wait_recv()
        relay(far, 1, left, 1, c).wait_recv()
    for copy in relays:
        copy.wait_send()


def tp_gather(block, n, cid):
    rows, width = block.shape
    return pl.pallas_call(
        functools.partial(tp_gather_kernel, n // 2),
        out_shape=jax.ShapeDtypeStruct((rows, width * n), block.dtype),
        in_specs=[pl.BlockSpec(memory_space=pl.ANY)],
        out_specs=pl.BlockSpec(memory_space=pl.ANY),
        scratch_shapes=[
            pltpu.SemaphoreType.DMA,
            pltpu.SemaphoreType.DMA,
            pltpu.SemaphoreType.DMA((2, 2)),
            pltpu.SemaphoreType.DMA((2, 2)),
            pltpu.SemaphoreType.DMA((2, 4)),
            pltpu.SemaphoreType.DMA((2, 4)),
            pltpu.SemaphoreType.DMA,
        ],
        compiler_params=pltpu.CompilerParams(collective_id=cid, has_side_effects=True),
    )(block)


def project_kernel(x_ref, g_ref, wq_ref, wk_ref, wv_ref, cos_ref, sin_ref, q_ref, k_ref, v_ref, kv_ref):
    x = x_ref[...].astype(jnp.float32)
    mean_sq = jnp.mean(x * x, axis=1, keepdims=True)
    gain = g_ref[...].astype(jnp.float32).reshape(1, x.shape[1])
    normed = (x * lax.rsqrt(mean_sq + 1e-05) * gain).astype(jnp.bfloat16)
    cosine = cos_ref[...]
    sine = sin_ref[...]

    def rotated(values):
        half = values.shape[1] // 2
        return values * cosine + pltpu.roll(values, half, 1) * sine

    queries = jnp.dot(normed, wq_ref[...], preferred_element_type=jnp.float32)
    for h in range(queries.shape[1] // HEAD):
        q_ref[0, :, h * HEAD:(h + 1) * HEAD] = rotated(queries[:, h * HEAD:(h + 1) * HEAD]).astype(q_ref.dtype)
    keys = jnp.dot(normed, wk_ref[...], preferred_element_type=jnp.float32)
    for h in range(keys.shape[1] // HEAD):
        part = rotated(keys[:, h * HEAD:(h + 1) * HEAD]).astype(k_ref.dtype)
        k_ref[:, h * HEAD:(h + 1) * HEAD] = part
        kv_ref[0, :, h * HEAD:(h + 1) * HEAD] = part
    values = jnp.dot(normed, wv_ref[...], preferred_element_type=jnp.float32).astype(v_ref.dtype)
    v_ref[...] = values
    kv_ref[1] = values


def project(gathered, norm_gain, w_query, w_key, w_value, cosine, sine, block):
    rows, width = gathered.shape
    steps = rows // block
    q_width = w_query.shape[1]
    kv_width = w_key.shape[1]
    whole = lambda i: (0, 0)
    return pl.pallas_call(
        project_kernel,
        grid=(steps,),
        out_shape=(
            jax.ShapeDtypeStruct((steps, block, q_width), jnp.bfloat16),
            jax.ShapeDtypeStruct((rows, kv_width), jnp.bfloat16),
            jax.ShapeDtypeStruct((rows, kv_width), jnp.bfloat16),
            jax.ShapeDtypeStruct((2, rows, kv_width), jnp.bfloat16),
        ),
        in_specs=[
            pl.BlockSpec((block, width), lambda i: (i, 0)),
            pl.BlockSpec(memory_space=pltpu.VMEM),
            pl.BlockSpec((width, q_width), whole),
            pl.BlockSpec((width, kv_width), whole),
            pl.BlockSpec((width, kv_width), whole),
            pl.BlockSpec((block, HEAD), lambda i: (i, 0)),
            pl.BlockSpec((block, HEAD), lambda i: (i, 0)),
        ],
        out_specs=(
            pl.BlockSpec((1, block, q_width), lambda i: (i, 0, 0)),
            pl.BlockSpec((block, kv_width), lambda i: (i, 0)),
            pl.BlockSpec((block, kv_width), lambda i: (i, 0)),
            pl.BlockSpec((2, block, kv_width), lambda i: (0, i, 0)),
        ),
        compiler_params=pltpu.CompilerParams(vmem_limit_bytes=60 * 1024 * 1024),
    )(gathered, norm_gain, w_query, w_key, w_value, cosine, sine)


def attention_kernel(
    scale, group_pages,
    wants, page_order, s_idx, s_cnt,
    q_ref, q_want, q_req, q_pos,
    p_ref,
    s_ref, s_tag, s_bound,
    o_ref, m_sc, l_sc, acc_sc, pm_sc, pl_sc, pacc_sc,
):
    prefixes, per_prefix = page_order.shape

    def update(m_ref, l_ref, acc_ref, score_list, value_list):
        run_max = m_ref[...]
        new_max = run_max
        for scores in score_list:
            new_max = jnp.maximum(new_max, jnp.max(scores, axis=1, keepdims=True))
        fade = jnp.exp(run_max - new_max)
        total = l_ref[...] * fade
        acc = acc_ref[...] * fade
        for scores, values in zip(score_list, value_list):
            weights = jnp.exp(scores - new_max)
            total = total + jnp.sum(weights, axis=1, keepdims=True)
            acc = acc + jnp.dot(weights.astype(jnp.bfloat16), values, preferred_element_type=jnp.float32)
        l_ref[...] = total
        acc_ref[...] = acc
        m_ref[...] = new_max

    for i in range(q_ref.shape[0]):
        m_sc[...] = jnp.full(m_sc.shape, -1e30, jnp.float32)
        l_sc[...] = jnp.zeros(l_sc.shape, jnp.float32)
        acc_sc[...] = jnp.zeros(acc_sc.shape, jnp.float32)
        heads = q_ref.shape[2] // q_ref.shape[1]
        size = q_ref.shape[1]
        query = jnp.concatenate([q_ref[i, :, h * size:(h + 1) * size] for h in range(heads)], axis=0)
        want = q_want[i]
        req = q_req[i]
        pos = q_pos[i]

        def score(keys):
            return lax.dot_general(
                query, keys, (((1,), (1,)), ((), ())), preferred_element_type=jnp.float32
            ) * scale

        for p in range(prefixes):
            @pl.when(wants[i, p] > 0)
            def _():
                pm_sc[...] = jnp.full(pm_sc.shape, -1e30, jnp.float32)
                pl_sc[...] = jnp.zeros(pl_sc.shape, jnp.float32)
                pacc_sc[...] = jnp.zeros(pacc_sc.shape, jnp.float32)

                def page_step(g, carry):
                    pages = [page_order[p, g * group_pages + j] for j in range(group_pages)]
                    blocks = [p_ref[b] for b in pages]
                    update(
                        pm_sc, pl_sc, pacc_sc,
                        [score(blk[:, :size]) for blk in blocks],
                        [blk[:, size:] for blk in blocks],
                    )
                    return carry

                lax.fori_loop(0, per_prefix // group_pages, page_step, 0)
                mine = want == p
                m_sc[...] = jnp.where(mine, pm_sc[...], m_sc[...])
                l_sc[...] = jnp.where(mine, pl_sc[...], l_sc[...])
                acc_sc[...] = jnp.where(mine, pacc_sc[...], acc_sc[...])

        def step(n, carry):
            b = s_idx[i, n]
            scores = score(s_ref[0, b])
            seen = (s_tag[b] == req) & (s_bound[b] <= pos)
            run_max = m_sc[...]
            new_max = jnp.maximum(
                run_max, jnp.max(jnp.where(seen, scores, -1e30), axis=1, keepdims=True)
            )
            weights = jnp.where(seen, jnp.exp(scores - new_max), 0.0)
            fade = jnp.exp(run_max - new_max)
            l_sc[...] = l_sc[...] * fade + jnp.sum(weights, axis=1, keepdims=True)
            acc_sc[...] = acc_sc[...] * fade + jnp.dot(
                weights.astype(jnp.bfloat16), s_ref[1, b], preferred_element_type=jnp.float32
            )
            m_sc[...] = new_max
            return carry

        lax.fori_loop(0, s_cnt[i], step, 0)
        result = (acc_sc[...] / l_sc[...]).astype(o_ref.dtype)
        for h in range(heads):
            o_ref[i, :, h * size:(h + 1) * size] = result[h * size:(h + 1) * size]


def block_attention(scale, lists, queries, query_meta, prefix_parts, suffix_parts):
    q_blocks, block_rows, q_width = queries.shape
    width = queries.shape[1]
    q_rows = q_width // width * block_rows
    smem = pl.BlockSpec(memory_space=pltpu.SMEM)
    vmem = pl.BlockSpec(memory_space=pltpu.VMEM)
    state = [
        pltpu.VMEM((q_rows, 1), jnp.float32),
        pltpu.VMEM((q_rows, 1), jnp.float32),
        pltpu.VMEM((q_rows, width), jnp.float32),
    ]
    return pl.pallas_call(
        functools.partial(attention_kernel, scale, 4),
        out_shape=jax.ShapeDtypeStruct((q_blocks, block_rows, q_width), jnp.bfloat16),
        in_specs=[smem] * 4 + [vmem] * 8,
        out_specs=vmem,
        scratch_shapes=state + state,
        compiler_params=pltpu.CompilerParams(vmem_limit_bytes=48 * 1024 * 1024),
    )(*lists, queries, *query_meta, *prefix_parts, *suffix_parts)


def visible_list(visible):
    count = visible.shape[1]
    ids = jnp.arange(count, dtype=jnp.int32)
    rank = jnp.sum((visible[:, :, None] & (ids[:, None] < ids[None, :])[None]).astype(jnp.int32), axis=1)
    pick = visible[:, None, :] & (rank[:, None, :] == ids[None, :, None])
    order = jnp.sum(jnp.where(pick, ids[None, None, :], 0), axis=2).astype(jnp.int32)
    return order, jnp.sum(visible.astype(jnp.int32), axis=1)


def body(
    seq_n,
    tp_n,
    hidden,
    norm_gain,
    w_query,
    w_key,
    w_value,
    prefix_keys,
    prefix_values,
    page_prefix,
    request_prefix,
    suffix_lengths,
    row_order,
):
    gathered_prefix = lax.all_gather(
        jnp.concatenate([prefix_keys, prefix_values], axis=1), "seq", axis=0, tiled=True
    )
    gathered = tp_gather(hidden, tp_n, 2)
    local_rows = gathered.shape[0]
    request_all, position_all, wanted_all = locate(row_order, suffix_lengths, request_prefix)
    offset = lax.axis_index("seq") * local_rows
    request = lax.dynamic_slice_in_dim(request_all, offset, local_rows)
    position = lax.dynamic_slice_in_dim(position_all, offset, local_rows)
    wanted = lax.dynamic_slice_in_dim(wanted_all, offset, local_rows)
    prefix_len = page_prefix.shape[0] * PAGE // PREFIXES
    rope_at = prefix_len + position
    q_heads = w_query.shape[1] // HEAD
    kv_heads = w_key.shape[1] // HEAD
    group_size = q_heads // kv_heads
    half_dim = HEAD // 2
    frequency = ROPE_BASE ** (-(jnp.arange(half_dim, dtype=jnp.float32) * 2.0 / HEAD))
    angles = rope_at.astype(jnp.float32)[:, None] * frequency[None, :]
    cosine = jnp.cos(angles)
    sine_part = jnp.sin(angles)
    cos_full = jnp.concatenate([cosine, cosine], axis=1)
    sin_signed = jnp.concatenate([-sine_part, sine_part], axis=1)
    stacked_q, new_keys, new_values, stacked_kv = project(
        gathered, norm_gain, w_query, w_key, w_value, cos_full, sin_signed, PAGE
    )
    score_scale = 1.0 / math.sqrt(HEAD)
    block = PAGE
    q_blocks = local_rows // block
    pages = page_prefix.shape[0]
    runs = row_order.shape[0] // block

    def per_query(values):
        spread = jnp.broadcast_to(values.reshape(q_blocks, 1, block), (q_blocks, group_size, block))
        return spread.reshape(q_blocks, group_size * block, 1).astype(jnp.int32)

    query_meta = (per_query(wanted), per_query(request + PREFIXES), per_query(position))
    want_blocks = wanted.reshape(q_blocks, block)
    block_wants = jnp.any(
        want_blocks[:, :, None] == jnp.arange(PREFIXES, dtype=jnp.int32)[None, None, :], axis=1
    )
    page_ids = jnp.arange(pages, dtype=jnp.int32)
    same = (page_prefix[:, None] == page_prefix[None, :]) & (page_ids[:, None] < page_ids[None, :])
    page_rank = jnp.sum(same.astype(jnp.int32), axis=0)
    per_prefix = pages // PREFIXES
    pick = (page_prefix[None, None, :] == jnp.arange(PREFIXES, dtype=jnp.int32)[:, None, None]) & (
        page_rank[None, None, :] == jnp.arange(per_prefix, dtype=jnp.int32)[None, :, None]
    )
    page_order = jnp.sum(jnp.where(pick, page_ids[None, None, :], 0), axis=2).astype(jnp.int32)
    local_place = lax.dynamic_slice_in_dim(row_order, offset, local_rows).reshape(q_blocks, block)
    first_seen = jnp.min(local_place - position.reshape(q_blocks, block), axis=1)
    last_seen = jnp.max(local_place, axis=1)
    run_place = row_order.reshape(runs, block)
    run_low = jnp.min(run_place, axis=1)
    run_high = jnp.max(run_place, axis=1)
    run_visible = (run_low[None, :] <= last_seen[:, None]) & (run_high[None, :] >= first_seen[:, None])
    s_idx, s_cnt = visible_list(run_visible)

    seq_n_blocks = seq_n
    prefix_parts = (gathered_prefix.reshape(pages, block, 2 * HEAD),)
    gathered_suffix = seq_gather(stacked_kv, seq_n_blocks, 1)
    suffix_parts = (
        gathered_suffix.reshape(2, runs, block, HEAD),
        (request_all + PREFIXES).reshape(runs, 1, block).astype(jnp.int32),
        position_all.reshape(runs, 1, block).astype(jnp.int32),
    )
    out = block_attention(
        score_scale, (block_wants.astype(jnp.int32), page_order, s_idx, s_cnt), stacked_q, query_meta, prefix_parts, suffix_parts
    )
    attended = out.reshape(local_rows, group_size * HEAD)
    return (attended, new_keys, new_values)


def solution(mesh):
    return jax.shard_map(
        functools.partial(body, mesh.shape["seq"], mesh.shape["tp"]),
        mesh=mesh,
        in_specs=(
            P("seq", "tp"),
            P(),
            P(None, "tp"),
            P(None, "tp"),
            P(None, "tp"),
            P("seq", "tp"),
            P("seq", "tp"),
            P(),
            P(),
            P(),
            P(),
        ),
        out_specs=(P("seq", "tp"), P("seq", "tp"), P("seq", "tp")),
        check_vma=False,
    )
```

```python
import functools
import math

import jax
import jax.numpy as jnp
from jax import lax
from jax.sharding import PartitionSpec as P
from jax.experimental import pallas as pl
from jax.experimental.pallas import tpu as pltpu

HEAD = 128
PAGE = 128
PREFIXES = 4


ROPE_BASE = 5000000.0


def rotate(tensor_in, positions):
    head_dim = tensor_in.shape[-1]
    half_dim = head_dim // 2
    frequency = ROPE_BASE ** (-(jnp.arange(half_dim, dtype=jnp.float32) * 2.0 / head_dim))
    angles = positions.astype(jnp.float32)[:, None] * frequency[None, :]
    cosine = jnp.cos(angles)[:, None, :]
    sine_part = jnp.sin(angles)[:, None, :]
    first_half = tensor_in[..., :half_dim]
    second_half = tensor_in[..., half_dim:]
    return jnp.concatenate(
        [
            first_half * cosine - second_half * sine_part,
            second_half * cosine + first_half * sine_part,
        ],
        axis=-1,
    )


def locate(row_order, suffix_lengths, request_prefix):
    end_rows = jnp.cumsum(suffix_lengths)
    starts = end_rows - suffix_lengths
    numbers = jnp.arange(suffix_lengths.shape[0], dtype=jnp.int32)
    request = jnp.sum((row_order[:, None] >= end_rows[None, :]).astype(jnp.int32), axis=1)
    chosen = request[:, None] == numbers[None, :]
    position = row_order - jnp.sum(jnp.where(chosen, starts[None, :], 0), axis=1)
    wanted = jnp.sum(jnp.where(chosen, request_prefix[None, :], 0), axis=1)
    return (request, position, wanted)


def seq_gather_kernel(
    zs, xs, x_ref, o_ref, z_send, z_recv, r_send, r_recv, f_send, f_recv, c_send, c_recv, local_sem
):
    me = lax.axis_index("seq")
    core = me % 2
    chip = me // 2
    za = chip // xs
    xb = chip % xs
    right = lax.rem(xb + 1, xs)
    left = lax.rem(xb + xs - 1, xs)
    parts = x_ref.shape[0]
    mesh_id = pl.DeviceIdType.MESH

    def seq_of(z, x, c):
        return (z * xs + x) * 2 + c

    def signal(sem, target):
        pl.semaphore_signal(sem, inc=1, device_id={"seq": target}, device_id_type=mesh_id)

    barrier = pltpu.get_barrier_semaphore()

    def greet(k, carry):
        signal(barrier, seq_of(lax.rem(za + k, zs), xb, core))
        return carry

    lax.fori_loop(1, zs, greet, 0)
    signal(barrier, seq_of(za, right, core))
    signal(barrier, seq_of(za, left, core))
    signal(barrier, seq_of(za, xb, 1 - core))
    pl.semaphore_wait(barrier, zs + 2)

    local = pltpu.make_async_copy(x_ref, o_ref.at[:, za, xb, core], local_sem)
    local.start()

    def z_copy(a, peer_z, slot_z):
        return pltpu.make_async_remote_copy(
            src_ref=x_ref.at[a],
            dst_ref=o_ref.at[a, slot_z, xb, core],
            send_sem=z_send.at[a, peer_z],
            recv_sem=z_recv.at[a, slot_z],
            device_id={"seq": seq_of(peer_z, xb, core)},
            device_id_type=mesh_id,
        )

    def ring_slot(a, slot, side, group, target_x, sem_side, src=None):
        return pltpu.make_async_remote_copy(
            src_ref=o_ref.at[a, slot, group, core] if src is None else src,
            dst_ref=o_ref.at[a, slot, group, core],
            send_sem=r_send.at[a, side, slot],
            recv_sem=r_recv.at[a, sem_side, slot],
            device_id={"seq": seq_of(za, target_x, core)},
            device_id_type=mesh_id,
        )

    def z_start(k, carry):
        peer_z = lax.rem(za + k, zs)
        for a in range(parts):
            z_copy(a, peer_z, za).start()
        return carry

    lax.fori_loop(1, zs, z_start, 0)
    for a in range(parts):
        ring_slot(a, za, 0, xb, right, 0, x_ref.at[a]).start()
        ring_slot(a, za, 1, xb, left, 1, x_ref.at[a]).start()

    def z_finish(k, carry):
        peer_z = lax.rem(za + k, zs)
        for a in range(parts):
            copy = z_copy(a, peer_z, peer_z)
            copy.wait_recv()
            ring_slot(a, peer_z, 0, xb, right, 0).start()
            ring_slot(a, peer_z, 1, xb, left, 1).start()
            copy.wait_send()
        return carry

    lax.fori_loop(1, zs, z_finish, 0)
    local.wait()

    def hand(a, group, slot):
        return pltpu.make_async_remote_copy(
            src_ref=o_ref.at[a, :, group, slot],
            dst_ref=o_ref.at[a, :, group, slot],
            send_sem=c_send.at[a, group],
            recv_sem=c_recv.at[a, group],
            device_id={"seq": seq_of(za, xb, 1 - core)},
            device_id_type=mesh_id,
        )

    across = []
    for a in range(parts):
        across.append(hand(a, xb, core))
        across[-1].start()

    far = lax.rem(xb + 2, xs)

    def relay(a, slot, group, target_x, src_group):
        return pltpu.make_async_remote_copy(
            src_ref=o_ref.at[a, slot, src_group, core],
            dst_ref=o_ref.at[a, slot, group, core],
            send_sem=f_send.at[a, slot],
            recv_sem=f_recv.at[a, slot],
            device_id={"seq": seq_of(za, target_x, core)},
            device_id_type=mesh_id,
        )

    for slot in range(zs):
        ring_slot(0, slot, 0, left, right, 0).wait_recv()
        relay(0, slot, left, right, left).start()
        ring_slot(1, slot, 1, right, left, 1).wait_recv()
        relay(1, slot, right, left, right).start()
    for slot in range(zs):
        ring_slot(1, slot, 0, left, right, 0).wait_recv()
        ring_slot(0, slot, 1, right, left, 1).wait_recv()
    for a in range(parts):
        for group in (left, right):
            across.append(hand(a, group, core))
            across[-1].start()
    for a in range(parts):
        for slot in range(zs):
            ring_slot(a, slot, 0, xb, right, 0).wait_send()
            ring_slot(a, slot, 1, xb, left, 1).wait_send()
    for slot in range(zs):
        relay(0, slot, far, right, left).wait_recv()
        relay(1, slot, far, left, right).wait_recv()
    for slot in range(zs):
        relay(0, slot, left, right, left).wait_send()
        relay(1, slot, right, left, right).wait_send()
    for a in range(parts):
        across.append(hand(a, far, core))
        across[-1].start()

    for copy in across:
        copy.wait_send()
    for a in range(parts):
        for g in range(xs):
            hand(a, g, 1 - core).wait_recv()


def seq_gather(stacked, n, cid):
    parts, rows, cols = stacked.shape
    chips = n // 2
    xs = 4
    zs = chips // xs
    return pl.pallas_call(
        functools.partial(seq_gather_kernel, zs, xs),
        out_shape=jax.ShapeDtypeStruct((parts, zs, xs, 2, rows, cols), stacked.dtype),
        in_specs=[pl.BlockSpec(memory_space=pl.ANY)],
        out_specs=pl.BlockSpec(memory_space=pl.ANY),
        scratch_shapes=[
            pltpu.SemaphoreType.DMA((parts, zs)),
            pltpu.SemaphoreType.DMA((parts, zs)),
            pltpu.SemaphoreType.DMA((parts, 2, zs)),
            pltpu.SemaphoreType.DMA((parts, 2, zs)),
            pltpu.SemaphoreType.DMA((parts, zs)),
            pltpu.SemaphoreType.DMA((parts, zs)),
            pltpu.SemaphoreType.DMA((parts, xs)),
            pltpu.SemaphoreType.DMA((parts, xs)),
            pltpu.SemaphoreType.DMA,
        ],
        compiler_params=pltpu.CompilerParams(collective_id=cid, has_side_effects=True),
    )(stacked)


def tp_gather_kernel(ys, x_ref, o_ref, p_send, p_recv, r_send, r_recv, f_send, f_recv, local_sem):
    me = lax.axis_index("tp")
    yy = me // 2
    zh = me % 2
    right = lax.rem(yy + 1, ys)
    left = lax.rem(yy + ys - 1, ys)
    far = lax.rem(yy + 2, ys)
    width = x_ref.shape[1]
    mesh_id = pl.DeviceIdType.MESH

    def cols(y, h):
        return pl.ds(pl.multiple_of((y * 2 + h) * width, 128), width)

    def pair(y):
        return pl.ds(pl.multiple_of(y * 2 * width, 128), 2 * width)

    def signal(target):
        pl.semaphore_signal(barrier, inc=1, device_id={"tp": target}, device_id_type=mesh_id)

    barrier = pltpu.get_barrier_semaphore()
    signal(yy * 2 + 1 - zh)
    signal(right * 2 + zh)
    signal(left * 2 + zh)
    pl.semaphore_wait(barrier, 3)

    local = pltpu.make_async_copy(x_ref, o_ref.at[:, cols(yy, zh)], local_sem)
    local.start()
    to_partner = pltpu.make_async_remote_copy(
        src_ref=x_ref,
        dst_ref=o_ref.at[:, cols(yy, zh)],
        send_sem=p_send,
        recv_sem=p_recv,
        device_id={"tp": yy * 2 + 1 - zh},
        device_id_type=mesh_id,
    )
    to_partner.start()

    def ring(src, h, group, target, side):
        return pltpu.make_async_remote_copy(
            src_ref=src,
            dst_ref=o_ref.at[:, cols(group, h)],
            send_sem=r_send.at[side, h],
            recv_sem=r_recv.at[side, h],
            device_id={"tp": target * 2 + zh},
            device_id_type=mesh_id,
        )

    outgoing = [ring(x_ref, zh, yy, right, 0), ring(x_ref, zh, yy, left, 1)]
    for copy in outgoing:
        copy.start()
    pltpu.make_async_remote_copy(
        src_ref=x_ref,
        dst_ref=o_ref.at[:, cols(yy, 1 - zh)],
        send_sem=p_send,
        recv_sem=p_recv,
        device_id={"tp": yy * 2 + 1 - zh},
        device_id_type=mesh_id,
    ).wait_recv()
    partner_src = o_ref.at[:, cols(yy, 1 - zh)]
    later = [ring(partner_src, 1 - zh, yy, right, 0), ring(partner_src, 1 - zh, yy, left, 1)]
    for copy in later:
        copy.start()
    local.wait()
    to_partner.wait_send()
    pieces = f_send.shape[1]
    span = x_ref.shape[0] // pieces

    def relay(group, h, target, side, c):
        rows = pl.ds(c * span, span)
        return pltpu.make_async_remote_copy(
            src_ref=o_ref.at[rows, cols(group, h)],
            dst_ref=o_ref.at[rows, cols(group, h)],
            send_sem=f_send.at[side, c],
            recv_sem=f_recv.at[side, c],
            device_id={"tp": target * 2 + zh},
            device_id_type=mesh_id,
        )

    relays = []
    ring(x_ref, 0, left, right, 0).wait_recv()
    for c in range(pieces):
        relays.append(relay(left, 0, right, 0, c))
        relays[-1].start()
    ring(x_ref, 1, right, left, 1).wait_recv()
    for c in range(pieces):
        relays.append(relay(right, 1, left, 1, c))
        relays[-1].start()
    ring(x_ref, 1, left, right, 0).wait_recv()
    ring(x_ref, 0, right, left, 1).wait_recv()
    for copy in outgoing + later:
        copy.wait_send()
    for c in range(pieces):
        relay(far, 0, right, 0, c).wait_recv()
        relay(far, 1, left, 1, c).wait_recv()
    for copy in relays:
        copy.wait_send()


def tp_gather(block, n, cid):
    rows, width = block.shape
    return pl.pallas_call(
        functools.partial(tp_gather_kernel, n // 2),
        out_shape=jax.ShapeDtypeStruct((rows, width * n), block.dtype),
        in_specs=[pl.BlockSpec(memory_space=pl.ANY)],
        out_specs=pl.BlockSpec(memory_space=pl.ANY),
        scratch_shapes=[
            pltpu.SemaphoreType.DMA,
            pltpu.SemaphoreType.DMA,
            pltpu.SemaphoreType.DMA((2, 2)),
            pltpu.SemaphoreType.DMA((2, 2)),
            pltpu.SemaphoreType.DMA((2, 4)),
            pltpu.SemaphoreType.DMA((2, 4)),
            pltpu.SemaphoreType.DMA,
        ],
        compiler_params=pltpu.CompilerParams(collective_id=cid, has_side_effects=True),
    )(block)


def project_kernel(x_ref, g_ref, wq_ref, wk_ref, wv_ref, cos_ref, sin_ref, q_ref, k_ref, v_ref, kv_ref):
    x = x_ref[...].astype(jnp.float32)
    mean_sq = jnp.mean(x * x, axis=1, keepdims=True)
    gain = g_ref[...].astype(jnp.float32).reshape(1, x.shape[1])
    normed = (x * lax.rsqrt(mean_sq + 1e-05) * gain).astype(jnp.bfloat16)
    cosine = cos_ref[...]
    sine = sin_ref[...]

    def rotated(values):
        half = values.shape[1] // 2
        return values * cosine + pltpu.roll(values, half, 1) * sine

    queries = jnp.dot(normed, wq_ref[...], preferred_element_type=jnp.float32)
    for h in range(queries.shape[1] // HEAD):
        q_ref[0, :, h * HEAD:(h + 1) * HEAD] = rotated(queries[:, h * HEAD:(h + 1) * HEAD]).astype(q_ref.dtype)
    keys = jnp.dot(normed, wk_ref[...], preferred_element_type=jnp.float32)
    for h in range(keys.shape[1] // HEAD):
        part = rotated(keys[:, h * HEAD:(h + 1) * HEAD]).astype(k_ref.dtype)
        k_ref[:, h * HEAD:(h + 1) * HEAD] = part
        kv_ref[0, :, h * HEAD:(h + 1) * HEAD] = part
    values = jnp.dot(normed, wv_ref[...], preferred_element_type=jnp.float32).astype(v_ref.dtype)
    v_ref[...] = values
    kv_ref[1] = values


def project(gathered, norm_gain, w_query, w_key, w_value, cosine, sine, block):
    rows, width = gathered.shape
    steps = rows // block
    q_width = w_query.shape[1]
    kv_width = w_key.shape[1]
    whole = lambda i: (0, 0)
    return pl.pallas_call(
        project_kernel,
        grid=(steps,),
        out_shape=(
            jax.ShapeDtypeStruct((steps, block, q_width), jnp.bfloat16),
            jax.ShapeDtypeStruct((rows, kv_width), jnp.bfloat16),
            jax.ShapeDtypeStruct((rows, kv_width), jnp.bfloat16),
            jax.ShapeDtypeStruct((2, rows, kv_width), jnp.bfloat16),
        ),
        in_specs=[
            pl.BlockSpec((block, width), lambda i: (i, 0)),
            pl.BlockSpec(memory_space=pltpu.VMEM),
            pl.BlockSpec((width, q_width), whole),
            pl.BlockSpec((width, kv_width), whole),
            pl.BlockSpec((width, kv_width), whole),
            pl.BlockSpec((block, HEAD), lambda i: (i, 0)),
            pl.BlockSpec((block, HEAD), lambda i: (i, 0)),
        ],
        out_specs=(
            pl.BlockSpec((1, block, q_width), lambda i: (i, 0, 0)),
            pl.BlockSpec((block, kv_width), lambda i: (i, 0)),
            pl.BlockSpec((block, kv_width), lambda i: (i, 0)),
            pl.BlockSpec((2, block, kv_width), lambda i: (0, i, 0)),
        ),
        compiler_params=pltpu.CompilerParams(vmem_limit_bytes=60 * 1024 * 1024),
    )(gathered, norm_gain, w_query, w_key, w_value, cosine, sine)


def attention_kernel(
    scale, group_pages,
    wants, page_order, s_idx, s_cnt,
    q_ref, q_meta,
    p_ref,
    s_ref, s_tag, s_bound,
    o_ref, m_sc, l_sc, acc_sc, pm_sc, pl_sc, pacc_sc,
):
    prefixes, per_prefix = page_order.shape

    def update(m_ref, l_ref, acc_ref, score_list, value_list):
        run_max = m_ref[...]
        new_max = run_max
        for scores in score_list:
            new_max = jnp.maximum(new_max, jnp.max(scores, axis=1, keepdims=True))
        fade = jnp.exp(run_max - new_max)
        total = l_ref[...] * fade
        acc = acc_ref[...] * fade
        for scores, values in zip(score_list, value_list):
            weights = jnp.exp(scores - new_max)
            total = total + jnp.sum(weights, axis=1, keepdims=True)
            acc = acc + jnp.dot(weights.astype(jnp.bfloat16), values, preferred_element_type=jnp.float32)
        l_ref[...] = total
        acc_ref[...] = acc
        m_ref[...] = new_max

    for i in range(q_ref.shape[0]):
        m_sc[...] = jnp.full(m_sc.shape, -1e30, jnp.float32)
        l_sc[...] = jnp.zeros(l_sc.shape, jnp.float32)
        acc_sc[...] = jnp.zeros(acc_sc.shape, jnp.float32)
        heads = q_ref.shape[2] // q_ref.shape[1]
        size = q_ref.shape[1]
        query = jnp.concatenate([q_ref[i, :, h * size:(h + 1) * size] for h in range(heads)], axis=0)
        want = q_meta[0, i]
        req = q_meta[1, i]
        pos = q_meta[2, i]

        def score(keys):
            return lax.dot_general(
                query, keys, (((1,), (1,)), ((), ())), preferred_element_type=jnp.float32
            ) * scale

        for p in range(prefixes):
            @pl.when(wants[i, p] > 0)
            def _():
                pm_sc[...] = jnp.full(pm_sc.shape, -1e30, jnp.float32)
                pl_sc[...] = jnp.zeros(pl_sc.shape, jnp.float32)
                pacc_sc[...] = jnp.zeros(pacc_sc.shape, jnp.float32)

                def page_step(g, carry):
                    pages = [page_order[p, g * group_pages + j] for j in range(group_pages)]
                    blocks = [p_ref[b] for b in pages]
                    update(
                        pm_sc, pl_sc, pacc_sc,
                        [score(blk[:, :size]) for blk in blocks],
                        [blk[:, size:] for blk in blocks],
                    )
                    return carry

                lax.fori_loop(0, per_prefix // group_pages, page_step, 0)
                mine = want == p
                m_sc[...] = jnp.where(mine, pm_sc[...], m_sc[...])
                l_sc[...] = jnp.where(mine, pl_sc[...], l_sc[...])
                acc_sc[...] = jnp.where(mine, pacc_sc[...], acc_sc[...])

        def step(n, carry):
            b = s_idx[i, n]
            scores = score(s_ref[0, b])
            seen = (s_tag[b] == req) & (s_bound[b] <= pos)
            run_max = m_sc[...]
            new_max = jnp.maximum(
                run_max, jnp.max(jnp.where(seen, scores, -1e30), axis=1, keepdims=True)
            )
            weights = jnp.where(seen, jnp.exp(scores - new_max), 0.0)
            fade = jnp.exp(run_max - new_max)
            l_sc[...] = l_sc[...] * fade + jnp.sum(weights, axis=1, keepdims=True)
            acc_sc[...] = acc_sc[...] * fade + jnp.dot(
                weights.astype(jnp.bfloat16), s_ref[1, b], preferred_element_type=jnp.float32
            )
            m_sc[...] = new_max
            return carry

        lax.fori_loop(0, s_cnt[i], step, 0)
        result = (acc_sc[...] / l_sc[...]).astype(o_ref.dtype)
        for h in range(heads):
            o_ref[i, :, h * size:(h + 1) * size] = result[h * size:(h + 1) * size]


def block_attention(scale, lists, queries, query_meta, prefix_parts, suffix_parts):
    q_blocks, block_rows, q_width = queries.shape
    width = queries.shape[1]
    q_rows = q_width // width * block_rows
    smem = pl.BlockSpec(memory_space=pltpu.SMEM)
    vmem = pl.BlockSpec(memory_space=pltpu.VMEM)
    state = [
        pltpu.VMEM((q_rows, 1), jnp.float32),
        pltpu.VMEM((q_rows, 1), jnp.float32),
        pltpu.VMEM((q_rows, width), jnp.float32),
    ]
    return pl.pallas_call(
        functools.partial(attention_kernel, scale, 4),
        out_shape=jax.ShapeDtypeStruct((q_blocks, block_rows, q_width), jnp.bfloat16),
        in_specs=[smem] * 4 + [vmem] * 6,
        out_specs=vmem,
        scratch_shapes=state + state,
        compiler_params=pltpu.CompilerParams(vmem_limit_bytes=48 * 1024 * 1024),
    )(*lists, queries, *query_meta, *prefix_parts, *suffix_parts)


def visible_list(visible):
    count = visible.shape[1]
    ids = jnp.arange(count, dtype=jnp.int32)
    rank = jnp.sum((visible[:, :, None] & (ids[:, None] < ids[None, :])[None]).astype(jnp.int32), axis=1)
    pick = visible[:, None, :] & (rank[:, None, :] == ids[None, :, None])
    order = jnp.sum(jnp.where(pick, ids[None, None, :], 0), axis=2).astype(jnp.int32)
    return order, jnp.sum(visible.astype(jnp.int32), axis=1)


def body(
    seq_n,
    tp_n,
    hidden,
    norm_gain,
    w_query,
    w_key,
    w_value,
    prefix_keys,
    prefix_values,
    page_prefix,
    request_prefix,
    suffix_lengths,
    row_order,
):
    gathered_prefix = lax.all_gather(
        jnp.concatenate([prefix_keys, prefix_values], axis=1), "seq", axis=0, tiled=True
    )
    gathered = tp_gather(hidden, tp_n, 2)
    local_rows = gathered.shape[0]
    request_all, position_all, wanted_all = locate(row_order, suffix_lengths, request_prefix)
    offset = lax.axis_index("seq") * local_rows
    request = lax.dynamic_slice_in_dim(request_all, offset, local_rows)
    position = lax.dynamic_slice_in_dim(position_all, offset, local_rows)
    wanted = lax.dynamic_slice_in_dim(wanted_all, offset, local_rows)
    prefix_len = page_prefix.shape[0] * PAGE // PREFIXES
    rope_at = prefix_len + position
    q_heads = w_query.shape[1] // HEAD
    kv_heads = w_key.shape[1] // HEAD
    group_size = q_heads // kv_heads
    half_dim = HEAD // 2
    frequency = ROPE_BASE ** (-(jnp.arange(half_dim, dtype=jnp.float32) * 2.0 / HEAD))
    frequency_full = jnp.concatenate([frequency, frequency])
    sign_full = jnp.concatenate([-jnp.ones((half_dim,), jnp.float32), jnp.ones((half_dim,), jnp.float32)])
    angles = rope_at.astype(jnp.float32)[:, None] * frequency_full[None, :]
    cos_full = jnp.cos(angles)
    sin_signed = jnp.sin(angles) * sign_full[None, :]
    stacked_q, new_keys, new_values, stacked_kv = project(
        gathered, norm_gain, w_query, w_key, w_value, cos_full, sin_signed, PAGE
    )
    score_scale = 1.0 / math.sqrt(HEAD)
    block = PAGE
    q_blocks = local_rows // block
    pages = page_prefix.shape[0]
    runs = row_order.shape[0] // block

    def per_query(values):
        kinds = values.shape[0]
        spread = jnp.broadcast_to(values.reshape(kinds, q_blocks, 1, block), (kinds, q_blocks, group_size, block))
        return spread.reshape(kinds, q_blocks, group_size * block, 1).astype(jnp.int32)

    query_meta = (per_query(jnp.stack([wanted, request + PREFIXES, position])),)
    want_blocks = wanted.reshape(q_blocks, block)
    block_wants = jnp.any(
        want_blocks[:, :, None] == jnp.arange(PREFIXES, dtype=jnp.int32)[None, None, :], axis=1
    )
    page_ids = jnp.arange(pages, dtype=jnp.int32)
    same = (page_prefix[:, None] == page_prefix[None, :]) & (page_ids[:, None] < page_ids[None, :])
    page_rank = jnp.sum(same.astype(jnp.int32), axis=0)
    per_prefix = pages // PREFIXES
    pick = (page_prefix[None, None, :] == jnp.arange(PREFIXES, dtype=jnp.int32)[:, None, None]) & (
        page_rank[None, None, :] == jnp.arange(per_prefix, dtype=jnp.int32)[None, :, None]
    )
    page_order = jnp.sum(jnp.where(pick, page_ids[None, None, :], 0), axis=2).astype(jnp.int32)
    local_place = lax.dynamic_slice_in_dim(row_order, offset, local_rows).reshape(q_blocks, block)
    first_seen = jnp.min(local_place - position.reshape(q_blocks, block), axis=1)
    last_seen = jnp.max(local_place, axis=1)
    run_place = row_order.reshape(runs, block)
    run_low = jnp.min(run_place, axis=1)
    run_high = jnp.max(run_place, axis=1)
    run_visible = (run_low[None, :] <= last_seen[:, None]) & (run_high[None, :] >= first_seen[:, None])
    s_idx, s_cnt = visible_list(run_visible)

    seq_n_blocks = seq_n
    prefix_parts = (gathered_prefix.reshape(pages, block, 2 * HEAD),)
    gathered_suffix = seq_gather(stacked_kv, seq_n_blocks, 1)
    suffix_parts = (
        gathered_suffix.reshape(2, runs, block, HEAD),
        (request_all + PREFIXES).reshape(runs, 1, block).astype(jnp.int32),
        position_all.reshape(runs, 1, block).astype(jnp.int32),
    )
    out = block_attention(
        score_scale, (block_wants.astype(jnp.int32), page_order, s_idx, s_cnt), stacked_q, query_meta, prefix_parts, suffix_parts
    )
    attended = out.reshape(local_rows, group_size * HEAD)
    return (attended, new_keys, new_values)


def solution(mesh):
    return jax.shard_map(
        functools.partial(body, mesh.shape["seq"], mesh.shape["tp"]),
        mesh=mesh,
        in_specs=(
            P("seq", "tp"),
            P(),
            P(None, "tp"),
            P(None, "tp"),
            P(None, "tp"),
            P("seq", "tp"),
            P("seq", "tp"),
            P(),
            P(),
            P(),
            P(),
        ),
        out_specs=(P("seq", "tp"), P("seq", "tp"), P("seq", "tp")),
        check_vma=False,
    )
```

```python
import functools
import math

import jax
import jax.numpy as jnp
from jax import lax
from jax.sharding import PartitionSpec as P
from jax.experimental import pallas as pl
from jax.experimental.pallas import tpu as pltpu

HEAD = 128
PAGE = 128
PREFIXES = 4


ROPE_BASE = 5000000.0


def rotate(tensor_in, positions):
    head_dim = tensor_in.shape[-1]
    half_dim = head_dim // 2
    frequency = ROPE_BASE ** (-(jnp.arange(half_dim, dtype=jnp.float32) * 2.0 / head_dim))
    angles = positions.astype(jnp.float32)[:, None] * frequency[None, :]
    cosine = jnp.cos(angles)[:, None, :]
    sine_part = jnp.sin(angles)[:, None, :]
    first_half = tensor_in[..., :half_dim]
    second_half = tensor_in[..., half_dim:]
    return jnp.concatenate(
        [
            first_half * cosine - second_half * sine_part,
            second_half * cosine + first_half * sine_part,
        ],
        axis=-1,
    )


def locate(row_order, suffix_lengths, request_prefix):
    end_rows = jnp.cumsum(suffix_lengths)
    starts = end_rows - suffix_lengths
    numbers = jnp.arange(suffix_lengths.shape[0], dtype=jnp.int32)
    request = jnp.sum((row_order[:, None] >= end_rows[None, :]).astype(jnp.int32), axis=1)
    chosen = request[:, None] == numbers[None, :]
    position = row_order - jnp.sum(jnp.where(chosen, starts[None, :], 0), axis=1)
    wanted = jnp.sum(jnp.where(chosen, request_prefix[None, :], 0), axis=1)
    return (request, position, wanted)


def seq_gather_kernel(
    zs, xs, x_ref, o_ref, z_send, z_recv, r_send, r_recv, f_send, f_recv, c_send, c_recv, local_sem
):
    me = lax.axis_index("seq")
    core = me % 2
    chip = me // 2
    za = chip // xs
    xb = chip % xs
    right = lax.rem(xb + 1, xs)
    left = lax.rem(xb + xs - 1, xs)
    parts = x_ref.shape[0]
    mesh_id = pl.DeviceIdType.MESH

    def seq_of(z, x, c):
        return (z * xs + x) * 2 + c

    def signal(sem, target):
        pl.semaphore_signal(sem, inc=1, device_id={"seq": target}, device_id_type=mesh_id)

    barrier = pltpu.get_barrier_semaphore()

    def greet(k, carry):
        signal(barrier, seq_of(lax.rem(za + k, zs), xb, core))
        return carry

    lax.fori_loop(1, zs, greet, 0)
    signal(barrier, seq_of(za, right, core))
    signal(barrier, seq_of(za, left, core))
    signal(barrier, seq_of(za, xb, 1 - core))
    pl.semaphore_wait(barrier, zs + 2)

    local = pltpu.make_async_copy(x_ref, o_ref.at[:, za, xb, core], local_sem)
    local.start()

    def z_copy(a, peer_z, slot_z):
        return pltpu.make_async_remote_copy(
            src_ref=x_ref.at[a],
            dst_ref=o_ref.at[a, slot_z, xb, core],
            send_sem=z_send.at[a, peer_z],
            recv_sem=z_recv.at[a, slot_z],
            device_id={"seq": seq_of(peer_z, xb, core)},
            device_id_type=mesh_id,
        )

    def ring_slot(a, slot, side, group, target_x, sem_side, src=None):
        return pltpu.make_async_remote_copy(
            src_ref=o_ref.at[a, slot, group, core] if src is None else src,
            dst_ref=o_ref.at[a, slot, group, core],
            send_sem=r_send.at[a, side, slot],
            recv_sem=r_recv.at[a, sem_side, slot],
            device_id={"seq": seq_of(za, target_x, core)},
            device_id_type=mesh_id,
        )

    def z_start(k, carry):
        peer_z = lax.rem(za + k, zs)
        for a in range(parts):
            z_copy(a, peer_z, za).start()
        return carry

    lax.fori_loop(1, zs, z_start, 0)
    for a in range(parts):
        ring_slot(a, za, 0, xb, right, 0, x_ref.at[a]).start()
        ring_slot(a, za, 1, xb, left, 1, x_ref.at[a]).start()

    def z_finish(k, carry):
        peer_z = lax.rem(za + k, zs)
        for a in range(parts):
            copy = z_copy(a, peer_z, peer_z)
            copy.wait_recv()
            ring_slot(a, peer_z, 0, xb, right, 0).start()
            ring_slot(a, peer_z, 1, xb, left, 1).start()
            copy.wait_send()
        return carry

    lax.fori_loop(1, zs, z_finish, 0)
    local.wait()

    def hand(a, group, slot):
        return pltpu.make_async_remote_copy(
            src_ref=o_ref.at[a, :, group, slot],
            dst_ref=o_ref.at[a, :, group, slot],
            send_sem=c_send.at[a, group],
            recv_sem=c_recv.at[a, group],
            device_id={"seq": seq_of(za, xb, 1 - core)},
            device_id_type=mesh_id,
        )

    across = []
    for a in range(parts):
        across.append(hand(a, xb, core))
        across[-1].start()

    far = lax.rem(xb + 2, xs)

    def relay(a, slot, group, target_x, src_group):
        return pltpu.make_async_remote_copy(
            src_ref=o_ref.at[a, slot, src_group, core],
            dst_ref=o_ref.at[a, slot, group, core],
            send_sem=f_send.at[a, slot],
            recv_sem=f_recv.at[a, slot],
            device_id={"seq": seq_of(za, target_x, core)},
            device_id_type=mesh_id,
        )

    for slot in range(zs):
        ring_slot(0, slot, 0, left, right, 0).wait_recv()
        relay(0, slot, left, right, left).start()
        ring_slot(1, slot, 1, right, left, 1).wait_recv()
        relay(1, slot, right, left, right).start()
    for slot in range(zs):
        ring_slot(1, slot, 0, left, right, 0).wait_recv()
        ring_slot(0, slot, 1, right, left, 1).wait_recv()
    for a in range(parts):
        for group in (left, right):
            across.append(hand(a, group, core))
            across[-1].start()
    for a in range(parts):
        for slot in range(zs):
            ring_slot(a, slot, 0, xb, right, 0).wait_send()
            ring_slot(a, slot, 1, xb, left, 1).wait_send()
    for slot in range(zs):
        relay(0, slot, far, right, left).wait_recv()
        relay(1, slot, far, left, right).wait_recv()
    for slot in range(zs):
        relay(0, slot, left, right, left).wait_send()
        relay(1, slot, right, left, right).wait_send()
    for a in range(parts):
        across.append(hand(a, far, core))
        across[-1].start()

    for copy in across:
        copy.wait_send()
    for a in range(parts):
        for g in range(xs):
            hand(a, g, 1 - core).wait_recv()


def seq_gather(stacked, n, cid):
    parts, rows, cols = stacked.shape
    chips = n // 2
    xs = 4
    zs = chips // xs
    return pl.pallas_call(
        functools.partial(seq_gather_kernel, zs, xs),
        out_shape=jax.ShapeDtypeStruct((parts, zs, xs, 2, rows, cols), stacked.dtype),
        in_specs=[pl.BlockSpec(memory_space=pl.ANY)],
        out_specs=pl.BlockSpec(memory_space=pl.ANY),
        scratch_shapes=[
            pltpu.SemaphoreType.DMA((parts, zs)),
            pltpu.SemaphoreType.DMA((parts, zs)),
            pltpu.SemaphoreType.DMA((parts, 2, zs)),
            pltpu.SemaphoreType.DMA((parts, 2, zs)),
            pltpu.SemaphoreType.DMA((parts, zs)),
            pltpu.SemaphoreType.DMA((parts, zs)),
            pltpu.SemaphoreType.DMA((parts, xs)),
            pltpu.SemaphoreType.DMA((parts, xs)),
            pltpu.SemaphoreType.DMA,
        ],
        compiler_params=pltpu.CompilerParams(collective_id=cid, has_side_effects=True),
    )(stacked)


def tp_gather_kernel(ys, x_ref, o_ref, p_send, p_recv, r_send, r_recv, f_send, f_recv, local_sem):
    me = lax.axis_index("tp")
    yy = me // 2
    zh = me % 2
    right = lax.rem(yy + 1, ys)
    left = lax.rem(yy + ys - 1, ys)
    far = lax.rem(yy + 2, ys)
    width = x_ref.shape[1]
    mesh_id = pl.DeviceIdType.MESH

    def cols(y, h):
        return pl.ds(pl.multiple_of((y * 2 + h) * width, 128), width)

    def pair(y):
        return pl.ds(pl.multiple_of(y * 2 * width, 128), 2 * width)

    def signal(target):
        pl.semaphore_signal(barrier, inc=1, device_id={"tp": target}, device_id_type=mesh_id)

    barrier = pltpu.get_barrier_semaphore()
    signal(yy * 2 + 1 - zh)
    signal(right * 2 + zh)
    signal(left * 2 + zh)
    pl.semaphore_wait(barrier, 3)

    local = pltpu.make_async_copy(x_ref, o_ref.at[:, cols(yy, zh)], local_sem)
    local.start()
    to_partner = pltpu.make_async_remote_copy(
        src_ref=x_ref,
        dst_ref=o_ref.at[:, cols(yy, zh)],
        send_sem=p_send,
        recv_sem=p_recv,
        device_id={"tp": yy * 2 + 1 - zh},
        device_id_type=mesh_id,
    )
    to_partner.start()

    def ring(src, h, group, target, side):
        return pltpu.make_async_remote_copy(
            src_ref=src,
            dst_ref=o_ref.at[:, cols(group, h)],
            send_sem=r_send.at[side, h],
            recv_sem=r_recv.at[side, h],
            device_id={"tp": target * 2 + zh},
            device_id_type=mesh_id,
        )

    outgoing = [ring(x_ref, zh, yy, right, 0), ring(x_ref, zh, yy, left, 1)]
    for copy in outgoing:
        copy.start()
    pltpu.make_async_remote_copy(
        src_ref=x_ref,
        dst_ref=o_ref.at[:, cols(yy, 1 - zh)],
        send_sem=p_send,
        recv_sem=p_recv,
        device_id={"tp": yy * 2 + 1 - zh},
        device_id_type=mesh_id,
    ).wait_recv()
    partner_src = o_ref.at[:, cols(yy, 1 - zh)]
    later = [ring(partner_src, 1 - zh, yy, right, 0), ring(partner_src, 1 - zh, yy, left, 1)]
    for copy in later:
        copy.start()
    local.wait()
    to_partner.wait_send()
    pieces = f_send.shape[1]
    span = x_ref.shape[0] // pieces

    def relay(group, h, target, side, c):
        rows = pl.ds(c * span, span)
        return pltpu.make_async_remote_copy(
            src_ref=o_ref.at[rows, cols(group, h)],
            dst_ref=o_ref.at[rows, cols(group, h)],
            send_sem=f_send.at[side, c],
            recv_sem=f_recv.at[side, c],
            device_id={"tp": target * 2 + zh},
            device_id_type=mesh_id,
        )

    relays = []
    ring(x_ref, 0, left, right, 0).wait_recv()
    for c in range(pieces):
        relays.append(relay(left, 0, right, 0, c))
        relays[-1].start()
    ring(x_ref, 1, right, left, 1).wait_recv()
    for c in range(pieces):
        relays.append(relay(right, 1, left, 1, c))
        relays[-1].start()
    ring(x_ref, 1, left, right, 0).wait_recv()
    ring(x_ref, 0, right, left, 1).wait_recv()
    for copy in outgoing + later:
        copy.wait_send()
    for c in range(pieces):
        relay(far, 0, right, 0, c).wait_recv()
        relay(far, 1, left, 1, c).wait_recv()
    for copy in relays:
        copy.wait_send()


def tp_gather(block, n, cid):
    rows, width = block.shape
    return pl.pallas_call(
        functools.partial(tp_gather_kernel, n // 2),
        out_shape=jax.ShapeDtypeStruct((rows, width * n), block.dtype),
        in_specs=[pl.BlockSpec(memory_space=pl.ANY)],
        out_specs=pl.BlockSpec(memory_space=pl.ANY),
        scratch_shapes=[
            pltpu.SemaphoreType.DMA,
            pltpu.SemaphoreType.DMA,
            pltpu.SemaphoreType.DMA((2, 2)),
            pltpu.SemaphoreType.DMA((2, 2)),
            pltpu.SemaphoreType.DMA((2, 4)),
            pltpu.SemaphoreType.DMA((2, 4)),
            pltpu.SemaphoreType.DMA,
        ],
        compiler_params=pltpu.CompilerParams(collective_id=cid, has_side_effects=True),
    )(block)


def project_kernel(x_ref, g_ref, wq_ref, wk_ref, wv_ref, cos_ref, sin_ref, q_ref, k_ref, v_ref, kv_ref):
    x = x_ref[...].astype(jnp.float32)
    mean_sq = jnp.mean(x * x, axis=1, keepdims=True)
    gain = g_ref[...].astype(jnp.float32).reshape(1, x.shape[1])
    normed = (x * lax.rsqrt(mean_sq + 1e-05) * gain).astype(jnp.bfloat16)
    cosine = cos_ref[...]
    sine = sin_ref[...]

    def rotated(values):
        half = values.shape[1] // 2
        return values * cosine + pltpu.roll(values, half, 1) * sine

    queries = jnp.dot(normed, wq_ref[...], preferred_element_type=jnp.float32)
    for h in range(queries.shape[1] // HEAD):
        q_ref[0, :, h * HEAD:(h + 1) * HEAD] = rotated(queries[:, h * HEAD:(h + 1) * HEAD]).astype(q_ref.dtype)
    keys = jnp.dot(normed, wk_ref[...], preferred_element_type=jnp.float32)
    for h in range(keys.shape[1] // HEAD):
        part = rotated(keys[:, h * HEAD:(h + 1) * HEAD]).astype(k_ref.dtype)
        k_ref[:, h * HEAD:(h + 1) * HEAD] = part
        kv_ref[0, :, h * HEAD:(h + 1) * HEAD] = part
    values = jnp.dot(normed, wv_ref[...], preferred_element_type=jnp.float32).astype(v_ref.dtype)
    v_ref[...] = values
    kv_ref[1] = values


def project(gathered, norm_gain, w_query, w_key, w_value, cosine, sine, block):
    rows, width = gathered.shape
    steps = rows // block
    q_width = w_query.shape[1]
    kv_width = w_key.shape[1]
    whole = lambda i: (0, 0)
    return pl.pallas_call(
        project_kernel,
        grid=(steps,),
        out_shape=(
            jax.ShapeDtypeStruct((steps, block, q_width), jnp.bfloat16),
            jax.ShapeDtypeStruct((rows, kv_width), jnp.bfloat16),
            jax.ShapeDtypeStruct((rows, kv_width), jnp.bfloat16),
            jax.ShapeDtypeStruct((2, rows, kv_width), jnp.bfloat16),
        ),
        in_specs=[
            pl.BlockSpec((block, width), lambda i: (i, 0)),
            pl.BlockSpec(memory_space=pltpu.VMEM),
            pl.BlockSpec((width, q_width), whole),
            pl.BlockSpec((width, kv_width), whole),
            pl.BlockSpec((width, kv_width), whole),
            pl.BlockSpec((block, HEAD), lambda i: (i, 0)),
            pl.BlockSpec((block, HEAD), lambda i: (i, 0)),
        ],
        out_specs=(
            pl.BlockSpec((1, block, q_width), lambda i: (i, 0, 0)),
            pl.BlockSpec((block, kv_width), lambda i: (i, 0)),
            pl.BlockSpec((block, kv_width), lambda i: (i, 0)),
            pl.BlockSpec((2, block, kv_width), lambda i: (0, i, 0)),
        ),
        compiler_params=pltpu.CompilerParams(vmem_limit_bytes=60 * 1024 * 1024),
    )(gathered, norm_gain, w_query, w_key, w_value, cosine, sine)


def attention_kernel(
    scale, group_pages,
    wants, page_order, s_idx, s_cnt,
    q_ref, q_meta,
    p_ref,
    s_ref, s_tag, s_bound,
    o_ref, m_sc, l_sc, acc_sc, pm_sc, pl_sc, pacc_sc,
):
    prefixes, per_prefix = page_order.shape

    def update(m_ref, l_ref, acc_ref, score_list, value_list):
        run_max = m_ref[...]
        new_max = run_max
        for scores in score_list:
            new_max = jnp.maximum(new_max, jnp.max(scores, axis=1, keepdims=True))
        fade = jnp.exp(run_max - new_max)
        total = l_ref[...] * fade
        acc = acc_ref[...] * fade
        for scores, values in zip(score_list, value_list):
            weights = jnp.exp(scores - new_max)
            total = total + jnp.sum(weights, axis=1, keepdims=True)
            acc = acc + jnp.dot(weights.astype(jnp.bfloat16), values, preferred_element_type=jnp.float32)
        l_ref[...] = total
        acc_ref[...] = acc
        m_ref[...] = new_max

    for i in range(q_ref.shape[0]):
        m_sc[...] = jnp.full(m_sc.shape, -1e30, jnp.float32)
        l_sc[...] = jnp.zeros(l_sc.shape, jnp.float32)
        acc_sc[...] = jnp.zeros(acc_sc.shape, jnp.float32)
        heads = q_ref.shape[2] // q_ref.shape[1]
        size = q_ref.shape[1]
        query = jnp.concatenate([q_ref[i, :, h * size:(h + 1) * size] for h in range(heads)], axis=0)
        want = q_meta[0, i]
        req = q_meta[1, i]
        pos = q_meta[2, i]

        def score(keys):
            return lax.dot_general(
                query, keys, (((1,), (1,)), ((), ())), preferred_element_type=jnp.float32
            ) * scale

        for p in range(prefixes):
            @pl.when(wants[i, p] > 0)
            def _():
                pm_sc[...] = jnp.full(pm_sc.shape, -1e30, jnp.float32)
                pl_sc[...] = jnp.zeros(pl_sc.shape, jnp.float32)
                pacc_sc[...] = jnp.zeros(pacc_sc.shape, jnp.float32)

                def page_step(g, carry):
                    pages = [page_order[p, g * group_pages + j] for j in range(group_pages)]
                    blocks = [p_ref[b] for b in pages]
                    update(
                        pm_sc, pl_sc, pacc_sc,
                        [score(blk[:, :size]) for blk in blocks],
                        [blk[:, size:] for blk in blocks],
                    )
                    return carry

                lax.fori_loop(0, per_prefix // group_pages, page_step, 0)
                mine = want == p
                m_sc[...] = jnp.where(mine, pm_sc[...], m_sc[...])
                l_sc[...] = jnp.where(mine, pl_sc[...], l_sc[...])
                acc_sc[...] = jnp.where(mine, pacc_sc[...], acc_sc[...])

        def step(n, carry):
            b = s_idx[i, n]
            scores = score(s_ref[0, b])
            seen = (s_tag[b] == req) & (s_bound[b] <= pos)
            run_max = m_sc[...]
            new_max = jnp.maximum(
                run_max, jnp.max(jnp.where(seen, scores, -1e30), axis=1, keepdims=True)
            )
            weights = jnp.where(seen, jnp.exp(scores - new_max), 0.0)
            fade = jnp.exp(run_max - new_max)
            l_sc[...] = l_sc[...] * fade + jnp.sum(weights, axis=1, keepdims=True)
            acc_sc[...] = acc_sc[...] * fade + jnp.dot(
                weights.astype(jnp.bfloat16), s_ref[1, b], preferred_element_type=jnp.float32
            )
            m_sc[...] = new_max
            return carry

        lax.fori_loop(0, s_cnt[i], step, 0)
        result = (acc_sc[...] / l_sc[...]).astype(o_ref.dtype)
        for h in range(heads):
            o_ref[i, :, h * size:(h + 1) * size] = result[h * size:(h + 1) * size]


def block_attention(scale, lists, queries, query_meta, prefix_parts, suffix_parts):
    q_blocks, block_rows, q_width = queries.shape
    width = queries.shape[1]
    q_rows = q_width // width * block_rows
    smem = pl.BlockSpec(memory_space=pltpu.SMEM)
    vmem = pl.BlockSpec(memory_space=pltpu.VMEM)
    state = [
        pltpu.VMEM((q_rows, 1), jnp.float32),
        pltpu.VMEM((q_rows, 1), jnp.float32),
        pltpu.VMEM((q_rows, width), jnp.float32),
    ]
    return pl.pallas_call(
        functools.partial(attention_kernel, scale, 4),
        out_shape=jax.ShapeDtypeStruct((q_blocks, block_rows, q_width), jnp.bfloat16),
        in_specs=[smem] * 4 + [vmem] * 6,
        out_specs=vmem,
        scratch_shapes=state + state,
        compiler_params=pltpu.CompilerParams(vmem_limit_bytes=48 * 1024 * 1024),
    )(*lists, queries, *query_meta, *prefix_parts, *suffix_parts)


def visible_list(visible):
    count = visible.shape[1]
    ids = jnp.arange(count, dtype=jnp.int32)
    rank = jnp.sum((visible[:, :, None] & (ids[:, None] < ids[None, :])[None]).astype(jnp.int32), axis=1)
    pick = visible[:, None, :] & (rank[:, None, :] == ids[None, :, None])
    order = jnp.sum(jnp.where(pick, ids[None, None, :], 0), axis=2).astype(jnp.int32)
    return order, jnp.sum(visible.astype(jnp.int32), axis=1)


def body(
    seq_n,
    tp_n,
    hidden,
    norm_gain,
    w_query,
    w_key,
    w_value,
    prefix_keys,
    prefix_values,
    page_prefix,
    request_prefix,
    suffix_lengths,
    row_order,
):
    gathered_prefix = lax.all_gather(
        jnp.concatenate([prefix_keys, prefix_values], axis=1), "seq", axis=0, tiled=True
    )
    gathered = tp_gather(hidden, tp_n, 2)
    local_rows = gathered.shape[0]
    request_all, position_all, wanted_all = locate(row_order, suffix_lengths, request_prefix)
    offset = lax.axis_index("seq") * local_rows
    request = lax.dynamic_slice_in_dim(request_all, offset, local_rows)
    position = lax.dynamic_slice_in_dim(position_all, offset, local_rows)
    wanted = lax.dynamic_slice_in_dim(wanted_all, offset, local_rows)
    prefix_len = page_prefix.shape[0] * PAGE // PREFIXES
    rope_at = prefix_len + position
    q_heads = w_query.shape[1] // HEAD
    kv_heads = w_key.shape[1] // HEAD
    group_size = q_heads // kv_heads
    half_dim = HEAD // 2
    frequency = ROPE_BASE ** (-(jnp.arange(half_dim, dtype=jnp.float32) * 2.0 / HEAD))
    angles = rope_at.astype(jnp.float32)[:, None] * frequency[None, :]
    cosine = jnp.cos(angles)
    sine_part = jnp.sin(angles)
    cos_full = jnp.concatenate([cosine, cosine], axis=1)
    sin_signed = jnp.concatenate([-sine_part, sine_part], axis=1)
    stacked_q, new_keys, new_values, stacked_kv = project(
        gathered, norm_gain, w_query, w_key, w_value, cos_full, sin_signed, PAGE
    )
    score_scale = 1.0 / math.sqrt(HEAD)
    block = PAGE
    q_blocks = local_rows // block
    pages = page_prefix.shape[0]
    runs = row_order.shape[0] // block

    def per_query(values):
        kinds = values.shape[0]
        spread = jnp.broadcast_to(values.reshape(kinds, q_blocks, 1, block), (kinds, q_blocks, group_size, block))
        return spread.reshape(kinds, q_blocks, group_size * block, 1).astype(jnp.int32)

    query_meta = (per_query(jnp.stack([wanted, request + PREFIXES, position])),)
    want_blocks = wanted.reshape(q_blocks, block)
    block_wants = jnp.any(
        want_blocks[:, :, None] == jnp.arange(PREFIXES, dtype=jnp.int32)[None, None, :], axis=1
    )
    page_ids = jnp.arange(pages, dtype=jnp.int32)
    same = (page_prefix[:, None] == page_prefix[None, :]) & (page_ids[:, None] < page_ids[None, :])
    page_rank = jnp.sum(same.astype(jnp.int32), axis=0)
    per_prefix = pages // PREFIXES
    pick = (page_prefix[None, None, :] == jnp.arange(PREFIXES, dtype=jnp.int32)[:, None, None]) & (
        page_rank[None, None, :] == jnp.arange(per_prefix, dtype=jnp.int32)[None, :, None]
    )
    page_order = jnp.sum(jnp.where(pick, page_ids[None, None, :], 0), axis=2).astype(jnp.int32)
    local_place = lax.dynamic_slice_in_dim(row_order, offset, local_rows).reshape(q_blocks, block)
    first_seen = jnp.min(local_place - position.reshape(q_blocks, block), axis=1)
    last_seen = jnp.max(local_place, axis=1)
    run_place = row_order.reshape(runs, block)
    run_low = jnp.min(run_place, axis=1)
    run_high = jnp.max(run_place, axis=1)
    run_visible = (run_low[None, :] <= last_seen[:, None]) & (run_high[None, :] >= first_seen[:, None])
    s_idx, s_cnt = visible_list(run_visible)

    seq_n_blocks = seq_n
    prefix_parts = (gathered_prefix.reshape(pages, block, 2 * HEAD),)
    gathered_suffix = seq_gather(stacked_kv, seq_n_blocks, 1)
    suffix_parts = (
        gathered_suffix.reshape(2, runs, block, HEAD),
        (request_all + PREFIXES).reshape(runs, 1, block).astype(jnp.int32),
        position_all.reshape(runs, 1, block).astype(jnp.int32),
    )
    out = block_attention(
        score_scale, (block_wants.astype(jnp.int32), page_order, s_idx, s_cnt), stacked_q, query_meta, prefix_parts, suffix_parts
    )
    attended = out.reshape(local_rows, group_size * HEAD)
    return (attended, new_keys, new_values)


def solution(mesh):
    return jax.shard_map(
        functools.partial(body, mesh.shape["seq"], mesh.shape["tp"]),
        mesh=mesh,
        in_specs=(
            P("seq", "tp"),
            P(),
            P(None, "tp"),
            P(None, "tp"),
            P(None, "tp"),
            P("seq", "tp"),
            P("seq", "tp"),
            P(),
            P(),
            P(),
            P(),
        ),
        out_specs=(P("seq", "tp"), P("seq", "tp"), P("seq", "tp")),
        check_vma=False,
    )
```

```python
import functools
import math

import jax
import jax.numpy as jnp
from jax import lax
from jax.sharding import PartitionSpec as P
from jax.experimental import pallas as pl
from jax.experimental.pallas import tpu as pltpu

HEAD = 128
PAGE = 128
PREFIXES = 4


ROPE_BASE = 5000000.0


def rotate(tensor_in, positions):
    head_dim = tensor_in.shape[-1]
    half_dim = head_dim // 2
    frequency = ROPE_BASE ** (-(jnp.arange(half_dim, dtype=jnp.float32) * 2.0 / head_dim))
    angles = positions.astype(jnp.float32)[:, None] * frequency[None, :]
    cosine = jnp.cos(angles)[:, None, :]
    sine_part = jnp.sin(angles)[:, None, :]
    first_half = tensor_in[..., :half_dim]
    second_half = tensor_in[..., half_dim:]
    return jnp.concatenate(
        [
            first_half * cosine - second_half * sine_part,
            second_half * cosine + first_half * sine_part,
        ],
        axis=-1,
    )


def locate(row_order, suffix_lengths, request_prefix):
    end_rows = jnp.cumsum(suffix_lengths)
    starts = end_rows - suffix_lengths
    numbers = jnp.arange(suffix_lengths.shape[0], dtype=jnp.int32)
    request = jnp.sum((row_order[:, None] >= end_rows[None, :]).astype(jnp.int32), axis=1)
    chosen = request[:, None] == numbers[None, :]
    position = row_order - jnp.sum(jnp.where(chosen, starts[None, :], 0), axis=1)
    wanted = jnp.sum(jnp.where(chosen, request_prefix[None, :], 0), axis=1)
    return (request, position, wanted)


def seq_gather_kernel(
    zs, xs, x_ref, o_ref, z_send, z_recv, r_send, r_recv, f_send, f_recv, c_send, c_recv, local_sem
):
    me = lax.axis_index("seq")
    core = me % 2
    chip = me // 2
    za = chip // xs
    xb = chip % xs
    right = lax.rem(xb + 1, xs)
    left = lax.rem(xb + xs - 1, xs)
    parts = x_ref.shape[0]
    mesh_id = pl.DeviceIdType.MESH

    def seq_of(z, x, c):
        return (z * xs + x) * 2 + c

    def signal(sem, target):
        pl.semaphore_signal(sem, inc=1, device_id={"seq": target}, device_id_type=mesh_id)

    barrier = pltpu.get_barrier_semaphore()

    def greet(k, carry):
        signal(barrier, seq_of(lax.rem(za + k, zs), xb, core))
        return carry

    lax.fori_loop(1, zs, greet, 0)
    signal(barrier, seq_of(za, right, core))
    signal(barrier, seq_of(za, left, core))
    signal(barrier, seq_of(za, xb, 1 - core))
    pl.semaphore_wait(barrier, zs + 2)

    local = pltpu.make_async_copy(x_ref, o_ref.at[:, za, xb, core], local_sem)
    local.start()

    def z_copy(a, peer_z, slot_z):
        return pltpu.make_async_remote_copy(
            src_ref=x_ref.at[a],
            dst_ref=o_ref.at[a, slot_z, xb, core],
            send_sem=z_send.at[a, peer_z],
            recv_sem=z_recv.at[a, slot_z],
            device_id={"seq": seq_of(peer_z, xb, core)},
            device_id_type=mesh_id,
        )

    def ring_slot(a, slot, side, group, target_x, sem_side, src=None):
        return pltpu.make_async_remote_copy(
            src_ref=o_ref.at[a, slot, group, core] if src is None else src,
            dst_ref=o_ref.at[a, slot, group, core],
            send_sem=r_send.at[a, side, slot],
            recv_sem=r_recv.at[a, sem_side, slot],
            device_id={"seq": seq_of(za, target_x, core)},
            device_id_type=mesh_id,
        )

    def z_start(k, carry):
        peer_z = lax.rem(za + k, zs)
        for a in range(parts):
            z_copy(a, peer_z, za).start()
        return carry

    lax.fori_loop(1, zs, z_start, 0)
    for a in range(parts):
        ring_slot(a, za, 0, xb, right, 0, x_ref.at[a]).start()
        ring_slot(a, za, 1, xb, left, 1, x_ref.at[a]).start()

    def z_finish(k, carry):
        peer_z = lax.rem(za + k, zs)
        for a in range(parts):
            copy = z_copy(a, peer_z, peer_z)
            copy.wait_recv()
            ring_slot(a, peer_z, 0, xb, right, 0).start()
            ring_slot(a, peer_z, 1, xb, left, 1).start()
            copy.wait_send()
        return carry

    lax.fori_loop(1, zs, z_finish, 0)
    local.wait()

    def hand(a, group, slot):
        return pltpu.make_async_remote_copy(
            src_ref=o_ref.at[a, :, group, slot],
            dst_ref=o_ref.at[a, :, group, slot],
            send_sem=c_send.at[a, group],
            recv_sem=c_recv.at[a, group],
            device_id={"seq": seq_of(za, xb, 1 - core)},
            device_id_type=mesh_id,
        )

    across = []
    for a in range(parts):
        across.append(hand(a, xb, core))
        across[-1].start()

    far = lax.rem(xb + 2, xs)

    def relay(a, slot, group, target_x, src_group):
        return pltpu.make_async_remote_copy(
            src_ref=o_ref.at[a, slot, src_group, core],
            dst_ref=o_ref.at[a, slot, group, core],
            send_sem=f_send.at[a, slot],
            recv_sem=f_recv.at[a, slot],
            device_id={"seq": seq_of(za, target_x, core)},
            device_id_type=mesh_id,
        )

    for slot in range(zs):
        ring_slot(0, slot, 0, left, right, 0).wait_recv()
        relay(0, slot, left, right, left).start()
        ring_slot(1, slot, 1, right, left, 1).wait_recv()
        relay(1, slot, right, left, right).start()
    for slot in range(zs):
        ring_slot(1, slot, 0, left, right, 0).wait_recv()
        ring_slot(0, slot, 1, right, left, 1).wait_recv()
    for a in range(parts):
        for group in (left, right):
            across.append(hand(a, group, core))
            across[-1].start()
    for a in range(parts):
        for slot in range(zs):
            ring_slot(a, slot, 0, xb, right, 0).wait_send()
            ring_slot(a, slot, 1, xb, left, 1).wait_send()
    for slot in range(zs):
        relay(0, slot, far, right, left).wait_recv()
        relay(1, slot, far, left, right).wait_recv()
    for slot in range(zs):
        relay(0, slot, left, right, left).wait_send()
        relay(1, slot, right, left, right).wait_send()
    for a in range(parts):
        across.append(hand(a, far, core))
        across[-1].start()

    for copy in across:
        copy.wait_send()
    for a in range(parts):
        for g in range(xs):
            hand(a, g, 1 - core).wait_recv()


def seq_gather(stacked, n, cid):
    parts, rows, cols = stacked.shape
    chips = n // 2
    xs = 4
    zs = chips // xs
    return pl.pallas_call(
        functools.partial(seq_gather_kernel, zs, xs),
        out_shape=jax.ShapeDtypeStruct((parts, zs, xs, 2, rows, cols), stacked.dtype),
        in_specs=[pl.BlockSpec(memory_space=pl.ANY)],
        out_specs=pl.BlockSpec(memory_space=pl.ANY),
        scratch_shapes=[
            pltpu.SemaphoreType.DMA((parts, zs)),
            pltpu.SemaphoreType.DMA((parts, zs)),
            pltpu.SemaphoreType.DMA((parts, 2, zs)),
            pltpu.SemaphoreType.DMA((parts, 2, zs)),
            pltpu.SemaphoreType.DMA((parts, zs)),
            pltpu.SemaphoreType.DMA((parts, zs)),
            pltpu.SemaphoreType.DMA((parts, xs)),
            pltpu.SemaphoreType.DMA((parts, xs)),
            pltpu.SemaphoreType.DMA,
        ],
        compiler_params=pltpu.CompilerParams(collective_id=cid, has_side_effects=True),
    )(stacked)


def tp_gather_kernel(ys, x_ref, o_ref, p_send, p_recv, r_send, r_recv, f_send, f_recv, local_sem):
    me = lax.axis_index("tp")
    yy = me // 2
    zh = me % 2
    right = lax.rem(yy + 1, ys)
    left = lax.rem(yy + ys - 1, ys)
    far = lax.rem(yy + 2, ys)
    width = x_ref.shape[1]
    mesh_id = pl.DeviceIdType.MESH

    def cols(y, h):
        return pl.ds(pl.multiple_of((y * 2 + h) * width, 128), width)

    def pair(y):
        return pl.ds(pl.multiple_of(y * 2 * width, 128), 2 * width)

    def signal(target):
        pl.semaphore_signal(barrier, inc=1, device_id={"tp": target}, device_id_type=mesh_id)

    barrier = pltpu.get_barrier_semaphore()
    signal(yy * 2 + 1 - zh)
    signal(right * 2 + zh)
    signal(left * 2 + zh)
    pl.semaphore_wait(barrier, 3)

    local = pltpu.make_async_copy(x_ref, o_ref.at[:, cols(yy, zh)], local_sem)
    local.start()
    to_partner = pltpu.make_async_remote_copy(
        src_ref=x_ref,
        dst_ref=o_ref.at[:, cols(yy, zh)],
        send_sem=p_send,
        recv_sem=p_recv,
        device_id={"tp": yy * 2 + 1 - zh},
        device_id_type=mesh_id,
    )
    to_partner.start()

    def ring(src, h, group, target, side):
        return pltpu.make_async_remote_copy(
            src_ref=src,
            dst_ref=o_ref.at[:, cols(group, h)],
            send_sem=r_send.at[side, h],
            recv_sem=r_recv.at[side, h],
            device_id={"tp": target * 2 + zh},
            device_id_type=mesh_id,
        )

    outgoing = [ring(x_ref, zh, yy, right, 0), ring(x_ref, zh, yy, left, 1)]
    for copy in outgoing:
        copy.start()
    pltpu.make_async_remote_copy(
        src_ref=x_ref,
        dst_ref=o_ref.at[:, cols(yy, 1 - zh)],
        send_sem=p_send,
        recv_sem=p_recv,
        device_id={"tp": yy * 2 + 1 - zh},
        device_id_type=mesh_id,
    ).wait_recv()
    partner_src = o_ref.at[:, cols(yy, 1 - zh)]
    later = [ring(partner_src, 1 - zh, yy, right, 0), ring(partner_src, 1 - zh, yy, left, 1)]
    for copy in later:
        copy.start()
    local.wait()
    to_partner.wait_send()
    pieces = f_send.shape[1]
    span = x_ref.shape[0] // pieces

    def relay(group, h, target, side, c):
        rows = pl.ds(c * span, span)
        return pltpu.make_async_remote_copy(
            src_ref=o_ref.at[rows, cols(group, h)],
            dst_ref=o_ref.at[rows, cols(group, h)],
            send_sem=f_send.at[side, c],
            recv_sem=f_recv.at[side, c],
            device_id={"tp": target * 2 + zh},
            device_id_type=mesh_id,
        )

    relays = []
    ring(x_ref, 0, left, right, 0).wait_recv()
    for c in range(pieces):
        relays.append(relay(left, 0, right, 0, c))
        relays[-1].start()
    ring(x_ref, 1, right, left, 1).wait_recv()
    for c in range(pieces):
        relays.append(relay(right, 1, left, 1, c))
        relays[-1].start()
    ring(x_ref, 1, left, right, 0).wait_recv()
    ring(x_ref, 0, right, left, 1).wait_recv()
    for copy in outgoing + later:
        copy.wait_send()
    for c in range(pieces):
        relay(far, 0, right, 0, c).wait_recv()
        relay(far, 1, left, 1, c).wait_recv()
    for copy in relays:
        copy.wait_send()


def tp_gather(block, n, cid):
    rows, width = block.shape
    return pl.pallas_call(
        functools.partial(tp_gather_kernel, n // 2),
        out_shape=jax.ShapeDtypeStruct((rows, width * n), block.dtype),
        in_specs=[pl.BlockSpec(memory_space=pl.ANY)],
        out_specs=pl.BlockSpec(memory_space=pl.ANY),
        scratch_shapes=[
            pltpu.SemaphoreType.DMA,
            pltpu.SemaphoreType.DMA,
            pltpu.SemaphoreType.DMA((2, 2)),
            pltpu.SemaphoreType.DMA((2, 2)),
            pltpu.SemaphoreType.DMA((2, 4)),
            pltpu.SemaphoreType.DMA((2, 4)),
            pltpu.SemaphoreType.DMA,
        ],
        compiler_params=pltpu.CompilerParams(collective_id=cid, has_side_effects=True),
    )(block)


def project_kernel(x_ref, g_ref, wq_ref, wk_ref, wv_ref, cos_ref, sin_ref, q_ref, k_ref, v_ref, kv_ref):
    x = x_ref[...].astype(jnp.float32)
    mean_sq = jnp.mean(x * x, axis=1, keepdims=True)
    gain = g_ref[...].astype(jnp.float32).reshape(1, x.shape[1])
    normed = (x * lax.rsqrt(mean_sq + 1e-05) * gain).astype(jnp.bfloat16)
    cosine = cos_ref[...]
    sine = sin_ref[...]

    def rotated(values):
        half = values.shape[1] // 2
        return values * cosine + pltpu.roll(values, half, 1) * sine

    queries = jnp.dot(normed, wq_ref[...], preferred_element_type=jnp.float32)
    for h in range(queries.shape[1] // HEAD):
        q_ref[0, :, h * HEAD:(h + 1) * HEAD] = rotated(queries[:, h * HEAD:(h + 1) * HEAD]).astype(q_ref.dtype)
    keys = jnp.dot(normed, wk_ref[...], preferred_element_type=jnp.float32)
    for h in range(keys.shape[1] // HEAD):
        part = rotated(keys[:, h * HEAD:(h + 1) * HEAD]).astype(k_ref.dtype)
        k_ref[:, h * HEAD:(h + 1) * HEAD] = part
        kv_ref[0, :, h * HEAD:(h + 1) * HEAD] = part
    values = jnp.dot(normed, wv_ref[...], preferred_element_type=jnp.float32).astype(v_ref.dtype)
    v_ref[...] = values
    kv_ref[1] = values


def project(gathered, norm_gain, w_query, w_key, w_value, cosine, sine, block):
    rows, width = gathered.shape
    steps = rows // block
    q_width = w_query.shape[1]
    kv_width = w_key.shape[1]
    whole = lambda i: (0, 0)
    return pl.pallas_call(
        project_kernel,
        grid=(steps,),
        out_shape=(
            jax.ShapeDtypeStruct((steps, block, q_width), jnp.bfloat16),
            jax.ShapeDtypeStruct((rows, kv_width), jnp.bfloat16),
            jax.ShapeDtypeStruct((rows, kv_width), jnp.bfloat16),
            jax.ShapeDtypeStruct((2, rows, kv_width), jnp.bfloat16),
        ),
        in_specs=[
            pl.BlockSpec((block, width), lambda i: (i, 0)),
            pl.BlockSpec(memory_space=pltpu.VMEM),
            pl.BlockSpec((width, q_width), whole),
            pl.BlockSpec((width, kv_width), whole),
            pl.BlockSpec((width, kv_width), whole),
            pl.BlockSpec((block, HEAD), lambda i: (i, 0)),
            pl.BlockSpec((block, HEAD), lambda i: (i, 0)),
        ],
        out_specs=(
            pl.BlockSpec((1, block, q_width), lambda i: (i, 0, 0)),
            pl.BlockSpec((block, kv_width), lambda i: (i, 0)),
            pl.BlockSpec((block, kv_width), lambda i: (i, 0)),
            pl.BlockSpec((2, block, kv_width), lambda i: (0, i, 0)),
        ),
        compiler_params=pltpu.CompilerParams(vmem_limit_bytes=60 * 1024 * 1024),
    )(gathered, norm_gain, w_query, w_key, w_value, cosine, sine)


def attention_kernel(
    scale, group_pages,
    wants, page_order, s_idx, s_cnt,
    q_ref, q_meta,
    p_ref,
    s_ref, s_meta,
    o_ref, m_sc, l_sc, acc_sc, pm_sc, pl_sc, pacc_sc,
):
    prefixes, per_prefix = page_order.shape

    def update(m_ref, l_ref, acc_ref, score_list, value_list):
        run_max = m_ref[...]
        new_max = run_max
        for scores in score_list:
            new_max = jnp.maximum(new_max, jnp.max(scores, axis=1, keepdims=True))
        fade = jnp.exp(run_max - new_max)
        total = l_ref[...] * fade
        acc = acc_ref[...] * fade
        for scores, values in zip(score_list, value_list):
            weights = jnp.exp(scores - new_max)
            total = total + jnp.sum(weights, axis=1, keepdims=True)
            acc = acc + jnp.dot(weights.astype(jnp.bfloat16), values, preferred_element_type=jnp.float32)
        l_ref[...] = total
        acc_ref[...] = acc
        m_ref[...] = new_max

    for i in range(q_ref.shape[0]):
        m_sc[...] = jnp.full(m_sc.shape, -1e30, jnp.float32)
        l_sc[...] = jnp.zeros(l_sc.shape, jnp.float32)
        acc_sc[...] = jnp.zeros(acc_sc.shape, jnp.float32)
        heads = q_ref.shape[2] // q_ref.shape[1]
        size = q_ref.shape[1]
        query = jnp.concatenate([q_ref[i, :, h * size:(h + 1) * size] for h in range(heads)], axis=0)
        want = q_meta[0, i]
        req = q_meta[1, i]
        pos = q_meta[2, i]

        def score(keys):
            return lax.dot_general(
                query, keys, (((1,), (1,)), ((), ())), preferred_element_type=jnp.float32
            ) * scale

        for p in range(prefixes):
            @pl.when(wants[i, p] > 0)
            def _():
                pm_sc[...] = jnp.full(pm_sc.shape, -1e30, jnp.float32)
                pl_sc[...] = jnp.zeros(pl_sc.shape, jnp.float32)
                pacc_sc[...] = jnp.zeros(pacc_sc.shape, jnp.float32)

                def page_step(g, carry):
                    pages = [page_order[p, g * group_pages + j] for j in range(group_pages)]
                    blocks = [p_ref[b] for b in pages]
                    update(
                        pm_sc, pl_sc, pacc_sc,
                        [score(blk[:, :size]) for blk in blocks],
                        [blk[:, size:] for blk in blocks],
                    )
                    return carry

                lax.fori_loop(0, per_prefix // group_pages, page_step, 0)
                mine = want == p
                m_sc[...] = jnp.where(mine, pm_sc[...], m_sc[...])
                l_sc[...] = jnp.where(mine, pl_sc[...], l_sc[...])
                acc_sc[...] = jnp.where(mine, pacc_sc[...], acc_sc[...])

        def step(n, carry):
            b = s_idx[i, n]
            scores = score(s_ref[0, b])
            seen = (s_meta[0, b] == req) & (s_meta[1, b] <= pos)
            run_max = m_sc[...]
            new_max = jnp.maximum(
                run_max, jnp.max(jnp.where(seen, scores, -1e30), axis=1, keepdims=True)
            )
            weights = jnp.where(seen, jnp.exp(scores - new_max), 0.0)
            fade = jnp.exp(run_max - new_max)
            l_sc[...] = l_sc[...] * fade + jnp.sum(weights, axis=1, keepdims=True)
            acc_sc[...] = acc_sc[...] * fade + jnp.dot(
                weights.astype(jnp.bfloat16), s_ref[1, b], preferred_element_type=jnp.float32
            )
            m_sc[...] = new_max
            return carry

        lax.fori_loop(0, s_cnt[i], step, 0)
        result = (acc_sc[...] / l_sc[...]).astype(o_ref.dtype)
        for h in range(heads):
            o_ref[i, :, h * size:(h + 1) * size] = result[h * size:(h + 1) * size]


def block_attention(scale, lists, queries, query_meta, prefix_parts, suffix_parts):
    q_blocks, block_rows, q_width = queries.shape
    width = queries.shape[1]
    q_rows = q_width // width * block_rows
    smem = pl.BlockSpec(memory_space=pltpu.SMEM)
    vmem = pl.BlockSpec(memory_space=pltpu.VMEM)
    state = [
        pltpu.VMEM((q_rows, 1), jnp.float32),
        pltpu.VMEM((q_rows, 1), jnp.float32),
        pltpu.VMEM((q_rows, width), jnp.float32),
    ]
    return pl.pallas_call(
        functools.partial(attention_kernel, scale, 4),
        out_shape=jax.ShapeDtypeStruct((q_blocks, block_rows, q_width), jnp.bfloat16),
        in_specs=[smem] * 4 + [vmem] * 5,
        out_specs=vmem,
        scratch_shapes=state + state,
        compiler_params=pltpu.CompilerParams(vmem_limit_bytes=48 * 1024 * 1024),
    )(*lists, queries, *query_meta, *prefix_parts, *suffix_parts)


def visible_list(visible):
    count = visible.shape[1]
    ids = jnp.arange(count, dtype=jnp.int32)
    rank = jnp.sum((visible[:, :, None] & (ids[:, None] < ids[None, :])[None]).astype(jnp.int32), axis=1)
    pick = visible[:, None, :] & (rank[:, None, :] == ids[None, :, None])
    order = jnp.sum(jnp.where(pick, ids[None, None, :], 0), axis=2).astype(jnp.int32)
    return order, jnp.sum(visible.astype(jnp.int32), axis=1)


def body(
    seq_n,
    tp_n,
    hidden,
    norm_gain,
    w_query,
    w_key,
    w_value,
    prefix_keys,
    prefix_values,
    page_prefix,
    request_prefix,
    suffix_lengths,
    row_order,
):
    gathered_prefix = lax.all_gather(
        jnp.concatenate([prefix_keys, prefix_values], axis=1), "seq", axis=0, tiled=True
    )
    gathered = tp_gather(hidden, tp_n, 2)
    local_rows = gathered.shape[0]
    request_all, position_all, wanted_all = locate(row_order, suffix_lengths, request_prefix)
    offset = lax.axis_index("seq") * local_rows
    request = lax.dynamic_slice_in_dim(request_all, offset, local_rows)
    position = lax.dynamic_slice_in_dim(position_all, offset, local_rows)
    wanted = lax.dynamic_slice_in_dim(wanted_all, offset, local_rows)
    prefix_len = page_prefix.shape[0] * PAGE // PREFIXES
    rope_at = prefix_len + position
    q_heads = w_query.shape[1] // HEAD
    kv_heads = w_key.shape[1] // HEAD
    group_size = q_heads // kv_heads
    half_dim = HEAD // 2
    frequency = ROPE_BASE ** (-(jnp.arange(half_dim, dtype=jnp.float32) * 2.0 / HEAD))
    angles = rope_at.astype(jnp.float32)[:, None] * frequency[None, :]
    cosine = jnp.cos(angles)
    sine_part = jnp.sin(angles)
    cos_full = jnp.concatenate([cosine, cosine], axis=1)
    sin_signed = jnp.concatenate([-sine_part, sine_part], axis=1)
    stacked_q, new_keys, new_values, stacked_kv = project(
        gathered, norm_gain, w_query, w_key, w_value, cos_full, sin_signed, PAGE
    )
    score_scale = 1.0 / math.sqrt(HEAD)
    block = PAGE
    q_blocks = local_rows // block
    pages = page_prefix.shape[0]
    runs = row_order.shape[0] // block

    def per_query(values):
        kinds = values.shape[0]
        spread = jnp.broadcast_to(values.reshape(kinds, q_blocks, 1, block), (kinds, q_blocks, group_size, block))
        return spread.reshape(kinds, q_blocks, group_size * block, 1).astype(jnp.int32)

    query_meta = (per_query(jnp.stack([wanted, request + PREFIXES, position])),)
    want_blocks = wanted.reshape(q_blocks, block)
    block_wants = jnp.any(
        want_blocks[:, :, None] == jnp.arange(PREFIXES, dtype=jnp.int32)[None, None, :], axis=1
    )
    page_ids = jnp.arange(pages, dtype=jnp.int32)
    same = (page_prefix[:, None] == page_prefix[None, :]) & (page_ids[:, None] < page_ids[None, :])
    page_rank = jnp.sum(same.astype(jnp.int32), axis=0)
    per_prefix = pages // PREFIXES
    pick = (page_prefix[None, None, :] == jnp.arange(PREFIXES, dtype=jnp.int32)[:, None, None]) & (
        page_rank[None, None, :] == jnp.arange(per_prefix, dtype=jnp.int32)[None, :, None]
    )
    page_order = jnp.sum(jnp.where(pick, page_ids[None, None, :], 0), axis=2).astype(jnp.int32)
    local_place = lax.dynamic_slice_in_dim(row_order, offset, local_rows).reshape(q_blocks, block)
    first_seen = jnp.min(local_place - position.reshape(q_blocks, block), axis=1)
    last_seen = jnp.max(local_place, axis=1)
    run_place = row_order.reshape(runs, block)
    run_low = jnp.min(run_place, axis=1)
    run_high = jnp.max(run_place, axis=1)
    run_visible = (run_low[None, :] <= last_seen[:, None]) & (run_high[None, :] >= first_seen[:, None])
    s_idx, s_cnt = visible_list(run_visible)

    seq_n_blocks = seq_n
    prefix_parts = (gathered_prefix.reshape(pages, block, 2 * HEAD),)
    gathered_suffix = seq_gather(stacked_kv, seq_n_blocks, 1)
    suffix_parts = (
        gathered_suffix.reshape(2, runs, block, HEAD),
        jnp.stack([request_all + PREFIXES, position_all]).reshape(2, runs, 1, block).astype(jnp.int32),
    )
    out = block_attention(
        score_scale, (block_wants.astype(jnp.int32), page_order, s_idx, s_cnt), stacked_q, query_meta, prefix_parts, suffix_parts
    )
    attended = out.reshape(local_rows, group_size * HEAD)
    return (attended, new_keys, new_values)


def solution(mesh):
    return jax.shard_map(
        functools.partial(body, mesh.shape["seq"], mesh.shape["tp"]),
        mesh=mesh,
        in_specs=(
            P("seq", "tp"),
            P(),
            P(None, "tp"),
            P(None, "tp"),
            P(None, "tp"),
            P("seq", "tp"),
            P("seq", "tp"),
            P(),
            P(),
            P(),
            P(),
        ),
        out_specs=(P("seq", "tp"), P("seq", "tp"), P("seq", "tp")),
        check_vma=False,
    )
```
